32 devices in a mesh: grp: 4 (over y, core), tok: 8 (over z, x).
Axes of the slice: x: 2, y: 2, z: 4, core: 2. Of those that a mesh axis runs over, the one named last changes fastest.
Arguments:
- tokens: bfloat16 [8192, 960], P(('grp', 'tok')), may hold values from -6 to 6
- w_query: bfloat16 [960, 960], P('tok'), may hold values from -0.1875 to 0.1875
- w_key: bfloat16 [960, 320], P('tok'), may hold values from -0.1875 to 0.1875
- w_value: bfloat16 [960, 320], P('tok'), may hold values from -0.1875 to 0.1875
- w_out: bfloat16 [960, 960], P('tok'), may hold values from -0.75 to 0.75
- w_gate: bfloat16 [960, 2560], P('tok'), may hold values from -0.1875 to 0.1875
- w_up: bfloat16 [960, 2560], P('tok'), may hold values from -0.1875 to 0.1875
- w_down: bfloat16 [2560, 960], P('tok'), may hold values from -0.125 to 0.125
- router: bfloat16 [960, 3], P('tok'), may hold values from -0.1875 to 0.1875
- norm_attn: bfloat16 [960], P('tok'), may hold values from 0.5 to 1.5
- norm_ffn: bfloat16 [960], P('tok'), may hold values from 0.5 to 1.5
- lengths: int32 [4, 2], P('grp'), may hold values from 1 to 1536, 2048 in all within a row
- depths: int32 [8192], P(('grp', 'tok')), may hold values from 1 to 3, as said below
- padding: int32 [8192], P(('grp', 'tok')), may hold values from 0 to 1
- cotangent: bfloat16 [8192, 960], P(('grp', 'tok')), may hold values from -6 to 6
Outputs:
- block_out: bfloat16 [8192, 960], P(('grp', 'tok'))
- grad_tokens: bfloat16 [8192, 960], P(('grp', 'tok'))
- grad_query: float32 [960, 960], P('tok')
- grad_key: float32 [960, 320], P('tok')
- grad_value: float32 [960, 320], P('tok')
- grad_out: float32 [960, 960], P('tok')
- grad_gate: float32 [960, 2560], P('tok')
- grad_up: float32 [960, 2560], P('tok')
- grad_down: float32 [2560, 960], P('tok')
- grad_router: float32 [960, 3], P('tok')
- grad_norm_attn: float32 [960], P('tok')
- grad_norm_ffn: float32 [960], P('tok')
The draws below stay inside these ranges and needn't reach their ends.
Inputs may be any that keep to these rules, and one draw needn't show every extreme that they name: Each row gives the lengths of the consecutive documents of one group of 2048 tokens and sums to 2048; the longest is at most 1536. `depths`: at most 192 tokens of one pack of 256 have padding 1 and depth 2 or more, and in each group one pack has exactly 192.
All inputs are finite; a program needn't handle non-finite values.
Results may differ from the reference program's by a relative error of at most 0.03.
Values may be sent and summed in bfloat16 or wider, within the bound.
A program may use at most 256 MiB of HBM per device.

```python
import math
import jax
import jax.numpy as jnp
import numpy as np
from jax import lax

D = 960
HEADS = 15
KV_HEADS = 5
HD = 64
FF = 2560
RECS = 3
TOK_DEV = 256
ROUTE_DEV = 192
GROUPS = 4
GROUP_TOK = 2048
DOCS = 2
DOC_MOST = 1536
PACKS = 32
TOKENS = 8192


def routing_draw(key):
    base = jax.random.fold_in(key, 7919)
    streams = jax.random.split(base, 5)
    per_group = GROUP_TOK // TOK_DEV
    groups = PACKS // per_group
    levels = jax.random.randint(streams[0], (PACKS, 1), 3, 9)
    chosen = jax.random.randint(streams[1], (groups, 1), 0, per_group)
    forced = (jnp.arange(per_group, dtype=jnp.int32)[None, :] == chosen).reshape(PACKS, 1)
    levels = jnp.where(forced, 8, levels)
    deep = jax.random.randint(streams[2], (PACKS, TOK_DEV), 0, 8) < levels
    padding = jnp.where(forced, 1, (jax.random.randint(streams[3], (PACKS, TOK_DEV), 0, 8) < 7).astype(jnp.int32))
    extra = jax.random.randint(streams[4], (PACKS, TOK_DEV), 0, 2)
    eligible = deep & (padding > 0)
    ranking = jnp.cumsum(eligible.astype(jnp.int32), axis=1)
    deep = deep & ((ranking <= ROUTE_DEV) | (padding == 0))
    depths = jnp.where(deep, 2 + extra, 1)
    return (depths.reshape(TOKENS).astype(jnp.int32), padding.reshape(TOKENS).astype(jnp.int32))


def draw_depths(key, part):
    return routing_draw(key)[0]


def draw_padding(key, part):
    return routing_draw(key)[1]


def shard_levels(own_key, shape, cuts, smallest, high):
    level = 1.0
    for axis_at, blocks in cuts:
        steps = jax.random.uniform(jax.random.fold_in(jax.random.fold_in(own_key, 6), axis_at), (blocks,), jnp.float32, smallest / len(cuts), high / len(cuts))
        level = level * jnp.repeat(jnp.exp(steps), shape[axis_at] // blocks).reshape((-1,) + (1,) * (len(shape) - 1 - axis_at))
    return level


def profile(amount, total, bound, skew):
    portions = [(1 << 20) // math.isqrt(standing ** skew) + 1 for standing in range(2, amount + 1)]
    rest, holding = total - bound - (amount - 1), [1] * (amount - 1)
    while rest > 0:
        movable = [i for i in range(amount - 1) if holding[i] < bound]
        pool, left = sum([portions[i] for i in movable]), rest
        for i in movable:
            addition = min(bound - holding[i], max(1, left * portions[i] // pool), rest)
            holding[i] = holding[i] + addition
            rest = rest - addition
    return np.array([bound] + holding)


def ragged(own_key, count, total, bound, slope):
    if count == 2:
        one = jax.random.randint(own_key, (), max(1, total - bound), min(bound, total - 1) + 1)
        return jnp.stack([one, total - one])
    sizes = jnp.asarray(profile(count, total, bound, slope), jnp.int32)
    pairs = (count - 1) // 2
    giver, sink = sizes[1:1 + 2 * pairs:2], sizes[2:2 + 2 * pairs:2]
    room = jnp.minimum(giver - 1, bound - sink)
    passed = jax.random.randint(jax.random.fold_in(own_key, 1), (pairs,), 0, 1 << 20) % (room + 1)
    sizes = sizes.at[1:1 + 2 * pairs:2].set(giver - passed).at[2:2 + 2 * pairs:2].set(sink + passed)
    return sizes[jax.random.permutation(jax.random.fold_in(own_key, 2), count)]


def gaussian(stream_key, extent, scale, bound, cuts=(), held_as=jnp.bfloat16):
    drawn = scale * jax.random.normal(stream_key, extent, jnp.float32)
    if cuts:
        drawn = drawn * shard_levels(stream_key, extent, cuts, -0.22, 0.18)
    return jnp.clip(drawn, -bound, bound).astype(held_as)


def setup_inputs(seed: int = 0) -> dict:
    seeds = jax.random.split(jax.random.key(seed), 16)
    tokens = gaussian(seeds[0], (TOKENS, D), 1.0, 6.0, ((0, 32),))
    w_query = gaussian(seeds[1], (D, HEADS * HD), D ** -0.5, 0.1875, ((0, 8),))
    w_key = gaussian(seeds[2], (D, KV_HEADS * HD), D ** -0.5, 0.1875, ((0, 8),))
    w_value = gaussian(seeds[3], (D, KV_HEADS * HD), D ** -0.5, 0.1875, ((0, 8),))
    w_out = gaussian(seeds[4], (HEADS * HD, D), (HEADS * HD // 16) ** -0.5, 0.75, ((0, 8),))
    w_gate = gaussian(seeds[5], (D, FF), D ** -0.5, 0.1875, ((0, 8),))
    w_up = gaussian(seeds[6], (D, FF), D ** -0.5, 0.1875, ((0, 8),))
    w_down = gaussian(seeds[7], (FF, D), FF ** -0.5, 0.125, ((0, 8),))
    router = gaussian(seeds[8], (D, RECS), D ** -0.5, 0.1875, ((0, 8),))
    norm_attn = jnp.clip(1.0 + 0.1 * jax.random.normal(seeds[9], (D,), jnp.float32), 0.5, 1.5).astype(jnp.bfloat16)
    norm_ffn = jnp.clip(1.0 + 0.1 * jax.random.normal(seeds[10], (D,), jnp.float32), 0.5, 1.5).astype(jnp.bfloat16)
    lengths = jax.vmap(lambda own: ragged(own, DOCS, GROUP_TOK, DOC_MOST, 1))(jax.random.split(seeds[11], GROUPS)).reshape((GROUPS, DOCS)).astype(jnp.int32)
    depths = draw_depths(jax.random.fold_in(seeds[15], 71), 0)
    padding = draw_padding(jax.random.fold_in(seeds[15], 71), 0)
    cotangent = gaussian(seeds[14], (TOKENS, D), 1.0, 6.0, ((0, 32),))
    return {"tokens": tokens, "w_query": w_query, "w_key": w_key, "w_value": w_value, "w_out": w_out, "w_gate": w_gate, "w_up": w_up, "w_down": w_down, "router": router, "norm_attn": norm_attn, "norm_ffn": norm_ffn, "lengths": lengths, "depths": depths, "padding": padding, "cotangent": cotangent}


@jax.custom_vjp
def low(v):
    return lax.optimization_barrier(v.astype(jnp.bfloat16)).astype(jnp.float32)

@jax.custom_vjp
def low_back(v):
    return v

def low_keep(v):
    return (low(v), None)

def low_pass(kept, grad):
    return (grad,)

def back_keep(v):
    return (v, None)

def back_low(kept, grad):
    return (low(grad),)
low.defvjp(low_keep, low_pass)
low_back.defvjp(back_keep, back_low)

def positions(length_row, first, count):
    doc_ends = jnp.cumsum(length_row).astype(jnp.int32)
    starts = (doc_ends - length_row).astype(jnp.int32)
    indices = (first + jnp.arange(count, dtype=jnp.int32)).astype(jnp.int32)
    doc_ids = lax.optimization_barrier(jnp.sum((indices[:, None] >= doc_ends[None, :]).astype(jnp.int32), axis=1)).astype(jnp.int32)
    onehot = doc_ids[:, None] == jnp.arange(length_row.shape[0], dtype=jnp.int32)[None, :]
    begin = lax.optimization_barrier(jnp.sum(jnp.where(onehot, starts[None, :], 0), axis=1)).astype(jnp.int32)
    return (indices, doc_ids, (indices - begin).astype(jnp.int32))

def normalize(state, gain):
    return state * lax.rsqrt(lax.optimization_barrier(jnp.mean(state * state, axis=-1, keepdims=True)) + 1e-05) * gain

def rotate(values, cosine_part, sine_part):
    half = values.shape[-1] // 2
    lower = values[..., :half]
    upper = values[..., half:]
    return jnp.concatenate([lower * cosine_part - upper * sine_part, upper * cosine_part + lower * sine_part], axis=-1)

def turning(places):
    freqs = 10000.0 ** (-(jnp.arange(HD // 2, dtype=jnp.float32) * 2.0 / HD))
    angles = places.astype(jnp.float32)[:, None] * freqs[None, :]
    return (jnp.cos(angles)[:, None, :], jnp.sin(angles)[:, None, :])

def project(state, w_query, w_key, w_value, norm_attn, cosine_part, sine_part, precision):
    count = state.shape[0]
    norm_one = low(normalize(state, norm_attn))
    query = low(rotate(low_back(jnp.dot(norm_one, w_query, precision=precision)).reshape(count, HEADS, HD), cosine_part, sine_part))
    keys = low(rotate(low_back(jnp.dot(norm_one, w_key, precision=precision)).reshape(count, KV_HEADS, HD), cosine_part, sine_part))
    values = low(low_back(jnp.dot(norm_one, w_value, precision=precision))).reshape(count, KV_HEADS, HD)
    return (query, keys, values)

def finish(state, mixed, w_out, w_gate, w_up, w_down, router, norm_ffn, recursion, active, precision):
    attended = low_back(jnp.dot(mixed, w_out, precision=precision))
    middle = state + attended
    norm_two = low(normalize(middle, norm_ffn))
    gated = low_back(jnp.dot(norm_two, w_gate, precision=precision))
    upward = low_back(jnp.dot(norm_two, w_up, precision=precision))
    hidden = low(jax.nn.silu(gated) * upward)
    fed = low_back(jnp.dot(hidden, w_down, precision=precision))
    gate = jax.nn.sigmoid(jnp.dot(state, router[:, recursion], precision=lax.Precision.HIGHEST))
    scale = active.astype(jnp.float32) * gate
    return state + scale[:, None] * (attended + fed)

def recurse(state, weights, recursion, orders, doc_ids, places, depths, padding):
    w_query, w_key, w_value, w_out, w_gate, w_up, w_down, router, norm_attn, norm_ffn = weights
    count = state.shape[0]
    highest = lax.Precision.HIGHEST
    cosine_part, sine_part = turning(places)
    active = (depths > recursion) & (padding > 0)
    query, keys, values = project(state, w_query, w_key, w_value, norm_attn, cosine_part, sine_part, highest)
    blocks = count // 512
    grouped = query.reshape(blocks, 512, KV_HEADS, HEADS // KV_HEADS, HD)

    def attend_block(inputs):
        query_block, order_block, doc_block = inputs
        scores = low_back(jnp.einsum('tkgd,ukd->kgtu', query_block, keys, precision=highest) * HD ** (-0.5))
        allowed = (doc_block[:, None] == doc_ids[None, :]) & (orders[None, :] <= order_block[:, None]) & active[None, :]
        allowed = allowed | (orders[None, :] == order_block[:, None])
        scores = jnp.where(allowed[None, None], scores, -1e+30)
        largest = lax.optimization_barrier(jnp.max(scores, axis=-1, keepdims=True))
        expos = jnp.exp(scores - largest)
        probs = low(expos / lax.optimization_barrier(jnp.sum(expos, axis=-1, keepdims=True)))
        return jnp.einsum('kgtu,ukd->tkgd', probs, values, precision=highest)
    mixed = lax.map(jax.checkpoint(attend_block), (grouped, orders.reshape(blocks, 512), doc_ids.reshape(blocks, 512)))
    mixed = low(low_back(mixed.reshape(count, HEADS * HD)))
    return finish(state, mixed, w_out, w_gate, w_up, w_down, router, norm_ffn, recursion, active, highest)

def run_group(block_in, weights, length_row, depth_row, pad_row):
    orders, doc_ids, places = positions(length_row, 0, block_in.shape[0])
    state = block_in
    for recursion in range(RECS):
        state = recurse(state, weights, recursion, orders, doc_ids, places, depth_row, pad_row)
    return state

def reference(tokens, w_query, w_key, w_value, w_out, w_gate, w_up, w_down, router, norm_attn, norm_ffn, lengths, depths, padding, cotangent):
    weights = tuple((matrix.astype(jnp.float32) for matrix in (w_query, w_key, w_value, w_out, w_gate, w_up, w_down, router, norm_attn, norm_ffn)))
    inputs = tokens.astype(jnp.float32).reshape(GROUPS, GROUP_TOK, D)
    depth_rows = depths.reshape(GROUPS, GROUP_TOK)
    pad_rows = padding.reshape(GROUPS, GROUP_TOK)

    def forward(inputs, weights):

        def advance(running, element):
            block_in, length_row, depth_row, pad_row = element
            return (running, jax.checkpoint(run_group)(block_in, weights, length_row, depth_row, pad_row))
        unused, outputs = lax.scan(advance, jnp.zeros((), jnp.float32), (inputs, lengths, depth_rows, pad_rows))
        return outputs
    result, pullback = jax.vjp(forward, inputs, weights)
    grad_in, grad_weights = pullback(cotangent.astype(jnp.float32).reshape(GROUPS, GROUP_TOK, D))
    return (result.reshape(TOKENS, D).astype(jnp.bfloat16), grad_in.reshape(TOKENS, D).astype(jnp.bfloat16), grad_weights[0], grad_weights[1], grad_weights[2], grad_weights[3], grad_weights[4], grad_weights[5], grad_weights[6], grad_weights[7], grad_weights[8], grad_weights[9])
```

```python
import functools

import jax
import jax.numpy as jnp
from jax import lax
from jax.experimental import pallas as pl
from jax.experimental.pallas import tpu as pltpu
from jax.sharding import PartitionSpec as P

HEADS = 15
KV_HEADS = 5
SHARES = HEADS // KV_HEADS
HD = 64
RECS = 3
EPS = 1e-05
BF = jnp.bfloat16
F32 = jnp.float32
BIG = -1e30
AXES = ("grp", "tok")


class Topo:
    def __init__(self, groups, spread):
        self.G = groups
        self.T = spread
        self.X = spread // groups
        self.Z = groups
        self.Y = groups // 2
        self.bits = {
            "z": self.Z.bit_length() - 1,
            "x": self.X.bit_length() - 1,
            "y": self.Y.bit_length() - 1,
            "c": 1,
        }

    def keys(self, dim):
        return [(dim, k) for k in range(self.bits[dim])]

    def masks(self, key):
        dim, k = key
        if dim == "c":
            return (1, 0)
        if dim == "y":
            return (2 << k, 0)
        if dim == "x":
            return (0, 1 << k)
        return (0, self.X << k)

    def pairs(self, key):
        mg, mt = self.masks(key)
        return [
            (g * self.T + t, (g ^ mg) * self.T + (t ^ mt))
            for g in range(self.G)
            for t in range(self.T)
        ]

    def swap_pairs(self):
        out = []
        for g in range(self.G):
            for t in range(self.T):
                z, x = t // self.X, t % self.X
                out.append((g * self.T + t, z * self.T + g * self.X + x))
        return out

    def bit(self, key):
        mg, mt = self.masks(key)
        if mg:
            return (lax.axis_index("grp") // mg) % 2
        return (lax.axis_index("tok") // mt) % 2


def exchange(topo, arr, key):
    return lax.ppermute(arr, AXES, topo.pairs(key))


def double(topo, arr, key, axis, stack):
    other = exchange(topo, arr, key)
    mine_is_high = topo.bit(key) == 1
    low = jnp.where(mine_is_high, other, arr)
    high = jnp.where(mine_is_high, arr, other)
    if stack:
        return jnp.stack([low, high], axis=axis)
    return jnp.concatenate([low, high], axis=axis)


def halve(topo, arr, key, axis, stack):
    mine_is_high = topo.bit(key) == 1
    if stack:
        low = lax.index_in_dim(arr, 0, axis, keepdims=False)
        high = lax.index_in_dim(arr, 1, axis, keepdims=False)
    else:
        half = arr.shape[axis] // 2
        low = lax.slice_in_dim(arr, 0, half, axis=axis)
        high = lax.slice_in_dim(arr, half, 2 * half, axis=axis)
    send = jnp.where(mine_is_high, low, high).astype(BF)
    keep = jnp.where(mine_is_high, high, low).astype(F32)
    return (keep + exchange(topo, send, key).astype(F32)).astype(BF)


def canonical(topo):
    return list(reversed(topo.keys("z"))) + list(reversed(topo.keys("x")))


def gather_rows(topo, shard, axis, order):
    me = lax.axis_index("grp")
    part = (me % 2) * topo.Y + me // 2
    pieces = jnp.stack(jnp.split(shard, topo.G, axis=axis), axis=0)
    arr = lax.dynamic_index_in_dim(pieces, part, 0, keepdims=False)
    held = []
    names = canonical(topo)
    for key in order:
        if key[0] in ("z", "x"):
            place = sum(1 for h in held if names.index(h) < names.index(key))
            arr = double(topo, arr, key, place, True)
            held.append(key)
        else:
            arr = double(topo, arr, key, axis - 2, False)
    return arr.reshape((topo.T,) + arr.shape[-2:])


def scatter_rows(topo, arr, axis, order):
    names = canonical(topo)
    held = list(names)
    arr = arr.reshape((2,) * len(names) + arr.shape[-2:])
    for key in order:
        if key[0] in ("z", "x"):
            arr = halve(topo, arr, key, held.index(key), True)
            held.remove(key)
        else:
            arr = halve(topo, arr, key, axis - 2, False)
    for key in topo.keys("y") + topo.keys("c"):
        arr = double(topo, arr, key, axis - 2, False)
    return arr


def group_order(topo):
    return list(reversed(topo.keys("y"))) + topo.keys("c") + list(reversed(topo.keys("x")))


def group_gather(topo, arr, order):
    names = group_order(topo)
    held = []
    shape = arr.shape
    for key in order:
        place = sum(1 for h in held if names.index(h) < names.index(key))
        arr = double(topo, arr, key, place, True)
        held.append(key)
    return arr.reshape((topo.T,) + shape)


def group_scatter(topo, arr, order):
    names = group_order(topo)
    held = list(names)
    arr = arr.reshape((2,) * len(names) + arr.shape[1:])
    for key in order:
        arr = halve(topo, arr, key, held.index(key), True)
        held.remove(key)
    return arr


def fill_bias(bias, key_ref, query_ref, rows, first, last):
    def body(t, carry):
        at = pl.ds(pl.multiple_of(t * rows, rows), rows)
        keys = key_ref[at, :]
        live, order = keys[:, 0:1], keys[:, 1:2]
        begin, place = query_ref[0:1, :], query_ref[1:2, :]
        allowed = ((live >= begin) & (live <= place)) | (order == place)
        bias[at, :] = jnp.where(allowed, 0.0, BIG)
        return carry

    lax.fori_loop(first, last, body, 0)


NT = (((1,), (1,)), ((), ()))
TN = (((0,), (0,)), ((), ()))


def attend_kernel(rows, span, key_ref, query_ref, kv_ref, q_ref, out_ref, stat_ref, bias, held):
    first, last = span[0], span[1]

    @pl.when(pl.program_id(0) == 0)
    def _():
        fill_bias(bias, key_ref, query_ref, rows, first, last)

    wide = q_ref.shape[1]
    queries = q_ref[0]

    def scores(t, top):
        at = pl.ds(pl.multiple_of(t * rows, rows), rows)
        s = lax.dot_general(kv_ref[at, :], queries, NT, preferred_element_type=F32) + bias[at, :]
        held[at, :] = s
        return jnp.maximum(top, jnp.max(s.reshape(rows // 8, 8, wide), axis=0))

    top = lax.fori_loop(first, last, scores, jnp.full((8, wide), BIG, F32))
    top = jnp.max(top, axis=0, keepdims=True)

    out_ref[0] = jnp.zeros(out_ref.shape[1:], F32)

    def mix(t, total):
        at = pl.ds(pl.multiple_of(t * rows, rows), rows)
        p = jnp.exp(held[at, :] - top)
        out_ref[0] += lax.dot_general(
            kv_ref[at, :], p.astype(BF), TN, preferred_element_type=F32
        )
        return total + jnp.sum(p.reshape(rows // 8, 8, wide), axis=0)

    total = lax.fori_loop(first, last, mix, jnp.zeros((8, wide), F32))
    total = jnp.sum(total, axis=0, keepdims=True)
    out_ref[0] = out_ref[0] / total
    stat_ref[0] = jnp.broadcast_to(top + jnp.log(total), (8, wide))


def attend(rows, span, key_labels, query_labels, kv_all, q_pad):
    count = kv_all.shape[0]
    wide = q_pad.shape[1]
    fixed = lambda h, s: (0, 0)
    return pl.pallas_call(
        functools.partial(attend_kernel, rows),
        grid_spec=pltpu.PrefetchScalarGridSpec(
            num_scalar_prefetch=1,
            grid=(KV_HEADS,),
            in_specs=[
                pl.BlockSpec((count, 8), fixed),
                pl.BlockSpec((8, wide), fixed),
                pl.BlockSpec((count, 2 * HD), lambda h, s: (0, h)),
                pl.BlockSpec((1, wide, 2 * HD), lambda h, s: (h, 0, 0)),
            ],
            out_specs=[
                pl.BlockSpec((1, 2 * HD, wide), lambda h, s: (h, 0, 0)),
                pl.BlockSpec((1, 8, wide), lambda h, s: (h, 0, 0)),
            ],
            scratch_shapes=[pltpu.VMEM((count, wide), F32), pltpu.VMEM((count, wide), F32)],
        ),
        out_shape=[
            jax.ShapeDtypeStruct((KV_HEADS, 2 * HD, wide), F32),
            jax.ShapeDtypeStruct((KV_HEADS, 8, wide), F32),
        ],
        compiler_params=pltpu.CompilerParams(vmem_limit_bytes=62 << 20),
        cost_estimate=pl.CostEstimate(
            flops=8 * KV_HEADS * wide * count * HD,
            bytes_accessed=2 * count * 2 * HD * KV_HEADS + 8 * KV_HEADS * wide * HD * 2,
            transcendentals=KV_HEADS * wide * count,
        ),
        name="attend",
    )(span, key_labels, query_labels, kv_all, q_pad)


def attend_back_kernel(
    rows, span, key_ref, query_ref, kv_ref, q_ref, stat_ref, delta_ref, dq_ref, dkv_ref, bias
):
    first, last = span[0], span[1]

    @pl.when(pl.program_id(0) == 0)
    def _():
        fill_bias(bias, key_ref, query_ref, rows, first, last)

    queries = q_ref[0]
    stat = stat_ref[0, 0:1, :]
    delta = delta_ref[0, 0:1, :]
    dkv_ref[...] = jnp.zeros(dkv_ref.shape, BF)
    dq_ref[0] = jnp.zeros(dq_ref.shape[1:], F32)
    low = lax.broadcasted_iota(jnp.int32, (rows, 2 * HD), 1) < HD

    def body(t, carry):
        at = pl.ds(pl.multiple_of(t * rows, rows), rows)
        kv = kv_ref[at, :]
        zero = jnp.zeros_like(kv)
        s = lax.dot_general(jnp.where(low, kv, zero), queries, NT, preferred_element_type=F32)
        p = jnp.exp(s + bias[at, :] - stat)
        dp = lax.dot_general(jnp.where(low, zero, kv), queries, NT, preferred_element_type=F32)
        ds = (p * (dp - delta)).astype(BF)
        dk = jnp.dot(ds, queries, preferred_element_type=F32)
        dv = jnp.dot(p.astype(BF), queries, preferred_element_type=F32)
        dkv_ref[at, :] = jnp.where(low, dk, dv).astype(BF)
        dq_ref[0] += lax.dot_general(kv, ds, TN, preferred_element_type=F32)
        return carry

    lax.fori_loop(first, last, body, 0)


def attend_back(rows, span, key_labels, query_labels, kv_all, q_do, stat, delta):
    count = kv_all.shape[0]
    wide = q_do.shape[1]
    fixed = lambda h, s: (0, 0)
    head = lambda h, s: (h, 0, 0)
    return pl.pallas_call(
        functools.partial(attend_back_kernel, rows),
        grid_spec=pltpu.PrefetchScalarGridSpec(
            num_scalar_prefetch=1,
            grid=(KV_HEADS,),
            in_specs=[
                pl.BlockSpec((count, 8), fixed),
                pl.BlockSpec((8, wide), fixed),
                pl.BlockSpec((count, 2 * HD), lambda h, s: (0, h)),
                pl.BlockSpec((1, wide, 2 * HD), head),
                pl.BlockSpec((1, 8, wide), head),
                pl.BlockSpec((1, 8, wide), head),
            ],
            out_specs=[
                pl.BlockSpec((1, 2 * HD, wide), head),
                pl.BlockSpec((count, 2 * HD), lambda h, s: (0, h)),
            ],
            scratch_shapes=[pltpu.VMEM((count, wide), F32)],
        ),
        out_shape=[
            jax.ShapeDtypeStruct((KV_HEADS, 2 * HD, wide), F32),
            jax.ShapeDtypeStruct((count, KV_HEADS * 2 * HD), BF),
        ],
        compiler_params=pltpu.CompilerParams(vmem_limit_bytes=62 << 20),
        cost_estimate=pl.CostEstimate(
            flops=20 * KV_HEADS * wide * count * HD,
            bytes_accessed=4 * count * 2 * HD * KV_HEADS + 8 * KV_HEADS * wide * HD * 2,
            transcendentals=KV_HEADS * wide * count,
        ),
        name="attend_back",
    )(span, key_labels, query_labels, kv_all, q_do, stat, delta)


def mm(a, b):
    return jnp.dot(a, b, preferred_element_type=F32)


def mm_nt(a, b):
    return lax.dot_general(a, b, NT, preferred_element_type=F32)


def mm_tn(a, b):
    return lax.dot_general(a, b, TN, preferred_element_type=F32)


def inverse_rms(v):
    return lax.rsqrt(jnp.mean(v * v, axis=-1, keepdims=True) + EPS)


def norm_back(grad, v, inv, gain):
    scaled = grad * gain
    dot = jnp.mean(scaled * v, axis=-1, keepdims=True)
    return (inv * scaled - v * (inv * inv * inv * dot), jnp.sum(grad * v * inv, axis=0))


def turn(values, cosine, sine):
    half = HD // 2
    lower, upper = values[..., :half], values[..., half:]
    return jnp.concatenate(
        [lower * cosine - upper * sine, upper * cosine + lower * sine], axis=-1
    )


def heads_first(v):
    n = v.shape[0]
    return v.reshape(n, HEADS, HD).transpose(1, 0, 2)


def heads_back(v):
    n = v.shape[-1] // SHARES
    return v.reshape(KV_HEADS, HD, SHARES, n).transpose(3, 0, 2, 1).reshape(n, HEADS, HD)


def pair_up(q, d):
    n = q.shape[1]
    return jnp.concatenate([q, d], axis=-1).reshape(KV_HEADS, SHARES * n, 2 * HD)


def per_device(topo, *args):
    (tokens, w_query, w_key, w_value, w_out, w_gate, w_up, w_down, router, norm_attn, norm_ffn,
     lengths, depths, padding, cotangent) = args
    rows, model = tokens.shape
    kv_cols = w_key.shape[1]
    ff = w_gate.shape[1]
    shard = w_query.shape[0]
    deep_rows = rows * 3 // 4
    zk, xk, yk, ck = (topo.keys(d) for d in "zxyc")
    zdown = list(reversed(zk))

    order_a = zdown + xk + yk + ck
    order_b = zdown + yk + xk if False else zdown + xk + yk + ck
    small = jnp.concatenate(
        [router, norm_attn[:, None], norm_ffn[:, None]], axis=1
    )
    small = jnp.pad(small, ((0, 0), (0, HD - small.shape[1])))
    w_kv = jnp.stack(
        [w_key.reshape(shard, KV_HEADS, HD), w_value.reshape(shard, KV_HEADS, HD)], axis=2
    ).reshape(shard, 2 * kv_cols)
    first = jnp.concatenate([w_query, small, w_kv], axis=1)
    first = jnp.pad(first, ((0, 0), (0, -first.shape[1] % (128 * topo.G))))
    second = jnp.concatenate([w_gate, w_up, w_out], axis=1)
    second = jnp.pad(second, ((0, 0), (0, -second.shape[1] % (128 * topo.G))))
    all_first = gather_rows(topo, first, 1, order_a).reshape(model, -1)

    own = lax.axis_index("tok") * rows + jnp.arange(rows, dtype=jnp.int32)
    eligible = (depths >= 2) & (padding > 0)
    flags = jnp.stack([eligible, ~eligible]).astype(BF)
    upto = (jnp.arange(rows)[:, None] <= jnp.arange(rows)[None, :]).astype(BF)
    counts = mm(flags, upto).astype(jnp.int32)
    slot = jnp.where(eligible, counts[0] - 1, counts[0, -1] + counts[1] - 1)
    chosen = jnp.arange(rows, dtype=jnp.int32)[:, None] == slot[None, :]
    onehot = chosen.astype(BF)
    doc_ends = jnp.cumsum(lengths[0])
    begins = jnp.sum(
        jnp.where(own[:, None] >= doc_ends[None, :], lengths[0][None, :], 0), axis=1
    )
    levels = jnp.where(padding > 0, depths, 0)
    labels = jnp.stack([own, begins, levels])
    labels = jnp.sum(jnp.where(chosen[None], labels[:, None, :], 0), axis=2)
    labels = jnp.pad(labels, ((0, 5), (0, 0)))
    swap = topo.swap_pairs()
    state = lax.ppermute(mm(onehot, tokens).astype(BF), AXES, swap).astype(F32)
    labels = lax.ppermute(labels, AXES, swap)
    gradient = lax.ppermute(mm(onehot, cotangent).astype(BF), AXES, swap).astype(F32)
    order_g = xk + yk + ck
    labels_all = group_gather(topo, labels, order_g)

    all_second = gather_rows(topo, second, 1, order_b).reshape(model, -1)
    all_down = gather_rows(topo, w_down, 0, order_a).reshape(ff, model)
    small = all_first[:, model:model + HD].astype(F32)
    gain_one, gain_two = small[:, RECS], small[:, RECS + 1]
    weight_q = all_first[:, :model]
    weight_kv = all_first[:, model + HD:model + HD + 2 * kv_cols]
    weight_gu = all_second[:, :2 * ff]
    weight_o = all_second[:, 2 * ff:2 * ff + model]
    weight_d = all_down

    pack = (lax.axis_index("grp") * topo.X) + lax.axis_index("tok") % topo.X
    begin_all, level_mine = labels[1], labels[2]
    lowest = jnp.min(labels[1])
    span = jnp.stack([lowest // rows, pack + 1]).astype(jnp.int32)
    places = (labels[0] - labels[1]).astype(F32)
    freqs = 10000.0 ** (-(jnp.arange(HD // 2, dtype=F32) * 2.0 / HD))
    angles = places[:, None] * freqs[None, :]
    cosine, sine = jnp.cos(angles), jnp.sin(angles)

    def forward(state, recursion):
        n = state.shape[0]
        cos_n, sin_n = cosine[:n], sine[:n]
        inv_one = inverse_rms(state)
        n1 = (state * inv_one * gain_one).astype(BF)
        q = heads_first(mm(n1, weight_q))
        q = (turn(q, cos_n, sin_n).astype(BF) * BF(HD ** -0.5)).astype(BF)
        kv = mm(n1, weight_kv).reshape(n, KV_HEADS, 2, HD)
        k = turn(kv[:, :, 0], cos_n[:, None], sin_n[:, None])
        kv = jnp.stack([k, kv[:, :, 1]], axis=2).reshape(n, 2 * kv_cols).astype(BF)
        kv_all = group_gather(topo, kv, order_g).reshape(topo.T * n, 2 * kv_cols)
        live = labels_all[:, 2, :n] > recursion
        order = labels_all[:, 0, :n]
        key_labels = jnp.stack([jnp.where(live, order, -1), order], axis=-1).reshape(-1, 2)
        key_labels = jnp.pad(key_labels, ((0, 0), (0, 6)))
        query_labels = jnp.stack([labels[1, :n], labels[0, :n]])
        query_labels = jnp.pad(jnp.tile(query_labels, (1, SHARES)), ((0, 6), (0, 0)))
        q_pad = pair_up(q, jnp.zeros_like(q))
        out, stat = attend(n, span, key_labels, query_labels, kv_all, q_pad)
        out = heads_back(out[:, HD:])
        mixed = out.reshape(n, HEADS * HD).astype(BF)
        attended = mm(mixed, weight_o)
        middle = state + attended
        inv_two = inverse_rms(middle)
        n2 = (middle * inv_two * gain_two).astype(BF)
        gu = mm(n2, weight_gu)
        gated, upward = gu[:, :ff], gu[:, ff:]
        hidden = (jax.nn.silu(gated) * upward).astype(BF)
        both = attended + mm(hidden, weight_d)
        gate = jax.nn.sigmoid(jnp.sum(state * small[:, recursion], axis=-1, keepdims=True))
        active = (labels[2, :n] > recursion).astype(F32)[:, None]
        new = state + active * gate * both
        kept = (state, inv_one, n1, q, kv_all, key_labels, query_labels, out, stat, mixed, middle,
                inv_two, n2, gu, hidden, both, gate, active)
        return (new, kept)

    def backward(gradient, recursion, kept):
        (state, inv_one, n1, q, kv_all, key_labels, query_labels, out, stat, mixed, middle,
         inv_two, n2, gu, hidden, both, gate, active) = kept
        n = state.shape[0]
        d_both = active * gate * gradient
        d_fed = d_both.astype(BF)
        d_gate = active * gate * (1.0 - gate) * jnp.sum(gradient * both, axis=-1, keepdims=True)
        d_router = jnp.sum(state * d_gate, axis=0)
        gated, upward = gu[:, :ff], gu[:, ff:]
        d_hidden = mm_nt(d_fed, weight_d)
        sig = jax.nn.sigmoid(gated)
        d_up = (d_hidden * gated * sig).astype(BF)
        d_gated = (d_hidden * upward * sig * (1.0 + gated * (1.0 - sig))).astype(BF)
        d_gu = jnp.concatenate([d_gated, d_up], axis=1)
        d_middle, d_gain_two = norm_back(mm_nt(d_gu, weight_gu), middle, inv_two, gain_two)
        d_att = (d_both + d_middle).astype(BF)
        gradient = gradient + d_gate * small[:, recursion] + d_middle
        d_mixed = mm_nt(d_att, weight_o).astype(BF)
        d_heads = heads_first(d_mixed)
        delta = jnp.sum(
            d_heads.astype(F32) * out.transpose(1, 0, 2), axis=-1
        ).reshape(KV_HEADS, 1, SHARES * n)
        delta = jnp.broadcast_to(delta, (KV_HEADS, 8, SHARES * n))
        dq, dkv = attend_back(
            n, span, key_labels, query_labels, kv_all, pair_up(q, d_heads), stat, delta
        )
        dkv = group_scatter(
            topo, dkv.reshape(topo.T, n, 2 * kv_cols), ck + yk + xk
        ).astype(F32).reshape(n, KV_HEADS, 2, HD)
        cos_n, sin_n = cosine[:n, None], sine[:n, None]
        dk = turn(dkv[:, :, 0], cos_n, -sin_n)
        dkv = jnp.stack([dk, dkv[:, :, 1]], axis=2).reshape(n, 2 * kv_cols).astype(BF)
        dq = turn(heads_back(dq[:, :HD]) * HD ** -0.5, cos_n, -sin_n)
        dq = dq.reshape(n, HEADS * HD).astype(BF)
        d_n1 = mm_nt(dq, weight_q) + mm_nt(dkv, weight_kv)
        d_state, d_gain_one = norm_back(d_n1, state, inv_one, gain_one)
        left = (n1, dq, dkv, mixed, d_att, n2, d_gu, hidden, d_fed)
        return (gradient + d_state, left, (d_router, d_gain_one, d_gain_two))

    whole_state, kept = forward(state, 0)
    deep = whole_state[:deep_rows]
    all_kept = [kept]
    for recursion in range(1, RECS):
        deep, kept = forward(deep, recursion)
        all_kept.append(kept)
    final = jnp.concatenate([deep, whole_state[deep_rows:]], axis=0).astype(BF)
    final = lax.ppermute(final, AXES, swap)

    deep_grad = gradient[:deep_rows]
    lefts, smalls = [], []
    for recursion in reversed(range(1, RECS)):
        deep_grad, left, tiny = backward(deep_grad, recursion, all_kept[recursion])
        lefts.append(left)
        smalls.append(tiny)
    gradient = jnp.concatenate([deep_grad, gradient[deep_rows:]], axis=0)
    gradient, left, tiny = backward(gradient, 0, all_kept[0])
    lefts.append(left)
    smalls.append(tiny)
    gradient = lax.ppermute(gradient.astype(BF), AXES, swap)

    n1, dq, dkv, mixed, d_att, n2, d_gu, hidden, d_fed = (
        jnp.concatenate(parts, axis=0) for parts in zip(*lefts)
    )
    spread = topo.T
    ring_a = ck + xk + yk + zk
    ring_b = ck + yk + xk + zk
    cut = lambda g: g.reshape(spread, -1, g.shape[-1])
    grad_down = scatter_rows(topo, cut(mm_tn(hidden, d_fed)), 0, ring_a).astype(F32)
    grad_gu = scatter_rows(topo, cut(mm_tn(n2, d_gu)), 1, ring_b).astype(F32)
    tiny = jnp.stack(
        [smalls[2][0], smalls[1][0], smalls[0][0],
         smalls[0][1] + smalls[1][1] + smalls[2][1],
         smalls[0][2] + smalls[1][2] + smalls[2][2]], axis=1
    )
    tiny = jnp.pad(tiny, ((0, 0), (0, HD - tiny.shape[1])))
    last = jnp.concatenate([mm_tn(n1, dq), tiny, mm_tn(n1, dkv), mm_tn(mixed, d_att)], axis=1)
    last = jnp.pad(last, ((0, 0), (0, -last.shape[1] % (128 * topo.G))))
    last = scatter_rows(topo, cut(last), 1, ring_a).astype(F32)
    grad_query = last[:, :model]
    tiny = last[:, model:model + HD]
    pair = last[:, model + HD:model + HD + 2 * kv_cols].reshape(shard, KV_HEADS, 2, HD)
    grad_key = pair[:, :, 0].reshape(shard, kv_cols)
    grad_value = pair[:, :, 1].reshape(shard, kv_cols)
    grad_out = last[:, model + HD + 2 * kv_cols:2 * model + HD + 2 * kv_cols]

    def unsort(v):
        return mm_tn(onehot, v).astype(BF)

    return (
        unsort(final), unsort(gradient), grad_query, grad_key, grad_value, grad_out,
        grad_gu[:, :ff], grad_gu[:, ff:], grad_down, tiny[:, :RECS], tiny[:, RECS],
        tiny[:, RECS + 1],
    )


def solution(mesh):
    topo = Topo(mesh.shape["grp"], mesh.shape["tok"])
    both = P(("grp", "tok"))
    wide = P(("grp", "tok"), None)
    rows = P("tok", None)
    row = P("tok")
    return jax.shard_map(
        functools.partial(per_device, topo),
        mesh=mesh,
        in_specs=(wide,) + (rows,) * 8 + (row, row, P("grp", None), both, both, wide),
        out_specs=(wide, wide) + (rows,) * 8 + (row, row),
        check_vma=False,
    )
```

```python
import functools

import jax
import jax.numpy as jnp
from jax import lax
from jax.experimental import pallas as pl
from jax.experimental.pallas import tpu as pltpu
from jax.sharding import PartitionSpec as P

HEADS = 15
KV_HEADS = 5
SHARES = HEADS // KV_HEADS
HD = 64
RECS = 3
EPS = 1e-05
BF = jnp.bfloat16
F32 = jnp.float32
BIG = -1e30
AXES = ("grp", "tok")


class Topo:
    def __init__(self, groups, spread):
        self.G = groups
        self.T = spread
        self.X = spread // groups
        self.Z = groups
        self.Y = groups // 2
        self.bits = {
            "z": self.Z.bit_length() - 1,
            "x": self.X.bit_length() - 1,
            "y": self.Y.bit_length() - 1,
            "c": 1,
        }

    def keys(self, dim):
        return [(dim, k) for k in range(self.bits[dim])]

    def masks(self, key):
        dim, k = key
        if dim == "c":
            return (1, 0)
        if dim == "y":
            return (2 << k, 0)
        if dim == "x":
            return (0, 1 << k)
        return (0, self.X << k)

    def pairs(self, key):
        mg, mt = self.masks(key)
        return [
            (g * self.T + t, (g ^ mg) * self.T + (t ^ mt))
            for g in range(self.G)
            for t in range(self.T)
        ]

    def swap_pairs(self):
        out = []
        for g in range(self.G):
            for t in range(self.T):
                z, x = t // self.X, t % self.X
                out.append((g * self.T + t, z * self.T + g * self.X + x))
        return out

    def bit(self, key):
        mg, mt = self.masks(key)
        if mg:
            return (lax.axis_index("grp") // mg) % 2
        return (lax.axis_index("tok") // mt) % 2


def exchange(topo, arr, key):
    return lax.ppermute(arr, AXES, topo.pairs(key))


def double(topo, arr, key, axis, stack):
    other = exchange(topo, arr, key)
    mine_is_high = topo.bit(key) == 1
    low = jnp.where(mine_is_high, other, arr)
    high = jnp.where(mine_is_high, arr, other)
    if stack:
        return jnp.stack([low, high], axis=axis)
    return jnp.concatenate([low, high], axis=axis)


def halve(topo, arr, key, axis, stack):
    mine_is_high = topo.bit(key) == 1
    if stack:
        low = lax.index_in_dim(arr, 0, axis, keepdims=False)
        high = lax.index_in_dim(arr, 1, axis, keepdims=False)
    else:
        half = arr.shape[axis] // 2
        low = lax.slice_in_dim(arr, 0, half, axis=axis)
        high = lax.slice_in_dim(arr, half, 2 * half, axis=axis)
    send = jnp.where(mine_is_high, low, high).astype(BF)
    keep = jnp.where(mine_is_high, high, low).astype(F32)
    return (keep + exchange(topo, send, key).astype(F32)).astype(BF)


def canonical(topo):
    return list(reversed(topo.keys("z"))) + list(reversed(topo.keys("x")))


def gather_rows(topo, shard, axis, order):
    me = lax.axis_index("grp")
    part = (me % 2) * topo.Y + me // 2
    pieces = jnp.stack(jnp.split(shard, topo.G, axis=axis), axis=0)
    arr = lax.dynamic_index_in_dim(pieces, part, 0, keepdims=False)
    held = []
    names = canonical(topo)
    for key in order:
        if key[0] in ("z", "x"):
            place = sum(1 for h in held if names.index(h) < names.index(key))
            arr = double(topo, arr, key, place, True)
            held.append(key)
        else:
            arr = double(topo, arr, key, axis - 2, False)
    return arr.reshape((topo.T,) + arr.shape[-2:])


def scatter_rows(topo, arr, axis, order):
    names = canonical(topo)
    held = list(names)
    arr = arr.reshape((2,) * len(names) + arr.shape[-2:])
    for key in order:
        if key[0] in ("z", "x"):
            arr = halve(topo, arr, key, held.index(key), True)
            held.remove(key)
        else:
            arr = halve(topo, arr, key, axis - 2, False)
    for key in topo.keys("y") + topo.keys("c"):
        arr = double(topo, arr, key, axis - 2, False)
    return arr


class Piece:
    def __init__(self, array, dim, start, size, core, part):
        self.array, self.dim, self.start, self.size = array, dim, start, size
        self.core, self.part = core, part

    def of(self, ref):
        if self.dim == 0:
            return ref.at[pl.ds(self.start, self.size), :]
        return ref.at[:, pl.ds(self.start, self.size)]


def cut_pieces(shapes):
    near = lambda v, unit: max(unit, int(round(v / unit)) * unit)
    wide_a, wide_g, wide_u, tall = shapes[0][1], shapes[1][1], shapes[2][1], shapes[3][0]
    a = near(wide_a * 0.634, 128)
    g = near(wide_g * 0.7, 128)
    u = near(wide_u * 0.65, 128)
    d = near(tall * 0.3, 8)
    return [
        Piece(1, 1, 0, g, 0, 0),
        Piece(0, 1, a, wide_a - a, 0, 2),
        Piece(1, 1, g, wide_g - g, 0, 2),
        Piece(0, 1, 0, a, 0, 1),
        Piece(2, 1, u, wide_u - u, 1, 0),
        Piece(3, 0, 0, d, 1, 0),
        Piece(3, 0, d, tall - d, 1, 2),
        Piece(2, 1, 0, u, 1, 1),
    ]


def coordinates(topo):
    g, t = lax.axis_index("grp"), lax.axis_index("tok")
    return lax.rem(t, topo.X), lax.div(g, 2), lax.div(t, topo.X), lax.rem(g, 2)


def gather_kernel(topo, pieces, *refs):
    shards, outs = refs[:4], refs[4:8]
    local_sem, recv_sem, z_sem, x_sem, y_sem, c_sem = refs[8:]
    x, y, z, c = coordinates(topo)
    X, Z, T = topo.X, topo.Z, topo.T
    g, me = lax.axis_index("grp"), lax.axis_index("tok")
    odd = lax.rem(y, 2)
    over_y = {"grp": g + 2 - 4 * odd, "tok": me}
    over_c = {"grp": g + 1 - 2 * c, "tok": me}

    def over_z(k):
        return {"grp": g, "tok": (z + k) * X + x}

    def over_x(k):
        return {"grp": g, "tok": z * X + lax.rem(x + k, X)}

    barrier = pltpu.get_barrier_semaphore()
    partners = [over_y, over_c] + [over_x(k) for k in range(1, X)]
    for partner in partners:
        pl.semaphore_signal(barrier, inc=1, device_id=partner, device_id_type=pl.DeviceIdType.MESH)
    below, above = z > 0, z < Z - 1

    def greet(k):
        pl.semaphore_signal(
            barrier, inc=1, device_id=over_z(k), device_id_type=pl.DeviceIdType.MESH
        )

    pl.when(below)(lambda: greet(-1))
    pl.when(above)(lambda: greet(1))
    own = [
        pltpu.make_async_copy(shards[i], outs[i].at[me], local_sem.at[i]) for i in range(4)
    ]
    for copy in own:
        copy.start()
    pl.semaphore_wait(barrier, len(partners) + below.astype(jnp.int32) + above.astype(jnp.int32))

    def send(p, t, sem, target, mine=False):
        piece = pieces[p]
        landing = piece.of(outs[piece.array].at[t])
        source = piece.of(shards[piece.array]) if mine else landing
        return pltpu.make_async_remote_copy(
            src_ref=source, dst_ref=landing, send_sem=sem, recv_sem=recv_sem.at[p, t],
            device_id=target, device_id_type=pl.DeviceIdType.MESH,
        )

    def arrived(p, t):
        send(p, t, c_sem.at[0, 0], over_c).wait_recv()

    def run(core):
        mine = [p for p in range(len(pieces)) if pieces[p].core == core]
        theirs = [p for p in range(len(pieces)) if pieces[p].core != core]
        slot = {p: i for i, p in enumerate(mine)}

        def inside(p, body):
            part = pieces[p].part
            if part == 1:
                body()
            else:
                pl.when(odd == part // 2)(body)

        def outside(p, body):
            if pieces[p].part != 1:
                pl.when(odd != pieces[p].part // 2)(body)

        def x_copies(p, zz, first):
            t = zz * X + x
            return [
                send(p, t, x_sem.at[slot[p], zz, k - 1], over_x(k), first) for k in range(1, X)
            ]

        def y_copy(p, t):
            return send(p, t, y_sem.at[slot[p], t], over_y)

        def c_copy(p, t):
            return send(p, t, c_sem.at[slot[p], t], over_c)

        def z_copy(p, zz, k, first):
            return send(p, zz * X + x, z_sem.at[slot[p], zz, (k + 1) // 2], over_z(k), first)

        for p in mine:
            def begin(p=p):
                pl.when(below)(lambda: z_copy(p, z, -1, True).start())
                pl.when(above)(lambda: z_copy(p, z, 1, True).start())
                for copy in x_copies(p, z, True):
                    copy.start()
            inside(p, begin)

        def share(p, t):
            if pieces[p].part != 1:
                y_copy(p, t).start()
            c_copy(p, t).start()

        def relay(p, zz, k):
            arrived(p, zz * X + x)
            pl.when(above if k > 0 else below)(lambda: z_copy(p, zz, k, False).start())
            for copy in x_copies(p, zz, False):
                copy.start()
            share(p, zz * X + x)

        def others(p, zz):
            for j in range(1, X):
                t = zz * X + lax.rem(x + j, X)
                arrived(p, t)
                share(p, t)

        def around(k, carry):
            low, high = z - k, z + k
            for p in mine:
                inside(p, lambda p=p: pl.when(low >= 0)(lambda: relay(p, low, 1)))
                inside(p, lambda p=p: pl.when(high < Z)(lambda: relay(p, high, -1)))
            low, high = z - k + 1, z + k - 1
            for p in mine:
                inside(p, lambda p=p: pl.when(low >= 0)(lambda: others(p, low)))
                inside(p, lambda p=p: pl.when((k > 1) & (high < Z))(lambda: others(p, high)))
            return carry

        lax.fori_loop(1, Z + 1, around, 0)

        def rest(t, carry):
            @pl.when(t != me)
            def _():
                for p in mine:
                    def forward(p=p):
                        arrived(p, t)
                        c_copy(p, t).start()
                    outside(p, forward)
            return carry

        lax.fori_loop(0, T, rest, 0)

        def finish(t, carry):
            @pl.when(t != me)
            def _():
                for p in theirs:
                    arrived(p, t)
                for p in mine:
                    c_copy(p, t).wait_send()
                    if pieces[p].part != 1:
                        inside(p, lambda p=p: y_copy(p, t).wait_send())
            return carry

        lax.fori_loop(0, T, finish, 0)
        for p in mine:
            def end(p=p):
                def each(zz, carry):
                    pl.when((zz <= z) & above)(lambda: z_copy(p, zz, 1, False).wait_send())
                    pl.when((zz >= z) & below)(lambda: z_copy(p, zz, -1, False).wait_send())
                    for copy in x_copies(p, zz, False):
                        copy.wait_send()
                    return carry
                lax.fori_loop(0, Z, each, 0)
            inside(p, end)

    pl.when(c == 0)(lambda: run(0))
    pl.when(c == 1)(lambda: run(1))
    for copy in own:
        copy.wait()


def gather_weights(topo, shards):
    pieces = cut_pieces([s.shape for s in shards])
    T = topo.T
    DMA = pltpu.SemaphoreType.DMA
    hbm = pl.BlockSpec(memory_space=pl.ANY)
    outs = pl.pallas_call(
        functools.partial(gather_kernel, topo, pieces),
        in_specs=[hbm] * 4,
        out_specs=[hbm] * 4,
        out_shape=[jax.ShapeDtypeStruct((T,) + s.shape, s.dtype) for s in shards],
        scratch_shapes=[
            DMA((4,)), DMA((len(pieces), T)), DMA((4, topo.Z, 2)), DMA((4, topo.Z, topo.X - 1)),
            DMA((4, T)), DMA((4, T)),
        ],
        compiler_params=pltpu.CompilerParams(collective_id=0, has_side_effects=True),
        name="gather_weights",
    )(*shards)
    return [o.reshape(-1, o.shape[-1]) for o in outs]


def group_order(topo):
    return list(reversed(topo.keys("y"))) + topo.keys("c") + list(reversed(topo.keys("x")))


def group_gather(topo, arr, order):
    names = group_order(topo)
    held = []
    shape = arr.shape
    for key in order:
        place = sum(1 for h in held if names.index(h) < names.index(key))
        arr = double(topo, arr, key, place, True)
        held.append(key)
    return arr.reshape((topo.T,) + shape)


def group_scatter(topo, arr, order):
    names = group_order(topo)
    held = list(names)
    arr = arr.reshape((2,) * len(names) + arr.shape[1:])
    for key in order:
        arr = halve(topo, arr, key, held.index(key), True)
        held.remove(key)
    return arr


def fill_bias(bias, key_ref, query_ref, rows, first, last):
    def body(t, carry):
        at = pl.ds(pl.multiple_of(t * rows, rows), rows)
        keys = key_ref[at, :]
        live, order = keys[:, 0:1], keys[:, 1:2]
        begin, place = query_ref[0:1, :], query_ref[1:2, :]
        allowed = ((live >= begin) & (live <= place)) | (order == place)
        bias[at, :] = jnp.where(allowed, 0.0, BIG)
        return carry

    lax.fori_loop(first, last, body, 0)


NT = (((1,), (1,)), ((), ()))
TN = (((0,), (0,)), ((), ()))


def attend_kernel(rows, span, key_ref, query_ref, kv_ref, q_ref, out_ref, stat_ref, bias, held):
    first, last = span[0], span[1]

    @pl.when(pl.program_id(0) == 0)
    def _():
        fill_bias(bias, key_ref, query_ref, rows, first, last)

    wide = q_ref.shape[1]
    queries = q_ref[0]

    def scores(t, top):
        at = pl.ds(pl.multiple_of(t * rows, rows), rows)
        s = lax.dot_general(kv_ref[at, :], queries, NT, preferred_element_type=F32) + bias[at, :]
        held[at, :] = s
        return jnp.maximum(top, jnp.max(s.reshape(rows // 8, 8, wide), axis=0))

    top = lax.fori_loop(first, last, scores, jnp.full((8, wide), BIG, F32))
    top = jnp.max(top, axis=0, keepdims=True)

    out_ref[0] = jnp.zeros(out_ref.shape[1:], F32)

    def mix(t, total):
        at = pl.ds(pl.multiple_of(t * rows, rows), rows)
        p = jnp.exp(held[at, :] - top)
        out_ref[0] += lax.dot_general(
            kv_ref[at, :], p.astype(BF), TN, preferred_element_type=F32
        )
        return total + jnp.sum(p.reshape(rows // 8, 8, wide), axis=0)

    total = lax.fori_loop(first, last, mix, jnp.zeros((8, wide), F32))
    total = jnp.sum(total, axis=0, keepdims=True)
    out_ref[0] = out_ref[0] / total
    stat_ref[0] = jnp.broadcast_to(top + jnp.log(total), (8, wide))


def attend(rows, span, key_labels, query_labels, kv_all, q_pad):
    count = kv_all.shape[0]
    wide = q_pad.shape[1]
    fixed = lambda h, s: (0, 0)
    return pl.pallas_call(
        functools.partial(attend_kernel, rows),
        grid_spec=pltpu.PrefetchScalarGridSpec(
            num_scalar_prefetch=1,
            grid=(KV_HEADS,),
            in_specs=[
                pl.BlockSpec((count, 8), fixed),
                pl.BlockSpec((8, wide), fixed),
                pl.BlockSpec((count, 2 * HD), lambda h, s: (0, h)),
                pl.BlockSpec((1, wide, 2 * HD), lambda h, s: (h, 0, 0)),
            ],
            out_specs=[
                pl.BlockSpec((1, 2 * HD, wide), lambda h, s: (h, 0, 0)),
                pl.BlockSpec((1, 8, wide), lambda h, s: (h, 0, 0)),
            ],
            scratch_shapes=[pltpu.VMEM((count, wide), F32), pltpu.VMEM((count, wide), F32)],
        ),
        out_shape=[
            jax.ShapeDtypeStruct((KV_HEADS, 2 * HD, wide), F32),
            jax.ShapeDtypeStruct((KV_HEADS, 8, wide), F32),
        ],
        compiler_params=pltpu.CompilerParams(vmem_limit_bytes=62 << 20),
        cost_estimate=pl.CostEstimate(
            flops=8 * KV_HEADS * wide * count * HD,
            bytes_accessed=2 * count * 2 * HD * KV_HEADS + 8 * KV_HEADS * wide * HD * 2,
            transcendentals=KV_HEADS * wide * count,
        ),
        name="attend",
    )(span, key_labels, query_labels, kv_all, q_pad)


def attend_back_kernel(
    rows, span, key_ref, query_ref, kv_ref, q_ref, stat_ref, delta_ref, dq_ref, dkv_ref, bias
):
    first, last = span[0], span[1]

    @pl.when(pl.program_id(0) == 0)
    def _():
        fill_bias(bias, key_ref, query_ref, rows, first, last)

    queries = q_ref[0]
    stat = stat_ref[0, 0:1, :]
    delta = delta_ref[0, 0:1, :]
    dkv_ref[...] = jnp.zeros(dkv_ref.shape, BF)
    dq_ref[0] = jnp.zeros(dq_ref.shape[1:], F32)
    low = lax.broadcasted_iota(jnp.int32, (rows, 2 * HD), 1) < HD

    def body(t, carry):
        at = pl.ds(pl.multiple_of(t * rows, rows), rows)
        kv = kv_ref[at, :]
        zero = jnp.zeros_like(kv)
        s = lax.dot_general(jnp.where(low, kv, zero), queries, NT, preferred_element_type=F32)
        p = jnp.exp(s + bias[at, :] - stat)
        dp = lax.dot_general(jnp.where(low, zero, kv), queries, NT, preferred_element_type=F32)
        ds = (p * (dp - delta)).astype(BF)
        dk = jnp.dot(ds, queries, preferred_element_type=F32)
        dv = jnp.dot(p.astype(BF), queries, preferred_element_type=F32)
        dkv_ref[at, :] = jnp.where(low, dk, dv).astype(BF)
        dq_ref[0] += lax.dot_general(kv, ds, TN, preferred_element_type=F32)
        return carry

    lax.fori_loop(first, last, body, 0)


def attend_back(rows, span, key_labels, query_labels, kv_all, q_do, stat, delta):
    count = kv_all.shape[0]
    wide = q_do.shape[1]
    fixed = lambda h, s: (0, 0)
    head = lambda h, s: (h, 0, 0)
    return pl.pallas_call(
        functools.partial(attend_back_kernel, rows),
        grid_spec=pltpu.PrefetchScalarGridSpec(
            num_scalar_prefetch=1,
            grid=(KV_HEADS,),
            in_specs=[
                pl.BlockSpec((count, 8), fixed),
                pl.BlockSpec((8, wide), fixed),
                pl.BlockSpec((count, 2 * HD), lambda h, s: (0, h)),
                pl.BlockSpec((1, wide, 2 * HD), head),
                pl.BlockSpec((1, 8, wide), head),
                pl.BlockSpec((1, 8, wide), head),
            ],
            out_specs=[
                pl.BlockSpec((1, 2 * HD, wide), head),
                pl.BlockSpec((count, 2 * HD), lambda h, s: (0, h)),
            ],
            scratch_shapes=[pltpu.VMEM((count, wide), F32)],
        ),
        out_shape=[
            jax.ShapeDtypeStruct((KV_HEADS, 2 * HD, wide), F32),
            jax.ShapeDtypeStruct((count, KV_HEADS * 2 * HD), BF),
        ],
        compiler_params=pltpu.CompilerParams(vmem_limit_bytes=62 << 20),
        cost_estimate=pl.CostEstimate(
            flops=20 * KV_HEADS * wide * count * HD,
            bytes_accessed=4 * count * 2 * HD * KV_HEADS + 8 * KV_HEADS * wide * HD * 2,
            transcendentals=KV_HEADS * wide * count,
        ),
        name="attend_back",
    )(span, key_labels, query_labels, kv_all, q_do, stat, delta)


def mm(a, b):
    return jnp.dot(a, b, preferred_element_type=F32)


def mm_nt(a, b):
    return lax.dot_general(a, b, NT, preferred_element_type=F32)


def mm_tn(a, b):
    return lax.dot_general(a, b, TN, preferred_element_type=F32)


def inverse_rms(v):
    return lax.rsqrt(jnp.mean(v * v, axis=-1, keepdims=True) + EPS)


def norm_back(grad, v, inv, gain):
    scaled = grad * gain
    dot = jnp.mean(scaled * v, axis=-1, keepdims=True)
    return (inv * scaled - v * (inv * inv * inv * dot), jnp.sum(grad * v * inv, axis=0))


def turn(values, cosine, sine):
    half = HD // 2
    lower, upper = values[..., :half], values[..., half:]
    return jnp.concatenate(
        [lower * cosine - upper * sine, upper * cosine + lower * sine], axis=-1
    )


def heads_first(v):
    n = v.shape[0]
    return v.reshape(n, HEADS, HD).transpose(1, 0, 2)


def heads_back(v):
    n = v.shape[-1] // SHARES
    return v.reshape(KV_HEADS, HD, SHARES, n).transpose(3, 0, 2, 1).reshape(n, HEADS, HD)


def pair_up(q, d):
    n = q.shape[1]
    return jnp.concatenate([q, d], axis=-1).reshape(KV_HEADS, SHARES * n, 2 * HD)


def per_device(topo, *args):
    (tokens, w_query, w_key, w_value, w_out, w_gate, w_up, w_down, router, norm_attn, norm_ffn,
     lengths, depths, padding, cotangent) = args
    rows, model = tokens.shape
    kv_cols = w_key.shape[1]
    ff = w_gate.shape[1]
    shard = w_query.shape[0]
    deep_rows = rows * 3 // 4
    zk, xk, yk, ck = (topo.keys(d) for d in "zxyc")

    small = jnp.concatenate([router, norm_attn[:, None], norm_ffn[:, None]], axis=1)
    small = jnp.pad(small, ((0, 0), (0, HD - small.shape[1])))
    w_kv = jnp.stack(
        [w_key.reshape(shard, KV_HEADS, HD), w_value.reshape(shard, KV_HEADS, HD)], axis=2
    ).reshape(shard, 2 * kv_cols)
    first = jnp.concatenate([w_query, small, w_kv, w_out], axis=1)
    all_first, weight_g, weight_u, weight_d = gather_weights(
        topo, [first, w_gate, w_up, w_down]
    )

    own = lax.axis_index("tok") * rows + jnp.arange(rows, dtype=jnp.int32)
    eligible = (depths >= 2) & (padding > 0)
    flags = jnp.stack([eligible, ~eligible]).astype(BF)
    upto = (jnp.arange(rows)[:, None] <= jnp.arange(rows)[None, :]).astype(BF)
    counts = mm(flags, upto).astype(jnp.int32)
    slot = jnp.where(eligible, counts[0] - 1, counts[0, -1] + counts[1] - 1)
    chosen = jnp.arange(rows, dtype=jnp.int32)[:, None] == slot[None, :]
    onehot = chosen.astype(BF)
    doc_ends = jnp.cumsum(lengths[0])
    begins = jnp.sum(
        jnp.where(own[:, None] >= doc_ends[None, :], lengths[0][None, :], 0), axis=1
    )
    levels = jnp.where(padding > 0, depths, 0)
    labels = jnp.stack([own, begins, levels])
    labels = jnp.sum(jnp.where(chosen[None], labels[:, None, :], 0), axis=2)
    labels = jnp.pad(labels, ((0, 5), (0, 0)))
    swap = topo.swap_pairs()
    state = lax.ppermute(mm(onehot, tokens).astype(BF), AXES, swap).astype(F32)
    labels = lax.ppermute(labels, AXES, swap)
    gradient = lax.ppermute(mm(onehot, cotangent).astype(BF), AXES, swap).astype(F32)
    order_g = xk + yk + ck
    labels_all = group_gather(topo, labels, order_g)

    small = all_first[:, model:model + HD].astype(F32)
    gain_one, gain_two = small[:, RECS], small[:, RECS + 1]
    weight_q = all_first[:, :model]
    weight_kv = all_first[:, model + HD:model + HD + 2 * kv_cols]
    weight_o = all_first[:, model + HD + 2 * kv_cols:]

    pack = (lax.axis_index("grp") * topo.X) + lax.axis_index("tok") % topo.X
    begin_all, level_mine = labels[1], labels[2]
    lowest = jnp.min(labels[1])
    span = jnp.stack([lowest // rows, pack + 1]).astype(jnp.int32)
    places = (labels[0] - labels[1]).astype(F32)
    freqs = 10000.0 ** (-(jnp.arange(HD // 2, dtype=F32) * 2.0 / HD))
    angles = places[:, None] * freqs[None, :]
    cosine, sine = jnp.cos(angles), jnp.sin(angles)

    def forward(state, recursion):
        n = state.shape[0]
        cos_n, sin_n = cosine[:n], sine[:n]
        inv_one = inverse_rms(state)
        n1 = (state * inv_one * gain_one).astype(BF)
        q = heads_first(mm(n1, weight_q))
        q = (turn(q, cos_n, sin_n).astype(BF) * BF(HD ** -0.5)).astype(BF)
        kv = mm(n1, weight_kv).reshape(n, KV_HEADS, 2, HD)
        k = turn(kv[:, :, 0], cos_n[:, None], sin_n[:, None])
        kv = jnp.stack([k, kv[:, :, 1]], axis=2).reshape(n, 2 * kv_cols).astype(BF)
        kv_all = group_gather(topo, kv, order_g).reshape(topo.T * n, 2 * kv_cols)
        live = labels_all[:, 2, :n] > recursion
        order = labels_all[:, 0, :n]
        key_labels = jnp.stack([jnp.where(live, order, -1), order], axis=-1).reshape(-1, 2)
        key_labels = jnp.pad(key_labels, ((0, 0), (0, 6)))
        query_labels = jnp.stack([labels[1, :n], labels[0, :n]])
        query_labels = jnp.pad(jnp.tile(query_labels, (1, SHARES)), ((0, 6), (0, 0)))
        q_pad = pair_up(q, jnp.zeros_like(q))
        out, stat = attend(n, span, key_labels, query_labels, kv_all, q_pad)
        out = heads_back(out[:, HD:])
        mixed = out.reshape(n, HEADS * HD).astype(BF)
        attended = mm(mixed, weight_o)
        middle = state + attended
        inv_two = inverse_rms(middle)
        n2 = (middle * inv_two * gain_two).astype(BF)
        gated, upward = mm(n2, weight_g), mm(n2, weight_u)
        hidden = (jax.nn.silu(gated) * upward).astype(BF)
        both = attended + mm(hidden, weight_d)
        gate = jax.nn.sigmoid(jnp.sum(state * small[:, recursion], axis=-1, keepdims=True))
        active = (labels[2, :n] > recursion).astype(F32)[:, None]
        new = state + active * gate * both
        kept = (state, inv_one, n1, q, kv_all, key_labels, query_labels, out, stat, mixed, middle,
                inv_two, n2, gated, upward, hidden, both, gate, active)
        return (new, kept)

    def backward(gradient, recursion, kept):
        (state, inv_one, n1, q, kv_all, key_labels, query_labels, out, stat, mixed, middle,
         inv_two, n2, gated, upward, hidden, both, gate, active) = kept
        n = state.shape[0]
        d_both = active * gate * gradient
        d_fed = d_both.astype(BF)
        d_gate = active * gate * (1.0 - gate) * jnp.sum(gradient * both, axis=-1, keepdims=True)
        d_router = jnp.sum(state * d_gate, axis=0)
        d_hidden = mm_nt(d_fed, weight_d)
        sig = jax.nn.sigmoid(gated)
        d_up = (d_hidden * gated * sig).astype(BF)
        d_gated = (d_hidden * upward * sig * (1.0 + gated * (1.0 - sig))).astype(BF)
        d_middle, d_gain_two = norm_back(
            mm_nt(d_gated, weight_g) + mm_nt(d_up, weight_u), middle, inv_two, gain_two)
        d_att = (d_both + d_middle).astype(BF)
        gradient = gradient + d_gate * small[:, recursion] + d_middle
        d_mixed = mm_nt(d_att, weight_o).astype(BF)
        d_heads = heads_first(d_mixed)
        delta = jnp.sum(
            d_heads.astype(F32) * out.transpose(1, 0, 2), axis=-1
        ).reshape(KV_HEADS, 1, SHARES * n)
        delta = jnp.broadcast_to(delta, (KV_HEADS, 8, SHARES * n))
        dq, dkv = attend_back(
            n, span, key_labels, query_labels, kv_all, pair_up(q, d_heads), stat, delta
        )
        dkv = group_scatter(
            topo, dkv.reshape(topo.T, n, 2 * kv_cols), ck + yk + xk
        ).astype(F32).reshape(n, KV_HEADS, 2, HD)
        cos_n, sin_n = cosine[:n, None], sine[:n, None]
        dk = turn(dkv[:, :, 0], cos_n, -sin_n)
        dkv = jnp.stack([dk, dkv[:, :, 1]], axis=2).reshape(n, 2 * kv_cols).astype(BF)
        dq = turn(heads_back(dq[:, :HD]) * HD ** -0.5, cos_n, -sin_n)
        dq = dq.reshape(n, HEADS * HD).astype(BF)
        d_n1 = mm_nt(dq, weight_q) + mm_nt(dkv, weight_kv)
        d_state, d_gain_one = norm_back(d_n1, state, inv_one, gain_one)
        left = (n1, dq, dkv, mixed, d_att, n2, d_gated, d_up, hidden, d_fed)
        return (gradient + d_state, left, (d_router, d_gain_one, d_gain_two))

    whole_state, kept = forward(state, 0)
    deep = whole_state[:deep_rows]
    all_kept = [kept]
    for recursion in range(1, RECS):
        deep, kept = forward(deep, recursion)
        all_kept.append(kept)
    final = jnp.concatenate([deep, whole_state[deep_rows:]], axis=0).astype(BF)
    final = lax.ppermute(final, AXES, swap)

    deep_grad = gradient[:deep_rows]
    lefts, smalls = [], []
    for recursion in reversed(range(1, RECS)):
        deep_grad, left, tiny = backward(deep_grad, recursion, all_kept[recursion])
        lefts.append(left)
        smalls.append(tiny)
    gradient = jnp.concatenate([deep_grad, gradient[deep_rows:]], axis=0)
    gradient, left, tiny = backward(gradient, 0, all_kept[0])
    lefts.append(left)
    smalls.append(tiny)
    gradient = lax.ppermute(gradient.astype(BF), AXES, swap)

    n1, dq, dkv, mixed, d_att, n2, d_gated, d_up, hidden, d_fed = (
        jnp.concatenate(parts, axis=0) for parts in zip(*lefts)
    )
    spread = topo.T
    ring_a = ck + xk + yk + zk
    ring_b = ck + yk + xk + zk
    cut = lambda g: g.reshape(spread, -1, g.shape[-1])
    grad_down = scatter_rows(topo, cut(mm_tn(hidden, d_fed)), 0, ring_a).astype(F32)
    grad_gate = scatter_rows(topo, cut(mm_tn(n2, d_gated)), 1, ring_b).astype(F32)
    grad_up = scatter_rows(topo, cut(mm_tn(n2, d_up)), 1, ring_b).astype(F32)
    tiny = jnp.stack(
        [smalls[2][0], smalls[1][0], smalls[0][0],
         smalls[0][1] + smalls[1][1] + smalls[2][1],
         smalls[0][2] + smalls[1][2] + smalls[2][2]], axis=1
    )
    tiny = jnp.pad(tiny, ((0, 0), (0, HD - tiny.shape[1])))
    last = jnp.concatenate([mm_tn(n1, dq), tiny, mm_tn(n1, dkv), mm_tn(mixed, d_att)], axis=1)
    last = jnp.pad(last, ((0, 0), (0, -last.shape[1] % (128 * topo.G))))
    last = scatter_rows(topo, cut(last), 1, ring_a).astype(F32)
    grad_query = last[:, :model]
    tiny = last[:, model:model + HD]
    pair = last[:, model + HD:model + HD + 2 * kv_cols].reshape(shard, KV_HEADS, 2, HD)
    grad_key = pair[:, :, 0].reshape(shard, kv_cols)
    grad_value = pair[:, :, 1].reshape(shard, kv_cols)
    grad_out = last[:, model + HD + 2 * kv_cols:2 * model + HD + 2 * kv_cols]

    def unsort(v):
        return mm_tn(onehot, v).astype(BF)

    return (
        unsort(final), unsort(gradient), grad_query, grad_key, grad_value, grad_out,
        grad_gate, grad_up, grad_down, tiny[:, :RECS], tiny[:, RECS],
        tiny[:, RECS + 1],
    )


def solution(mesh):
    topo = Topo(mesh.shape["grp"], mesh.shape["tok"])
    both = P(("grp", "tok"))
    wide = P(("grp", "tok"), None)
    rows = P("tok", None)
    row = P("tok")
    return jax.shard_map(
        functools.partial(per_device, topo),
        mesh=mesh,
        in_specs=(wide,) + (rows,) * 8 + (row, row, P("grp", None), both, both, wide),
        out_specs=(wide, wide) + (rows,) * 8 + (row, row),
        check_vma=False,
    )
```

```python
import functools

import jax
import jax.numpy as jnp
from jax import lax
from jax.experimental import pallas as pl
from jax.experimental.pallas import tpu as pltpu
from jax.sharding import PartitionSpec as P

HEADS = 15
KV_HEADS = 5
SHARES = HEADS // KV_HEADS
HD = 64
RECS = 3
EPS = 1e-05
BF = jnp.bfloat16
F32 = jnp.float32
BIG = -1e30
AXES = ("grp", "tok")


class Topo:
    def __init__(self, groups, spread):
        self.G = groups
        self.T = spread
        self.X = spread // groups
        self.Z = groups
        self.Y = groups // 2
        self.bits = {
            "z": self.Z.bit_length() - 1,
            "x": self.X.bit_length() - 1,
            "y": self.Y.bit_length() - 1,
            "c": 1,
        }

    def keys(self, dim):
        return [(dim, k) for k in range(self.bits[dim])]

    def masks(self, key):
        dim, k = key
        if dim == "c":
            return (1, 0)
        if dim == "y":
            return (2 << k, 0)
        if dim == "x":
            return (0, 1 << k)
        return (0, self.X << k)

    def pairs(self, key):
        mg, mt = self.masks(key)
        return [
            (g * self.T + t, (g ^ mg) * self.T + (t ^ mt))
            for g in range(self.G)
            for t in range(self.T)
        ]

    def swap_pairs(self):
        out = []
        for g in range(self.G):
            for t in range(self.T):
                z, x = t // self.X, t % self.X
                out.append((g * self.T + t, z * self.T + g * self.X + x))
        return out

    def bit(self, key):
        mg, mt = self.masks(key)
        if mg:
            return (lax.axis_index("grp") // mg) % 2
        return (lax.axis_index("tok") // mt) % 2


def exchange(topo, arr, key):
    return lax.ppermute(arr, AXES, topo.pairs(key))


def double(topo, arr, key, axis, stack):
    other = exchange(topo, arr, key)
    mine_is_high = topo.bit(key) == 1
    low = jnp.where(mine_is_high, other, arr)
    high = jnp.where(mine_is_high, arr, other)
    if stack:
        return jnp.stack([low, high], axis=axis)
    return jnp.concatenate([low, high], axis=axis)


def halve(topo, arr, key, axis, stack):
    mine_is_high = topo.bit(key) == 1
    if stack:
        low = lax.index_in_dim(arr, 0, axis, keepdims=False)
        high = lax.index_in_dim(arr, 1, axis, keepdims=False)
    else:
        half = arr.shape[axis] // 2
        low = lax.slice_in_dim(arr, 0, half, axis=axis)
        high = lax.slice_in_dim(arr, half, 2 * half, axis=axis)
    send = jnp.where(mine_is_high, low, high).astype(BF)
    keep = jnp.where(mine_is_high, high, low).astype(F32)
    return (keep + exchange(topo, send, key).astype(F32)).astype(BF)


class Piece:
    def __init__(self, array, dim, start, size, core, part):
        self.array, self.dim, self.start, self.size = array, dim, start, size
        self.core, self.part = core, part

    def of(self, ref):
        if self.dim == 0:
            return ref.at[pl.ds(self.start, self.size), :]
        return ref.at[:, pl.ds(self.start, self.size)]


def cut_pieces(shapes):
    near = lambda v, unit: max(unit, int(round(v / unit)) * unit)
    wide_a, wide_g, wide_u, tall = shapes[0][1], shapes[1][1], shapes[2][1], shapes[3][0]
    a = near(wide_a * 0.634, 128)
    g = near(wide_g * 0.7, 128)
    u = near(wide_u * 0.65, 128)
    d = near(tall * 0.3, 8)
    return [
        Piece(1, 1, 0, g, 0, 0),
        Piece(0, 1, a, wide_a - a, 0, 2),
        Piece(1, 1, g, wide_g - g, 0, 2),
        Piece(0, 1, 0, a, 0, 1),
        Piece(2, 1, u, wide_u - u, 1, 0),
        Piece(3, 0, 0, d, 1, 0),
        Piece(3, 0, d, tall - d, 1, 2),
        Piece(2, 1, 0, u, 1, 1),
    ]


def coordinates(topo):
    g, t = lax.axis_index("grp"), lax.axis_index("tok")
    return lax.rem(t, topo.X), lax.div(g, 2), lax.div(t, topo.X), lax.rem(g, 2)


def gather_kernel(topo, pieces, *refs):
    shards, outs = refs[:4], refs[4:8]
    local_sem, recv_sem, z_sem, x_sem, y_sem, c_sem = refs[8:]
    x, y, z, c = coordinates(topo)
    X, Z, T = topo.X, topo.Z, topo.T
    g, me = lax.axis_index("grp"), lax.axis_index("tok")
    odd = lax.rem(y, 2)
    over_y = {"grp": g + 2 - 4 * odd, "tok": me}
    over_c = {"grp": g + 1 - 2 * c, "tok": me}

    def over_z(k):
        return {"grp": g, "tok": (z + k) * X + x}

    def over_x(k):
        return {"grp": g, "tok": z * X + lax.rem(x + k, X)}

    barrier = pltpu.get_barrier_semaphore()
    partners = [over_y, over_c] + [over_x(k) for k in range(1, X)]
    for partner in partners:
        pl.semaphore_signal(barrier, inc=1, device_id=partner, device_id_type=pl.DeviceIdType.MESH)
    below, above = z > 0, z < Z - 1

    def greet(k):
        pl.semaphore_signal(
            barrier, inc=1, device_id=over_z(k), device_id_type=pl.DeviceIdType.MESH
        )

    pl.when(below)(lambda: greet(-1))
    pl.when(above)(lambda: greet(1))
    own = [
        pltpu.make_async_copy(shards[i], outs[i].at[me], local_sem.at[i]) for i in range(4)
    ]
    for copy in own:
        copy.start()
    pl.semaphore_wait(barrier, len(partners) + below.astype(jnp.int32) + above.astype(jnp.int32))

    def send(p, t, sem, target, mine=False):
        piece = pieces[p]
        landing = piece.of(outs[piece.array].at[t])
        source = piece.of(shards[piece.array]) if mine else landing
        return pltpu.make_async_remote_copy(
            src_ref=source, dst_ref=landing, send_sem=sem, recv_sem=recv_sem.at[p, t],
            device_id=target, device_id_type=pl.DeviceIdType.MESH,
        )

    def arrived(p, t):
        send(p, t, c_sem.at[0, 0], over_c).wait_recv()

    def run(core):
        mine = [p for p in range(len(pieces)) if pieces[p].core == core]
        theirs = [p for p in range(len(pieces)) if pieces[p].core != core]
        slot = {p: i for i, p in enumerate(mine)}

        def inside(p, body):
            part = pieces[p].part
            if part == 1:
                body()
            else:
                pl.when(odd == part // 2)(body)

        def outside(p, body):
            if pieces[p].part != 1:
                pl.when(odd != pieces[p].part // 2)(body)

        def x_copies(p, zz, first):
            t = zz * X + x
            return [
                send(p, t, x_sem.at[slot[p], zz, k - 1], over_x(k), first) for k in range(1, X)
            ]

        def y_copy(p, t):
            return send(p, t, y_sem.at[slot[p], t], over_y)

        def c_copy(p, t):
            return send(p, t, c_sem.at[slot[p], t], over_c)

        def z_copy(p, zz, k, first):
            return send(p, zz * X + x, z_sem.at[slot[p], zz, (k + 1) // 2], over_z(k), first)

        for p in mine:
            def begin(p=p):
                pl.when(below)(lambda: z_copy(p, z, -1, True).start())
                pl.when(above)(lambda: z_copy(p, z, 1, True).start())
                for copy in x_copies(p, z, True):
                    copy.start()
            inside(p, begin)

        def share(p, t):
            if pieces[p].part != 1:
                y_copy(p, t).start()
            c_copy(p, t).start()

        def relay(p, zz, k):
            arrived(p, zz * X + x)
            pl.when(above if k > 0 else below)(lambda: z_copy(p, zz, k, False).start())
            for copy in x_copies(p, zz, False):
                copy.start()
            share(p, zz * X + x)

        def others(p, zz):
            for j in range(1, X):
                t = zz * X + lax.rem(x + j, X)
                arrived(p, t)
                share(p, t)

        def around(k, carry):
            low, high = z - k, z + k
            for p in mine:
                inside(p, lambda p=p: pl.when(low >= 0)(lambda: relay(p, low, 1)))
                inside(p, lambda p=p: pl.when(high < Z)(lambda: relay(p, high, -1)))
            low, high = z - k + 1, z + k - 1
            for p in mine:
                inside(p, lambda p=p: pl.when(low >= 0)(lambda: others(p, low)))
                inside(p, lambda p=p: pl.when((k > 1) & (high < Z))(lambda: others(p, high)))
            return carry

        lax.fori_loop(1, Z + 1, around, 0)

        def rest(t, carry):
            @pl.when(t != me)
            def _():
                for p in mine:
                    def forward(p=p):
                        arrived(p, t)
                        c_copy(p, t).start()
                    outside(p, forward)
            return carry

        lax.fori_loop(0, T, rest, 0)

        def finish(t, carry):
            @pl.when(t != me)
            def _():
                for p in theirs:
                    arrived(p, t)
                for p in mine:
                    c_copy(p, t).wait_send()
                    if pieces[p].part != 1:
                        inside(p, lambda p=p: y_copy(p, t).wait_send())
            return carry

        lax.fori_loop(0, T, finish, 0)
        for p in mine:
            def end(p=p):
                def each(zz, carry):
                    pl.when((zz <= z) & above)(lambda: z_copy(p, zz, 1, False).wait_send())
                    pl.when((zz >= z) & below)(lambda: z_copy(p, zz, -1, False).wait_send())
                    for copy in x_copies(p, zz, False):
                        copy.wait_send()
                    return carry
                lax.fori_loop(0, Z, each, 0)
            inside(p, end)

    pl.when(c == 0)(lambda: run(0))
    pl.when(c == 1)(lambda: run(1))
    for copy in own:
        copy.wait()


def gather_weights(topo, shards):
    pieces = cut_pieces([s.shape for s in shards])
    T = topo.T
    DMA = pltpu.SemaphoreType.DMA
    hbm = pl.BlockSpec(memory_space=pl.ANY)
    outs = pl.pallas_call(
        functools.partial(gather_kernel, topo, pieces),
        in_specs=[hbm] * 4,
        out_specs=[hbm] * 4,
        out_shape=[jax.ShapeDtypeStruct((T,) + s.shape, s.dtype) for s in shards],
        scratch_shapes=[
            DMA((4,)), DMA((len(pieces), T)), DMA((4, topo.Z, 2)), DMA((4, topo.Z, topo.X - 1)),
            DMA((4, T)), DMA((4, T)),
        ],
        compiler_params=pltpu.CompilerParams(collective_id=0, has_side_effects=True),
        name="gather_weights",
    )(*shards)
    return [o.reshape(-1, o.shape[-1]) for o in outs]


class Share:
    def __init__(self, array, start, shape, part):
        self.array, self.start, self.shape, self.part = array, start, shape, part

    def of(self, ref, core, *lead):
        rows, columns = self.shape
        if self.array == 2:
            return ref.at[(core,) + lead + (slice(None), pl.ds(self.start, columns))]
        if self.array == 3:
            at = pl.multiple_of(core * rows, rows)
            return ref.at[lead + (pl.ds(at, rows), slice(None))]
        at = pl.multiple_of(core * columns, 128)
        return ref.at[lead + (slice(None), pl.ds(at, columns))]


def cut_shares(shapes):
    rows, ff = shapes[2][2], shapes[2][3]
    one = ff * 3 // 20 // 128 * 128
    two = ff * 33 // 40 // 128 * 128
    return [
        Share(2, one, (rows, two - one), 0),
        Share(3, 0, (shapes[3][1] // 2, shapes[3][2]), 2),
        Share(2, two, (rows, ff - two), 2),
        Share(0, 0, (rows, shapes[0][2] // 2), 1),
        Share(1, 0, (rows, shapes[1][2] // 2), 1),
        Share(2, 0, (rows, one), 1),
    ]


def reduce_kernel(topo, shares, *refs):
    grads, outs = refs[:4], refs[4:8]
    count = len(shares)
    groups = []
    at = 8
    for _ in range(7):
        groups.append(refs[at:at + count])
        at += count
    held, from_c, from_y, from_x, from_low, from_high, from_f = groups
    (load_sem, c_send, c_recv, y_send, y_recv, x_send, x_recv, z_send, z_recv, f_send, f_recv,
     o_send, o_recv, o_local) = refs[at:]
    x, y, z, c = coordinates(topo)
    X, Z, T = topo.X, topo.Z, topo.T
    g, me = lax.axis_index("grp"), lax.axis_index("tok")
    odd = lax.rem(y, 2)
    below, above = z > 0, z < Z - 1
    kind = pl.DeviceIdType.MESH

    def over_y(k):
        high = lax.rem(lax.div(y, 1 << k), 2)
        return {"grp": g + (2 - 4 * high) * (1 << k), "tok": me}

    over_c = {"grp": g + 1 - 2 * c, "tok": me}

    def over_z(k):
        return {"grp": g, "tok": (z + k) * X + x}

    def over_x(k):
        return {"grp": g, "tok": z * X + lax.rem(x + k, X)}

    barrier = pltpu.get_barrier_semaphore()
    partners = [over_c] + [over_y(k) for k in range(topo.bits["y"])]
    partners += [over_x(k) for k in range(1, X)]

    def greet(partner):
        pl.semaphore_signal(barrier, inc=1, device_id=partner, device_id_type=kind)

    for partner in partners:
        greet(partner)
    pl.when(below)(lambda: greet(over_z(-1)))
    pl.when(above)(lambda: greet(over_z(1)))
    every = range(count)

    def load(p, t):
        s = shares[p]
        return pltpu.make_async_copy(
            s.of(grads[s.array], c, t), held[p].at[t], load_sem.at[p, t]
        )

    def remote(source, landing, send, recv, target):
        return pltpu.make_async_remote_copy(
            src_ref=source, dst_ref=landing, send_sem=send, recv_sem=recv, device_id=target,
            device_id_type=kind,
        )

    def c_copy(p, t):
        s = shares[p]
        return remote(
            s.of(grads[s.array], 1 - c, t), from_c[p].at[t], c_send.at[p, t], c_recv.at[p, t],
            over_c,
        )

    def y_copy(p, t):
        return remote(
            held[p].at[t], from_y[p].at[t], y_send.at[p, t], y_recv.at[p, t], over_y(0)
        )

    def x_copy(p, zz, k):
        t = zz * X + lax.rem(x + k, X)
        return remote(
            held[p].at[t], from_x[p].at[zz, k - 1], x_send.at[p, zz, k - 1],
            x_recv.at[p, zz, k - 1], over_x(k),
        )

    def z_copy(p, zz, k):
        landing = from_low if k > 0 else from_high
        way = (k + 1) // 2
        return remote(
            held[p].at[zz * X + x], landing[p].at[zz], z_send.at[p, zz, way],
            z_recv.at[p, zz, way], over_z(k),
        )

    def f_copy(p, k):
        return remote(
            held[p].at[me], from_f[p].at[k], f_send.at[p, k], f_recv.at[p, k], over_y(k)
        )

    def o_copy(p):
        s = shares[p]
        return remote(
            held[p].at[me], s.of(outs[s.array], c), o_send.at[p], o_recv.at[p], over_c
        )

    def o_arrived(p):
        s = shares[p]
        return remote(
            held[p].at[me], s.of(outs[s.array], 1 - c), o_send.at[p], o_recv.at[p], over_c
        )

    def o_keep(p):
        s = shares[p]
        return pltpu.make_async_copy(held[p].at[me], s.of(outs[s.array], c), o_local.at[p])

    def add(p, t, other):
        held[p][t] = held[p][t] + other

    def layers(body):
        def step(i, carry):
            k = Z - 1 - i
            pl.when(z + k < Z)(lambda: body(z + k))
            pl.when((k > 0) & (z - k >= 0))(lambda: body(z - k))
            return carry
        return step

    def inside(p, body):
        if shares[p].part == 1:
            body()
        else:
            pl.when(odd == shares[p].part // 2)(body)

    def outside(p, body):
        if shares[p].part != 1:
            pl.when(odd != shares[p].part // 2)(body)

    def start_loads(zz):
        def each(j, carry):
            t = zz * X + lax.rem(x + j, X)
            for p in every:
                load(p, t).start()
            return carry
        lax.fori_loop(0, X, each, 0)

    lax.fori_loop(0, Z, layers(start_loads), 0)
    pl.semaphore_wait(barrier, len(partners) + below.astype(jnp.int32) + above.astype(jnp.int32))

    def start_cores(zz):
        def each(j, carry):
            t = zz * X + lax.rem(x + j, X)
            for p in every:
                c_copy(p, t).start()
            return carry
        lax.fori_loop(0, X, each, 0)

    lax.fori_loop(0, Z, layers(start_cores), 0)

    def cores(zz):
        def each(j, carry):
            t = zz * X + lax.rem(x + j + 1, X)
            for p in every:
                load(p, t).wait()
                c_copy(p, t).wait_recv()
                add(p, t, from_c[p][t])
                outside(p, lambda p=p: y_copy(p, t).start())
                if shares[p].part == 1:
                    for k in range(1, X):
                        pl.when(j + 1 == k)(lambda p=p, k=k: x_copy(p, zz, k).start())
            return carry
        lax.fori_loop(0, X, each, 0)

    lax.fori_loop(0, Z, layers(cores), 0)

    def over(zz):
        def each(j, carry):
            t = zz * X + lax.rem(x + j + 1, X)
            for p in every:
                if shares[p].part != 1:
                    def body(p=p):
                        y_copy(p, t).wait_recv()
                        add(p, t, from_y[p][t])
                        for k in range(1, X):
                            pl.when(j + 1 == k)(lambda: x_copy(p, zz, k).start())
                    inside(p, body)
            return carry
        lax.fori_loop(0, X, each, 0)

    def join(p, zz):
        t = zz * X + x
        for k in range(1, X):
            x_copy(p, zz, k).wait_recv()
            add(p, t, from_x[p][zz, k - 1])

        def low():
            z_copy(p, zz, 1).wait_recv()
            add(p, t, from_low[p][zz])

        def high():
            z_copy(p, zz, -1).wait_recv()
            add(p, t, from_high[p][zz])

        pl.when((zz >= z) & below)(low)
        pl.when((zz <= z) & above)(high)
        pl.when(zz > z)(lambda: z_copy(p, zz, 1).start())
        pl.when(zz < z)(lambda: z_copy(p, zz, -1).start())

    def first_joins(zz):
        for p in every:
            if shares[p].part == 1:
                join(p, zz)

    def last_joins(zz):
        for p in every:
            if shares[p].part != 1:
                inside(p, lambda p=p: join(p, zz))

    def main(i, carry):
        @pl.when(i < Z)
        def _():
            layers(first_joins)(i, 0)
            layers(over)(i, 0)

        @pl.when(i > 0)
        def _():
            layers(last_joins)(i - 1, 0)

        return carry

    lax.fori_loop(0, Z + 1, main, 0)

    for k in range(1, topo.bits["y"]):
        for p in every:
            inside(p, lambda p=p: f_copy(p, k).start())
        for p in every:
            def fold(p=p):
                f_copy(p, k).wait()
                add(p, me, from_f[p][k])
            inside(p, fold)
    for p in every:
        inside(p, lambda p=p: f_copy(p, 0).start())
    for p in every:
        if shares[p].part == 1:
            f_copy(p, 0).wait()
            add(p, me, from_f[p][0])
        else:
            def take(p=p):
                f_copy(p, 0).wait_recv()
                held[p][me] = from_f[p][0]
            outside(p, lambda p=p: y_copy(p, me).wait_send())
            outside(p, take)
        o_copy(p).start()
        o_keep(p).start()

    def ends(t, carry):
        for p in every:
            c_copy(p, t).wait_send()
            outside(p, lambda p=p: pl.when(t != me)(lambda: y_copy(p, t).wait_send()))
        return carry

    lax.fori_loop(0, T, ends, 0)

    def z_ends(zz, carry):
        for p in every:
            def body(p=p):
                for k in range(1, X):
                    x_copy(p, zz, k).wait_send()
                pl.when(zz > z)(lambda: z_copy(p, zz, 1).wait_send())
                pl.when(zz < z)(lambda: z_copy(p, zz, -1).wait_send())
            inside(p, body)
        return carry

    lax.fori_loop(0, Z, z_ends, 0)
    for p in every:
        if shares[p].part != 1:
            inside(p, lambda p=p: f_copy(p, 0).wait_send())
        o_copy(p).wait_send()
        o_arrived(p).wait_recv()
        o_keep(p).wait()


def reduce_gradients(topo, grads):
    shares = cut_shares([v.shape for v in grads])
    X, Z, T = topo.X, topo.Z, topo.T
    n = len(shares)
    folds = max(1, topo.bits["y"])
    DMA = pltpu.SemaphoreType.DMA
    hbm = pl.BlockSpec(memory_space=pl.ANY)
    lead = [(T,), (T,), (T,), (Z, X - 1), (Z,), (Z,), (folds,)]
    rooms = [
        pltpu.VMEM(front + s.shape, BF)
        for front in lead for s in shares
    ]
    outs = [grads[0].shape[1:], grads[1].shape[1:], (2,) + grads[2].shape[2:], grads[3].shape[1:]]
    return pl.pallas_call(
        functools.partial(reduce_kernel, topo, shares),
        in_specs=[hbm] * 4,
        out_specs=[hbm] * 4,
        out_shape=[jax.ShapeDtypeStruct(s, BF) for s in outs],
        scratch_shapes=rooms + [
            DMA((n, T)), DMA((n, T)), DMA((n, T)), DMA((n, T)), DMA((n, T)),
            DMA((n, Z, X - 1)), DMA((n, Z, X - 1)), DMA((n, Z, 2)), DMA((n, Z, 2)),
            DMA((n, folds)), DMA((n, folds)), DMA((n,)), DMA((n,)), DMA((n,)),
        ],
        compiler_params=pltpu.CompilerParams(
            collective_id=1, has_side_effects=True, vmem_limit_bytes=60 << 20
        ),
        name="reduce_gradients",
    )(*grads)


def group_order(topo):
    return list(reversed(topo.keys("y"))) + topo.keys("c") + list(reversed(topo.keys("x")))


def group_gather(topo, arr, order):
    names = group_order(topo)
    held = []
    shape = arr.shape
    for key in order:
        place = sum(1 for h in held if names.index(h) < names.index(key))
        arr = double(topo, arr, key, place, True)
        held.append(key)
    return arr.reshape((topo.T,) + shape)


def group_scatter(topo, arr, order):
    names = group_order(topo)
    held = list(names)
    arr = arr.reshape((2,) * len(names) + arr.shape[1:])
    for key in order:
        arr = halve(topo, arr, key, held.index(key), True)
        held.remove(key)
    return arr


def fill_bias(bias, key_ref, query_ref, rows, first, last):
    def body(t, carry):
        at = pl.ds(pl.multiple_of(t * rows, rows), rows)
        keys = key_ref[at, :]
        live, order = keys[:, 0:1], keys[:, 1:2]
        begin, place = query_ref[0:1, :], query_ref[1:2, :]
        allowed = ((live >= begin) & (live <= place)) | (order == place)
        bias[at, :] = jnp.where(allowed, 0.0, BIG)
        return carry

    lax.fori_loop(first, last, body, 0)


NT = (((1,), (1,)), ((), ()))
TN = (((0,), (0,)), ((), ()))


def attend_kernel(rows, span, key_ref, query_ref, kv_ref, q_ref, out_ref, stat_ref, bias, held):
    first, last = span[0], span[1]

    @pl.when(pl.program_id(0) == 0)
    def _():
        fill_bias(bias, key_ref, query_ref, rows, first, last)

    wide = q_ref.shape[1]
    queries = q_ref[0]

    def scores(t, top):
        at = pl.ds(pl.multiple_of(t * rows, rows), rows)
        s = lax.dot_general(kv_ref[at, :], queries, NT, preferred_element_type=F32) + bias[at, :]
        held[at, :] = s
        return jnp.maximum(top, jnp.max(s.reshape(rows // 8, 8, wide), axis=0))

    top = lax.fori_loop(first, last, scores, jnp.full((8, wide), BIG, F32))
    top = jnp.max(top, axis=0, keepdims=True)

    out_ref[0] = jnp.zeros(out_ref.shape[1:], F32)

    def mix(t, total):
        at = pl.ds(pl.multiple_of(t * rows, rows), rows)
        p = jnp.exp(held[at, :] - top)
        out_ref[0] += lax.dot_general(
            kv_ref[at, :], p.astype(BF), TN, preferred_element_type=F32
        )
        return total + jnp.sum(p.reshape(rows // 8, 8, wide), axis=0)

    total = lax.fori_loop(first, last, mix, jnp.zeros((8, wide), F32))
    total = jnp.sum(total, axis=0, keepdims=True)
    out_ref[0] = out_ref[0] / total
    stat_ref[0] = jnp.broadcast_to(top + jnp.log(total), (8, wide))


def attend(rows, span, key_labels, query_labels, kv_all, q_pad):
    count = kv_all.shape[0]
    wide = q_pad.shape[1]
    fixed = lambda h, s: (0, 0)
    return pl.pallas_call(
        functools.partial(attend_kernel, rows),
        grid_spec=pltpu.PrefetchScalarGridSpec(
            num_scalar_prefetch=1,
            grid=(KV_HEADS,),
            in_specs=[
                pl.BlockSpec((count, 8), fixed),
                pl.BlockSpec((8, wide), fixed),
                pl.BlockSpec((count, 2 * HD), lambda h, s: (0, h)),
                pl.BlockSpec((1, wide, 2 * HD), lambda h, s: (h, 0, 0)),
            ],
            out_specs=[
                pl.BlockSpec((1, 2 * HD, wide), lambda h, s: (h, 0, 0)),
                pl.BlockSpec((1, 8, wide), lambda h, s: (h, 0, 0)),
            ],
            scratch_shapes=[pltpu.VMEM((count, wide), F32), pltpu.VMEM((count, wide), F32)],
        ),
        out_shape=[
            jax.ShapeDtypeStruct((KV_HEADS, 2 * HD, wide), F32),
            jax.ShapeDtypeStruct((KV_HEADS, 8, wide), F32),
        ],
        compiler_params=pltpu.CompilerParams(vmem_limit_bytes=62 << 20),
        cost_estimate=pl.CostEstimate(
            flops=8 * KV_HEADS * wide * count * HD,
            bytes_accessed=2 * count * 2 * HD * KV_HEADS + 8 * KV_HEADS * wide * HD * 2,
            transcendentals=KV_HEADS * wide * count,
        ),
        name="attend",
    )(span, key_labels, query_labels, kv_all, q_pad)


def attend_back_kernel(
    rows, span, key_ref, query_ref, kv_ref, q_ref, stat_ref, delta_ref, dq_ref, dkv_ref, bias
):
    first, last = span[0], span[1]

    @pl.when(pl.program_id(0) == 0)
    def _():
        fill_bias(bias, key_ref, query_ref, rows, first, last)

    queries = q_ref[0]
    stat = stat_ref[0, 0:1, :]
    delta = delta_ref[0, 0:1, :]
    dkv_ref[...] = jnp.zeros(dkv_ref.shape, BF)
    dq_ref[0] = jnp.zeros(dq_ref.shape[1:], F32)
    low = lax.broadcasted_iota(jnp.int32, (rows, 2 * HD), 1) < HD

    def body(t, carry):
        at = pl.ds(pl.multiple_of(t * rows, rows), rows)
        kv = kv_ref[at, :]
        zero = jnp.zeros_like(kv)
        s = lax.dot_general(jnp.where(low, kv, zero), queries, NT, preferred_element_type=F32)
        p = jnp.exp(s + bias[at, :] - stat)
        dp = lax.dot_general(jnp.where(low, zero, kv), queries, NT, preferred_element_type=F32)
        ds = (p * (dp - delta)).astype(BF)
        dk = jnp.dot(ds, queries, preferred_element_type=F32)
        dv = jnp.dot(p.astype(BF), queries, preferred_element_type=F32)
        dkv_ref[at, :] = jnp.where(low, dk, dv).astype(BF)
        dq_ref[0] += lax.dot_general(kv, ds, TN, preferred_element_type=F32)
        return carry

    lax.fori_loop(first, last, body, 0)


def attend_back(rows, span, key_labels, query_labels, kv_all, q_do, stat, delta):
    count = kv_all.shape[0]
    wide = q_do.shape[1]
    fixed = lambda h, s: (0, 0)
    head = lambda h, s: (h, 0, 0)
    return pl.pallas_call(
        functools.partial(attend_back_kernel, rows),
        grid_spec=pltpu.PrefetchScalarGridSpec(
            num_scalar_prefetch=1,
            grid=(KV_HEADS,),
            in_specs=[
                pl.BlockSpec((count, 8), fixed),
                pl.BlockSpec((8, wide), fixed),
                pl.BlockSpec((count, 2 * HD), lambda h, s: (0, h)),
                pl.BlockSpec((1, wide, 2 * HD), head),
                pl.BlockSpec((1, 8, wide), head),
                pl.BlockSpec((1, 8, wide), head),
            ],
            out_specs=[
                pl.BlockSpec((1, 2 * HD, wide), head),
                pl.BlockSpec((count, 2 * HD), lambda h, s: (0, h)),
            ],
            scratch_shapes=[pltpu.VMEM((count, wide), F32)],
        ),
        out_shape=[
            jax.ShapeDtypeStruct((KV_HEADS, 2 * HD, wide), F32),
            jax.ShapeDtypeStruct((count, KV_HEADS * 2 * HD), BF),
        ],
        compiler_params=pltpu.CompilerParams(vmem_limit_bytes=62 << 20),
        cost_estimate=pl.CostEstimate(
            flops=20 * KV_HEADS * wide * count * HD,
            bytes_accessed=4 * count * 2 * HD * KV_HEADS + 8 * KV_HEADS * wide * HD * 2,
            transcendentals=KV_HEADS * wide * count,
        ),
        name="attend_back",
    )(span, key_labels, query_labels, kv_all, q_do, stat, delta)


def mm(a, b):
    return jnp.dot(a, b, preferred_element_type=F32)


def mm_nt(a, b):
    return lax.dot_general(a, b, NT, preferred_element_type=F32)


def mm_tn(a, b):
    return lax.dot_general(a, b, TN, preferred_element_type=F32)


def inverse_rms(v):
    return lax.rsqrt(jnp.mean(v * v, axis=-1, keepdims=True) + EPS)


def norm_back(grad, v, inv, gain):
    scaled = grad * gain
    dot = jnp.mean(scaled * v, axis=-1, keepdims=True)
    return (inv * scaled - v * (inv * inv * inv * dot), jnp.sum(grad * v * inv, axis=0))


def turn(values, cosine, sine):
    half = HD // 2
    lower, upper = values[..., :half], values[..., half:]
    return jnp.concatenate(
        [lower * cosine - upper * sine, upper * cosine + lower * sine], axis=-1
    )


def heads_first(v):
    n = v.shape[0]
    return v.reshape(n, HEADS, HD).transpose(1, 0, 2)


def heads_back(v):
    n = v.shape[-1] // SHARES
    return v.reshape(KV_HEADS, HD, SHARES, n).transpose(3, 0, 2, 1).reshape(n, HEADS, HD)


def pair_up(q, d):
    n = q.shape[1]
    return jnp.concatenate([q, d], axis=-1).reshape(KV_HEADS, SHARES * n, 2 * HD)


def per_device(topo, *args):
    (tokens, w_query, w_key, w_value, w_out, w_gate, w_up, w_down, router, norm_attn, norm_ffn,
     lengths, depths, padding, cotangent) = args
    rows, model = tokens.shape
    kv_cols = w_key.shape[1]
    ff = w_gate.shape[1]
    shard = w_query.shape[0]
    deep_rows = rows * 3 // 4
    xk, yk, ck = (topo.keys(d) for d in "xyc")

    small = jnp.concatenate([router, norm_attn[:, None], norm_ffn[:, None]], axis=1)
    small = jnp.pad(small, ((0, 0), (0, HD - small.shape[1])))
    w_kv = jnp.stack(
        [w_key.reshape(shard, KV_HEADS, HD), w_value.reshape(shard, KV_HEADS, HD)], axis=2
    ).reshape(shard, 2 * kv_cols)
    first = jnp.concatenate([w_query, small, w_kv, w_out], axis=1)
    all_first, weight_g, weight_u, weight_d = gather_weights(
        topo, [first, w_gate, w_up, w_down]
    )

    own = lax.axis_index("tok") * rows + jnp.arange(rows, dtype=jnp.int32)
    eligible = (depths >= 2) & (padding > 0)
    flags = jnp.stack([eligible, ~eligible]).astype(BF)
    upto = (jnp.arange(rows)[:, None] <= jnp.arange(rows)[None, :]).astype(BF)
    counts = mm(flags, upto).astype(jnp.int32)
    slot = jnp.where(eligible, counts[0] - 1, counts[0, -1] + counts[1] - 1)
    chosen = jnp.arange(rows, dtype=jnp.int32)[:, None] == slot[None, :]
    onehot = chosen.astype(BF)
    doc_ends = jnp.cumsum(lengths[0])
    begins = jnp.sum(
        jnp.where(own[:, None] >= doc_ends[None, :], lengths[0][None, :], 0), axis=1
    )
    levels = jnp.where(padding > 0, depths, 0)
    labels = jnp.stack([own, begins, levels])
    labels = jnp.sum(jnp.where(chosen[None], labels[:, None, :], 0), axis=2)
    labels = jnp.pad(labels, ((0, 5), (0, 0)))
    swap = topo.swap_pairs()
    state = lax.ppermute(mm(onehot, tokens).astype(BF), AXES, swap).astype(F32)
    labels = lax.ppermute(labels, AXES, swap)
    gradient = lax.ppermute(mm(onehot, cotangent).astype(BF), AXES, swap).astype(F32)
    order_g = xk + yk + ck
    labels_all = group_gather(topo, labels, order_g)

    small = all_first[:, model:model + HD].astype(F32)
    gain_one, gain_two = small[:, RECS], small[:, RECS + 1]
    weight_q = all_first[:, :model]
    weight_kv = all_first[:, model + HD:model + HD + 2 * kv_cols]
    weight_o = all_first[:, model + HD + 2 * kv_cols:]

    pack = (lax.axis_index("grp") * topo.X) + lax.axis_index("tok") % topo.X
    begin_all, level_mine = labels[1], labels[2]
    lowest = jnp.min(labels[1])
    span = jnp.stack([lowest // rows, pack + 1]).astype(jnp.int32)
    places = (labels[0] - labels[1]).astype(F32)
    freqs = 10000.0 ** (-(jnp.arange(HD // 2, dtype=F32) * 2.0 / HD))
    angles = places[:, None] * freqs[None, :]
    cosine, sine = jnp.cos(angles), jnp.sin(angles)

    def forward(state, recursion):
        n = state.shape[0]
        cos_n, sin_n = cosine[:n], sine[:n]
        inv_one = inverse_rms(state)
        n1 = (state * inv_one * gain_one).astype(BF)
        q = heads_first(mm(n1, weight_q))
        q = (turn(q, cos_n, sin_n).astype(BF) * BF(HD ** -0.5)).astype(BF)
        kv = mm(n1, weight_kv).reshape(n, KV_HEADS, 2, HD)
        k = turn(kv[:, :, 0], cos_n[:, None], sin_n[:, None])
        kv = jnp.stack([k, kv[:, :, 1]], axis=2).reshape(n, 2 * kv_cols).astype(BF)
        kv_all = group_gather(topo, kv, order_g).reshape(topo.T * n, 2 * kv_cols)
        live = labels_all[:, 2, :n] > recursion
        order = labels_all[:, 0, :n]
        key_labels = jnp.stack([jnp.where(live, order, -1), order], axis=-1).reshape(-1, 2)
        key_labels = jnp.pad(key_labels, ((0, 0), (0, 6)))
        query_labels = jnp.stack([labels[1, :n], labels[0, :n]])
        query_labels = jnp.pad(jnp.tile(query_labels, (1, SHARES)), ((0, 6), (0, 0)))
        q_pad = pair_up(q, jnp.zeros_like(q))
        out, stat = attend(n, span, key_labels, query_labels, kv_all, q_pad)
        out = heads_back(out[:, HD:])
        mixed = out.reshape(n, HEADS * HD).astype(BF)
        attended = mm(mixed, weight_o)
        middle = state + attended
        inv_two = inverse_rms(middle)
        n2 = (middle * inv_two * gain_two).astype(BF)
        gated, upward = mm(n2, weight_g), mm(n2, weight_u)
        hidden = (jax.nn.silu(gated) * upward).astype(BF)
        both = attended + mm(hidden, weight_d)
        gate = jax.nn.sigmoid(jnp.sum(state * small[:, recursion], axis=-1, keepdims=True))
        active = (labels[2, :n] > recursion).astype(F32)[:, None]
        new = state + active * gate * both
        kept = (state, inv_one, n1, q, kv_all, key_labels, query_labels, out, stat, mixed, middle,
                inv_two, n2, gated, upward, hidden, both, gate, active)
        return (new, kept)

    def backward(gradient, recursion, kept):
        (state, inv_one, n1, q, kv_all, key_labels, query_labels, out, stat, mixed, middle,
         inv_two, n2, gated, upward, hidden, both, gate, active) = kept
        n = state.shape[0]
        d_both = active * gate * gradient
        d_fed = d_both.astype(BF)
        d_gate = active * gate * (1.0 - gate) * jnp.sum(gradient * both, axis=-1, keepdims=True)
        d_router = jnp.sum(state * d_gate, axis=0)
        d_hidden = mm_nt(d_fed, weight_d)
        sig = jax.nn.sigmoid(gated)
        d_up = (d_hidden * gated * sig).astype(BF)
        d_gated = (d_hidden * upward * sig * (1.0 + gated * (1.0 - sig))).astype(BF)
        d_middle, d_gain_two = norm_back(
            mm_nt(d_gated, weight_g) + mm_nt(d_up, weight_u), middle, inv_two, gain_two)
        d_att = (d_both + d_middle).astype(BF)
        gradient = gradient + d_gate * small[:, recursion] + d_middle
        d_mixed = mm_nt(d_att, weight_o).astype(BF)
        d_heads = heads_first(d_mixed)
        delta = jnp.sum(
            d_heads.astype(F32) * out.transpose(1, 0, 2), axis=-1
        ).reshape(KV_HEADS, 1, SHARES * n)
        delta = jnp.broadcast_to(delta, (KV_HEADS, 8, SHARES * n))
        dq, dkv = attend_back(
            n, span, key_labels, query_labels, kv_all, pair_up(q, d_heads), stat, delta
        )
        dkv = group_scatter(
            topo, dkv.reshape(topo.T, n, 2 * kv_cols), ck + yk + xk
        ).astype(F32).reshape(n, KV_HEADS, 2, HD)
        cos_n, sin_n = cosine[:n, None], sine[:n, None]
        dk = turn(dkv[:, :, 0], cos_n, -sin_n)
        dkv = jnp.stack([dk, dkv[:, :, 1]], axis=2).reshape(n, 2 * kv_cols).astype(BF)
        dq = turn(heads_back(dq[:, :HD]) * HD ** -0.5, cos_n, -sin_n)
        dq = dq.reshape(n, HEADS * HD).astype(BF)
        d_n1 = mm_nt(dq, weight_q) + mm_nt(dkv, weight_kv)
        d_state, d_gain_one = norm_back(d_n1, state, inv_one, gain_one)
        blank = jnp.zeros((n, HD), BF)
        dqkv = jnp.concatenate([dq, blank, dkv], axis=1)
        dqkv = jnp.pad(dqkv, ((0, 0), (0, -dqkv.shape[1] % 256)))
        left = (n1, dqkv, mixed, d_att, n2, d_gated, d_up, hidden, d_fed)
        return (gradient + d_state, left, (d_router, d_gain_one, d_gain_two))

    whole_state, kept = forward(state, 0)
    deep = whole_state[:deep_rows]
    all_kept = [kept]
    for recursion in range(1, RECS):
        deep, kept = forward(deep, recursion)
        all_kept.append(kept)
    final = jnp.concatenate([deep, whole_state[deep_rows:]], axis=0).astype(BF)
    final = lax.ppermute(final, AXES, swap)

    deep_grad = gradient[:deep_rows]
    lefts, smalls = [], []
    for recursion in reversed(range(1, RECS)):
        deep_grad, left, tiny = backward(deep_grad, recursion, all_kept[recursion])
        lefts.append(left)
        smalls.append(tiny)
    gradient = jnp.concatenate([deep_grad, gradient[deep_rows:]], axis=0)
    gradient, left, tiny = backward(gradient, 0, all_kept[0])
    lefts.append(left)
    smalls.append(tiny)
    gradient = lax.ppermute(gradient.astype(BF), AXES, swap)

    n1, dqkv, mixed, d_att, n2, d_gated, d_up, hidden, d_fed = (
        jnp.concatenate(parts, axis=0) for parts in zip(*lefts)
    )
    cut = lambda v: v.astype(BF).reshape(topo.T, -1, v.shape[-1])
    tiny = jnp.stack(
        [smalls[2][0], smalls[1][0], smalls[0][0],
         smalls[0][1] + smalls[1][1] + smalls[2][1],
         smalls[0][2] + smalls[1][2] + smalls[2][2]], axis=1
    )
    wide_out = -(-(model + tiny.shape[1]) // 256) * 256
    tiny = jnp.pad(tiny, ((0, 0), (0, wide_out - model - tiny.shape[1])))
    grad_qkv, grad_o, grad_gu, grad_down = reduce_gradients(topo, [
        cut(mm_tn(n1, dqkv)),
        cut(jnp.concatenate([mm_tn(mixed, d_att), tiny], axis=1)),
        jnp.stack([cut(mm_tn(n2, d_gated)), cut(mm_tn(n2, d_up))]),
        cut(mm_tn(hidden, d_fed)),
    ])
    grad_query = grad_qkv[:, :model].astype(F32)
    pair = grad_qkv[:, model + HD:model + HD + 2 * kv_cols].astype(F32)
    pair = pair.reshape(shard, KV_HEADS, 2, HD)
    grad_key = pair[:, :, 0].reshape(shard, kv_cols)
    grad_value = pair[:, :, 1].reshape(shard, kv_cols)
    grad_out = grad_o[:, :model].astype(F32)
    tiny = grad_o[:, model:].astype(F32)
    grad_gate, grad_up = grad_gu[0].astype(F32), grad_gu[1].astype(F32)
    grad_down = grad_down.astype(F32)

    def unsort(v):
        return mm_tn(onehot, v).astype(BF)

    return (
        unsort(final), unsort(gradient), grad_query, grad_key, grad_value, grad_out,
        grad_gate, grad_up, grad_down, tiny[:, :RECS], tiny[:, RECS],
        tiny[:, RECS + 1],
    )


def solution(mesh):
    topo = Topo(mesh.shape["grp"], mesh.shape["tok"])
    both = P(("grp", "tok"))
    wide = P(("grp", "tok"), None)
    rows = P("tok", None)
    row = P("tok")
    return jax.shard_map(
        functools.partial(per_device, topo),
        mesh=mesh,
        in_specs=(wide,) + (rows,) * 8 + (row, row, P("grp", None), both, both, wide),
        out_specs=(wide, wide) + (rows,) * 8 + (row, row),
        check_vma=False,
    )
```

```python
import functools

import jax
import jax.numpy as jnp
from jax import lax
from jax.experimental import pallas as pl
from jax.experimental.pallas import tpu as pltpu
from jax.sharding import PartitionSpec as P

HEADS = 15
KV_HEADS = 5
SHARES = HEADS // KV_HEADS
HD = 64
RECS = 3
EPS = 1e-05
BF = jnp.bfloat16
F32 = jnp.float32
BIG = -1e30
AXES = ("grp", "tok")


class Topo:
    def __init__(self, groups, spread):
        self.G = groups
        self.T = spread
        self.X = spread // groups
        self.Z = groups
        self.Y = groups // 2
        self.bits = {
            "z": self.Z.bit_length() - 1,
            "x": self.X.bit_length() - 1,
            "y": self.Y.bit_length() - 1,
            "c": 1,
        }

    def keys(self, dim):
        return [(dim, k) for k in range(self.bits[dim])]

    def masks(self, key):
        dim, k = key
        if dim == "c":
            return (1, 0)
        if dim == "y":
            return (2 << k, 0)
        if dim == "x":
            return (0, 1 << k)
        return (0, self.X << k)

    def pairs(self, key):
        mg, mt = self.masks(key)
        return [
            (g * self.T + t, (g ^ mg) * self.T + (t ^ mt))
            for g in range(self.G)
            for t in range(self.T)
        ]

    def swap_pairs(self):
        out = []
        for g in range(self.G):
            for t in range(self.T):
                z, x = t // self.X, t % self.X
                out.append((g * self.T + t, z * self.T + g * self.X + x))
        return out

    def bit(self, key):
        mg, mt = self.masks(key)
        if mg:
            return (lax.axis_index("grp") // mg) % 2
        return (lax.axis_index("tok") // mt) % 2


def exchange(topo, arr, key):
    return lax.ppermute(arr, AXES, topo.pairs(key))


def double(topo, arr, key, axis, stack):
    other = exchange(topo, arr, key)
    mine_is_high = topo.bit(key) == 1
    low = jnp.where(mine_is_high, other, arr)
    high = jnp.where(mine_is_high, arr, other)
    if stack:
        return jnp.stack([low, high], axis=axis)
    return jnp.concatenate([low, high], axis=axis)


def halve(topo, arr, key, axis, stack):
    mine_is_high = topo.bit(key) == 1
    if stack:
        low = lax.index_in_dim(arr, 0, axis, keepdims=False)
        high = lax.index_in_dim(arr, 1, axis, keepdims=False)
    else:
        half = arr.shape[axis] // 2
        low = lax.slice_in_dim(arr, 0, half, axis=axis)
        high = lax.slice_in_dim(arr, half, 2 * half, axis=axis)
    send = jnp.where(mine_is_high, low, high).astype(BF)
    keep = jnp.where(mine_is_high, high, low).astype(F32)
    return (keep + exchange(topo, send, key).astype(F32)).astype(BF)


class Piece:
    def __init__(self, array, dim, start, size, core, part):
        self.array, self.dim, self.start, self.size = array, dim, start, size
        self.core, self.part = core, part

    def of(self, ref):
        if self.dim == 0:
            return ref.at[pl.ds(self.start, self.size), :]
        return ref.at[:, pl.ds(self.start, self.size)]


def cut_pieces(shapes):
    near = lambda v, unit: max(unit, int(round(v / unit)) * unit)
    wide_a, wide_g, wide_u, tall = shapes[0][1], shapes[1][1], shapes[2][1], shapes[3][0]
    g = near(wide_g * 0.7, 128)
    u = near(wide_u * 0.65, 128)
    d = near(tall * 0.3, 8)
    return [
        Piece(1, 1, 0, g, 0, 0),
        Piece(4, 1, 0, shapes[4][1], 0, 2),
        Piece(1, 1, g, wide_g - g, 0, 2),
        Piece(0, 1, 0, wide_a, 0, 1),
        Piece(2, 1, u, wide_u - u, 1, 0),
        Piece(3, 0, 0, d, 1, 0),
        Piece(3, 0, d, tall - d, 1, 2),
        Piece(2, 1, 0, u, 1, 1),
    ]


def coordinates(topo):
    g, t = lax.axis_index("grp"), lax.axis_index("tok")
    return lax.rem(t, topo.X), lax.div(g, 2), lax.div(t, topo.X), lax.rem(g, 2)


def gather_kernel(topo, pieces, *refs):
    shards, outs = refs[:5], refs[5:10]
    local_sem, recv_sem, z_sem, x_sem, y_sem, c_sem = refs[10:]
    x, y, z, c = coordinates(topo)
    X, Z, T = topo.X, topo.Z, topo.T
    g, me = lax.axis_index("grp"), lax.axis_index("tok")
    odd = lax.rem(y, 2)
    over_y = {"grp": g + 2 - 4 * odd, "tok": me}
    over_c = {"grp": g + 1 - 2 * c, "tok": me}

    def over_z(k):
        return {"grp": g, "tok": (z + k) * X + x}

    def over_x(k):
        return {"grp": g, "tok": z * X + lax.rem(x + k, X)}

    barrier = pltpu.get_barrier_semaphore()
    partners = [over_y, over_c] + [over_x(k) for k in range(1, X)]
    for partner in partners:
        pl.semaphore_signal(barrier, inc=1, device_id=partner, device_id_type=pl.DeviceIdType.MESH)
    below, above = z > 0, z < Z - 1

    def greet(k):
        pl.semaphore_signal(
            barrier, inc=1, device_id=over_z(k), device_id_type=pl.DeviceIdType.MESH
        )

    pl.when(below)(lambda: greet(-1))
    pl.when(above)(lambda: greet(1))
    own = [
        pltpu.make_async_copy(shards[i], outs[i].at[me], local_sem.at[i]) for i in range(5)
    ]
    for copy in own:
        copy.start()
    pl.semaphore_wait(barrier, len(partners) + below.astype(jnp.int32) + above.astype(jnp.int32))

    def send(p, t, sem, target, mine=False):
        piece = pieces[p]
        landing = piece.of(outs[piece.array].at[t])
        source = piece.of(shards[piece.array]) if mine else landing
        return pltpu.make_async_remote_copy(
            src_ref=source, dst_ref=landing, send_sem=sem, recv_sem=recv_sem.at[p, t],
            device_id=target, device_id_type=pl.DeviceIdType.MESH,
        )

    def arrived(p, t):
        send(p, t, c_sem.at[0, 0], over_c).wait_recv()

    def run(core):
        mine = [p for p in range(len(pieces)) if pieces[p].core == core]
        theirs = [p for p in range(len(pieces)) if pieces[p].core != core]
        slot = {p: i for i, p in enumerate(mine)}

        def inside(p, body):
            part = pieces[p].part
            if part == 1:
                body()
            else:
                pl.when(odd == part // 2)(body)

        def outside(p, body):
            if pieces[p].part != 1:
                pl.when(odd != pieces[p].part // 2)(body)

        def x_copies(p, zz, first):
            t = zz * X + x
            return [
                send(p, t, x_sem.at[slot[p], zz, k - 1], over_x(k), first) for k in range(1, X)
            ]

        def y_copy(p, t):
            return send(p, t, y_sem.at[slot[p], t], over_y)

        def c_copy(p, t):
            return send(p, t, c_sem.at[slot[p], t], over_c)

        def z_copy(p, zz, k, first):
            return send(p, zz * X + x, z_sem.at[slot[p], zz, (k + 1) // 2], over_z(k), first)

        for p in mine:
            def begin(p=p):
                pl.when(below)(lambda: z_copy(p, z, -1, True).start())
                pl.when(above)(lambda: z_copy(p, z, 1, True).start())
                for copy in x_copies(p, z, True):
                    copy.start()
            inside(p, begin)

        def share(p, t):
            if pieces[p].part != 1:
                y_copy(p, t).start()
            c_copy(p, t).start()

        def relay(p, zz, k):
            arrived(p, zz * X + x)
            pl.when(above if k > 0 else below)(lambda: z_copy(p, zz, k, False).start())
            for copy in x_copies(p, zz, False):
                copy.start()
            share(p, zz * X + x)

        def others(p, zz):
            for j in range(1, X):
                t = zz * X + lax.rem(x + j, X)
                arrived(p, t)
                share(p, t)

        def around(k, carry):
            low, high = z - k, z + k
            for p in mine:
                inside(p, lambda p=p: pl.when(low >= 0)(lambda: relay(p, low, 1)))
                inside(p, lambda p=p: pl.when(high < Z)(lambda: relay(p, high, -1)))
            low, high = z - k + 1, z + k - 1
            for p in mine:
                inside(p, lambda p=p: pl.when(low >= 0)(lambda: others(p, low)))
                inside(p, lambda p=p: pl.when((k > 1) & (high < Z))(lambda: others(p, high)))
            return carry

        lax.fori_loop(1, Z + 1, around, 0)

        def rest(t, carry):
            @pl.when(t != me)
            def _():
                for p in mine:
                    def forward(p=p):
                        arrived(p, t)
                        c_copy(p, t).start()
                    outside(p, forward)
            return carry

        lax.fori_loop(0, T, rest, 0)

        def finish(t, carry):
            @pl.when(t != me)
            def _():
                for p in theirs:
                    arrived(p, t)
                for p in mine:
                    c_copy(p, t).wait_send()
                    if pieces[p].part != 1:
                        inside(p, lambda p=p: y_copy(p, t).wait_send())
            return carry

        lax.fori_loop(0, T, finish, 0)
        for p in mine:
            def end(p=p):
                def each(zz, carry):
                    pl.when((zz <= z) & above)(lambda: z_copy(p, zz, 1, False).wait_send())
                    pl.when((zz >= z) & below)(lambda: z_copy(p, zz, -1, False).wait_send())
                    for copy in x_copies(p, zz, False):
                        copy.wait_send()
                    return carry
                lax.fori_loop(0, Z, each, 0)
            inside(p, end)

    pl.when(c == 0)(lambda: run(0))
    pl.when(c == 1)(lambda: run(1))
    for copy in own:
        copy.wait()


def gather_weights(topo, shards):
    pieces = cut_pieces([s.shape for s in shards])
    T = topo.T
    DMA = pltpu.SemaphoreType.DMA
    hbm = pl.BlockSpec(memory_space=pl.ANY)
    outs = pl.pallas_call(
        functools.partial(gather_kernel, topo, pieces),
        in_specs=[hbm] * 5,
        out_specs=[hbm] * 5,
        out_shape=[jax.ShapeDtypeStruct((T,) + s.shape, s.dtype) for s in shards],
        scratch_shapes=[
            DMA((5,)), DMA((len(pieces), T)), DMA((4, topo.Z, 2)), DMA((4, topo.Z, topo.X - 1)),
            DMA((4, T)), DMA((4, T)),
        ],
        compiler_params=pltpu.CompilerParams(collective_id=0, has_side_effects=True),
        name="gather_weights",
    )(*shards)
    return [o.reshape(-1, o.shape[-1]) for o in outs]


class Share:
    def __init__(self, array, start, shape, part):
        self.array, self.start, self.shape, self.part = array, start, shape, part

    def of(self, ref, core, *lead):
        rows, columns = self.shape
        if self.array == 2:
            return ref.at[(core,) + lead + (slice(None), pl.ds(self.start, columns))]
        if self.array == 3:
            at = pl.multiple_of(core * rows, rows)
            return ref.at[lead + (pl.ds(at, rows), slice(None))]
        at = pl.multiple_of(core * columns, 128)
        return ref.at[lead + (slice(None), pl.ds(at, columns))]


def cut_shares(shapes):
    rows, ff = shapes[2][2], shapes[2][3]
    one = ff * 3 // 20 // 128 * 128
    two = ff * 33 // 40 // 128 * 128
    return [
        Share(2, one, (rows, two - one), 0),
        Share(3, 0, (shapes[3][1] // 2, shapes[3][2]), 2),
        Share(2, two, (rows, ff - two), 2),
        Share(0, 0, (rows, shapes[0][2] // 2), 1),
        Share(1, 0, (rows, shapes[1][2] // 2), 1),
        Share(2, 0, (rows, one), 1),
    ]


def reduce_kernel(topo, shares, *refs):
    grads, outs = refs[:4], refs[4:8]
    count = len(shares)
    groups = []
    at = 8
    for _ in range(7):
        groups.append(refs[at:at + count])
        at += count
    held, from_c, from_y, from_x, from_low, from_high, from_f = groups
    (load_sem, c_send, c_recv, y_send, y_recv, x_send, x_recv, z_send, z_recv, f_send, f_recv,
     o_send, o_recv, o_local) = refs[at:]
    x, y, z, c = coordinates(topo)
    X, Z, T = topo.X, topo.Z, topo.T
    g, me = lax.axis_index("grp"), lax.axis_index("tok")
    odd = lax.rem(y, 2)
    below, above = z > 0, z < Z - 1
    kind = pl.DeviceIdType.MESH

    def over_y(k):
        high = lax.rem(lax.div(y, 1 << k), 2)
        return {"grp": g + (2 - 4 * high) * (1 << k), "tok": me}

    over_c = {"grp": g + 1 - 2 * c, "tok": me}

    def over_z(k):
        return {"grp": g, "tok": (z + k) * X + x}

    def over_x(k):
        return {"grp": g, "tok": z * X + lax.rem(x + k, X)}

    barrier = pltpu.get_barrier_semaphore()
    partners = [over_c] + [over_y(k) for k in range(topo.bits["y"])]
    partners += [over_x(k) for k in range(1, X)]

    def greet(partner):
        pl.semaphore_signal(barrier, inc=1, device_id=partner, device_id_type=kind)

    for partner in partners:
        greet(partner)
    pl.when(below)(lambda: greet(over_z(-1)))
    pl.when(above)(lambda: greet(over_z(1)))
    every = range(count)

    def load(p, t):
        s = shares[p]
        return pltpu.make_async_copy(
            s.of(grads[s.array], c, t), held[p].at[t], load_sem.at[p, t]
        )

    def remote(source, landing, send, recv, target):
        return pltpu.make_async_remote_copy(
            src_ref=source, dst_ref=landing, send_sem=send, recv_sem=recv, device_id=target,
            device_id_type=kind,
        )

    def c_copy(p, t):
        s = shares[p]
        return remote(
            s.of(grads[s.array], 1 - c, t), from_c[p].at[t], c_send.at[p, t], c_recv.at[p, t],
            over_c,
        )

    def y_copy(p, t):
        return remote(
            held[p].at[t], from_y[p].at[t], y_send.at[p, t], y_recv.at[p, t], over_y(0)
        )

    def x_copy(p, zz, k):
        t = zz * X + lax.rem(x + k, X)
        return remote(
            held[p].at[t], from_x[p].at[zz, k - 1], x_send.at[p, zz, k - 1],
            x_recv.at[p, zz, k - 1], over_x(k),
        )

    def z_copy(p, zz, k):
        landing = from_low if k > 0 else from_high
        way = (k + 1) // 2
        return remote(
            held[p].at[zz * X + x], landing[p].at[zz], z_send.at[p, zz, way],
            z_recv.at[p, zz, way], over_z(k),
        )

    def f_copy(p, k):
        return remote(
            held[p].at[me], from_f[p].at[k], f_send.at[p, k], f_recv.at[p, k], over_y(k)
        )

    def o_copy(p):
        s = shares[p]
        return remote(
            held[p].at[me], s.of(outs[s.array], c), o_send.at[p], o_recv.at[p], over_c
        )

    def o_arrived(p):
        s = shares[p]
        return remote(
            held[p].at[me], s.of(outs[s.array], 1 - c), o_send.at[p], o_recv.at[p], over_c
        )

    def o_keep(p):
        s = shares[p]
        return pltpu.make_async_copy(held[p].at[me], s.of(outs[s.array], c), o_local.at[p])

    def add(p, t, other):
        held[p][t] = held[p][t] + other

    def layers(body):
        def step(i, carry):
            k = Z - 1 - i
            pl.when(z + k < Z)(lambda: body(z + k))
            pl.when((k > 0) & (z - k >= 0))(lambda: body(z - k))
            return carry
        return step

    def inside(p, body):
        if shares[p].part == 1:
            body()
        else:
            pl.when(odd == shares[p].part // 2)(body)

    def outside(p, body):
        if shares[p].part != 1:
            pl.when(odd != shares[p].part // 2)(body)

    def start_loads(zz):
        def each(j, carry):
            t = zz * X + lax.rem(x + j, X)
            for p in every:
                load(p, t).start()
            return carry
        lax.fori_loop(0, X, each, 0)

    lax.fori_loop(0, Z, layers(start_loads), 0)
    pl.semaphore_wait(barrier, len(partners) + below.astype(jnp.int32) + above.astype(jnp.int32))

    def start_cores(zz):
        def each(j, carry):
            t = zz * X + lax.rem(x + j, X)
            for p in every:
                c_copy(p, t).start()
            return carry
        lax.fori_loop(0, X, each, 0)

    lax.fori_loop(0, Z, layers(start_cores), 0)

    def cores(zz):
        def each(j, carry):
            t = zz * X + lax.rem(x + j + 1, X)
            for p in every:
                load(p, t).wait()
                c_copy(p, t).wait_recv()
                add(p, t, from_c[p][t])
                outside(p, lambda p=p: y_copy(p, t).start())
                if shares[p].part == 1:
                    for k in range(1, X):
                        pl.when(j + 1 == k)(lambda p=p, k=k: x_copy(p, zz, k).start())
            return carry
        lax.fori_loop(0, X, each, 0)

    lax.fori_loop(0, Z, layers(cores), 0)

    def over(zz):
        def each(j, carry):
            t = zz * X + lax.rem(x + j + 1, X)
            for p in every:
                if shares[p].part != 1:
                    def body(p=p):
                        y_copy(p, t).wait_recv()
                        add(p, t, from_y[p][t])
                        for k in range(1, X):
                            pl.when(j + 1 == k)(lambda: x_copy(p, zz, k).start())
                    inside(p, body)
            return carry
        lax.fori_loop(0, X, each, 0)

    def join(p, zz):
        t = zz * X + x
        for k in range(1, X):
            x_copy(p, zz, k).wait_recv()
            add(p, t, from_x[p][zz, k - 1])

        def low():
            z_copy(p, zz, 1).wait_recv()
            add(p, t, from_low[p][zz])

        def high():
            z_copy(p, zz, -1).wait_recv()
            add(p, t, from_high[p][zz])

        pl.when((zz >= z) & below)(low)
        pl.when((zz <= z) & above)(high)
        pl.when(zz > z)(lambda: z_copy(p, zz, 1).start())
        pl.when(zz < z)(lambda: z_copy(p, zz, -1).start())

    def first_joins(zz):
        for p in every:
            if shares[p].part == 1:
                join(p, zz)

    def last_joins(zz):
        for p in every:
            if shares[p].part != 1:
                inside(p, lambda p=p: join(p, zz))

    def main(i, carry):
        @pl.when(i < Z)
        def _():
            layers(first_joins)(i, 0)
            layers(over)(i, 0)

        @pl.when(i > 0)
        def _():
            layers(last_joins)(i - 1, 0)

        return carry

    lax.fori_loop(0, Z + 1, main, 0)

    for k in range(1, topo.bits["y"]):
        for p in every:
            inside(p, lambda p=p: f_copy(p, k).start())
        for p in every:
            def fold(p=p):
                f_copy(p, k).wait()
                add(p, me, from_f[p][k])
            inside(p, fold)
    for p in every:
        inside(p, lambda p=p: f_copy(p, 0).start())
    for p in every:
        if shares[p].part == 1:
            f_copy(p, 0).wait()
            add(p, me, from_f[p][0])
        else:
            def take(p=p):
                f_copy(p, 0).wait_recv()
                held[p][me] = from_f[p][0]
            outside(p, lambda p=p: y_copy(p, me).wait_send())
            outside(p, take)
        o_copy(p).start()
        o_keep(p).start()

    def ends(t, carry):
        for p in every:
            c_copy(p, t).wait_send()
            outside(p, lambda p=p: pl.when(t != me)(lambda: y_copy(p, t).wait_send()))
        return carry

    lax.fori_loop(0, T, ends, 0)

    def z_ends(zz, carry):
        for p in every:
            def body(p=p):
                for k in range(1, X):
                    x_copy(p, zz, k).wait_send()
                pl.when(zz > z)(lambda: z_copy(p, zz, 1).wait_send())
                pl.when(zz < z)(lambda: z_copy(p, zz, -1).wait_send())
            inside(p, body)
        return carry

    lax.fori_loop(0, Z, z_ends, 0)
    for p in every:
        if shares[p].part != 1:
            inside(p, lambda p=p: f_copy(p, 0).wait_send())
        o_copy(p).wait_send()
        o_arrived(p).wait_recv()
        o_keep(p).wait()


def reduce_gradients(topo, grads):
    shares = cut_shares([v.shape for v in grads])
    X, Z, T = topo.X, topo.Z, topo.T
    n = len(shares)
    folds = max(1, topo.bits["y"])
    DMA = pltpu.SemaphoreType.DMA
    hbm = pl.BlockSpec(memory_space=pl.ANY)
    lead = [(T,), (T,), (T,), (Z, X - 1), (Z,), (Z,), (folds,)]
    rooms = [
        pltpu.VMEM(front + s.shape, BF)
        for front in lead for s in shares
    ]
    outs = [grads[0].shape[1:], grads[1].shape[1:], (2,) + grads[2].shape[2:], grads[3].shape[1:]]
    return pl.pallas_call(
        functools.partial(reduce_kernel, topo, shares),
        in_specs=[hbm] * 4,
        out_specs=[hbm] * 4,
        out_shape=[jax.ShapeDtypeStruct(s, BF) for s in outs],
        scratch_shapes=rooms + [
            DMA((n, T)), DMA((n, T)), DMA((n, T)), DMA((n, T)), DMA((n, T)),
            DMA((n, Z, X - 1)), DMA((n, Z, X - 1)), DMA((n, Z, 2)), DMA((n, Z, 2)),
            DMA((n, folds)), DMA((n, folds)), DMA((n,)), DMA((n,)), DMA((n,)),
        ],
        compiler_params=pltpu.CompilerParams(
            collective_id=1, has_side_effects=True, vmem_limit_bytes=60 << 20
        ),
        name="reduce_gradients",
    )(*grads)


def group_order(topo):
    return list(reversed(topo.keys("y"))) + topo.keys("c") + list(reversed(topo.keys("x")))


def group_gather(topo, arr, order):
    names = group_order(topo)
    held = []
    shape = arr.shape
    for key in order:
        place = sum(1 for h in held if names.index(h) < names.index(key))
        arr = double(topo, arr, key, place, True)
        held.append(key)
    return arr.reshape((topo.T,) + shape)


def group_scatter(topo, arr, order):
    names = group_order(topo)
    held = list(names)
    arr = arr.reshape((2,) * len(names) + arr.shape[1:])
    for key in order:
        arr = halve(topo, arr, key, held.index(key), True)
        held.remove(key)
    return arr


def small_layer(topo):
    return topo.X == 2 and topo.Y == 2


class Layer:
    def __init__(self, topo):
        self.topo = topo
        x, y, z, c = coordinates(topo)
        self.c = c
        far_x, far_y = 1 - x, 1 - y
        a = (x + c * (far_x - x), far_y + c * (y - far_y))
        b = (far_x + c * (x - far_x), y + c * (far_y - y))
        self.chips = [(x, y), a, b, (far_x, far_y)]
        self.z = z

    def pack(self, slot, core):
        x, y = self.chips[slot]
        return (y * 2 + core) * self.topo.X + x

    def device(self, slot, core):
        x, y = self.chips[slot]
        return {"grp": y * 2 + core, "tok": self.z * self.topo.X + x}

    def meet(self):
        barrier = pltpu.get_barrier_semaphore()
        for target in (self.device(1, self.c), self.device(2, self.c), self.device(0, 1 - self.c)):
            pl.semaphore_signal(
                barrier, inc=1, device_id=target, device_id_type=pl.DeviceIdType.MESH
            )
        pl.semaphore_wait(barrier, 3)


def remote_copy(source, landing, send, recv, target):
    return pltpu.make_async_remote_copy(
        src_ref=source, dst_ref=landing, send_sem=send, recv_sem=recv, device_id=target,
        device_id_type=pl.DeviceIdType.MESH,
    )


def group_gather_kernel(topo, count, *refs):
    mine, outs = refs[:count], refs[count:2 * count]
    local_sem, send_sem, recv_sem = refs[2 * count:]
    layer = Layer(topo)
    c = layer.c
    arrays = range(count)
    a, b, sibling = layer.device(1, c), layer.device(2, c), layer.device(0, 1 - c)
    own = layer.pack(0, c)

    def send(i, way, pack, target):
        landing = outs[i].at[pack]
        source = mine[i] if way in (0, 1, 3) else landing
        return remote_copy(source, landing, send_sem.at[i, way], recv_sem.at[i, pack], target)

    ways = [
        (0, own, a), (1, own, b), (2, layer.pack(1, c), b), (3, own, sibling),
        (4, layer.pack(1, c), sibling), (5, layer.pack(2, c), sibling),
        (6, layer.pack(3, c), sibling),
    ]

    def start(k):
        for i in arrays:
            send(i, *ways[k]).start()

    def arrived(pack):
        for i in arrays:
            send(i, 2, pack, sibling).wait_recv()

    keep = [pltpu.make_async_copy(mine[i], outs[i].at[own], local_sem.at[i]) for i in arrays]
    for copy in keep:
        copy.start()
    layer.meet()
    start(0)
    start(1)
    start(3)
    arrived(layer.pack(1, c))
    start(2)
    start(4)
    arrived(layer.pack(2, c))
    start(5)
    arrived(layer.pack(3, c))
    start(6)
    for slot in range(4):
        arrived(layer.pack(slot, 1 - c))
    for way in ways:
        for i in arrays:
            send(i, *way).wait_send()
    for copy in keep:
        copy.wait()


def gather_layer(topo, arrays, ident):
    DMA = pltpu.SemaphoreType.DMA
    hbm = pl.BlockSpec(memory_space=pl.ANY)
    n = len(arrays)
    return pl.pallas_call(
        functools.partial(group_gather_kernel, topo, n),
        in_specs=[hbm] * n,
        out_specs=[hbm] * n,
        out_shape=[jax.ShapeDtypeStruct((topo.T,) + v.shape, v.dtype) for v in arrays],
        scratch_shapes=[DMA((n,)), DMA((n, 7)), DMA((n, topo.T))],
        compiler_params=pltpu.CompilerParams(collective_id=ident, has_side_effects=True),
        name="gather_layer",
    )(*arrays)


def group_reduce_kernel(topo, grads, out, held, from_c, from_b, from_a, load_sem, c_send, c_recv,
                        send_sem, recv_sem):
    layer = Layer(topo)
    c = layer.c
    a, b, sibling = layer.device(1, c), layer.device(2, c), layer.device(0, 1 - c)
    order = (3, 2, 1, 0)

    def load(slot):
        return pltpu.make_async_copy(
            grads.at[layer.pack(slot, c)], held.at[slot], load_sem.at[slot]
        )

    def c_copy(slot):
        theirs = (0, 2, 1, 3)[slot]
        return remote_copy(
            grads.at[layer.pack(slot, 1 - c)], from_c.at[theirs], c_send.at[theirs],
            c_recv.at[theirs], sibling,
        )

    def c_arrived(slot):
        remote_copy(
            grads.at[layer.pack(slot, c)], from_c.at[slot], c_send.at[slot], c_recv.at[slot],
            sibling,
        ).wait_recv()

    across = remote_copy(held.at[3], from_b.at[1], send_sem.at[0], recv_sem.at[0], b)
    direct = remote_copy(held.at[2], from_b.at[0], send_sem.at[1], recv_sem.at[1], b)
    passed = remote_copy(held.at[1], from_a, send_sem.at[2], recv_sem.at[2], a)

    for slot in order:
        load(slot).start()
    layer.meet()
    for slot in (3, 1, 2, 0):
        c_copy(slot).start()
    for slot in order:
        load(slot).wait()
        c_arrived(slot)
        held[slot] = held[slot] + from_c[slot]
        if slot == 3:
            across.start()
        if slot == 2:
            direct.start()
    across.wait_recv()
    held[1] = held[1] + from_b[1]
    passed.start()
    direct.wait_recv()
    held[0] = held[0] + from_b[0]
    passed.wait_recv()
    out[...] = held[0] + from_a[...]
    across.wait_send()
    direct.wait_send()
    passed.wait_send()
    for slot in range(4):
        c_copy(slot).wait_send()


def reduce_layer(topo, grads, ident):
    DMA = pltpu.SemaphoreType.DMA
    block = grads.shape[1:]
    return pl.pallas_call(
        functools.partial(group_reduce_kernel, topo),
        in_specs=[pl.BlockSpec(memory_space=pl.ANY)],
        out_specs=pl.BlockSpec(memory_space=pltpu.VMEM),
        out_shape=jax.ShapeDtypeStruct(block, BF),
        scratch_shapes=[
            pltpu.VMEM((4,) + block, BF), pltpu.VMEM((4,) + block, BF),
            pltpu.VMEM((2,) + block, BF), pltpu.VMEM(block, BF),
            DMA((4,)), DMA((4,)), DMA((4,)), DMA((3,)), DMA((3,)),
        ],
        compiler_params=pltpu.CompilerParams(
            collective_id=ident, has_side_effects=True, vmem_limit_bytes=32 << 20
        ),
        name="reduce_layer",
    )(grads)


NT = (((1,), (1,)), ((), ()))
TN = (((0,), (0,)), ((), ()))
LANES = 2 * HD
CHUNKS = (HEADS + 1) // 2
ROOM = 60 << 20


def lanes_of(rows):
    return lax.broadcasted_iota(jnp.int32, (rows, LANES), 1)


def spin(v):
    first = lax.rem(lanes_of(v.shape[0]), HD) < HD // 2
    return jnp.where(first, -pltpu.roll(v, LANES - HD // 2, 1), pltpu.roll(v, HD // 2, 1))


def whole(*shape):
    return pl.BlockSpec(shape, lambda *i: (0,) * len(shape))


def normed(v, gain):
    return v * lax.rsqrt(jnp.mean(v * v, axis=-1, keepdims=True) + EPS) * gain


def project_kernel(state_ref, gain_ref, w_ref, turn_ref, n1_ref, q_ref, kv_ref):
    n1 = normed(state_ref[...], gain_ref[...]).astype(BF)
    n1_ref[...] = n1
    cosine, sine = turn_ref[0], turn_ref[1]
    key = lanes_of(n1.shape[0]) < HD
    columns = w_ref.shape[1]
    for start in range(0, columns, 2 * LANES):
        wide = min(2 * LANES, columns - start)
        both = jnp.dot(n1, w_ref[:, start:start + wide], preferred_element_type=F32)
        for half in range(wide // LANES):
            j = start // LANES + half
            v = both[:, half * LANES:(half + 1) * LANES]
            turned = v * cosine + spin(v) * sine
            if j < CHUNKS:
                q_ref[j] = (turned * HD ** -0.5).astype(BF)
            else:
                j -= CHUNKS
                kv_ref[:, j * LANES:(j + 1) * LANES] = jnp.where(key, turned, v).astype(BF)


def project(state, gain, w, turns):
    n, model = state.shape
    return pl.pallas_call(
        project_kernel,
        grid=(1,),
        in_specs=[whole(n, model), whole(1, model), whole(*w.shape), whole(*turns.shape)],
        out_specs=[whole(n, model), whole(CHUNKS, n, LANES), whole(n, KV_HEADS * LANES)],
        out_shape=[
            jax.ShapeDtypeStruct((n, model), BF),
            jax.ShapeDtypeStruct((CHUNKS, n, LANES), BF),
            jax.ShapeDtypeStruct((n, KV_HEADS * LANES), BF),
        ],
        compiler_params=pltpu.CompilerParams(vmem_limit_bytes=ROOM),
        name="project",
    )(state, gain, w, turns)


def fill_bias(bias, key_ref, query_ref, rows, first, last):
    def body(t, carry):
        at = pl.ds(pl.multiple_of(t * rows, rows), rows)
        keys = key_ref[at, :]
        live, order = keys[:, 0:1], keys[:, 1:2]
        begin, place = query_ref[0:1, :], query_ref[1:2, :]
        allowed = ((live >= begin) & (live <= place)) | (order == place)
        bias[at, :] = jnp.where(allowed, 0.0, BIG)
        return carry

    lax.fori_loop(first, last, body, 0)


def attend_kernel(rows, span, key_ref, query_ref, kv_ref, q_ref, mixed_ref, out_ref, stat_ref,
                  bias, held, stacked, mixing, heads):
    first, last = span[0], span[1]
    group = pl.program_id(0)

    @pl.when(group == 0)
    def _():
        fill_bias(bias, key_ref, query_ref, rows, first, last)

    low = lanes_of(rows) < HD
    for j in range(SHARES):
        head = group * SHARES + j
        chunk = q_ref[head // 2].astype(F32)
        chunk = jnp.where(lax.rem(head, 2) == 1, pltpu.roll(chunk, HD, 1), chunk)
        stacked[j * rows:(j + 1) * rows, :] = jnp.where(low, chunk, 0.0).astype(BF)
    wide = stacked.shape[0]
    queries = stacked[...]

    def scores(t, top):
        at = pl.ds(pl.multiple_of(t * rows, rows), rows)
        s = lax.dot_general(kv_ref[at, :], queries, NT, preferred_element_type=F32) + bias[at, :]
        held[at, :] = s
        return jnp.maximum(top, jnp.max(s.reshape(rows // 8, 8, wide), axis=0))

    top = lax.fori_loop(first, last, scores, jnp.full((8, wide), BIG, F32))
    top = jnp.max(top, axis=0, keepdims=True)
    mixing[...] = jnp.zeros(mixing.shape, F32)

    def mix(t, total):
        at = pl.ds(pl.multiple_of(t * rows, rows), rows)
        p = jnp.exp(held[at, :] - top)
        mixing[...] += lax.dot_general(
            kv_ref[at, :], p.astype(BF), TN, preferred_element_type=F32
        )
        return total + jnp.sum(p.reshape(rows // 8, 8, wide), axis=0)

    total = lax.fori_loop(first, last, mix, jnp.zeros((8, wide), F32))
    total = jnp.sum(total, axis=0, keepdims=True)
    stat_ref[0] = jnp.broadcast_to(top + jnp.log(total), (8, wide))
    out = jnp.transpose(mixing[...] / total)
    for j in range(SHARES):
        heads[group * SHARES + j] = out[j * rows:(j + 1) * rows, :]

    @pl.when(group == KV_HEADS - 1)
    def _():
        for j in range(CHUNKS):
            even = pltpu.roll(heads[2 * j], HD, 1)
            odd = heads[2 * j + 1] if 2 * j + 1 < HEADS else jnp.zeros((rows, LANES), F32)
            both = jnp.where(low, even, odd)
            out_ref[j] = both
            size = min(LANES, HEADS * HD - j * LANES)
            mixed_ref[:, j * LANES:j * LANES + size] = both.astype(BF)[:, :size]


def attend(rows, span, key_labels, query_labels, kv_all, q):
    count = kv_all.shape[0]
    wide = SHARES * rows
    return pl.pallas_call(
        functools.partial(attend_kernel, rows),
        grid_spec=pltpu.PrefetchScalarGridSpec(
            num_scalar_prefetch=1,
            grid=(KV_HEADS,),
            in_specs=[
                whole(count, 8),
                whole(8, wide),
                pl.BlockSpec((count, LANES), lambda h, s: (0, h)),
                whole(CHUNKS, rows, LANES),
            ],
            out_specs=[
                whole(rows, HEADS * HD),
                whole(CHUNKS, rows, LANES),
                pl.BlockSpec((1, 8, wide), lambda h, s: (h, 0, 0)),
            ],
            scratch_shapes=[
                pltpu.VMEM((count, wide), F32), pltpu.VMEM((count, wide), F32),
                pltpu.VMEM((wide, LANES), BF), pltpu.VMEM((LANES, wide), F32),
                pltpu.VMEM((HEADS, rows, LANES), F32),
            ],
        ),
        out_shape=[
            jax.ShapeDtypeStruct((rows, HEADS * HD), BF),
            jax.ShapeDtypeStruct((CHUNKS, rows, LANES), F32),
            jax.ShapeDtypeStruct((KV_HEADS, 8, wide), F32),
        ],
        compiler_params=pltpu.CompilerParams(vmem_limit_bytes=62 << 20),
        name="attend",
    )(span, key_labels, query_labels, kv_all, q)


def attend_back_kernel(rows, span, key_ref, query_ref, kv_ref, q_ref, d_ref, out_ref, stat_ref,
                       turn_ref, dq_ref, dkv_ref, bias, stacked, part, mixing, heads):
    first, last = span[0], span[1]
    group = pl.program_id(0)

    @pl.when(group == 0)
    def _():
        fill_bias(bias, key_ref, query_ref, rows, first, last)

    low = lanes_of(rows) < HD
    for j in range(SHARES):
        head = group * SHARES + j
        odd = lax.rem(head, 2) == 1
        mine = low != odd
        q = q_ref[head // 2].astype(F32)
        d = d_ref[head // 2].astype(F32)
        q_low = jnp.where(odd, pltpu.roll(q, HD, 1), q)
        d_high = jnp.where(odd, d, pltpu.roll(d, HD, 1))
        at = pl.ds(j * rows, rows)
        stacked[at, :] = jnp.where(low, q_low, d_high).astype(BF)
        part[at, :] = jnp.where(mine, d * out_ref[head // 2], 0.0)
    wide = stacked.shape[0]
    queries = stacked[...]
    ones = jnp.ones((8, LANES), BF)
    coarse = part[...].astype(BF)
    fine = (part[...] - coarse.astype(F32)).astype(BF)
    delta = lax.dot_general(ones, coarse, NT, preferred_element_type=F32)
    delta += lax.dot_general(ones, fine, NT, preferred_element_type=F32)
    delta = delta[0:1, :]
    stat = stat_ref[0, 0:1, :]
    dkv_ref[...] = jnp.zeros(dkv_ref.shape, BF)
    mixing[...] = jnp.zeros(mixing.shape, F32)

    def body(t, carry):
        at = pl.ds(pl.multiple_of(t * rows, rows), rows)
        kv = kv_ref[at, :]
        zero = jnp.zeros_like(kv)
        s = lax.dot_general(jnp.where(low, kv, zero), queries, NT, preferred_element_type=F32)
        p = jnp.exp(s + bias[at, :] - stat)
        dp = lax.dot_general(jnp.where(low, zero, kv), queries, NT, preferred_element_type=F32)
        ds = (p * (dp - delta)).astype(BF)
        dk = jnp.dot(ds, queries, preferred_element_type=F32)
        dv = jnp.dot(p.astype(BF), queries, preferred_element_type=F32)
        dkv_ref[at, :] = jnp.where(low, dk, dv).astype(BF)
        mixing[...] += lax.dot_general(kv, ds, TN, preferred_element_type=F32)
        return carry

    lax.fori_loop(first, last, body, 0)
    back = jnp.transpose(mixing[...])
    for j in range(SHARES):
        heads[group * SHARES + j] = back[j * rows:(j + 1) * rows, :]

    @pl.when(group == KV_HEADS - 1)
    def _():
        cosine, sine = turn_ref[0], turn_ref[1]
        for j in range(CHUNKS):
            odd = jnp.zeros((rows, LANES), F32)
            if 2 * j + 1 < HEADS:
                odd = pltpu.roll(heads[2 * j + 1], HD, 1)
            both = jnp.where(low, heads[2 * j], odd) * HD ** -0.5
            both = both * cosine - spin(both) * sine
            dq_ref[:, j * LANES:(j + 1) * LANES] = both.astype(BF)


def attend_back(rows, span, key_labels, query_labels, kv_all, q, d_mixed, out, stat, turns):
    count = kv_all.shape[0]
    wide = SHARES * rows
    return pl.pallas_call(
        functools.partial(attend_back_kernel, rows),
        grid_spec=pltpu.PrefetchScalarGridSpec(
            num_scalar_prefetch=1,
            grid=(KV_HEADS,),
            in_specs=[
                whole(count, 8),
                whole(8, wide),
                pl.BlockSpec((count, LANES), lambda h, s: (0, h)),
                whole(CHUNKS, rows, LANES),
                whole(CHUNKS, rows, LANES),
                whole(CHUNKS, rows, LANES),
                pl.BlockSpec((1, 8, wide), lambda h, s: (h, 0, 0)),
                whole(*turns.shape),
            ],
            out_specs=[
                whole(rows, CHUNKS * LANES),
                pl.BlockSpec((count, LANES), lambda h, s: (0, h)),
            ],
            scratch_shapes=[
                pltpu.VMEM((count, wide), F32), pltpu.VMEM((wide, LANES), BF),
                pltpu.VMEM((wide, LANES), F32), pltpu.VMEM((LANES, wide), F32),
                pltpu.VMEM((HEADS, rows, LANES), F32),
            ],
        ),
        out_shape=[
            jax.ShapeDtypeStruct((rows, CHUNKS * LANES), BF),
            jax.ShapeDtypeStruct((count, KV_HEADS * LANES), BF),
        ],
        compiler_params=pltpu.CompilerParams(vmem_limit_bytes=62 << 20),
        name="attend_back",
    )(span, key_labels, query_labels, kv_all, q, d_mixed, out, stat, turns)


def out_back_kernel(d_ref, w_ref, out_ref):
    d = d_ref[...]
    for j in range(CHUNKS):
        size = min(LANES, w_ref.shape[0] - j * LANES)
        v = lax.dot_general(
            d, w_ref[j * LANES:j * LANES + size, :], NT, preferred_element_type=F32
        ).astype(BF)
        if size < LANES:
            v = jnp.concatenate([v, jnp.zeros((d.shape[0], LANES - size), BF)], axis=1)
        out_ref[j] = v


def out_back(d_att, w_out):
    n = d_att.shape[0]
    return pl.pallas_call(
        out_back_kernel,
        grid=(1,),
        in_specs=[whole(*d_att.shape), whole(*w_out.shape)],
        out_specs=whole(CHUNKS, n, LANES),
        out_shape=jax.ShapeDtypeStruct((CHUNKS, n, LANES), BF),
        compiler_params=pltpu.CompilerParams(vmem_limit_bytes=ROOM),
        name="out_back",
    )(d_att, w_out)


def project_back_kernel(gradient_ref, state_ref, gain_ref, w_ref, turn_ref, dq_ref, raw_ref,
                        grad_ref, dkv_ref, dgain_ref):
    cosine, sine = turn_ref[0], turn_ref[1]
    key = lanes_of(dq_ref.shape[0]) < HD
    for j in range(KV_HEADS):
        v = raw_ref[:, j * LANES:(j + 1) * LANES].astype(F32)
        turned = v * cosine - spin(v) * sine
        dkv_ref[:, j * LANES:(j + 1) * LANES] = jnp.where(key, turned, v).astype(BF)
    split = CHUNKS * LANES
    d = lax.dot_general(dq_ref[...], w_ref[:, :split], NT, preferred_element_type=F32)
    d += lax.dot_general(dkv_ref[...], w_ref[:, split:], NT, preferred_element_type=F32)
    v = state_ref[...]
    inv = lax.rsqrt(jnp.mean(v * v, axis=-1, keepdims=True) + EPS)
    scaled = d * gain_ref[...]
    dot = jnp.mean(scaled * v, axis=-1, keepdims=True)
    grad_ref[...] = gradient_ref[...] + inv * scaled - v * (inv * inv * inv * dot)
    dgain_ref[...] = jnp.sum(d * v * inv, axis=0, keepdims=True)


def project_back(gradient, state, gain, w, turns, dq, dkv):
    n, model = state.shape
    return pl.pallas_call(
        project_back_kernel,
        grid=(1,),
        in_specs=[
            whole(n, model), whole(n, model), whole(1, model), whole(*w.shape),
            whole(*turns.shape), whole(*dq.shape), whole(*dkv.shape),
        ],
        out_specs=[whole(n, model), whole(*dkv.shape), whole(1, model)],
        out_shape=[
            jax.ShapeDtypeStruct((n, model), F32),
            jax.ShapeDtypeStruct(dkv.shape, BF),
            jax.ShapeDtypeStruct((1, model), F32),
        ],
        compiler_params=pltpu.CompilerParams(vmem_limit_bytes=ROOM),
        name="project_back",
    )(gradient, state, gain, w, turns, dq, dkv)


def outer_columns_kernel(count, x_ref, *refs):
    ds, out_ref, turned = refs[:count], refs[count], refs[count + 1]

    @pl.when((pl.program_id(0) == 0) & (pl.program_id(1) == 0))
    def _():
        turned[...] = jnp.transpose(x_ref[...])

    for i in range(count):
        @pl.when(pl.program_id(0) == i)
        def _(i=i):
            out_ref[0] = jnp.dot(
                turned[...], ds[i][...], preferred_element_type=F32
            ).astype(BF)


def outer_columns(x, ds, tile):
    n, rows = x.shape
    columns = ds[0].shape[1]
    count = len(ds)

    def taken(i):
        return lambda a, j: (0, jnp.where(a == i, j, jnp.where(a < i, 0, columns // tile - 1)))

    return pl.pallas_call(
        functools.partial(outer_columns_kernel, count),
        grid=(count, columns // tile),
        in_specs=[whole(n, rows)] + [pl.BlockSpec((n, tile), taken(i)) for i in range(count)],
        out_specs=pl.BlockSpec((1, rows, tile), lambda a, j: (a, 0, j)),
        out_shape=jax.ShapeDtypeStruct((count, rows, columns), BF),
        scratch_shapes=[pltpu.VMEM((rows, n), BF)],
        compiler_params=pltpu.CompilerParams(vmem_limit_bytes=ROOM),
        cost_estimate=pl.CostEstimate(
            flops=2 * n * rows * columns * count, transcendentals=0,
            bytes_accessed=2 * count * (n * columns + rows * columns) + 2 * n * rows,
        ),
        name="outer_columns",
    )(x, *ds)


def outer_rows_kernel(x_ref, d_ref, out_ref):
    out_ref[...] = jnp.dot(
        jnp.transpose(x_ref[...]), d_ref[...], preferred_element_type=F32
    ).astype(BF)


def outer_rows(x, d, tile):
    n, rows = x.shape
    columns = d.shape[1]
    return pl.pallas_call(
        outer_rows_kernel,
        grid=(rows // tile,),
        in_specs=[pl.BlockSpec((n, tile), lambda i: (0, i)), whole(n, columns)],
        out_specs=pl.BlockSpec((tile, columns), lambda i: (i, 0)),
        out_shape=jax.ShapeDtypeStruct((rows, columns), BF),
        compiler_params=pltpu.CompilerParams(vmem_limit_bytes=ROOM),
        cost_estimate=pl.CostEstimate(
            flops=2 * n * rows * columns, transcendentals=0,
            bytes_accessed=2 * (n * columns + n * rows + rows * columns),
        ),
        name="outer_rows",
    )(x, d)


def mm(a, b):
    return jnp.dot(a, b, preferred_element_type=F32)


def mm_nt(a, b):
    return lax.dot_general(a, b, NT, preferred_element_type=F32)


def mm_tn(a, b):
    return lax.dot_general(a, b, TN, preferred_element_type=F32)


def inverse_rms(v):
    return lax.rsqrt(jnp.mean(v * v, axis=-1, keepdims=True) + EPS)


def norm_back(grad, v, inv, gain):
    scaled = grad * gain
    dot = jnp.mean(scaled * v, axis=-1, keepdims=True)
    return (inv * scaled - v * (inv * inv * inv * dot), jnp.sum(grad * v * inv, axis=0))


def per_device(topo, *args):
    (tokens, w_query, w_key, w_value, w_out, w_gate, w_up, w_down, router, norm_attn, norm_ffn,
     lengths, depths, padding, cotangent) = args
    rows, model = tokens.shape
    kv_cols = w_key.shape[1]
    ff = w_gate.shape[1]
    shard = w_query.shape[0]
    deep_rows = rows * 3 // 4
    xk, yk, ck = (topo.keys(d) for d in "xyc")

    small = jnp.concatenate([router, norm_attn[:, None], norm_ffn[:, None]], axis=1)
    small = jnp.pad(small, ((0, 0), (0, HD - small.shape[1])))
    w_kv = jnp.stack(
        [w_key.reshape(shard, KV_HEADS, HD), w_value.reshape(shard, KV_HEADS, HD)], axis=2
    ).reshape(shard, 2 * kv_cols)
    first = jnp.concatenate([w_query, small, w_kv], axis=1)
    weight_qkv, weight_g, weight_u, weight_d, weight_o = gather_weights(
        topo, [first, w_gate, w_up, w_down, w_out]
    )

    own = lax.axis_index("tok") * rows + jnp.arange(rows, dtype=jnp.int32)
    eligible = (depths >= 2) & (padding > 0)
    flags = jnp.stack([eligible, ~eligible]).astype(BF)
    upto = (jnp.arange(rows)[:, None] <= jnp.arange(rows)[None, :]).astype(BF)
    counts = mm(flags, upto).astype(jnp.int32)
    slot = jnp.where(eligible, counts[0] - 1, counts[0, -1] + counts[1] - 1)
    chosen = jnp.arange(rows, dtype=jnp.int32)[:, None] == slot[None, :]
    onehot = chosen.astype(BF)
    doc_ends = jnp.cumsum(lengths[0])
    begins = jnp.sum(
        jnp.where(own[:, None] >= doc_ends[None, :], lengths[0][None, :], 0), axis=1
    )
    levels = jnp.where(padding > 0, depths, 0)
    labels = jnp.stack([own, begins, levels])
    labels = jnp.sum(jnp.where(chosen[None], labels[:, None, :], 0), axis=2)
    labels = jnp.pad(labels, ((0, 5), (0, 0)))
    swap = topo.swap_pairs()
    state = lax.ppermute(mm(onehot, tokens).astype(BF), AXES, swap).astype(F32)
    labels = lax.ppermute(labels, AXES, swap)
    gradient, weight_qkv = lax.optimization_barrier(
        (mm(onehot, cotangent).astype(BF), weight_qkv)
    )
    gradient = lax.ppermute(gradient, AXES, swap).astype(F32)
    order_g = xk + yk + ck

    def collect(arrays, ident):
        if small_layer(topo):
            return gather_layer(topo, arrays, ident)
        return [group_gather(topo, v, order_g) for v in arrays]

    def distribute(grads, ident):
        if small_layer(topo):
            return reduce_layer(topo, grads, ident)
        return group_scatter(topo, grads, ck + yk + xk)


    small = weight_qkv[:, model:model + HD].astype(F32)
    gain_one, gain_two = small[:, RECS][None], small[:, RECS + 1][None]

    pack = (lax.axis_index("grp") * topo.X) + lax.axis_index("tok") % topo.X
    begin_all, level_mine = labels[1], labels[2]
    lowest = jnp.min(labels[1])
    span = jnp.stack([lowest // rows, pack + 1]).astype(jnp.int32)
    places = (labels[0] - labels[1]).astype(F32)
    freqs = 10000.0 ** (-(jnp.arange(HD // 2, dtype=F32) * 2.0 / HD))
    angles = places[:, None] * freqs[None, :]
    turns = jnp.stack([jnp.cos(angles), jnp.sin(angles)])
    turns = jnp.tile(turns, (1, 1, LANES * 2 // HD))

    def forward(state, recursion, labels_all=None):
        n = state.shape[0]
        n1, q, kv = project(state, gain_one, weight_qkv, turns[:, :n])
        if recursion == 0:
            kv_all, labels_all = collect([kv, labels], 2)
        else:
            kv_all, = collect([kv], 3)
        kv_all = kv_all.reshape(topo.T * n, 2 * kv_cols)
        live = labels_all[:, 2, :n] > recursion
        order = labels_all[:, 0, :n]
        key_labels = jnp.stack([jnp.where(live, order, -1), order], axis=-1).reshape(-1, 2)
        key_labels = jnp.pad(key_labels, ((0, 0), (0, 6)))
        query_labels = jnp.stack([labels[1, :n], labels[0, :n]])
        query_labels = jnp.pad(jnp.tile(query_labels, (1, SHARES)), ((0, 6), (0, 0)))
        mixed, out, stat = attend(n, span, key_labels, query_labels, kv_all, q)
        attended = mm(mixed, weight_o)
        middle = state + attended
        inv_two = inverse_rms(middle)
        n2 = (middle * inv_two * gain_two).astype(BF)
        gated, upward = mm(n2, weight_g), mm(n2, weight_u)
        hidden = (jax.nn.silu(gated) * upward).astype(BF)
        both = attended + mm(hidden, weight_d)
        gate = jax.nn.sigmoid(jnp.sum(state * small[:, recursion], axis=-1, keepdims=True))
        active = (labels[2, :n] > recursion).astype(F32)[:, None]
        new = state + active * gate * both
        kept = (state, n1, q, kv_all, key_labels, query_labels, out, stat, mixed, middle,
                inv_two, n2, gated, upward, hidden, both, gate, active)
        return (new, kept, labels_all)

    def backward(gradient, recursion, kept):
        (state, n1, q, kv_all, key_labels, query_labels, out, stat, mixed, middle,
         inv_two, n2, gated, upward, hidden, both, gate, active) = kept
        n = state.shape[0]
        d_both = active * gate * gradient
        d_fed = d_both.astype(BF)
        d_gate = active * gate * (1.0 - gate) * jnp.sum(gradient * both, axis=-1, keepdims=True)
        d_router = jnp.sum(state * d_gate, axis=0)
        d_hidden = mm_nt(d_fed, weight_d)
        sig = jax.nn.sigmoid(gated)
        d_up = (d_hidden * gated * sig).astype(BF)
        d_gated = (d_hidden * upward * sig * (1.0 + gated * (1.0 - sig))).astype(BF)
        d_middle, d_gain_two = norm_back(
            mm_nt(d_gated, weight_g) + mm_nt(d_up, weight_u), middle, inv_two, gain_two)
        d_att = (d_both + d_middle).astype(BF)
        gradient = gradient + d_gate * small[:, recursion] + d_middle
        dq, dkv = attend_back(
            n, span, key_labels, query_labels, kv_all, q, out_back(d_att, weight_o), out, stat,
            turns[:, :n],
        )
        dkv = distribute(dkv.reshape(topo.T, n, 2 * kv_cols), 5 if recursion else 4)
        gradient, dkv, d_gain_one = project_back(
            gradient, state, gain_one, weight_qkv, turns[:, :n], dq, dkv
        )
        left = (n1, dq, dkv, mixed, d_att, n2, d_gated, d_up, hidden, d_fed)
        return (gradient, left, (d_router, d_gain_one[0], d_gain_two))

    whole_state, kept, labels_all = forward(state, 0)
    deep = whole_state[:deep_rows]
    all_kept = [kept]
    for recursion in range(1, RECS):
        deep, kept, _ = forward(deep, recursion, labels_all)
        all_kept.append(kept)
    final = jnp.concatenate([deep, whole_state[deep_rows:]], axis=0).astype(BF)

    deep_grad = gradient[:deep_rows]
    lefts, smalls = [], []
    for recursion in reversed(range(1, RECS)):
        deep_grad, left, tiny = backward(deep_grad, recursion, all_kept[recursion])
        lefts.append(left)
        smalls.append(tiny)
    gradient = jnp.concatenate([deep_grad, gradient[deep_rows:]], axis=0)
    gradient, left, tiny = backward(gradient, 0, all_kept[0])
    lefts.append(left)
    smalls.append(tiny)
    final, gradient = lax.optimization_barrier((final, gradient.astype(BF)))
    final = lax.ppermute(final, AXES, swap)
    gradient = lax.ppermute(gradient, AXES, swap)

    n1, dq, dkv, mixed, d_att, n2, d_gated, d_up, hidden, d_fed = (
        jnp.concatenate(parts, axis=0) for parts in zip(*lefts)
    )
    dqkv = jnp.concatenate([dq, dkv], axis=1)
    dqkv = jnp.pad(dqkv, ((0, 0), (0, -dqkv.shape[1] % 256)))
    cut = lambda v: v.astype(BF).reshape(topo.T, -1, v.shape[-1])
    tiny = jnp.stack(
        [smalls[2][0], smalls[1][0], smalls[0][0],
         smalls[0][1] + smalls[1][1] + smalls[2][1],
         smalls[0][2] + smalls[1][2] + smalls[2][2]], axis=1
    )
    wide_out = -(-(model + tiny.shape[1]) // 256) * 256
    tiny = jnp.pad(tiny, ((0, 0), (0, wide_out - model - tiny.shape[1])))
    grad_qkv, grad_o, grad_gu, grad_down = reduce_gradients(topo, [
        cut(mm_tn(n1, dqkv)),
        cut(jnp.concatenate([mm_tn(mixed, d_att), tiny], axis=1)),
        outer_columns(n2, [d_gated, d_up], 640).reshape(2, topo.T, -1, ff),
        outer_rows(hidden, d_fed, 640).reshape(topo.T, -1, model),
    ])
    grad_query = grad_qkv[:, :model].astype(F32)
    pair = grad_qkv[:, model + HD:model + HD + 2 * kv_cols].astype(F32)
    pair = pair.reshape(shard, KV_HEADS, 2, HD)
    grad_key = pair[:, :, 0].reshape(shard, kv_cols)
    grad_value = pair[:, :, 1].reshape(shard, kv_cols)
    grad_out = grad_o[:, :model].astype(F32)
    tiny = grad_o[:, model:].astype(F32)
    grad_gate, grad_up = grad_gu[0].astype(F32), grad_gu[1].astype(F32)
    grad_down = grad_down.astype(F32)

    def unsort(v):
        return mm_tn(onehot, v).astype(BF)

    return (
        unsort(final), unsort(gradient), grad_query, grad_key, grad_value, grad_out,
        grad_gate, grad_up, grad_down, tiny[:, :RECS], tiny[:, RECS],
        tiny[:, RECS + 1],
    )


def solution(mesh):
    topo = Topo(mesh.shape["grp"], mesh.shape["tok"])
    both = P(("grp", "tok"))
    wide = P(("grp", "tok"), None)
    rows = P("tok", None)
    row = P("tok")
    return jax.shard_map(
        functools.partial(per_device, topo),
        mesh=mesh,
        in_specs=(wide,) + (rows,) * 8 + (row, row, P("grp", None), both, both, wide),
        out_specs=(wide, wide) + (rows,) * 8 + (row, row),
        check_vma=False,
    )
```

```python
import functools

import jax
import jax.numpy as jnp
from jax import lax
from jax.experimental import pallas as pl
from jax.experimental.pallas import tpu as pltpu
from jax.sharding import PartitionSpec as P

HEADS = 15
KV_HEADS = 5
SHARES = HEADS // KV_HEADS
HD = 64
RECS = 3
EPS = 1e-05
BF = jnp.bfloat16
F32 = jnp.float32
BIG = -1e30
AXES = ("grp", "tok")


class Topo:
    def __init__(self, groups, spread):
        self.G = groups
        self.T = spread
        self.X = spread // groups
        self.Z = groups
        self.Y = groups // 2
        self.bits = {
            "z": self.Z.bit_length() - 1,
            "x": self.X.bit_length() - 1,
            "y": self.Y.bit_length() - 1,
            "c": 1,
        }

    def keys(self, dim):
        return [(dim, k) for k in range(self.bits[dim])]

    def masks(self, key):
        dim, k = key
        if dim == "c":
            return (1, 0)
        if dim == "y":
            return (2 << k, 0)
        if dim == "x":
            return (0, 1 << k)
        return (0, self.X << k)

    def pairs(self, key):
        mg, mt = self.masks(key)
        return [
            (g * self.T + t, (g ^ mg) * self.T + (t ^ mt))
            for g in range(self.G)
            for t in range(self.T)
        ]

    def swap_pairs(self):
        out = []
        for g in range(self.G):
            for t in range(self.T):
                z, x = t // self.X, t % self.X
                out.append((g * self.T + t, z * self.T + g * self.X + x))
        return out

    def bit(self, key):
        mg, mt = self.masks(key)
        if mg:
            return (lax.axis_index("grp") // mg) % 2
        return (lax.axis_index("tok") // mt) % 2


def exchange(topo, arr, key):
    return lax.ppermute(arr, AXES, topo.pairs(key))


def double(topo, arr, key, axis, stack):
    other = exchange(topo, arr, key)
    mine_is_high = topo.bit(key) == 1
    low = jnp.where(mine_is_high, other, arr)
    high = jnp.where(mine_is_high, arr, other)
    if stack:
        return jnp.stack([low, high], axis=axis)
    return jnp.concatenate([low, high], axis=axis)


def halve(topo, arr, key, axis, stack):
    mine_is_high = topo.bit(key) == 1
    if stack:
        low = lax.index_in_dim(arr, 0, axis, keepdims=False)
        high = lax.index_in_dim(arr, 1, axis, keepdims=False)
    else:
        half = arr.shape[axis] // 2
        low = lax.slice_in_dim(arr, 0, half, axis=axis)
        high = lax.slice_in_dim(arr, half, 2 * half, axis=axis)
    send = jnp.where(mine_is_high, low, high).astype(BF)
    keep = jnp.where(mine_is_high, high, low).astype(F32)
    return (keep + exchange(topo, send, key).astype(F32)).astype(BF)


class Piece:
    def __init__(self, array, dim, start, size, core, part):
        self.array, self.dim, self.start, self.size = array, dim, start, size
        self.core, self.part = core, part

    def of(self, ref):
        if self.dim == 0:
            return ref.at[pl.ds(self.start, self.size), :]
        return ref.at[:, pl.ds(self.start, self.size)]


def cut_pieces(shapes):
    near = lambda v, unit: max(unit, int(round(v / unit)) * unit)
    wide_a, wide_g, wide_u, tall = shapes[0][1], shapes[1][1], shapes[2][1], shapes[3][0]
    g = near(wide_g * 0.7, 128)
    u = near(wide_u * 0.65, 128)
    d = near(tall * 0.3, 8)
    return [
        Piece(1, 1, 0, g, 0, 0),
        Piece(4, 1, 0, shapes[4][1], 0, 2),
        Piece(1, 1, g, wide_g - g, 0, 2),
        Piece(0, 1, 0, wide_a, 0, 1),
        Piece(2, 1, u, wide_u - u, 1, 0),
        Piece(3, 0, 0, d, 1, 0),
        Piece(3, 0, d, tall - d, 1, 2),
        Piece(2, 1, 0, u, 1, 1),
    ]


def coordinates(topo):
    g, t = lax.axis_index("grp"), lax.axis_index("tok")
    return lax.rem(t, topo.X), lax.div(g, 2), lax.div(t, topo.X), lax.rem(g, 2)


def gather_kernel(topo, pieces, *refs):
    shards, outs = refs[:5], refs[5:10]
    local_sem, recv_sem, z_sem, x_sem, y_sem, c_sem = refs[10:]
    x, y, z, c = coordinates(topo)
    X, Z, T = topo.X, topo.Z, topo.T
    g, me = lax.axis_index("grp"), lax.axis_index("tok")
    odd = lax.rem(y, 2)
    over_y = {"grp": g + 2 - 4 * odd, "tok": me}
    over_c = {"grp": g + 1 - 2 * c, "tok": me}

    def over_z(k):
        return {"grp": g, "tok": (z + k) * X + x}

    def over_x(k):
        return {"grp": g, "tok": z * X + lax.rem(x + k, X)}

    barrier = pltpu.get_barrier_semaphore()
    partners = [over_y, over_c] + [over_x(k) for k in range(1, X)]
    for partner in partners:
        pl.semaphore_signal(barrier, inc=1, device_id=partner, device_id_type=pl.DeviceIdType.MESH)
    below, above = z > 0, z < Z - 1

    def greet(k):
        pl.semaphore_signal(
            barrier, inc=1, device_id=over_z(k), device_id_type=pl.DeviceIdType.MESH
        )

    pl.when(below)(lambda: greet(-1))
    pl.when(above)(lambda: greet(1))
    own = [
        pltpu.make_async_copy(shards[i], outs[i].at[me], local_sem.at[i]) for i in range(5)
    ]
    for copy in own:
        copy.start()
    pl.semaphore_wait(barrier, len(partners) + below.astype(jnp.int32) + above.astype(jnp.int32))

    def send(p, t, sem, target, mine=False):
        piece = pieces[p]
        landing = piece.of(outs[piece.array].at[t])
        source = piece.of(shards[piece.array]) if mine else landing
        return pltpu.make_async_remote_copy(
            src_ref=source, dst_ref=landing, send_sem=sem, recv_sem=recv_sem.at[p, t],
            device_id=target, device_id_type=pl.DeviceIdType.MESH,
        )

    def arrived(p, t):
        send(p, t, c_sem.at[0, 0], over_c).wait_recv()

    def run(core):
        mine = [p for p in range(len(pieces)) if pieces[p].core == core]
        theirs = [p for p in range(len(pieces)) if pieces[p].core != core]
        slot = {p: i for i, p in enumerate(mine)}

        def inside(p, body):
            part = pieces[p].part
            if part == 1:
                body()
            else:
                pl.when(odd == part // 2)(body)

        def outside(p, body):
            if pieces[p].part != 1:
                pl.when(odd != pieces[p].part // 2)(body)

        def x_copies(p, zz, first):
            t = zz * X + x
            return [
                send(p, t, x_sem.at[slot[p], zz, k - 1], over_x(k), first) for k in range(1, X)
            ]

        def y_copy(p, t):
            return send(p, t, y_sem.at[slot[p], t], over_y)

        def c_copy(p, t):
            return send(p, t, c_sem.at[slot[p], t], over_c)

        def z_copy(p, zz, k, first):
            return send(p, zz * X + x, z_sem.at[slot[p], zz, (k + 1) // 2], over_z(k), first)

        for p in mine:
            def begin(p=p):
                pl.when(below)(lambda: z_copy(p, z, -1, True).start())
                pl.when(above)(lambda: z_copy(p, z, 1, True).start())
                for copy in x_copies(p, z, True):
                    copy.start()
            inside(p, begin)

        def share(p, t):
            if pieces[p].part != 1:
                y_copy(p, t).start()
            c_copy(p, t).start()

        def relay(p, zz, k):
            arrived(p, zz * X + x)
            pl.when(above if k > 0 else below)(lambda: z_copy(p, zz, k, False).start())
            for copy in x_copies(p, zz, False):
                copy.start()
            share(p, zz * X + x)

        def others(p, zz):
            for j in range(1, X):
                t = zz * X + lax.rem(x + j, X)
                arrived(p, t)
                share(p, t)

        def around(k, carry):
            low, high = z - k, z + k
            for p in mine:
                inside(p, lambda p=p: pl.when(low >= 0)(lambda: relay(p, low, 1)))
                inside(p, lambda p=p: pl.when(high < Z)(lambda: relay(p, high, -1)))
            low, high = z - k + 1, z + k - 1
            for p in mine:
                inside(p, lambda p=p: pl.when(low >= 0)(lambda: others(p, low)))
                inside(p, lambda p=p: pl.when((k > 1) & (high < Z))(lambda: others(p, high)))
            return carry

        lax.fori_loop(1, Z + 1, around, 0)

        def rest(t, carry):
            @pl.when(t != me)
            def _():
                for p in mine:
                    def forward(p=p):
                        arrived(p, t)
                        c_copy(p, t).start()
                    outside(p, forward)
            return carry

        lax.fori_loop(0, T, rest, 0)

        def finish(t, carry):
            @pl.when(t != me)
            def _():
                for p in theirs:
                    arrived(p, t)
                for p in mine:
                    c_copy(p, t).wait_send()
                    if pieces[p].part != 1:
                        inside(p, lambda p=p: y_copy(p, t).wait_send())
            return carry

        lax.fori_loop(0, T, finish, 0)
        for p in mine:
            def end(p=p):
                def each(zz, carry):
                    pl.when((zz <= z) & above)(lambda: z_copy(p, zz, 1, False).wait_send())
                    pl.when((zz >= z) & below)(lambda: z_copy(p, zz, -1, False).wait_send())
                    for copy in x_copies(p, zz, False):
                        copy.wait_send()
                    return carry
                lax.fori_loop(0, Z, each, 0)
            inside(p, end)

    pl.when(c == 0)(lambda: run(0))
    pl.when(c == 1)(lambda: run(1))
    for copy in own:
        copy.wait()


def gather_weights(topo, shards):
    pieces = cut_pieces([s.shape for s in shards])
    T = topo.T
    DMA = pltpu.SemaphoreType.DMA
    hbm = pl.BlockSpec(memory_space=pl.ANY)
    outs = pl.pallas_call(
        functools.partial(gather_kernel, topo, pieces),
        in_specs=[hbm] * 5,
        out_specs=[hbm] * 5,
        out_shape=[jax.ShapeDtypeStruct((T,) + s.shape, s.dtype) for s in shards],
        scratch_shapes=[
            DMA((5,)), DMA((len(pieces), T)), DMA((4, topo.Z, 2)), DMA((4, topo.Z, topo.X - 1)),
            DMA((4, T)), DMA((4, T)),
        ],
        compiler_params=pltpu.CompilerParams(collective_id=0, has_side_effects=True),
        name="gather_weights",
    )(*shards)
    return [o.reshape(-1, o.shape[-1]) for o in outs]


class Share:
    def __init__(self, array, start, shape, part):
        self.array, self.start, self.shape, self.part = array, start, shape, part

    def of(self, ref, core, *lead):
        rows, columns = self.shape
        if self.array == 2:
            return ref.at[(core,) + lead + (slice(None), pl.ds(self.start, columns))]
        if self.array == 3:
            at = pl.multiple_of(core * rows, rows)
            return ref.at[lead + (pl.ds(at, rows), slice(None))]
        at = pl.multiple_of(core * columns, 128)
        return ref.at[lead + (slice(None), pl.ds(at, columns))]


def cut_shares(shapes):
    rows, ff = shapes[2][2], shapes[2][3]
    one = ff * 3 // 20 // 128 * 128
    two = ff * 33 // 40 // 128 * 128
    return [
        Share(2, one, (rows, two - one), 0),
        Share(3, 0, (shapes[3][1] // 2, shapes[3][2]), 2),
        Share(2, two, (rows, ff - two), 2),
        Share(0, 0, (rows, shapes[0][2] // 2), 1),
        Share(1, 0, (rows, shapes[1][2] // 2), 1),
        Share(2, 0, (rows, one), 1),
    ]


def reduce_kernel(topo, shares, *refs):
    grads, outs = refs[:4], refs[4:8]
    count = len(shares)
    groups = []
    at = 8
    for _ in range(7):
        groups.append(refs[at:at + count])
        at += count
    held, from_c, from_y, from_x, from_low, from_high, from_f = groups
    (load_sem, c_send, c_recv, y_send, y_recv, x_send, x_recv, z_send, z_recv, f_send, f_recv,
     o_send, o_recv, o_local) = refs[at:]
    x, y, z, c = coordinates(topo)
    X, Z, T = topo.X, topo.Z, topo.T
    g, me = lax.axis_index("grp"), lax.axis_index("tok")
    odd = lax.rem(y, 2)
    below, above = z > 0, z < Z - 1
    kind = pl.DeviceIdType.MESH

    def over_y(k):
        high = lax.rem(lax.div(y, 1 << k), 2)
        return {"grp": g + (2 - 4 * high) * (1 << k), "tok": me}

    over_c = {"grp": g + 1 - 2 * c, "tok": me}

    def over_z(k):
        return {"grp": g, "tok": (z + k) * X + x}

    def over_x(k):
        return {"grp": g, "tok": z * X + lax.rem(x + k, X)}

    barrier = pltpu.get_barrier_semaphore()
    partners = [over_c] + [over_y(k) for k in range(topo.bits["y"])]
    partners += [over_x(k) for k in range(1, X)]

    def greet(partner):
        pl.semaphore_signal(barrier, inc=1, device_id=partner, device_id_type=kind)

    for partner in partners:
        greet(partner)
    pl.when(below)(lambda: greet(over_z(-1)))
    pl.when(above)(lambda: greet(over_z(1)))
    every = range(count)

    def load(p, t):
        s = shares[p]
        return pltpu.make_async_copy(
            s.of(grads[s.array], c, t), held[p].at[t], load_sem.at[p, t]
        )

    def remote(source, landing, send, recv, target):
        return pltpu.make_async_remote_copy(
            src_ref=source, dst_ref=landing, send_sem=send, recv_sem=recv, device_id=target,
            device_id_type=kind,
        )

    def c_copy(p, t):
        s = shares[p]
        return remote(
            s.of(grads[s.array], 1 - c, t), from_c[p].at[t], c_send.at[p, t], c_recv.at[p, t],
            over_c,
        )

    def y_copy(p, t):
        return remote(
            held[p].at[t], from_y[p].at[t], y_send.at[p, t], y_recv.at[p, t], over_y(0)
        )

    def x_copy(p, zz, k):
        t = zz * X + lax.rem(x + k, X)
        return remote(
            held[p].at[t], from_x[p].at[zz, k - 1], x_send.at[p, zz, k - 1],
            x_recv.at[p, zz, k - 1], over_x(k),
        )

    def z_copy(p, zz, k):
        landing = from_low if k > 0 else from_high
        way = (k + 1) // 2
        return remote(
            held[p].at[zz * X + x], landing[p].at[zz], z_send.at[p, zz, way],
            z_recv.at[p, zz, way], over_z(k),
        )

    def f_copy(p, k):
        return remote(
            held[p].at[me], from_f[p].at[k], f_send.at[p, k], f_recv.at[p, k], over_y(k)
        )

    def o_copy(p):
        s = shares[p]
        return remote(
            held[p].at[me], s.of(outs[s.array], c), o_send.at[p], o_recv.at[p], over_c
        )

    def o_arrived(p):
        s = shares[p]
        return remote(
            held[p].at[me], s.of(outs[s.array], 1 - c), o_send.at[p], o_recv.at[p], over_c
        )

    def o_keep(p):
        s = shares[p]
        return pltpu.make_async_copy(held[p].at[me], s.of(outs[s.array], c), o_local.at[p])

    def add(p, t, other):
        held[p][t] = held[p][t] + other

    def layers(body):
        def step(i, carry):
            k = Z - 1 - i
            pl.when(z + k < Z)(lambda: body(z + k))
            pl.when((k > 0) & (z - k >= 0))(lambda: body(z - k))
            return carry
        return step

    def inside(p, body):
        if shares[p].part == 1:
            body()
        else:
            pl.when(odd == shares[p].part // 2)(body)

    def outside(p, body):
        if shares[p].part != 1:
            pl.when(odd != shares[p].part // 2)(body)

    def start_loads(zz):
        def each(j, carry):
            t = zz * X + lax.rem(x + j, X)
            for p in every:
                load(p, t).start()
            return carry
        lax.fori_loop(0, X, each, 0)

    lax.fori_loop(0, Z, layers(start_loads), 0)
    pl.semaphore_wait(barrier, len(partners) + below.astype(jnp.int32) + above.astype(jnp.int32))

    def start_cores(zz):
        def each(j, carry):
            t = zz * X + lax.rem(x + j, X)
            for p in every:
                c_copy(p, t).start()
            return carry
        lax.fori_loop(0, X, each, 0)

    lax.fori_loop(0, Z, layers(start_cores), 0)

    def cores(zz):
        def each(j, carry):
            t = zz * X + lax.rem(x + j + 1, X)
            for p in every:
                load(p, t).wait()
                c_copy(p, t).wait_recv()
                add(p, t, from_c[p][t])
                outside(p, lambda p=p: y_copy(p, t).start())
                if shares[p].part == 1:
                    for k in range(1, X):
                        pl.when(j + 1 == k)(lambda p=p, k=k: x_copy(p, zz, k).start())
            return carry
        lax.fori_loop(0, X, each, 0)

    lax.fori_loop(0, Z, layers(cores), 0)

    def over(zz):
        def each(j, carry):
            t = zz * X + lax.rem(x + j + 1, X)
            for p in every:
                if shares[p].part != 1:
                    def body(p=p):
                        y_copy(p, t).wait_recv()
                        add(p, t, from_y[p][t])
                        for k in range(1, X):
                            pl.when(j + 1 == k)(lambda: x_copy(p, zz, k).start())
                    inside(p, body)
            return carry
        lax.fori_loop(0, X, each, 0)

    def join(p, zz):
        t = zz * X + x
        for k in range(1, X):
            x_copy(p, zz, k).wait_recv()
            add(p, t, from_x[p][zz, k - 1])

        def low():
            z_copy(p, zz, 1).wait_recv()
            add(p, t, from_low[p][zz])

        def high():
            z_copy(p, zz, -1).wait_recv()
            add(p, t, from_high[p][zz])

        pl.when((zz >= z) & below)(low)
        pl.when((zz <= z) & above)(high)
        pl.when(zz > z)(lambda: z_copy(p, zz, 1).start())
        pl.when(zz < z)(lambda: z_copy(p, zz, -1).start())

    single = topo.bits["y"] == 1

    def first_joins(zz):
        for p in every:
            if shares[p].part == 1:
                join(p, zz)
                if single:
                    pl.when(zz == z)(lambda p=p: f_copy(p, 0).start())

    def last_joins(zz):
        for p in every:
            if shares[p].part != 1:
                def body(p=p):
                    join(p, zz)
                    if single:
                        pl.when(zz == z)(lambda: f_copy(p, 0).start())
                inside(p, body)

    def main(i, carry):
        @pl.when(i < Z)
        def _():
            layers(first_joins)(i, 0)
            layers(over)(i, 0)

        @pl.when(i > 0)
        def _():
            layers(last_joins)(i - 1, 0)

        return carry

    lax.fori_loop(0, Z + 1, main, 0)

    for k in range(1, topo.bits["y"]):
        for p in every:
            inside(p, lambda p=p: f_copy(p, k).start())
        for p in every:
            def fold(p=p):
                f_copy(p, k).wait()
                add(p, me, from_f[p][k])
            inside(p, fold)
    if not single:
        for p in every:
            inside(p, lambda p=p: f_copy(p, 0).start())
    for p in every:
        if shares[p].part == 1:
            f_copy(p, 0).wait()
            add(p, me, from_f[p][0])
        else:
            def take(p=p):
                f_copy(p, 0).wait_recv()
                held[p][me] = from_f[p][0]
            outside(p, lambda p=p: y_copy(p, me).wait_send())
            outside(p, take)
        o_copy(p).start()
        o_keep(p).start()

    def ends(t, carry):
        for p in every:
            c_copy(p, t).wait_send()
            outside(p, lambda p=p: pl.when(t != me)(lambda: y_copy(p, t).wait_send()))
        return carry

    lax.fori_loop(0, T, ends, 0)

    def z_ends(zz, carry):
        for p in every:
            def body(p=p):
                for k in range(1, X):
                    x_copy(p, zz, k).wait_send()
                pl.when(zz > z)(lambda: z_copy(p, zz, 1).wait_send())
                pl.when(zz < z)(lambda: z_copy(p, zz, -1).wait_send())
            inside(p, body)
        return carry

    lax.fori_loop(0, Z, z_ends, 0)
    for p in every:
        if shares[p].part != 1:
            inside(p, lambda p=p: f_copy(p, 0).wait_send())
        o_copy(p).wait_send()
        o_arrived(p).wait_recv()
        o_keep(p).wait()


def reduce_gradients(topo, grads):
    shares = cut_shares([v.shape for v in grads])
    X, Z, T = topo.X, topo.Z, topo.T
    n = len(shares)
    folds = max(1, topo.bits["y"])
    DMA = pltpu.SemaphoreType.DMA
    hbm = pl.BlockSpec(memory_space=pl.ANY)
    lead = [(T,), (T,), (T,), (Z, X - 1), (Z,), (Z,), (folds,)]
    rooms = [
        pltpu.VMEM(front + s.shape, BF)
        for front in lead for s in shares
    ]
    outs = [grads[0].shape[1:], grads[1].shape[1:], (2,) + grads[2].shape[2:], grads[3].shape[1:]]
    return pl.pallas_call(
        functools.partial(reduce_kernel, topo, shares),
        in_specs=[hbm] * 4,
        out_specs=[hbm] * 4,
        out_shape=[jax.ShapeDtypeStruct(s, BF) for s in outs],
        scratch_shapes=rooms + [
            DMA((n, T)), DMA((n, T)), DMA((n, T)), DMA((n, T)), DMA((n, T)),
            DMA((n, Z, X - 1)), DMA((n, Z, X - 1)), DMA((n, Z, 2)), DMA((n, Z, 2)),
            DMA((n, folds)), DMA((n, folds)), DMA((n,)), DMA((n,)), DMA((n,)),
        ],
        compiler_params=pltpu.CompilerParams(
            collective_id=1, has_side_effects=True, vmem_limit_bytes=60 << 20
        ),
        name="reduce_gradients",
    )(*grads)


def group_order(topo):
    return list(reversed(topo.keys("y"))) + topo.keys("c") + list(reversed(topo.keys("x")))


def group_gather(topo, arr, order):
    names = group_order(topo)
    held = []
    shape = arr.shape
    for key in order:
        place = sum(1 for h in held if names.index(h) < names.index(key))
        arr = double(topo, arr, key, place, True)
        held.append(key)
    return arr.reshape((topo.T,) + shape)


def group_scatter(topo, arr, order):
    names = group_order(topo)
    held = list(names)
    arr = arr.reshape((2,) * len(names) + arr.shape[1:])
    for key in order:
        arr = halve(topo, arr, key, held.index(key), True)
        held.remove(key)
    return arr


def small_layer(topo):
    return topo.X == 2 and topo.Y == 2


class Layer:
    def __init__(self, topo):
        self.topo = topo
        x, y, z, c = coordinates(topo)
        self.c = c
        far_x, far_y = 1 - x, 1 - y
        a = (x + c * (far_x - x), far_y + c * (y - far_y))
        b = (far_x + c * (x - far_x), y + c * (far_y - y))
        self.chips = [(x, y), a, b, (far_x, far_y)]
        self.z = z

    def pack(self, slot, core):
        x, y = self.chips[slot]
        return (y * 2 + core) * self.topo.X + x

    def device(self, slot, core):
        x, y = self.chips[slot]
        return {"grp": y * 2 + core, "tok": self.z * self.topo.X + x}

    def meet(self):
        barrier = pltpu.get_barrier_semaphore()
        for target in (self.device(1, self.c), self.device(2, self.c), self.device(0, 1 - self.c)):
            pl.semaphore_signal(
                barrier, inc=1, device_id=target, device_id_type=pl.DeviceIdType.MESH
            )
        pl.semaphore_wait(barrier, 3)


def remote_copy(source, landing, send, recv, target):
    return pltpu.make_async_remote_copy(
        src_ref=source, dst_ref=landing, send_sem=send, recv_sem=recv, device_id=target,
        device_id_type=pl.DeviceIdType.MESH,
    )


def group_gather_kernel(topo, count, *refs):
    mine, outs = refs[:count], refs[count:2 * count]
    local_sem, send_sem, recv_sem = refs[2 * count:]
    layer = Layer(topo)
    c = layer.c
    arrays = range(count)
    a, b, sibling = layer.device(1, c), layer.device(2, c), layer.device(0, 1 - c)
    own = layer.pack(0, c)

    def send(i, way, pack, target):
        landing = outs[i].at[pack]
        source = mine[i] if way in (0, 1, 3) else landing
        return remote_copy(source, landing, send_sem.at[i, way], recv_sem.at[i, pack], target)

    ways = [
        (0, own, a), (1, own, b), (2, layer.pack(1, c), b), (3, own, sibling),
        (4, layer.pack(1, c), sibling), (5, layer.pack(2, c), sibling),
        (6, layer.pack(3, c), sibling),
    ]

    def start(k):
        for i in arrays:
            send(i, *ways[k]).start()

    def arrived(pack):
        for i in arrays:
            send(i, 2, pack, sibling).wait_recv()

    keep = [pltpu.make_async_copy(mine[i], outs[i].at[own], local_sem.at[i]) for i in arrays]
    for copy in keep:
        copy.start()
    layer.meet()
    start(0)
    start(1)
    start(3)
    arrived(layer.pack(1, c))
    start(2)
    start(4)
    arrived(layer.pack(2, c))
    start(5)
    arrived(layer.pack(3, c))
    start(6)
    for slot in range(4):
        arrived(layer.pack(slot, 1 - c))
    for way in ways:
        for i in arrays:
            send(i, *way).wait_send()
    for copy in keep:
        copy.wait()


def gather_layer(topo, arrays, ident):
    DMA = pltpu.SemaphoreType.DMA
    hbm = pl.BlockSpec(memory_space=pl.ANY)
    n = len(arrays)
    return pl.pallas_call(
        functools.partial(group_gather_kernel, topo, n),
        in_specs=[hbm] * n,
        out_specs=[hbm] * n,
        out_shape=[jax.ShapeDtypeStruct((topo.T,) + v.shape, v.dtype) for v in arrays],
        scratch_shapes=[DMA((n,)), DMA((n, 7)), DMA((n, topo.T))],
        compiler_params=pltpu.CompilerParams(collective_id=ident, has_side_effects=True),
        name="gather_layer",
    )(*arrays)


def group_reduce_kernel(topo, grads, out, held, from_c, from_b, from_a, load_sem, c_send, c_recv,
                        send_sem, recv_sem):
    layer = Layer(topo)
    c = layer.c
    a, b, sibling = layer.device(1, c), layer.device(2, c), layer.device(0, 1 - c)
    order = (3, 2, 1, 0)

    def load(slot):
        return pltpu.make_async_copy(
            grads.at[layer.pack(slot, c)], held.at[slot], load_sem.at[slot]
        )

    def c_copy(slot):
        theirs = (0, 2, 1, 3)[slot]
        return remote_copy(
            grads.at[layer.pack(slot, 1 - c)], from_c.at[theirs], c_send.at[theirs],
            c_recv.at[theirs], sibling,
        )

    def c_arrived(slot):
        remote_copy(
            grads.at[layer.pack(slot, c)], from_c.at[slot], c_send.at[slot], c_recv.at[slot],
            sibling,
        ).wait_recv()

    across = remote_copy(held.at[3], from_b.at[1], send_sem.at[0], recv_sem.at[0], b)
    direct = remote_copy(held.at[2], from_b.at[0], send_sem.at[1], recv_sem.at[1], b)
    passed = remote_copy(held.at[1], from_a, send_sem.at[2], recv_sem.at[2], a)

    for slot in order:
        load(slot).start()
    layer.meet()
    for slot in (3, 1, 2, 0):
        c_copy(slot).start()
    for slot in order:
        load(slot).wait()
        c_arrived(slot)
        held[slot] = held[slot] + from_c[slot]
        if slot == 3:
            across.start()
        if slot == 2:
            direct.start()
    across.wait_recv()
    held[1] = held[1] + from_b[1]
    passed.start()
    direct.wait_recv()
    held[0] = held[0] + from_b[0]
    passed.wait_recv()
    out[...] = held[0] + from_a[...]
    across.wait_send()
    direct.wait_send()
    passed.wait_send()
    for slot in range(4):
        c_copy(slot).wait_send()


def reduce_layer(topo, grads, ident):
    DMA = pltpu.SemaphoreType.DMA
    block = grads.shape[1:]
    return pl.pallas_call(
        functools.partial(group_reduce_kernel, topo),
        in_specs=[pl.BlockSpec(memory_space=pl.ANY)],
        out_specs=pl.BlockSpec(memory_space=pltpu.VMEM),
        out_shape=jax.ShapeDtypeStruct(block, BF),
        scratch_shapes=[
            pltpu.VMEM((4,) + block, BF), pltpu.VMEM((4,) + block, BF),
            pltpu.VMEM((2,) + block, BF), pltpu.VMEM(block, BF),
            DMA((4,)), DMA((4,)), DMA((4,)), DMA((3,)), DMA((3,)),
        ],
        compiler_params=pltpu.CompilerParams(
            collective_id=ident, has_side_effects=True, vmem_limit_bytes=32 << 20
        ),
        name="reduce_layer",
    )(grads)


NT = (((1,), (1,)), ((), ()))
TN = (((0,), (0,)), ((), ()))
LANES = 2 * HD
CHUNKS = (HEADS + 1) // 2
ROOM = 60 << 20


def lanes_of(rows):
    return lax.broadcasted_iota(jnp.int32, (rows, LANES), 1)


def spin(v):
    first = lax.rem(lanes_of(v.shape[0]), HD) < HD // 2
    return jnp.where(first, -pltpu.roll(v, LANES - HD // 2, 1), pltpu.roll(v, HD // 2, 1))


def whole(*shape):
    return pl.BlockSpec(shape, lambda *i: (0,) * len(shape))


def normed(v, gain):
    return v * lax.rsqrt(jnp.mean(v * v, axis=-1, keepdims=True) + EPS) * gain


def project_kernel(state_ref, gain_ref, w_ref, turn_ref, n1_ref, q_ref, kv_ref):
    n1 = normed(state_ref[...], gain_ref[...]).astype(BF)
    n1_ref[...] = n1
    cosine, sine = turn_ref[0], turn_ref[1]
    key = lanes_of(n1.shape[0]) < HD
    columns = w_ref.shape[1]
    for start in range(0, columns, 2 * LANES):
        wide = min(2 * LANES, columns - start)
        both = jnp.dot(n1, w_ref[:, start:start + wide], preferred_element_type=F32)
        for half in range(wide // LANES):
            j = start // LANES + half
            v = both[:, half * LANES:(half + 1) * LANES]
            turned = v * cosine + spin(v) * sine
            if j < CHUNKS:
                q_ref[j] = (turned * HD ** -0.5).astype(BF)
            else:
                j -= CHUNKS
                kv_ref[:, j * LANES:(j + 1) * LANES] = jnp.where(key, turned, v).astype(BF)


def project(state, gain, w, turns):
    n, model = state.shape
    return pl.pallas_call(
        project_kernel,
        grid=(1,),
        in_specs=[whole(n, model), whole(1, model), whole(*w.shape), whole(*turns.shape)],
        out_specs=[whole(n, model), whole(CHUNKS, n, LANES), whole(n, KV_HEADS * LANES)],
        out_shape=[
            jax.ShapeDtypeStruct((n, model), BF),
            jax.ShapeDtypeStruct((CHUNKS, n, LANES), BF),
            jax.ShapeDtypeStruct((n, KV_HEADS * LANES), BF),
        ],
        compiler_params=pltpu.CompilerParams(vmem_limit_bytes=ROOM),
        name="project",
    )(state, gain, w, turns)


def attend_kernel(rows, span, key_ref, query_ref, kv_ref, q_ref, mixed_ref, out_ref, stat_ref,
                  stacked, mixing, tops, sums):
    low = lanes_of(rows) < HD
    wide = SHARES * rows
    for h in range(KV_HEADS):
        for j in range(SHARES):
            head = h * SHARES + j
            chunk = q_ref[head // 2].astype(F32)
            if head % 2:
                chunk = pltpu.roll(chunk, HD, 1)
            stacked[h, j * rows:(j + 1) * rows, :] = jnp.where(low, chunk, 0.0).astype(BF)
    mixing[...] = jnp.zeros(mixing.shape, F32)
    sums[...] = jnp.zeros(sums.shape, F32)
    tops[...] = jnp.full(tops.shape, BIG, F32)

    def body(t, carry):
        at = pl.ds(pl.multiple_of(t * rows, rows), rows)
        bias = block_bias(key_ref[at, :], query_ref)
        def score(h):
            kv = kv_ref[at, h * LANES:(h + 1) * LANES]
            return lax.dot_general(kv, stacked[h], NT, preferred_element_type=F32) + bias

        def end(h, p, fade):
            kv = kv_ref[at, h * LANES:(h + 1) * LANES]
            mixing[h] = mixing[h] * fade + lax.dot_general(
                kv[:, HD:], p, TN, preferred_element_type=F32
            )

        ahead = score(0)
        before = None
        for h in range(KV_HEADS):
            s = ahead
            if h + 1 < KV_HEADS:
                ahead = score(h + 1)
            if before is not None:
                end(*before)
            old = tops[h, 0:1, :]
            top = jnp.max(s.reshape(rows // 8, 8, wide), axis=0)
            top = jnp.maximum(old, jnp.max(top, axis=0, keepdims=True))
            p = jnp.exp(s - top)
            fade = jnp.exp(old - top)
            sums[h] = sums[h] * fade + jnp.sum(p.reshape(rows // 8, 8, wide), axis=0)
            tops[h] = jnp.broadcast_to(top, (8, wide))
            before = (h, p.astype(BF), fade)
        end(*before)
        return carry

    lax.fori_loop(span[0], span[1], body, 0)
    for h in range(KV_HEADS):
        total = jnp.sum(sums[h], axis=0, keepdims=True)
        stat_ref[h] = tops[h] + jnp.log(total)
        mixing[h] = mixing[h] / total
    for j in range(CHUNKS):
        both = head_pair(mixing, j, rows)
        out_ref[j] = both
        size = min(LANES, HEADS * HD - j * LANES)
        mixed_ref[:, j * LANES:j * LANES + size] = both.astype(BF)[:, :size]


def block_bias(keys, query_ref):
    live, order = keys[:, 0:1], keys[:, 1:2]
    begin, place = query_ref[0:1, :], query_ref[1:2, :]
    allowed = ((live >= begin) & (live <= place)) | (order == place)
    return jnp.where(allowed, 0.0, BIG)


def head_pair(mixing, j, rows):
    def one(head):
        if head >= HEADS:
            return jnp.zeros((HD, rows), F32)
        at = head % SHARES * rows
        return mixing[head // SHARES, :, at:at + rows]

    return jnp.transpose(jnp.concatenate([one(2 * j), one(2 * j + 1)], axis=0))


def attend(rows, span, key_labels, query_labels, kv_all, q):
    count, columns = kv_all.shape
    wide = SHARES * rows
    return pl.pallas_call(
        functools.partial(attend_kernel, rows),
        grid_spec=pltpu.PrefetchScalarGridSpec(
            num_scalar_prefetch=1,
            grid=(1,),
            in_specs=[
                whole(count, 8), whole(8, wide), whole(count, columns),
                whole(CHUNKS, rows, LANES),
            ],
            out_specs=[
                whole(rows, HEADS * HD), whole(CHUNKS, rows, LANES), whole(KV_HEADS, 8, wide),
            ],
            scratch_shapes=[
                pltpu.VMEM((KV_HEADS, wide, LANES), BF), pltpu.VMEM((KV_HEADS, HD, wide), F32),
                pltpu.VMEM((KV_HEADS, 8, wide), F32), pltpu.VMEM((KV_HEADS, 8, wide), F32),
            ],
        ),
        out_shape=[
            jax.ShapeDtypeStruct((rows, HEADS * HD), BF),
            jax.ShapeDtypeStruct((CHUNKS, rows, LANES), F32),
            jax.ShapeDtypeStruct((KV_HEADS, 8, wide), F32),
        ],
        compiler_params=pltpu.CompilerParams(vmem_limit_bytes=62 << 20),
        name="attend",
    )(span, key_labels, query_labels, kv_all, q)


def attend_back_kernel(rows, span, key_ref, query_ref, kv_ref, q_ref, d_ref, out_ref, stat_ref,
                       turn_ref, dq_ref, dkv_ref, stacked, part, mixing, deltas):
    low = lanes_of(rows) < HD
    wide = SHARES * rows
    ones = jnp.ones((8, LANES), BF)
    for h in range(KV_HEADS):
        for j in range(SHARES):
            head = h * SHARES + j
            q = q_ref[head // 2].astype(F32)
            d = d_ref[head // 2].astype(F32)
            if head % 2:
                q = pltpu.roll(q, HD, 1)
            product = d * out_ref[head // 2]
            mine = ~low if head % 2 else low
            if head % 2 == 0:
                d = pltpu.roll(d, HD, 1)
            at = pl.ds(j * rows, rows)
            stacked[h, at, :] = jnp.where(low, q, d).astype(BF)
            part[at, :] = jnp.where(mine, product, 0.0)
        coarse = part[...].astype(BF)
        fine = (part[...] - coarse.astype(F32)).astype(BF)
        deltas[h] = lax.dot_general(
            ones, coarse, NT, preferred_element_type=F32
        ) + lax.dot_general(ones, fine, NT, preferred_element_type=F32)
    dkv_ref[...] = jnp.zeros(dkv_ref.shape, BF)
    mixing[...] = jnp.zeros(mixing.shape, F32)

    def body(t, carry):
        at = pl.ds(pl.multiple_of(t * rows, rows), rows)
        bias = block_bias(key_ref[at, :], query_ref)
        for h in range(KV_HEADS):
            kv = kv_ref[at, h * LANES:(h + 1) * LANES]
            zero = jnp.zeros_like(kv)
            queries = stacked[h]
            s = lax.dot_general(jnp.where(low, kv, zero), queries, NT, preferred_element_type=F32)
            p = jnp.exp(s + bias - stat_ref[h, 0:1, :])
            dp = lax.dot_general(jnp.where(low, zero, kv), queries, NT, preferred_element_type=F32)
            ds = (p * (dp - deltas[h, 0:1, :])).astype(BF)
            dk = jnp.dot(ds, queries, preferred_element_type=F32)
            dv = jnp.dot(p.astype(BF), queries, preferred_element_type=F32)
            dkv_ref[at, h * LANES:(h + 1) * LANES] = jnp.where(low, dk, dv).astype(BF)
            mixing[h] += lax.dot_general(kv[:, :HD], ds, TN, preferred_element_type=F32)
        return carry

    lax.fori_loop(span[0], span[1], body, 0)
    cosine, sine = turn_ref[0], turn_ref[1]
    for j in range(CHUNKS):
        both = head_pair(mixing, j, rows) * HD ** -0.5
        both = both * cosine - spin(both) * sine
        dq_ref[:, j * LANES:(j + 1) * LANES] = both.astype(BF)


def attend_back(rows, span, key_labels, query_labels, kv_all, q, d_mixed, out, stat, turns):
    count, columns = kv_all.shape
    wide = SHARES * rows
    return pl.pallas_call(
        functools.partial(attend_back_kernel, rows),
        grid_spec=pltpu.PrefetchScalarGridSpec(
            num_scalar_prefetch=1,
            grid=(1,),
            in_specs=[
                whole(count, 8), whole(8, wide), whole(count, columns),
                whole(CHUNKS, rows, LANES), whole(CHUNKS, rows, LANES),
                whole(CHUNKS, rows, LANES), whole(KV_HEADS, 8, wide), whole(*turns.shape),
            ],
            out_specs=[whole(rows, CHUNKS * LANES), whole(count, columns)],
            scratch_shapes=[
                pltpu.VMEM((KV_HEADS, wide, LANES), BF), pltpu.VMEM((wide, LANES), F32),
                pltpu.VMEM((KV_HEADS, HD, wide), F32), pltpu.VMEM((KV_HEADS, 8, wide), F32),
            ],
        ),
        out_shape=[
            jax.ShapeDtypeStruct((rows, CHUNKS * LANES), BF),
            jax.ShapeDtypeStruct((count, columns), BF),
        ],
        compiler_params=pltpu.CompilerParams(vmem_limit_bytes=62 << 20),
        name="attend_back",
    )(span, key_labels, query_labels, kv_all, q, d_mixed, out, stat, turns)


def out_back_kernel(d_ref, w_ref, out_ref):
    d = d_ref[...]
    for j in range(CHUNKS):
        size = min(LANES, w_ref.shape[0] - j * LANES)
        v = lax.dot_general(
            d, w_ref[j * LANES:j * LANES + size, :], NT, preferred_element_type=F32
        ).astype(BF)
        if size < LANES:
            v = jnp.concatenate([v, jnp.zeros((d.shape[0], LANES - size), BF)], axis=1)
        out_ref[j] = v


def out_back(d_att, w_out):
    n = d_att.shape[0]
    return pl.pallas_call(
        out_back_kernel,
        grid=(1,),
        in_specs=[whole(*d_att.shape), whole(*w_out.shape)],
        out_specs=whole(CHUNKS, n, LANES),
        out_shape=jax.ShapeDtypeStruct((CHUNKS, n, LANES), BF),
        compiler_params=pltpu.CompilerParams(vmem_limit_bytes=ROOM),
        name="out_back",
    )(d_att, w_out)


def project_back_kernel(gradient_ref, state_ref, gain_ref, w_ref, turn_ref, dq_ref, raw_ref,
                        grad_ref, dkv_ref, dgain_ref):
    cosine, sine = turn_ref[0], turn_ref[1]
    key = lanes_of(dq_ref.shape[0]) < HD
    for j in range(KV_HEADS):
        v = raw_ref[:, j * LANES:(j + 1) * LANES].astype(F32)
        turned = v * cosine - spin(v) * sine
        dkv_ref[:, j * LANES:(j + 1) * LANES] = jnp.where(key, turned, v).astype(BF)
    split = CHUNKS * LANES
    d = lax.dot_general(dq_ref[...], w_ref[:, :split], NT, preferred_element_type=F32)
    d += lax.dot_general(dkv_ref[...], w_ref[:, split:], NT, preferred_element_type=F32)
    v = state_ref[...]
    inv = lax.rsqrt(jnp.mean(v * v, axis=-1, keepdims=True) + EPS)
    scaled = d * gain_ref[...]
    dot = jnp.mean(scaled * v, axis=-1, keepdims=True)
    grad_ref[...] = gradient_ref[...] + inv * scaled - v * (inv * inv * inv * dot)
    dgain_ref[...] = jnp.sum(d * v * inv, axis=0, keepdims=True)


def project_back(gradient, state, gain, w, turns, dq, dkv):
    n, model = state.shape
    return pl.pallas_call(
        project_back_kernel,
        grid=(1,),
        in_specs=[
            whole(n, model), whole(n, model), whole(1, model), whole(*w.shape),
            whole(*turns.shape), whole(*dq.shape), whole(*dkv.shape),
        ],
        out_specs=[whole(n, model), whole(*dkv.shape), whole(1, model)],
        out_shape=[
            jax.ShapeDtypeStruct((n, model), F32),
            jax.ShapeDtypeStruct(dkv.shape, BF),
            jax.ShapeDtypeStruct((1, model), F32),
        ],
        compiler_params=pltpu.CompilerParams(vmem_limit_bytes=ROOM),
        name="project_back",
    )(gradient, state, gain, w, turns, dq, dkv)


def outer_columns_kernel(count, x_ref, *refs):
    ds, out_ref, turned = refs[:count], refs[count], refs[count + 1]

    @pl.when((pl.program_id(0) == 0) & (pl.program_id(1) == 0))
    def _():
        turned[...] = jnp.transpose(x_ref[...])

    for i in range(count):
        @pl.when(pl.program_id(0) == i)
        def _(i=i):
            out_ref[0] = jnp.dot(
                turned[...], ds[i][...], preferred_element_type=F32
            ).astype(BF)


def outer_columns(x, ds, tile):
    n, rows = x.shape
    columns = ds[0].shape[1]
    count = len(ds)

    def taken(i):
        return lambda a, j: (0, jnp.where(a == i, j, jnp.where(a < i, 0, columns // tile - 1)))

    return pl.pallas_call(
        functools.partial(outer_columns_kernel, count),
        grid=(count, columns // tile),
        in_specs=[whole(n, rows)] + [pl.BlockSpec((n, tile), taken(i)) for i in range(count)],
        out_specs=pl.BlockSpec((1, rows, tile), lambda a, j: (a, 0, j)),
        out_shape=jax.ShapeDtypeStruct((count, rows, columns), BF),
        scratch_shapes=[pltpu.VMEM((rows, n), BF)],
        compiler_params=pltpu.CompilerParams(vmem_limit_bytes=ROOM),
        cost_estimate=pl.CostEstimate(
            flops=2 * n * rows * columns * count, transcendentals=0,
            bytes_accessed=2 * count * (n * columns + rows * columns) + 2 * n * rows,
        ),
        name="outer_columns",
    )(x, *ds)


def outer_rows_kernel(x_ref, d_ref, out_ref):
    out_ref[...] = jnp.dot(
        jnp.transpose(x_ref[...]), d_ref[...], preferred_element_type=F32
    ).astype(BF)


def outer_rows(x, d, tile):
    n, rows = x.shape
    columns = d.shape[1]
    return pl.pallas_call(
        outer_rows_kernel,
        grid=(rows // tile,),
        in_specs=[pl.BlockSpec((n, tile), lambda i: (0, i)), whole(n, columns)],
        out_specs=pl.BlockSpec((tile, columns), lambda i: (i, 0)),
        out_shape=jax.ShapeDtypeStruct((rows, columns), BF),
        compiler_params=pltpu.CompilerParams(vmem_limit_bytes=ROOM),
        cost_estimate=pl.CostEstimate(
            flops=2 * n * rows * columns, transcendentals=0,
            bytes_accessed=2 * (n * columns + n * rows + rows * columns),
        ),
        name="outer_rows",
    )(x, d)


def mm(a, b):
    return jnp.dot(a, b, preferred_element_type=F32)


def mm_nt(a, b):
    return lax.dot_general(a, b, NT, preferred_element_type=F32)


def mm_tn(a, b):
    return lax.dot_general(a, b, TN, preferred_element_type=F32)


def inverse_rms(v):
    return lax.rsqrt(jnp.mean(v * v, axis=-1, keepdims=True) + EPS)


def norm_back(grad, v, inv, gain):
    scaled = grad * gain
    dot = jnp.mean(scaled * v, axis=-1, keepdims=True)
    return (inv * scaled - v * (inv * inv * inv * dot), jnp.sum(grad * v * inv, axis=0))


def per_device(topo, *args):
    (tokens, w_query, w_key, w_value, w_out, w_gate, w_up, w_down, router, norm_attn, norm_ffn,
     lengths, depths, padding, cotangent) = args
    rows, model = tokens.shape
    kv_cols = w_key.shape[1]
    ff = w_gate.shape[1]
    shard = w_query.shape[0]
    deep_rows = rows * 3 // 4
    xk, yk, ck = (topo.keys(d) for d in "xyc")

    small = jnp.concatenate([router, norm_attn[:, None], norm_ffn[:, None]], axis=1)
    small = jnp.pad(small, ((0, 0), (0, HD - small.shape[1])))
    w_kv = jnp.stack(
        [w_key.reshape(shard, KV_HEADS, HD), w_value.reshape(shard, KV_HEADS, HD)], axis=2
    ).reshape(shard, 2 * kv_cols)
    first = jnp.concatenate([w_query, small, w_kv], axis=1)
    weight_qkv, weight_g, weight_u, weight_d, weight_o = gather_weights(
        topo, [first, w_gate, w_up, w_down, w_out]
    )

    own = lax.axis_index("tok") * rows + jnp.arange(rows, dtype=jnp.int32)
    eligible = (depths >= 2) & (padding > 0)
    flags = jnp.stack([eligible, ~eligible]).astype(BF)
    upto = (jnp.arange(rows)[:, None] <= jnp.arange(rows)[None, :]).astype(BF)
    counts = mm(flags, upto).astype(jnp.int32)
    slot = jnp.where(eligible, counts[0] - 1, counts[0, -1] + counts[1] - 1)
    chosen = jnp.arange(rows, dtype=jnp.int32)[:, None] == slot[None, :]
    onehot = chosen.astype(BF)
    doc_ends = jnp.cumsum(lengths[0])
    begins = jnp.sum(
        jnp.where(own[:, None] >= doc_ends[None, :], lengths[0][None, :], 0), axis=1
    )
    levels = jnp.where(padding > 0, depths, 0)
    labels = jnp.stack([own, begins, levels])
    labels = jnp.sum(jnp.where(chosen[None], labels[:, None, :], 0), axis=2)
    labels = jnp.pad(labels, ((0, 5), (0, 0)))
    swap = topo.swap_pairs()
    state = lax.ppermute(mm(onehot, tokens).astype(BF), AXES, swap).astype(F32)
    labels = lax.ppermute(labels, AXES, swap)
    cotangent = mm(onehot, cotangent).astype(BF)

    def collect(arrays, ident):
        if small_layer(topo):
            return gather_layer(topo, arrays, ident)
        return [group_gather(topo, v, xk + yk + ck) for v in arrays]

    def distribute(grads, ident):
        if small_layer(topo):
            return reduce_layer(topo, grads, ident)
        return group_scatter(topo, grads, ck + yk + xk)


    small = weight_qkv[:, model:model + HD].astype(F32)
    gain_one, gain_two = small[:, RECS][None], small[:, RECS + 1][None]

    pack = (lax.axis_index("grp") * topo.X) + lax.axis_index("tok") % topo.X
    begin_all, level_mine = labels[1], labels[2]
    lowest = jnp.min(labels[1])
    span = jnp.stack([lowest // rows, pack + 1]).astype(jnp.int32)
    places = (labels[0] - labels[1]).astype(F32)
    freqs = 10000.0 ** (-(jnp.arange(HD // 2, dtype=F32) * 2.0 / HD))
    angles = places[:, None] * freqs[None, :]
    turns = jnp.stack([jnp.cos(angles), jnp.sin(angles)])
    turns = jnp.tile(turns, (1, 1, LANES * 2 // HD))

    def forward(state, recursion, labels_all=None):
        n = state.shape[0]
        extra = None
        n1, q, kv = project(state, gain_one, weight_qkv, turns[:, :n])
        if recursion == 0:
            kv_all, labels_all = collect([kv, labels], 2)
            kv_all, later = lax.optimization_barrier((kv_all, cotangent))
            extra = (labels_all, lax.ppermute(later, AXES, swap).astype(F32))
        else:
            kv_all, = collect([kv], 3)
        kv_all = kv_all.reshape(topo.T * n, 2 * kv_cols)
        live = labels_all[:, 2, :n] > recursion
        order = labels_all[:, 0, :n]
        key_labels = jnp.stack([jnp.where(live, order, -1), order], axis=-1).reshape(-1, 2)
        key_labels = jnp.pad(key_labels, ((0, 0), (0, 6)))
        query_labels = jnp.stack([labels[1, :n], labels[0, :n]])
        query_labels = jnp.pad(jnp.tile(query_labels, (1, SHARES)), ((0, 6), (0, 0)))
        mixed, out, stat = attend(n, span, key_labels, query_labels, kv_all, q)
        attended = mm(mixed, weight_o)
        middle = state + attended
        inv_two = inverse_rms(middle)
        n2 = (middle * inv_two * gain_two).astype(BF)
        gated, upward = mm(n2, weight_g), mm(n2, weight_u)
        hidden = (jax.nn.silu(gated) * upward).astype(BF)
        both = attended + mm(hidden, weight_d)
        gate = jax.nn.sigmoid(jnp.sum(state * small[:, recursion], axis=-1, keepdims=True))
        active = (labels[2, :n] > recursion).astype(F32)[:, None]
        new = state + active * gate * both
        kept = (state, n1, q, kv_all, key_labels, query_labels, out, stat, mixed, middle,
                inv_two, n2, gated, upward, hidden, both, gate, active)
        return (new, kept, extra)

    def backward(gradient, recursion, kept):
        (state, n1, q, kv_all, key_labels, query_labels, out, stat, mixed, middle,
         inv_two, n2, gated, upward, hidden, both, gate, active) = kept
        n = state.shape[0]
        d_both = active * gate * gradient
        d_fed = d_both.astype(BF)
        d_gate = active * gate * (1.0 - gate) * jnp.sum(gradient * both, axis=-1, keepdims=True)
        d_router = jnp.sum(state * d_gate, axis=0)
        d_hidden = mm_nt(d_fed, weight_d)
        sig = jax.nn.sigmoid(gated)
        d_up = (d_hidden * gated * sig).astype(BF)
        d_gated = (d_hidden * upward * sig * (1.0 + gated * (1.0 - sig))).astype(BF)
        d_middle, d_gain_two = norm_back(
            mm_nt(d_gated, weight_g) + mm_nt(d_up, weight_u), middle, inv_two, gain_two)
        d_att = (d_both + d_middle).astype(BF)
        gradient = gradient + d_gate * small[:, recursion] + d_middle
        dq, dkv = attend_back(
            n, span, key_labels, query_labels, kv_all, q, out_back(d_att, weight_o), out, stat,
            turns[:, :n],
        )
        dkv = distribute(dkv.reshape(topo.T, n, 2 * kv_cols), 5 if recursion else 4)
        gradient, dkv, d_gain_one = project_back(
            gradient, state, gain_one, weight_qkv, turns[:, :n], dq, dkv
        )
        left = (n1, dq, dkv, mixed, d_att, n2, d_gated, d_up, hidden, d_fed)
        return (gradient, left, (d_router, d_gain_one[0], d_gain_two))

    whole_state, kept, (labels_all, gradient) = forward(state, 0)
    deep = whole_state[:deep_rows]
    all_kept = [kept]
    for recursion in range(1, RECS):
        deep, kept, _ = forward(deep, recursion, labels_all)
        all_kept.append(kept)
    final = jnp.concatenate([deep, whole_state[deep_rows:]], axis=0).astype(BF)

    deep_grad = gradient[:deep_rows]
    lefts, smalls = [], []
    for recursion in reversed(range(1, RECS)):
        deep_grad, left, tiny = backward(deep_grad, recursion, all_kept[recursion])
        lefts.append(left)
        smalls.append(tiny)
    gradient = jnp.concatenate([deep_grad, gradient[deep_rows:]], axis=0)
    gradient, left, tiny = backward(gradient, 0, all_kept[0])
    lefts.append(left)
    smalls.append(tiny)
    final, gradient = lax.optimization_barrier((final, gradient.astype(BF)))
    final = lax.ppermute(final, AXES, swap)
    gradient = lax.ppermute(gradient, AXES, swap)

    n1, dq, dkv, mixed, d_att, n2, d_gated, d_up, hidden, d_fed = (
        jnp.concatenate(parts, axis=0) for parts in zip(*lefts)
    )
    dqkv = jnp.concatenate([dq, dkv], axis=1)
    dqkv = jnp.pad(dqkv, ((0, 0), (0, -dqkv.shape[1] % 256)))
    cut = lambda v: v.astype(BF).reshape(topo.T, -1, v.shape[-1])
    tiny = jnp.stack(
        [smalls[2][0], smalls[1][0], smalls[0][0],
         smalls[0][1] + smalls[1][1] + smalls[2][1],
         smalls[0][2] + smalls[1][2] + smalls[2][2]], axis=1
    )
    wide_out = -(-(model + tiny.shape[1]) // 256) * 256
    tiny = jnp.pad(tiny, ((0, 0), (0, wide_out - model - tiny.shape[1])))
    grad_qkv, grad_o, grad_gu, grad_down = reduce_gradients(topo, [
        cut(outer_columns(n1, [dqkv], 256)[0]),
        cut(jnp.concatenate([mm_tn(mixed, d_att), tiny], axis=1)),
        outer_columns(n2, [d_gated, d_up], 512).reshape(2, topo.T, -1, ff),
        outer_rows(hidden, d_fed, 640).reshape(topo.T, -1, model),
    ])
    grad_query = grad_qkv[:, :model].astype(F32)
    pair = grad_qkv[:, model + HD:model + HD + 2 * kv_cols].astype(F32)
    pair = pair.reshape(shard, KV_HEADS, 2, HD)
    grad_key = pair[:, :, 0].reshape(shard, kv_cols)
    grad_value = pair[:, :, 1].reshape(shard, kv_cols)
    grad_out = grad_o[:, :model].astype(F32)
    tiny = grad_o[:, model:].astype(F32)
    grad_gate, grad_up = grad_gu[0].astype(F32), grad_gu[1].astype(F32)
    grad_down = grad_down.astype(F32)

    def unsort(v):
        return mm_tn(onehot, v).astype(BF)

    return (
        unsort(final), unsort(gradient), grad_query, grad_key, grad_value, grad_out,
        grad_gate, grad_up, grad_down, tiny[:, :RECS], tiny[:, RECS],
        tiny[:, RECS + 1],
    )


def solution(mesh):
    topo = Topo(mesh.shape["grp"], mesh.shape["tok"])
    both = P(("grp", "tok"))
    wide = P(("grp", "tok"), None)
    rows = P("tok", None)
    row = P("tok")
    return jax.shard_map(
        functools.partial(per_device, topo),
        mesh=mesh,
        in_specs=(wide,) + (rows,) * 8 + (row, row, P("grp", None), both, both, wide),
        out_specs=(wide, wide) + (rows,) * 8 + (row, row),
        check_vma=False,
    )
```

```python
import functools

import jax
import jax.numpy as jnp
from jax import lax
from jax.experimental import pallas as pl
from jax.experimental.pallas import tpu as pltpu
from jax.sharding import PartitionSpec as P

HEADS = 15
KV_HEADS = 5
SHARES = HEADS // KV_HEADS
HD = 64
RECS = 3
EPS = 1e-05
BF = jnp.bfloat16
F32 = jnp.float32
BIG = -1e30
AXES = ("grp", "tok")


class Topo:
    def __init__(self, groups, spread):
        self.G = groups
        self.T = spread
        self.X = spread // groups
        self.Z = groups
        self.Y = groups // 2
        self.bits = {
            "z": self.Z.bit_length() - 1,
            "x": self.X.bit_length() - 1,
            "y": self.Y.bit_length() - 1,
            "c": 1,
        }

    def keys(self, dim):
        return [(dim, k) for k in range(self.bits[dim])]

    def masks(self, key):
        dim, k = key
        if dim == "c":
            return (1, 0)
        if dim == "y":
            return (2 << k, 0)
        if dim == "x":
            return (0, 1 << k)
        return (0, self.X << k)

    def pairs(self, key):
        mg, mt = self.masks(key)
        return [
            (g * self.T + t, (g ^ mg) * self.T + (t ^ mt))
            for g in range(self.G)
            for t in range(self.T)
        ]

    def swap_pairs(self):
        out = []
        for g in range(self.G):
            for t in range(self.T):
                z, x = t // self.X, t % self.X
                out.append((g * self.T + t, z * self.T + g * self.X + x))
        return out

    def bit(self, key):
        mg, mt = self.masks(key)
        if mg:
            return (lax.axis_index("grp") // mg) % 2
        return (lax.axis_index("tok") // mt) % 2


def exchange(topo, arr, key):
    return lax.ppermute(arr, AXES, topo.pairs(key))


def double(topo, arr, key, axis, stack):
    other = exchange(topo, arr, key)
    mine_is_high = topo.bit(key) == 1
    low = jnp.where(mine_is_high, other, arr)
    high = jnp.where(mine_is_high, arr, other)
    if stack:
        return jnp.stack([low, high], axis=axis)
    return jnp.concatenate([low, high], axis=axis)


def halve(topo, arr, key, axis, stack):
    mine_is_high = topo.bit(key) == 1
    if stack:
        low = lax.index_in_dim(arr, 0, axis, keepdims=False)
        high = lax.index_in_dim(arr, 1, axis, keepdims=False)
    else:
        half = arr.shape[axis] // 2
        low = lax.slice_in_dim(arr, 0, half, axis=axis)
        high = lax.slice_in_dim(arr, half, 2 * half, axis=axis)
    send = jnp.where(mine_is_high, low, high).astype(BF)
    keep = jnp.where(mine_is_high, high, low).astype(F32)
    return (keep + exchange(topo, send, key).astype(F32)).astype(BF)


class Piece:
    def __init__(self, array, dim, start, size, core, part):
        self.array, self.dim, self.start, self.size = array, dim, start, size
        self.core, self.part = core, part

    def of(self, ref):
        if self.dim == 0:
            return ref.at[pl.ds(self.start, self.size), :]
        return ref.at[:, pl.ds(self.start, self.size)]


def cut_pieces(shapes):
    near = lambda v, unit: max(unit, int(round(v / unit)) * unit)
    wide_a, wide_g, wide_u, tall = shapes[0][1], shapes[1][1], shapes[2][1], shapes[3][0]
    g = near(wide_g * 0.7, 128)
    u = near(wide_u * 0.65, 128)
    d = near(tall * 0.3, 8)
    return [
        Piece(1, 1, 0, g, 0, 0),
        Piece(4, 1, 0, shapes[4][1], 0, 2),
        Piece(1, 1, g, wide_g - g, 0, 2),
        Piece(0, 1, 0, wide_a, 0, 1),
        Piece(2, 1, u, wide_u - u, 1, 0),
        Piece(3, 0, 0, d, 1, 0),
        Piece(3, 0, d, tall - d, 1, 2),
        Piece(2, 1, 0, u, 1, 1),
    ]


def coordinates(topo):
    g, t = lax.axis_index("grp"), lax.axis_index("tok")
    return lax.rem(t, topo.X), lax.div(g, 2), lax.div(t, topo.X), lax.rem(g, 2)


def gather_kernel(topo, pieces, *refs):
    shards, outs = refs[:5], refs[5:10]
    local_sem, recv_sem, z_sem, x_sem, y_sem, c_sem = refs[10:]
    x, y, z, c = coordinates(topo)
    X, Z, T = topo.X, topo.Z, topo.T
    g, me = lax.axis_index("grp"), lax.axis_index("tok")
    odd = lax.rem(y, 2)
    over_y = {"grp": g + 2 - 4 * odd, "tok": me}
    over_c = {"grp": g + 1 - 2 * c, "tok": me}

    def over_z(k):
        return {"grp": g, "tok": (z + k) * X + x}

    def over_x(k):
        return {"grp": g, "tok": z * X + lax.rem(x + k, X)}

    barrier = pltpu.get_barrier_semaphore()
    partners = [over_y, over_c] + [over_x(k) for k in range(1, X)]
    for partner in partners:
        pl.semaphore_signal(barrier, inc=1, device_id=partner, device_id_type=pl.DeviceIdType.MESH)
    below, above = z > 0, z < Z - 1

    def greet(k):
        pl.semaphore_signal(
            barrier, inc=1, device_id=over_z(k), device_id_type=pl.DeviceIdType.MESH
        )

    pl.when(below)(lambda: greet(-1))
    pl.when(above)(lambda: greet(1))
    own = [
        pltpu.make_async_copy(shards[i], outs[i].at[me], local_sem.at[i]) for i in range(5)
    ]
    for copy in own:
        copy.start()
    pl.semaphore_wait(barrier, len(partners) + below.astype(jnp.int32) + above.astype(jnp.int32))

    def send(p, t, sem, target, mine=False):
        piece = pieces[p]
        landing = piece.of(outs[piece.array].at[t])
        source = piece.of(shards[piece.array]) if mine else landing
        return pltpu.make_async_remote_copy(
            src_ref=source, dst_ref=landing, send_sem=sem, recv_sem=recv_sem.at[p, t],
            device_id=target, device_id_type=pl.DeviceIdType.MESH,
        )

    def arrived(p, t):
        send(p, t, c_sem.at[0, 0], over_c).wait_recv()

    def run(core):
        mine = [p for p in range(len(pieces)) if pieces[p].core == core]
        theirs = [p for p in range(len(pieces)) if pieces[p].core != core]
        slot = {p: i for i, p in enumerate(mine)}

        def inside(p, body):
            part = pieces[p].part
            if part == 1:
                body()
            else:
                pl.when(odd == part // 2)(body)

        def outside(p, body):
            if pieces[p].part != 1:
                pl.when(odd != pieces[p].part // 2)(body)

        def x_copies(p, zz, first):
            t = zz * X + x
            return [
                send(p, t, x_sem.at[slot[p], zz, k - 1], over_x(k), first) for k in range(1, X)
            ]

        def y_copy(p, t):
            return send(p, t, y_sem.at[slot[p], t], over_y)

        def c_copy(p, t):
            return send(p, t, c_sem.at[slot[p], t], over_c)

        def z_copy(p, zz, k, first):
            return send(p, zz * X + x, z_sem.at[slot[p], zz, (k + 1) // 2], over_z(k), first)

        for p in mine:
            def begin(p=p):
                pl.when(below)(lambda: z_copy(p, z, -1, True).start())
                pl.when(above)(lambda: z_copy(p, z, 1, True).start())
                for copy in x_copies(p, z, True):
                    copy.start()
            inside(p, begin)

        def share(p, t):
            if pieces[p].part != 1:
                y_copy(p, t).start()
            c_copy(p, t).start()

        def relay(p, zz, k):
            arrived(p, zz * X + x)
            pl.when(above if k > 0 else below)(lambda: z_copy(p, zz, k, False).start())
            for copy in x_copies(p, zz, False):
                copy.start()
            share(p, zz * X + x)

        def others(p, zz):
            for j in range(1, X):
                t = zz * X + lax.rem(x + j, X)
                arrived(p, t)
                share(p, t)

        def around(k, carry):
            low, high = z - k, z + k
            for p in mine:
                inside(p, lambda p=p: pl.when(low >= 0)(lambda: relay(p, low, 1)))
                inside(p, lambda p=p: pl.when(high < Z)(lambda: relay(p, high, -1)))
            low, high = z - k + 1, z + k - 1
            for p in mine:
                inside(p, lambda p=p: pl.when(low >= 0)(lambda: others(p, low)))
                inside(p, lambda p=p: pl.when((k > 1) & (high < Z))(lambda: others(p, high)))
            return carry

        lax.fori_loop(1, Z + 1, around, 0)

        def rest(t, carry):
            @pl.when(t != me)
            def _():
                for p in mine:
                    def forward(p=p):
                        arrived(p, t)
                        c_copy(p, t).start()
                    outside(p, forward)
            return carry

        lax.fori_loop(0, T, rest, 0)

        def finish(t, carry):
            @pl.when(t != me)
            def _():
                for p in theirs:
                    arrived(p, t)
                for p in mine:
                    c_copy(p, t).wait_send()
                    if pieces[p].part != 1:
                        inside(p, lambda p=p: y_copy(p, t).wait_send())
            return carry

        lax.fori_loop(0, T, finish, 0)
        for p in mine:
            def end(p=p):
                def each(zz, carry):
                    pl.when((zz <= z) & above)(lambda: z_copy(p, zz, 1, False).wait_send())
                    pl.when((zz >= z) & below)(lambda: z_copy(p, zz, -1, False).wait_send())
                    for copy in x_copies(p, zz, False):
                        copy.wait_send()
                    return carry
                lax.fori_loop(0, Z, each, 0)
            inside(p, end)

    pl.when(c == 0)(lambda: run(0))
    pl.when(c == 1)(lambda: run(1))
    for copy in own:
        copy.wait()


def gather_weights(topo, shards):
    pieces = cut_pieces([s.shape for s in shards])
    T = topo.T
    DMA = pltpu.SemaphoreType.DMA
    hbm = pl.BlockSpec(memory_space=pl.ANY)
    outs = pl.pallas_call(
        functools.partial(gather_kernel, topo, pieces),
        in_specs=[hbm] * 5,
        out_specs=[hbm] * 5,
        out_shape=[jax.ShapeDtypeStruct((T,) + s.shape, s.dtype) for s in shards],
        scratch_shapes=[
            DMA((5,)), DMA((len(pieces), T)), DMA((4, topo.Z, 2)), DMA((4, topo.Z, topo.X - 1)),
            DMA((4, T)), DMA((4, T)),
        ],
        compiler_params=pltpu.CompilerParams(collective_id=0, has_side_effects=True),
        name="gather_weights",
    )(*shards)
    return [o.reshape(-1, o.shape[-1]) for o in outs]


class Share:
    def __init__(self, array, start, shape, part):
        self.array, self.start, self.shape, self.part = array, start, shape, part

    def of(self, ref, core, *lead):
        rows, columns = self.shape
        if self.array == 2:
            return ref.at[lead + (slice(None), pl.ds(self.start, columns))]
        if self.array == 3:
            at = pl.multiple_of(core * rows, rows)
            return ref.at[lead + (pl.ds(at, rows), slice(None))]
        at = pl.multiple_of(core * columns, 128)
        return ref.at[lead + (slice(None), pl.ds(at, columns))]


def cut_shares(shapes):
    rows, ff = shapes[2][1], shapes[2][2]
    one = ff * 3 // 20 // 128 * 128
    two = ff * 33 // 40 // 128 * 128
    return [
        Share(2, one, (rows, two - one), 0),
        Share(3, 0, (shapes[3][1] // 2, shapes[3][2]), 2),
        Share(2, two, (rows, ff - two), 2),
        Share(0, 0, (rows, shapes[0][2] // 2), 1),
        Share(1, 0, (rows, shapes[1][2] // 2), 1),
        Share(2, 0, (rows, one), 1),
    ]


def reduce_kernel(topo, shares, *refs):
    grads, outs = refs[:5], refs[5:9]
    count = len(shares)
    groups = []
    at = 9
    for _ in range(7):
        groups.append(refs[at:at + count])
        at += count
    held, from_c, from_y, from_x, from_low, from_high, from_f = groups
    (load_sem, c_send, c_recv, y_send, y_recv, x_send, x_recv, z_send, z_recv, f_send, f_recv,
     o_send, o_recv, o_local) = refs[at:]
    x, y, z, c = coordinates(topo)
    X, Z, T = topo.X, topo.Z, topo.T
    g, me = lax.axis_index("grp"), lax.axis_index("tok")
    odd = lax.rem(y, 2)
    below, above = z > 0, z < Z - 1
    kind = pl.DeviceIdType.MESH

    def over_y(k):
        high = lax.rem(lax.div(y, 1 << k), 2)
        return {"grp": g + (2 - 4 * high) * (1 << k), "tok": me}

    over_c = {"grp": g + 1 - 2 * c, "tok": me}

    def over_z(k):
        return {"grp": g, "tok": (z + k) * X + x}

    def over_x(k):
        return {"grp": g, "tok": z * X + lax.rem(x + k, X)}

    barrier = pltpu.get_barrier_semaphore()
    partners = [over_c] + [over_y(k) for k in range(topo.bits["y"])]
    partners += [over_x(k) for k in range(1, X)]

    def greet(partner):
        pl.semaphore_signal(barrier, inc=1, device_id=partner, device_id_type=kind)

    for partner in partners:
        greet(partner)
    pl.when(below)(lambda: greet(over_z(-1)))
    pl.when(above)(lambda: greet(over_z(1)))
    every = range(count)

    def source(s, core, t, up):
        place = {2: 4 if up else 2, 3: 3}.get(s.array, s.array)
        return s.of(grads[place], core, t)

    def load(p, t, up=False):
        return pltpu.make_async_copy(
            source(shares[p], c, t, up), held[p].at[t], load_sem.at[p, t]
        )

    def start(p, make, up_core):
        if shares[p].array == 2:
            pl.when(c != up_core)(lambda: make(False).start())
            pl.when(c == up_core)(lambda: make(True).start())
        else:
            make(False).start()

    def remote(source, landing, send, recv, target):
        return pltpu.make_async_remote_copy(
            src_ref=source, dst_ref=landing, send_sem=send, recv_sem=recv, device_id=target,
            device_id_type=kind,
        )

    def c_copy(p, t, up=False):
        return remote(
            source(shares[p], 1 - c, t, up), from_c[p].at[t], c_send.at[p, t], c_recv.at[p, t],
            over_c,
        )

    def y_copy(p, t):
        return remote(
            held[p].at[t], from_y[p].at[t], y_send.at[p, t], y_recv.at[p, t], over_y(0)
        )

    def x_copy(p, zz, k):
        t = zz * X + lax.rem(x + k, X)
        return remote(
            held[p].at[t], from_x[p].at[zz, k - 1], x_send.at[p, zz, k - 1],
            x_recv.at[p, zz, k - 1], over_x(k),
        )

    def z_copy(p, zz, k):
        landing = from_low if k > 0 else from_high
        way = (k + 1) // 2
        return remote(
            held[p].at[zz * X + x], landing[p].at[zz], z_send.at[p, zz, way],
            z_recv.at[p, zz, way], over_z(k),
        )

    def f_copy(p, k):
        return remote(
            held[p].at[me], from_f[p].at[k], f_send.at[p, k], f_recv.at[p, k], over_y(k)
        )

    def result(s, core):
        if s.array == 2:
            return outs[2].at[core, :, pl.ds(s.start, s.shape[1])]
        return s.of(outs[s.array], core)

    def o_copy(p):
        s = shares[p]
        return remote(
            held[p].at[me], result(s, c), o_send.at[p], o_recv.at[p], over_c
        )

    def o_arrived(p):
        s = shares[p]
        return remote(
            held[p].at[me], result(s, 1 - c), o_send.at[p], o_recv.at[p], over_c
        )

    def o_keep(p):
        s = shares[p]
        return pltpu.make_async_copy(held[p].at[me], result(s, c), o_local.at[p])

    def add(p, t, other):
        held[p][t] = held[p][t] + other

    def layers(body):
        def step(i, carry):
            k = Z - 1 - i
            pl.when(z + k < Z)(lambda: body(z + k))
            pl.when((k > 0) & (z - k >= 0))(lambda: body(z - k))
            return carry
        return step

    def inside(p, body):
        if shares[p].part == 1:
            body()
        else:
            pl.when(odd == shares[p].part // 2)(body)

    def outside(p, body):
        if shares[p].part != 1:
            pl.when(odd != shares[p].part // 2)(body)

    def start_loads(zz):
        def each(j, carry):
            t = zz * X + lax.rem(x + j, X)
            for p in every:
                start(p, lambda up, p=p: load(p, t, up), 1)
            return carry
        lax.fori_loop(0, X, each, 0)

    lax.fori_loop(0, Z, layers(start_loads), 0)
    pl.semaphore_wait(barrier, len(partners) + below.astype(jnp.int32) + above.astype(jnp.int32))

    def start_cores(zz):
        def each(j, carry):
            t = zz * X + lax.rem(x + j, X)
            for p in every:
                start(p, lambda up, p=p: c_copy(p, t, up), 0)
            return carry
        lax.fori_loop(0, X, each, 0)

    lax.fori_loop(0, Z, layers(start_cores), 0)

    def cores(zz):
        def each(j, carry):
            t = zz * X + lax.rem(x + j + 1, X)
            for p in every:
                load(p, t).wait()
                c_copy(p, t).wait_recv()
                add(p, t, from_c[p][t])
                outside(p, lambda p=p: y_copy(p, t).start())
                if shares[p].part == 1:
                    for k in range(1, X):
                        pl.when(j + 1 == k)(lambda p=p, k=k: x_copy(p, zz, k).start())
            return carry
        lax.fori_loop(0, X, each, 0)

    lax.fori_loop(0, Z, layers(cores), 0)

    def over(zz):
        def each(j, carry):
            t = zz * X + lax.rem(x + j + 1, X)
            for p in every:
                if shares[p].part != 1:
                    def body(p=p):
                        y_copy(p, t).wait_recv()
                        add(p, t, from_y[p][t])
                        for k in range(1, X):
                            pl.when(j + 1 == k)(lambda: x_copy(p, zz, k).start())
                    inside(p, body)
            return carry
        lax.fori_loop(0, X, each, 0)

    def join(p, zz):
        t = zz * X + x
        for k in range(1, X):
            x_copy(p, zz, k).wait_recv()
            add(p, t, from_x[p][zz, k - 1])

        def low():
            z_copy(p, zz, 1).wait_recv()
            add(p, t, from_low[p][zz])

        def high():
            z_copy(p, zz, -1).wait_recv()
            add(p, t, from_high[p][zz])

        pl.when((zz >= z) & below)(low)
        pl.when((zz <= z) & above)(high)
        pl.when(zz > z)(lambda: z_copy(p, zz, 1).start())
        pl.when(zz < z)(lambda: z_copy(p, zz, -1).start())

    single = topo.bits["y"] == 1

    def first_joins(zz):
        for p in every:
            if shares[p].part == 1:
                join(p, zz)
                if single:
                    pl.when(zz == z)(lambda p=p: f_copy(p, 0).start())

    def last_joins(zz):
        for p in every:
            if shares[p].part != 1:
                def body(p=p):
                    join(p, zz)
                    if single:
                        pl.when(zz == z)(lambda: f_copy(p, 0).start())
                inside(p, body)

    def main(i, carry):
        @pl.when(i < Z)
        def _():
            layers(first_joins)(i, 0)
            layers(over)(i, 0)

        @pl.when(i > 0)
        def _():
            layers(last_joins)(i - 1, 0)

        return carry

    lax.fori_loop(0, Z + 1, main, 0)

    for k in range(1, topo.bits["y"]):
        for p in every:
            inside(p, lambda p=p: f_copy(p, k).start())
        for p in every:
            def fold(p=p):
                f_copy(p, k).wait()
                add(p, me, from_f[p][k])
            inside(p, fold)
    if not single:
        for p in every:
            inside(p, lambda p=p: f_copy(p, 0).start())
    for p in every:
        if shares[p].part == 1:
            f_copy(p, 0).wait()
            add(p, me, from_f[p][0])
        else:
            def take(p=p):
                f_copy(p, 0).wait_recv()
                held[p][me] = from_f[p][0]
            outside(p, lambda p=p: y_copy(p, me).wait_send())
            outside(p, take)
        o_copy(p).start()
        o_keep(p).start()

    def ends(t, carry):
        for p in every:
            c_copy(p, t).wait_send()
            outside(p, lambda p=p: pl.when(t != me)(lambda: y_copy(p, t).wait_send()))
        return carry

    lax.fori_loop(0, T, ends, 0)

    def z_ends(zz, carry):
        for p in every:
            def body(p=p):
                for k in range(1, X):
                    x_copy(p, zz, k).wait_send()
                pl.when(zz > z)(lambda: z_copy(p, zz, 1).wait_send())
                pl.when(zz < z)(lambda: z_copy(p, zz, -1).wait_send())
            inside(p, body)
        return carry

    lax.fori_loop(0, Z, z_ends, 0)
    for p in every:
        if shares[p].part != 1:
            inside(p, lambda p=p: f_copy(p, 0).wait_send())
        o_copy(p).wait_send()
        o_arrived(p).wait_recv()
        o_keep(p).wait()


def reduce_gradients(topo, grads):
    shares = cut_shares([v.shape for v in grads])
    X, Z, T = topo.X, topo.Z, topo.T
    n = len(shares)
    folds = max(1, topo.bits["y"])
    DMA = pltpu.SemaphoreType.DMA
    hbm = pl.BlockSpec(memory_space=pl.ANY)
    lead = [(T,), (T,), (T,), (Z, X - 1), (Z,), (Z,), (folds,)]
    rooms = [
        pltpu.VMEM(front + s.shape, BF)
        for front in lead for s in shares
    ]
    outs = [grads[0].shape[1:], grads[1].shape[1:], (2,) + grads[2].shape[1:], grads[3].shape[1:]]
    return pl.pallas_call(
        functools.partial(reduce_kernel, topo, shares),
        in_specs=[hbm] * 5,
        out_specs=[hbm] * 4,
        out_shape=[jax.ShapeDtypeStruct(s, BF) for s in outs],
        scratch_shapes=rooms + [
            DMA((n, T)), DMA((n, T)), DMA((n, T)), DMA((n, T)), DMA((n, T)),
            DMA((n, Z, X - 1)), DMA((n, Z, X - 1)), DMA((n, Z, 2)), DMA((n, Z, 2)),
            DMA((n, folds)), DMA((n, folds)), DMA((n,)), DMA((n,)), DMA((n,)),
        ],
        compiler_params=pltpu.CompilerParams(
            collective_id=1, has_side_effects=True, vmem_limit_bytes=60 << 20
        ),
        name="reduce_gradients",
    )(*grads)


def group_order(topo):
    return list(reversed(topo.keys("y"))) + topo.keys("c") + list(reversed(topo.keys("x")))


def group_gather(topo, arr, order):
    names = group_order(topo)
    held = []
    shape = arr.shape
    for key in order:
        place = sum(1 for h in held if names.index(h) < names.index(key))
        arr = double(topo, arr, key, place, True)
        held.append(key)
    return arr.reshape((topo.T,) + shape)


def group_scatter(topo, arr, order):
    names = group_order(topo)
    held = list(names)
    arr = arr.reshape((2,) * len(names) + arr.shape[1:])
    for key in order:
        arr = halve(topo, arr, key, held.index(key), True)
        held.remove(key)
    return arr


def small_layer(topo):
    return topo.X == 2 and topo.Y == 2


class Layer:
    def __init__(self, topo):
        self.topo = topo
        x, y, z, c = coordinates(topo)
        self.c = c
        far_x, far_y = 1 - x, 1 - y
        a = (x + c * (far_x - x), far_y + c * (y - far_y))
        b = (far_x + c * (x - far_x), y + c * (far_y - y))
        self.chips = [(x, y), a, b, (far_x, far_y)]
        self.z = z

    def pack(self, slot, core):
        x, y = self.chips[slot]
        return (y * 2 + core) * self.topo.X + x

    def device(self, slot, core):
        x, y = self.chips[slot]
        return {"grp": y * 2 + core, "tok": self.z * self.topo.X + x}

    def meet(self):
        barrier = pltpu.get_barrier_semaphore()
        for target in (self.device(1, self.c), self.device(2, self.c), self.device(0, 1 - self.c)):
            pl.semaphore_signal(
                barrier, inc=1, device_id=target, device_id_type=pl.DeviceIdType.MESH
            )
        pl.semaphore_wait(barrier, 3)


def remote_copy(source, landing, send, recv, target):
    return pltpu.make_async_remote_copy(
        src_ref=source, dst_ref=landing, send_sem=send, recv_sem=recv, device_id=target,
        device_id_type=pl.DeviceIdType.MESH,
    )


def group_gather_kernel(topo, count, *refs):
    mine, outs = refs[:count], refs[count:2 * count]
    local_sem, send_sem, recv_sem = refs[2 * count:]
    layer = Layer(topo)
    c = layer.c
    arrays = range(count)
    a, b, sibling = layer.device(1, c), layer.device(2, c), layer.device(0, 1 - c)
    own = layer.pack(0, c)

    def send(i, way, pack, target):
        landing = outs[i].at[pack]
        source = mine[i] if way in (0, 1, 3) else landing
        return remote_copy(source, landing, send_sem.at[i, way], recv_sem.at[i, pack], target)

    ways = [
        (0, own, a), (1, own, b), (2, layer.pack(1, c), b), (3, own, sibling),
        (4, layer.pack(1, c), sibling), (5, layer.pack(2, c), sibling),
        (6, layer.pack(3, c), sibling),
    ]

    def start(k):
        for i in arrays:
            send(i, *ways[k]).start()

    def arrived(pack):
        for i in arrays:
            send(i, 2, pack, sibling).wait_recv()

    keep = [pltpu.make_async_copy(mine[i], outs[i].at[own], local_sem.at[i]) for i in arrays]
    for copy in keep:
        copy.start()
    layer.meet()
    start(0)
    start(1)
    start(3)
    arrived(layer.pack(1, c))
    start(2)
    start(4)
    arrived(layer.pack(2, c))
    start(5)
    arrived(layer.pack(3, c))
    start(6)
    for slot in range(4):
        arrived(layer.pack(slot, 1 - c))
    for way in ways:
        for i in arrays:
            send(i, *way).wait_send()
    for copy in keep:
        copy.wait()


def gather_layer(topo, arrays, ident):
    DMA = pltpu.SemaphoreType.DMA
    hbm = pl.BlockSpec(memory_space=pl.ANY)
    n = len(arrays)
    return pl.pallas_call(
        functools.partial(group_gather_kernel, topo, n),
        in_specs=[hbm] * n,
        out_specs=[hbm] * n,
        out_shape=[jax.ShapeDtypeStruct((topo.T,) + v.shape, v.dtype) for v in arrays],
        scratch_shapes=[DMA((n,)), DMA((n, 7)), DMA((n, topo.T))],
        compiler_params=pltpu.CompilerParams(collective_id=ident, has_side_effects=True),
        name="gather_layer",
    )(*arrays)


def group_reduce_kernel(topo, grads, out, held, from_c, from_b, from_a, load_sem, c_send, c_recv,
                        send_sem, recv_sem):
    layer = Layer(topo)
    c = layer.c
    a, b, sibling = layer.device(1, c), layer.device(2, c), layer.device(0, 1 - c)
    order = (3, 2, 1, 0)

    def load(slot):
        return pltpu.make_async_copy(
            grads.at[layer.pack(slot, c)], held.at[slot], load_sem.at[slot]
        )

    def c_copy(slot):
        theirs = (0, 2, 1, 3)[slot]
        return remote_copy(
            grads.at[layer.pack(slot, 1 - c)], from_c.at[theirs], c_send.at[theirs],
            c_recv.at[theirs], sibling,
        )

    def c_arrived(slot):
        remote_copy(
            grads.at[layer.pack(slot, c)], from_c.at[slot], c_send.at[slot], c_recv.at[slot],
            sibling,
        ).wait_recv()

    across = remote_copy(held.at[3], from_b.at[1], send_sem.at[0], recv_sem.at[0], b)
    direct = remote_copy(held.at[2], from_b.at[0], send_sem.at[1], recv_sem.at[1], b)
    passed = remote_copy(held.at[1], from_a, send_sem.at[2], recv_sem.at[2], a)

    for slot in order:
        load(slot).start()
    layer.meet()
    for slot in (3, 1, 2, 0):
        c_copy(slot).start()
    for slot in order:
        load(slot).wait()
        c_arrived(slot)
        held[slot] = held[slot] + from_c[slot]
        if slot == 3:
            across.start()
        if slot == 2:
            direct.start()
    across.wait_recv()
    held[1] = held[1] + from_b[1]
    passed.start()
    direct.wait_recv()
    held[0] = held[0] + from_b[0]
    passed.wait_recv()
    out[...] = held[0] + from_a[...]
    across.wait_send()
    direct.wait_send()
    passed.wait_send()
    for slot in range(4):
        c_copy(slot).wait_send()


def reduce_layer(topo, grads, ident):
    DMA = pltpu.SemaphoreType.DMA
    block = grads.shape[1:]
    return pl.pallas_call(
        functools.partial(group_reduce_kernel, topo),
        in_specs=[pl.BlockSpec(memory_space=pl.ANY)],
        out_specs=pl.BlockSpec(memory_space=pltpu.VMEM),
        out_shape=jax.ShapeDtypeStruct(block, BF),
        scratch_shapes=[
            pltpu.VMEM((4,) + block, BF), pltpu.VMEM((4,) + block, BF),
            pltpu.VMEM((2,) + block, BF), pltpu.VMEM(block, BF),
            DMA((4,)), DMA((4,)), DMA((4,)), DMA((3,)), DMA((3,)),
        ],
        compiler_params=pltpu.CompilerParams(
            collective_id=ident, has_side_effects=True, vmem_limit_bytes=32 << 20
        ),
        name="reduce_layer",
    )(grads)


NT = (((1,), (1,)), ((), ()))
TN = (((0,), (0,)), ((), ()))
LANES = 2 * HD
CHUNKS = (HEADS + 1) // 2
ROOM = 60 << 20


def lanes_of(rows):
    return lax.broadcasted_iota(jnp.int32, (rows, LANES), 1)


def spin(v):
    first = lax.rem(lanes_of(v.shape[0]), HD) < HD // 2
    return jnp.where(first, -pltpu.roll(v, LANES - HD // 2, 1), pltpu.roll(v, HD // 2, 1))


def whole(*shape):
    return pl.BlockSpec(shape, lambda *i: (0,) * len(shape))


def normed(v, gain):
    return v * lax.rsqrt(jnp.mean(v * v, axis=-1, keepdims=True) + EPS) * gain


def project_kernel(state_ref, gain_ref, w_ref, turn_ref, n1_ref, q_ref, kv_ref):
    project_into(state_ref[...], gain_ref[...], w_ref, turn_ref, n1_ref, q_ref, kv_ref)


def project(state, gain, w, turns):
    n, model = state.shape
    return pl.pallas_call(
        project_kernel,
        grid=(1,),
        in_specs=[whole(n, model), whole(1, model), whole(*w.shape), whole(*turns.shape)],
        out_specs=[whole(n, model), whole(CHUNKS, n, LANES), whole(n, KV_HEADS * LANES)],
        out_shape=[
            jax.ShapeDtypeStruct((n, model), BF),
            jax.ShapeDtypeStruct((CHUNKS, n, LANES), BF),
            jax.ShapeDtypeStruct((n, KV_HEADS * LANES), BF),
        ],
        compiler_params=pltpu.CompilerParams(vmem_limit_bytes=ROOM),
        name="project",
    )(state, gain, w, turns)


def attend_kernel(rows, span, key_ref, query_ref, kv_ref, q_ref, mixed_ref, out_ref, stat_ref,
                  stacked, mixing, tops, sums):
    low = lanes_of(rows) < HD
    wide = SHARES * rows
    for h in range(KV_HEADS):
        for j in range(SHARES):
            head = h * SHARES + j
            chunk = q_ref[head // 2].astype(F32)
            if head % 2:
                chunk = pltpu.roll(chunk, HD, 1)
            stacked[h, j * rows:(j + 1) * rows, :] = jnp.where(low, chunk, 0.0).astype(BF)
    mixing[...] = jnp.zeros(mixing.shape, F32)
    sums[...] = jnp.zeros(sums.shape, F32)
    tops[...] = jnp.full(tops.shape, BIG, F32)

    def body(t, carry):
        at = pl.ds(pl.multiple_of(t * rows, rows), rows)
        bias = block_bias(key_ref[at, :], query_ref)
        def score(h):
            kv = kv_ref[at, h * LANES:(h + 1) * LANES]
            return lax.dot_general(kv, stacked[h], NT, preferred_element_type=F32) + bias

        def end(h, p, fade):
            kv = kv_ref[at, h * LANES:(h + 1) * LANES]
            mixing[h] = mixing[h] * fade + lax.dot_general(
                kv[:, HD:], p, TN, preferred_element_type=F32
            )

        ahead = score(0)
        before = None
        for h in range(KV_HEADS):
            s = ahead
            if h + 1 < KV_HEADS:
                ahead = score(h + 1)
            if before is not None:
                end(*before)
            old = tops[h, 0:1, :]
            top = jnp.max(s.reshape(rows // 8, 8, wide), axis=0)
            top = jnp.maximum(old, jnp.max(top, axis=0, keepdims=True))
            p = jnp.exp(s - top)
            fade = jnp.exp(old - top)
            sums[h] = sums[h] * fade + jnp.sum(p.reshape(rows // 8, 8, wide), axis=0)
            tops[h] = jnp.broadcast_to(top, (8, wide))
            before = (h, p.astype(BF), fade)
        end(*before)
        return carry

    lax.fori_loop(span[0], span[1], body, 0)
    for h in range(KV_HEADS):
        total = jnp.sum(sums[h], axis=0, keepdims=True)
        stat_ref[h] = tops[h] + jnp.log(total)
        mixing[h] = mixing[h] / total
    for j in range(CHUNKS):
        both = head_pair(mixing, j, rows)
        out_ref[j] = both
        size = min(LANES, HEADS * HD - j * LANES)
        mixed_ref[:, j * LANES:j * LANES + size] = both.astype(BF)[:, :size]


def block_bias(keys, query_ref):
    live, order = keys[:, 0:1], keys[:, 1:2]
    begin, place = query_ref[0:1, :], query_ref[1:2, :]
    allowed = ((live >= begin) & (live <= place)) | (order == place)
    return jnp.where(allowed, 0.0, BIG)


def head_pair(mixing, j, rows):
    def one(head):
        if head >= HEADS:
            return jnp.zeros((HD, rows), F32)
        at = head % SHARES * rows
        return mixing[head // SHARES, :, at:at + rows]

    return jnp.transpose(jnp.concatenate([one(2 * j), one(2 * j + 1)], axis=0))


def attend(rows, span, key_labels, query_labels, kv_all, q):
    count, columns = kv_all.shape
    wide = SHARES * rows
    return pl.pallas_call(
        functools.partial(attend_kernel, rows),
        grid_spec=pltpu.PrefetchScalarGridSpec(
            num_scalar_prefetch=1,
            grid=(1,),
            in_specs=[
                whole(count, 8), whole(8, wide), whole(count, columns),
                whole(CHUNKS, rows, LANES),
            ],
            out_specs=[
                whole(rows, HEADS * HD), whole(CHUNKS, rows, LANES), whole(KV_HEADS, 8, wide),
            ],
            scratch_shapes=[
                pltpu.VMEM((KV_HEADS, wide, LANES), BF), pltpu.VMEM((KV_HEADS, HD, wide), F32),
                pltpu.VMEM((KV_HEADS, 8, wide), F32), pltpu.VMEM((KV_HEADS, 8, wide), F32),
            ],
        ),
        out_shape=[
            jax.ShapeDtypeStruct((rows, HEADS * HD), BF),
            jax.ShapeDtypeStruct((CHUNKS, rows, LANES), F32),
            jax.ShapeDtypeStruct((KV_HEADS, 8, wide), F32),
        ],
        compiler_params=pltpu.CompilerParams(vmem_limit_bytes=62 << 20),
        cost_estimate=pl.CostEstimate(
            flops=16 * KV_HEADS * wide * count * HD, bytes_accessed=4 * count * columns,
            transcendentals=KV_HEADS * wide * count,
        ),
        name="attend",
    )(span, key_labels, query_labels, kv_all, q)


def attend_back_kernel(rows, span, key_ref, query_ref, kv_ref, q_ref, d_ref, out_ref, stat_ref,
                       turn_ref, dq_ref, dkv_ref, stacked, part, mixing, deltas):
    low = lanes_of(rows) < HD
    wide = SHARES * rows
    ones = jnp.ones((8, LANES), BF)
    for h in range(KV_HEADS):
        for j in range(SHARES):
            head = h * SHARES + j
            q = q_ref[head // 2].astype(F32)
            d = d_ref[head // 2].astype(F32)
            if head % 2:
                q = pltpu.roll(q, HD, 1)
            product = d * out_ref[head // 2]
            mine = ~low if head % 2 else low
            if head % 2 == 0:
                d = pltpu.roll(d, HD, 1)
            at = pl.ds(j * rows, rows)
            stacked[h, at, :] = jnp.where(low, q, d).astype(BF)
            part[at, :] = jnp.where(mine, product, 0.0)
        coarse = part[...].astype(BF)
        fine = (part[...] - coarse.astype(F32)).astype(BF)
        deltas[h] = lax.dot_general(
            ones, coarse, NT, preferred_element_type=F32
        ) + lax.dot_general(ones, fine, NT, preferred_element_type=F32)
    dkv_ref[...] = jnp.zeros(dkv_ref.shape, BF)
    mixing[...] = jnp.zeros(mixing.shape, F32)

    def body(t, carry):
        at = pl.ds(pl.multiple_of(t * rows, rows), rows)
        bias = block_bias(key_ref[at, :], query_ref)
        for h in range(KV_HEADS):
            kv = kv_ref[at, h * LANES:(h + 1) * LANES]
            zero = jnp.zeros_like(kv)
            queries = stacked[h]
            s = lax.dot_general(jnp.where(low, kv, zero), queries, NT, preferred_element_type=F32)
            p = jnp.exp(s + bias - stat_ref[h, 0:1, :])
            dp = lax.dot_general(jnp.where(low, zero, kv), queries, NT, preferred_element_type=F32)
            ds = (p * (dp - deltas[h, 0:1, :])).astype(BF)
            dk = jnp.dot(ds, queries, preferred_element_type=F32)
            dv = jnp.dot(p.astype(BF), queries, preferred_element_type=F32)
            dkv_ref[at, h * LANES:(h + 1) * LANES] = jnp.where(low, dk, dv).astype(BF)
            mixing[h] += lax.dot_general(kv[:, :HD], ds, TN, preferred_element_type=F32)
        return carry

    lax.fori_loop(span[0], span[1], body, 0)
    cosine, sine = turn_ref[0], turn_ref[1]
    for j in range(CHUNKS):
        both = head_pair(mixing, j, rows) * HD ** -0.5
        both = both * cosine - spin(both) * sine
        dq_ref[:, j * LANES:(j + 1) * LANES] = both.astype(BF)


def attend_back(rows, span, key_labels, query_labels, kv_all, q, d_mixed, out, stat, turns):
    count, columns = kv_all.shape
    wide = SHARES * rows
    return pl.pallas_call(
        functools.partial(attend_back_kernel, rows),
        grid_spec=pltpu.PrefetchScalarGridSpec(
            num_scalar_prefetch=1,
            grid=(1,),
            in_specs=[
                whole(count, 8), whole(8, wide), whole(count, columns),
                whole(CHUNKS, rows, LANES), whole(CHUNKS, rows, LANES),
                whole(CHUNKS, rows, LANES), whole(KV_HEADS, 8, wide), whole(*turns.shape),
            ],
            out_specs=[whole(rows, CHUNKS * LANES), whole(count, columns)],
            scratch_shapes=[
                pltpu.VMEM((KV_HEADS, wide, LANES), BF), pltpu.VMEM((wide, LANES), F32),
                pltpu.VMEM((KV_HEADS, HD, wide), F32), pltpu.VMEM((KV_HEADS, 8, wide), F32),
            ],
        ),
        out_shape=[
            jax.ShapeDtypeStruct((rows, CHUNKS * LANES), BF),
            jax.ShapeDtypeStruct((count, columns), BF),
        ],
        compiler_params=pltpu.CompilerParams(vmem_limit_bytes=62 << 20),
        name="attend_back",
    )(span, key_labels, query_labels, kv_all, q, d_mixed, out, stat, turns)


def out_back_kernel(d_ref, w_ref, out_ref):
    d = d_ref[...]
    for j in range(CHUNKS):
        size = min(LANES, w_ref.shape[0] - j * LANES)
        v = lax.dot_general(
            d, w_ref[j * LANES:j * LANES + size, :], NT, preferred_element_type=F32
        ).astype(BF)
        if size < LANES:
            v = jnp.concatenate([v, jnp.zeros((d.shape[0], LANES - size), BF)], axis=1)
        out_ref[j] = v


def project_back_kernel(gradient_ref, state_ref, gain_ref, w_ref, turn_ref, dq_ref, raw_ref,
                        grad_ref, joint_ref, dgain_ref):
    cosine, sine = turn_ref[0], turn_ref[1]
    key = lanes_of(dq_ref.shape[0]) < HD
    for j in range(KV_HEADS):
        v = raw_ref[:, j * LANES:(j + 1) * LANES].astype(F32)
        turned = v * cosine - spin(v) * sine
        at = (CHUNKS + j) * LANES
        joint_ref[:, at:at + LANES] = jnp.where(key, turned, v).astype(BF)
    split, full = CHUNKS * LANES, w_ref.shape[1]
    joint_ref[:, :split] = dq_ref[...]
    if joint_ref.shape[1] > full:
        joint_ref[:, full:] = jnp.zeros((key.shape[0], joint_ref.shape[1] - full), BF)
    d = lax.dot_general(joint_ref[:, :full], w_ref[...], NT, preferred_element_type=F32)
    v = state_ref[...]
    inv = lax.rsqrt(jnp.mean(v * v, axis=-1, keepdims=True) + EPS)
    scaled = d * gain_ref[...]
    dot = jnp.mean(scaled * v, axis=-1, keepdims=True)
    grad_ref[...] = gradient_ref[...] + inv * scaled - v * (inv * inv * inv * dot)
    dgain_ref[...] = jnp.sum(d * v * inv, axis=0, keepdims=True)


def project_back(gradient, state, gain, w, turns, dq, dkv):
    n, model = state.shape
    joint = -(-w.shape[1] // 256) * 256
    return pl.pallas_call(
        project_back_kernel,
        grid=(1,),
        in_specs=[
            whole(n, model), whole(n, model), whole(1, model), whole(*w.shape),
            whole(*turns.shape), whole(*dq.shape), whole(*dkv.shape),
        ],
        out_specs=[whole(n, model), whole(n, joint), whole(1, model)],
        out_shape=[
            jax.ShapeDtypeStruct((n, model), F32),
            jax.ShapeDtypeStruct((n, joint), BF),
            jax.ShapeDtypeStruct((1, model), F32),
        ],
        compiler_params=pltpu.CompilerParams(vmem_limit_bytes=ROOM),
        name="project_back",
    )(gradient, state, gain, w, turns, dq, dkv)


def project_into(state, gain, w_ref, turn_ref, n1_ref, q_ref, kv_ref):
    n1 = normed(state, gain).astype(BF)
    n1_ref[...] = n1
    rows = n1.shape[0]
    cosine, sine = turn_ref[0, :rows], turn_ref[1, :rows]
    key = lanes_of(rows) < HD
    columns = w_ref.shape[1]
    for start in range(0, columns, 2 * LANES):
        wide = min(2 * LANES, columns - start)
        both = jnp.dot(n1, w_ref[:, start:start + wide], preferred_element_type=F32)
        for half in range(wide // LANES):
            j = start // LANES + half
            v = both[:, half * LANES:(half + 1) * LANES]
            turned = v * cosine + spin(v) * sine
            if j < CHUNKS:
                q_ref[j] = (turned * HD ** -0.5).astype(BF)
            else:
                j -= CHUNKS
                kv_ref[:, j * LANES:(j + 1) * LANES] = jnp.where(key, turned, v).astype(BF)


def feed_kernel(following, mixed_ref, state_ref, w_out_ref, gain_ref, router_ref, active_ref,
                w_gate_ref, w_up_ref, w_down_ref, *refs):
    if following:
        next_gain_ref, w_ref, turn_ref = refs[:3]
        refs = refs[3:]
    (new_ref, middle_ref, n2_ref, gated_ref, up_ref, hidden_ref, both_ref, gate_ref) = refs[:8]
    step = pl.program_id(0)

    @pl.when(step == 0)
    def _():
        att = jnp.dot(mixed_ref[...], w_out_ref[...], preferred_element_type=F32)
        middle = state_ref[...] + att
        middle_ref[...] = middle
        n2_ref[...] = normed(middle, gain_ref[...]).astype(BF)
        both_ref[...] = att

    n2 = n2_ref[...]
    gated = jnp.dot(n2, w_gate_ref[...], preferred_element_type=F32)
    upward = jnp.dot(n2, w_up_ref[...], preferred_element_type=F32)
    hidden = (gated * jax.nn.sigmoid(gated) * upward).astype(BF)
    gated_ref[...] = gated.astype(BF)
    up_ref[...] = upward.astype(BF)
    hidden_ref[...] = hidden
    both_ref[...] += jnp.dot(hidden, w_down_ref[...], preferred_element_type=F32)

    @pl.when(step == pl.num_programs(0) - 1)
    def _():
        state = state_ref[...]
        gate = jax.nn.sigmoid(jnp.sum(state * router_ref[...], axis=-1, keepdims=True))
        gate_ref[...] = gate
        new_ref[...] = state + active_ref[...] * gate * both_ref[...]
        if following:
            project_into(
                new_ref[:following, :], next_gain_ref[...], w_ref, turn_ref, *refs[8:11]
            )


def feed(mixed, state, w_out, gain, router, active, w_gate, w_up, w_down, following, then=()):
    n, model = state.shape
    ff = w_gate.shape[1]
    tile = 512 if ff % 512 == 0 else ff
    across = pl.BlockSpec((model, tile), lambda i: (0, i))
    made = pl.BlockSpec((n, tile), lambda i: (0, i))
    out_specs = [
        whole(n, model), whole(n, model), whole(n, model), made, made, made, whole(n, model),
        whole(n, 1),
    ]
    wide = lambda dtype: jax.ShapeDtypeStruct((n, model), dtype)
    tall = jax.ShapeDtypeStruct((n, ff), BF)
    out_shape = [
        wide(F32), wide(F32), wide(BF), tall, tall, tall, wide(F32),
        jax.ShapeDtypeStruct((n, 1), F32),
    ]
    if following:
        shapes = [(following, model), (CHUNKS, following, LANES), (following, KV_HEADS * LANES)]
        out_specs += [whole(*s) for s in shapes]
        out_shape += [jax.ShapeDtypeStruct(s, BF) for s in shapes]
    return pl.pallas_call(
        functools.partial(feed_kernel, following),
        grid=(ff // tile,),
        in_specs=[
            whole(n, model), whole(n, model), whole(*w_out.shape), whole(1, model),
            whole(1, model), whole(n, 1), across, across,
            pl.BlockSpec((tile, model), lambda i: (i, 0)),
        ] + [whole(*v.shape) for v in then],
        out_specs=out_specs,
        out_shape=out_shape,
        compiler_params=pltpu.CompilerParams(vmem_limit_bytes=ROOM),
        name="feed",
    )(mixed, state, w_out, gain, router, active, w_gate, w_up, w_down, *then)


def feed_back_kernel(gradient_ref, both_ref, gate_ref, active_ref, state_ref, router_ref,
                     middle_ref, gain_ref, w_out_ref, gated_ref, up_ref, w_gate_ref, w_up_ref,
                     w_down_ref, d_fed_ref, d_gated_ref, d_up_ref, d_att_ref, grad_ref,
                     d_mixed_ref, d_router_ref, d_gain_ref, total):
    step = pl.program_id(0)

    @pl.when(step == 0)
    def _():
        d_fed_ref[...] = (active_ref[...] * gate_ref[...] * gradient_ref[...]).astype(BF)
        total[...] = jnp.zeros(total.shape, F32)

    d_hidden = lax.dot_general(d_fed_ref[...], w_down_ref[...], NT, preferred_element_type=F32)
    gated, upward = gated_ref[...].astype(F32), up_ref[...].astype(F32)
    sig = jax.nn.sigmoid(gated)
    part = d_hidden * sig
    d_up = (part * gated).astype(BF)
    d_gated = (part * upward * (1.0 + gated * (1.0 - sig))).astype(BF)
    d_up_ref[...] = d_up
    d_gated_ref[...] = d_gated
    total[...] += lax.dot_general(
        d_gated, w_gate_ref[...], NT, preferred_element_type=F32
    ) + lax.dot_general(d_up, w_up_ref[...], NT, preferred_element_type=F32)

    @pl.when(step == pl.num_programs(0) - 1)
    def _():
        gradient, gate, active = gradient_ref[...], gate_ref[...], active_ref[...]
        d = total[...]
        v = middle_ref[...]
        inv = lax.rsqrt(jnp.mean(v * v, axis=-1, keepdims=True) + EPS)
        d_gain_ref[...] = jnp.sum(d * v * inv, axis=0, keepdims=True)
        scaled = d * gain_ref[...]
        dot = jnp.mean(scaled * v, axis=-1, keepdims=True)
        d_middle = inv * scaled - v * (inv * inv * inv * dot)
        d_gate = active * gate * (1.0 - gate) * jnp.sum(
            gradient * both_ref[...], axis=-1, keepdims=True
        )
        d_router_ref[...] = jnp.sum(state_ref[...] * d_gate, axis=0, keepdims=True)
        grad_ref[...] = gradient + d_gate * router_ref[...] + d_middle
        d_att_ref[...] = (active * gate * gradient + d_middle).astype(BF)
        out_back_kernel(d_att_ref, w_out_ref, d_mixed_ref)


def feed_back(gradient, both, gate, active, state, router, middle, gain, w_out, gated, upward,
              w_gate, w_up, w_down):
    n, model = state.shape
    ff = w_gate.shape[1]
    tile = 512 if ff % 512 == 0 else ff
    across = pl.BlockSpec((model, tile), lambda i: (0, i))
    made = pl.BlockSpec((n, tile), lambda i: (0, i))
    wide = whole(n, model)
    flat = lambda dtype: jax.ShapeDtypeStruct((n, model), dtype)
    tall = jax.ShapeDtypeStruct((n, ff), BF)
    row = jax.ShapeDtypeStruct((1, model), F32)
    return pl.pallas_call(
        feed_back_kernel,
        grid=(ff // tile,),
        in_specs=[
            wide, wide, whole(n, 1), whole(n, 1), wide, whole(1, model), wide, whole(1, model),
            whole(*w_out.shape), made, made, across, across,
            pl.BlockSpec((tile, model), lambda i: (i, 0)),
        ],
        out_specs=[
            wide, made, made, wide, wide, whole(CHUNKS, n, LANES), whole(1, model),
            whole(1, model),
        ],
        out_shape=[
            flat(BF), tall, tall, flat(BF), flat(F32),
            jax.ShapeDtypeStruct((CHUNKS, n, LANES), BF), row, row,
        ],
        scratch_shapes=[pltpu.VMEM((n, model), F32)],
        compiler_params=pltpu.CompilerParams(vmem_limit_bytes=ROOM),
        name="feed_back",
    )(gradient, both, gate, active, state, router, middle, gain, w_out, gated, upward, w_gate,
      w_up, w_down)


def outer_rows_kernel(count, *refs):
    xs, ds, out_ref = refs[:count], refs[count:2 * count], refs[2 * count]
    total = None
    for x_ref, d_ref in zip(xs, ds):
        part = jnp.dot(jnp.transpose(x_ref[...]), d_ref[...], preferred_element_type=F32)
        total = part if total is None else total + part
    out_ref[...] = total.astype(BF)


def outer_rows(xs, ds, tile):
    rows, columns = xs[0].shape[1], ds[0].shape[1]
    tokens = sum(x.shape[0] for x in xs)
    return pl.pallas_call(
        functools.partial(outer_rows_kernel, len(xs)),
        grid=(rows // tile,),
        in_specs=[pl.BlockSpec((x.shape[0], tile), lambda i: (0, i)) for x in xs]
        + [whole(*d.shape) for d in ds],
        out_specs=pl.BlockSpec((tile, columns), lambda i: (i, 0)),
        out_shape=jax.ShapeDtypeStruct((rows, columns), BF),
        compiler_params=pltpu.CompilerParams(vmem_limit_bytes=ROOM),
        cost_estimate=pl.CostEstimate(
            flops=2 * tokens * rows * columns, transcendentals=0,
            bytes_accessed=2 * (tokens * (columns + rows) + rows * columns),
        ),
        name="outer_rows",
    )(*xs, *ds)


def mm(a, b):
    return jnp.dot(a, b, preferred_element_type=F32)


def mm_tn(a, b):
    return lax.dot_general(a, b, TN, preferred_element_type=F32)


def per_device(topo, *args):
    (tokens, w_query, w_key, w_value, w_out, w_gate, w_up, w_down, router, norm_attn, norm_ffn,
     lengths, depths, padding, cotangent) = args
    rows, model = tokens.shape
    kv_cols = w_key.shape[1]
    ff = w_gate.shape[1]
    shard = w_query.shape[0]
    deep_rows = rows * 3 // 4
    xk, yk, ck = (topo.keys(d) for d in "xyc")

    small = jnp.concatenate([router, norm_attn[:, None], norm_ffn[:, None]], axis=1)
    small = jnp.pad(small, ((0, 0), (0, HD - small.shape[1])))
    w_kv = jnp.stack(
        [w_key.reshape(shard, KV_HEADS, HD), w_value.reshape(shard, KV_HEADS, HD)], axis=2
    ).reshape(shard, 2 * kv_cols)
    first = jnp.concatenate([w_query, small, w_kv], axis=1)
    weight_qkv, weight_g, weight_u, weight_d, weight_o = gather_weights(
        topo, [first, w_gate, w_up, w_down, w_out]
    )

    own = lax.axis_index("tok") * rows + jnp.arange(rows, dtype=jnp.int32)
    eligible = (depths >= 2) & (padding > 0)
    flags = jnp.stack([eligible, ~eligible]).astype(BF)
    upto = (jnp.arange(rows)[:, None] <= jnp.arange(rows)[None, :]).astype(BF)
    counts = mm(flags, upto).astype(jnp.int32)
    slot = jnp.where(eligible, counts[0] - 1, counts[0, -1] + counts[1] - 1)
    chosen = jnp.arange(rows, dtype=jnp.int32)[:, None] == slot[None, :]
    onehot = chosen.astype(BF)
    doc_ends = jnp.cumsum(lengths[0])
    begins = jnp.sum(
        jnp.where(own[:, None] >= doc_ends[None, :], lengths[0][None, :], 0), axis=1
    )
    levels = jnp.where(padding > 0, depths, 0)
    labels = jnp.stack([own, begins, levels])
    labels = jnp.sum(jnp.where(chosen[None], labels[:, None, :], 0), axis=2)
    labels = jnp.pad(labels, ((0, 5), (0, 0)))
    swap = topo.swap_pairs()
    state = lax.ppermute(mm(onehot, tokens).astype(BF), AXES, swap).astype(F32)
    labels = lax.ppermute(labels, AXES, swap)
    cotangent = mm(onehot, cotangent).astype(BF)

    def collect(arrays, ident):
        if small_layer(topo):
            return gather_layer(topo, arrays, ident)
        return [group_gather(topo, v, xk + yk + ck) for v in arrays]

    def distribute(grads, ident):
        if small_layer(topo):
            return reduce_layer(topo, grads, ident)
        return group_scatter(topo, grads, ck + yk + xk)


    small = weight_qkv[:, model:model + HD].astype(F32)
    gain_one, gain_two = small[:, RECS][None], small[:, RECS + 1][None]

    pack = (lax.axis_index("grp") * topo.X) + lax.axis_index("tok") % topo.X
    begin_all, level_mine = labels[1], labels[2]
    lowest = jnp.min(labels[1])
    span = jnp.stack([lowest // rows, pack + 1]).astype(jnp.int32)
    places = (labels[0] - labels[1]).astype(F32)
    freqs = 10000.0 ** (-(jnp.arange(HD // 2, dtype=F32) * 2.0 / HD))
    angles = places[:, None] * freqs[None, :]
    turns = jnp.stack([jnp.cos(angles), jnp.sin(angles)])
    turns = jnp.tile(turns, (1, 1, LANES * 2 // HD))

    routers = [small[:, r][None] for r in range(RECS)]

    def forward(state, projected, recursion, labels_all=None):
        n = state.shape[0]
        extra = None
        n1, q, kv = projected
        if recursion == 0:
            kv_all, labels_all = collect([kv, labels], 2)
            kv_all, later = lax.optimization_barrier((kv_all, cotangent))
            later = lax.ppermute(later, AXES, swap)
        else:
            kv_all, = collect([kv], 3)
        kv_all = kv_all.reshape(topo.T * n, 2 * kv_cols)
        live = labels_all[:, 2, :n] > recursion
        order = labels_all[:, 0, :n]
        key_labels = jnp.stack([jnp.where(live, order, -1), order], axis=-1).reshape(-1, 2)
        key_labels = jnp.pad(key_labels, ((0, 0), (0, 6)))
        query_labels = jnp.stack([labels[1, :n], labels[0, :n]])
        query_labels = jnp.pad(jnp.tile(query_labels, (1, SHARES)), ((0, 6), (0, 0)))
        mixed, out, stat = attend(n, span, key_labels, query_labels, kv_all, q)
        if recursion == 0:
            mixed, later = lax.optimization_barrier((mixed, later))
            extra = (labels_all, later.astype(F32))
        active = (labels[2, :n] > recursion).astype(F32)[:, None]
        following = deep_rows if recursion + 1 < RECS else 0
        new, middle, n2, gated, upward, hidden, both, gate, *projected = feed(
            mixed, state, weight_o, gain_two, routers[recursion], active, weight_g, weight_u,
            weight_d, following, (gain_one, weight_qkv, turns) if following else (),
        )
        kept = (state, n1, q, kv_all, key_labels, query_labels, out, stat, mixed, middle,
                n2, gated, upward, hidden, both, gate, active)
        return (new, projected, kept, extra)

    def backward(gradient, recursion, kept):
        (state, n1, q, kv_all, key_labels, query_labels, out, stat, mixed, middle,
         n2, gated, upward, hidden, both, gate, active) = kept
        n = state.shape[0]
        d_fed, d_gated, d_up, d_att, gradient, d_mixed, d_router, d_gain_two = feed_back(
            gradient, both, gate, active, state, routers[recursion], middle, gain_two, weight_o,
            gated, upward, weight_g, weight_u, weight_d,
        )
        dq, dkv = attend_back(
            n, span, key_labels, query_labels, kv_all, q, d_mixed, out, stat, turns[:, :n]
        )
        dkv = distribute(dkv.reshape(topo.T, n, 2 * kv_cols), 5 if recursion else 4)
        gradient, dqkv, d_gain_one = project_back(
            gradient, state, gain_one, weight_qkv, turns[:, :n], dq, dkv
        )
        left = (n1, dqkv, mixed, d_att, n2, d_gated, d_up, hidden, d_fed)
        return (gradient, left, (d_router[0], d_gain_one[0], d_gain_two[0]))

    projected = project(state, gain_one, weight_qkv, turns)
    whole_state, projected, kept, (labels_all, gradient) = forward(state, projected, 0)
    deep = whole_state[:deep_rows]
    all_kept = [kept]
    for recursion in range(1, RECS):
        deep, projected, kept, _ = forward(deep, projected, recursion, labels_all)
        all_kept.append(kept)
    final = jnp.concatenate([deep, whole_state[deep_rows:]], axis=0).astype(BF)

    deep_grad = gradient[:deep_rows]
    lefts, smalls = [], []
    for recursion in reversed(range(1, RECS)):
        deep_grad, left, tiny = backward(deep_grad, recursion, all_kept[recursion])
        lefts.append(left)
        smalls.append(tiny)
    gradient = jnp.concatenate([deep_grad, gradient[deep_rows:]], axis=0)
    gradient, left, tiny = backward(gradient, 0, all_kept[0])
    lefts.append(left)
    smalls.append(tiny)
    final, gradient = lax.optimization_barrier((final, gradient.astype(BF)))
    final = lax.ppermute(final, AXES, swap)
    gradient = lax.ppermute(gradient, AXES, swap)

    n1, dqkv, mixed, d_att, n2, d_gated, d_up, hidden, d_fed = zip(*lefts)

    def outer(xs, ds):
        return mm_tn(jnp.concatenate(xs, axis=0), jnp.concatenate(ds, axis=0))

    cut = lambda v: v.astype(BF).reshape(topo.T, -1, v.shape[-1])
    tiny = jnp.stack(
        [smalls[2][0], smalls[1][0], smalls[0][0],
         smalls[0][1] + smalls[1][1] + smalls[2][1],
         smalls[0][2] + smalls[1][2] + smalls[2][2]], axis=1
    )
    wide_out = -(-(model + tiny.shape[1]) // 256) * 256
    tiny = jnp.pad(tiny, ((0, 0), (0, wide_out - model - tiny.shape[1])))
    grad_qkv, grad_o, grad_gu, grad_down = reduce_gradients(topo, [
        cut(outer(n1, dqkv)),
        cut(jnp.concatenate([outer(mixed, d_att), tiny], axis=1)),
        cut(outer(n2, d_gated)),
        outer_rows(hidden, d_fed, 640).reshape(topo.T, -1, model),
        cut(outer(n2, d_up)),
    ])
    grad_query = grad_qkv[:, :model].astype(F32)
    pair = grad_qkv[:, model + HD:model + HD + 2 * kv_cols].astype(F32)
    pair = pair.reshape(shard, KV_HEADS, 2, HD)
    grad_key = pair[:, :, 0].reshape(shard, kv_cols)
    grad_value = pair[:, :, 1].reshape(shard, kv_cols)
    grad_out = grad_o[:, :model].astype(F32)
    tiny = grad_o[:, model:].astype(F32)
    grad_gate, grad_up = grad_gu[0].astype(F32), grad_gu[1].astype(F32)
    grad_down = grad_down.astype(F32)

    def unsort(v):
        return mm_tn(onehot, v).astype(BF)

    return (
        unsort(final), unsort(gradient), grad_query, grad_key, grad_value, grad_out,
        grad_gate, grad_up, grad_down, tiny[:, :RECS], tiny[:, RECS],
        tiny[:, RECS + 1],
    )


def solution(mesh):
    topo = Topo(mesh.shape["grp"], mesh.shape["tok"])
    both = P(("grp", "tok"))
    wide = P(("grp", "tok"), None)
    rows = P("tok", None)
    row = P("tok")
    return jax.shard_map(
        functools.partial(per_device, topo),
        mesh=mesh,
        in_specs=(wide,) + (rows,) * 8 + (row, row, P("grp", None), both, both, wide),
        out_specs=(wide, wide) + (rows,) * 8 + (row, row),
        check_vma=False,
    )
```

```python
import functools

import jax
import jax.numpy as jnp
from jax import lax
from jax.experimental import pallas as pl
from jax.experimental.pallas import tpu as pltpu
from jax.sharding import PartitionSpec as P

HEADS = 15
KV_HEADS = 5
SHARES = HEADS // KV_HEADS
HD = 64
RECS = 3
EPS = 1e-05
BF = jnp.bfloat16
F32 = jnp.float32
BIG = -1e30
AXES = ("grp", "tok")


class Topo:
    def __init__(self, groups, spread):
        self.G = groups
        self.T = spread
        self.X = spread // groups
        self.Z = groups
        self.Y = groups // 2
        self.bits = {
            "z": self.Z.bit_length() - 1,
            "x": self.X.bit_length() - 1,
            "y": self.Y.bit_length() - 1,
            "c": 1,
        }

    def keys(self, dim):
        return [(dim, k) for k in range(self.bits[dim])]

    def masks(self, key):
        dim, k = key
        if dim == "c":
            return (1, 0)
        if dim == "y":
            return (2 << k, 0)
        if dim == "x":
            return (0, 1 << k)
        return (0, self.X << k)

    def pairs(self, key):
        mg, mt = self.masks(key)
        return [
            (g * self.T + t, (g ^ mg) * self.T + (t ^ mt))
            for g in range(self.G)
            for t in range(self.T)
        ]

    def swap_pairs(self):
        out = []
        for g in range(self.G):
            for t in range(self.T):
                z, x = t // self.X, t % self.X
                out.append((g * self.T + t, z * self.T + g * self.X + x))
        return out

    def bit(self, key):
        mg, mt = self.masks(key)
        if mg:
            return (lax.axis_index("grp") // mg) % 2
        return (lax.axis_index("tok") // mt) % 2


def exchange(topo, arr, key):
    return lax.ppermute(arr, AXES, topo.pairs(key))


def double(topo, arr, key, axis, stack):
    other = exchange(topo, arr, key)
    mine_is_high = topo.bit(key) == 1
    low = jnp.where(mine_is_high, other, arr)
    high = jnp.where(mine_is_high, arr, other)
    if stack:
        return jnp.stack([low, high], axis=axis)
    return jnp.concatenate([low, high], axis=axis)


def halve(topo, arr, key, axis, stack):
    mine_is_high = topo.bit(key) == 1
    if stack:
        low = lax.index_in_dim(arr, 0, axis, keepdims=False)
        high = lax.index_in_dim(arr, 1, axis, keepdims=False)
    else:
        half = arr.shape[axis] // 2
        low = lax.slice_in_dim(arr, 0, half, axis=axis)
        high = lax.slice_in_dim(arr, half, 2 * half, axis=axis)
    send = jnp.where(mine_is_high, low, high).astype(BF)
    keep = jnp.where(mine_is_high, high, low).astype(F32)
    return (keep + exchange(topo, send, key).astype(F32)).astype(BF)


class Piece:
    def __init__(self, array, dim, start, size, core, part):
        self.array, self.dim, self.start, self.size = array, dim, start, size
        self.core, self.part = core, part

    def of(self, ref):
        if self.dim == 0:
            return ref.at[pl.ds(self.start, self.size), :]
        return ref.at[:, pl.ds(self.start, self.size)]


def cut_pieces(shapes):
    near = lambda v, unit: max(unit, int(round(v / unit)) * unit)
    wide_a, wide_g, wide_u, tall = shapes[0][1], shapes[1][1], shapes[2][1], shapes[3][0]
    g = near(wide_g * 0.7, 128)
    u = near(wide_u * 0.65, 128)
    d = near(tall * 0.3, 8)
    return [
        Piece(1, 1, 0, g, 0, 0),
        Piece(4, 1, 0, shapes[4][1], 0, 2),
        Piece(1, 1, g, wide_g - g, 0, 2),
        Piece(0, 1, 0, wide_a, 0, 1),
        Piece(2, 1, u, wide_u - u, 1, 0),
        Piece(3, 0, 0, d, 1, 0),
        Piece(3, 0, d, tall - d, 1, 2),
        Piece(2, 1, 0, u, 1, 1),
    ]


def coordinates(topo):
    g, t = lax.axis_index("grp"), lax.axis_index("tok")
    return lax.rem(t, topo.X), lax.div(g, 2), lax.div(t, topo.X), lax.rem(g, 2)


def gather_kernel(topo, pieces, *refs):
    shards, outs = refs[:5], refs[5:10]
    local_sem, recv_sem, z_sem, x_sem, y_sem, c_sem = refs[10:]
    x, y, z, c = coordinates(topo)
    X, Z, T = topo.X, topo.Z, topo.T
    g, me = lax.axis_index("grp"), lax.axis_index("tok")
    odd = lax.rem(y, 2)
    over_y = {"grp": g + 2 - 4 * odd, "tok": me}
    over_c = {"grp": g + 1 - 2 * c, "tok": me}

    def over_z(k):
        return {"grp": g, "tok": (z + k) * X + x}

    def over_x(k):
        return {"grp": g, "tok": z * X + lax.rem(x + k, X)}

    barrier = pltpu.get_barrier_semaphore()
    partners = [over_y, over_c] + [over_x(k) for k in range(1, X)]
    for partner in partners:
        pl.semaphore_signal(barrier, inc=1, device_id=partner, device_id_type=pl.DeviceIdType.MESH)
    below, above = z > 0, z < Z - 1

    def greet(k):
        pl.semaphore_signal(
            barrier, inc=1, device_id=over_z(k), device_id_type=pl.DeviceIdType.MESH
        )

    pl.when(below)(lambda: greet(-1))
    pl.when(above)(lambda: greet(1))
    own = [
        pltpu.make_async_copy(shards[i], outs[i].at[me], local_sem.at[i]) for i in range(5)
    ]
    for copy in own:
        copy.start()
    pl.semaphore_wait(barrier, len(partners) + below.astype(jnp.int32) + above.astype(jnp.int32))

    def send(p, t, sem, target, mine=False):
        piece = pieces[p]
        landing = piece.of(outs[piece.array].at[t])
        source = piece.of(shards[piece.array]) if mine else landing
        return pltpu.make_async_remote_copy(
            src_ref=source, dst_ref=landing, send_sem=sem, recv_sem=recv_sem.at[p, t],
            device_id=target, device_id_type=pl.DeviceIdType.MESH,
        )

    def arrived(p, t):
        send(p, t, c_sem.at[0, 0], over_c).wait_recv()

    def run(core):
        mine = [p for p in range(len(pieces)) if pieces[p].core == core]
        theirs = [p for p in range(len(pieces)) if pieces[p].core != core]
        slot = {p: i for i, p in enumerate(mine)}

        def inside(p, body):
            part = pieces[p].part
            if part == 1:
                body()
            else:
                pl.when(odd == part // 2)(body)

        def outside(p, body):
            if pieces[p].part != 1:
                pl.when(odd != pieces[p].part // 2)(body)

        def x_copies(p, zz, first):
            t = zz * X + x
            return [
                send(p, t, x_sem.at[slot[p], zz, k - 1], over_x(k), first) for k in range(1, X)
            ]

        def y_copy(p, t):
            return send(p, t, y_sem.at[slot[p], t], over_y)

        def c_copy(p, t):
            return send(p, t, c_sem.at[slot[p], t], over_c)

        def z_copy(p, zz, k, first):
            return send(p, zz * X + x, z_sem.at[slot[p], zz, (k + 1) // 2], over_z(k), first)

        for p in mine:
            def begin(p=p):
                pl.when(below)(lambda: z_copy(p, z, -1, True).start())
                pl.when(above)(lambda: z_copy(p, z, 1, True).start())
                for copy in x_copies(p, z, True):
                    copy.start()
            inside(p, begin)

        def share(p, t):
            if pieces[p].part != 1:
                y_copy(p, t).start()
            c_copy(p, t).start()

        def relay(p, zz, k):
            arrived(p, zz * X + x)
            pl.when(above if k > 0 else below)(lambda: z_copy(p, zz, k, False).start())
            for copy in x_copies(p, zz, False):
                copy.start()
            share(p, zz * X + x)

        def others(p, zz):
            for j in range(1, X):
                t = zz * X + lax.rem(x + j, X)
                arrived(p, t)
                share(p, t)

        def around(k, carry):
            low, high = z - k, z + k
            for p in mine:
                inside(p, lambda p=p: pl.when(low >= 0)(lambda: relay(p, low, 1)))
                inside(p, lambda p=p: pl.when(high < Z)(lambda: relay(p, high, -1)))
            low, high = z - k + 1, z + k - 1
            for p in mine:
                inside(p, lambda p=p: pl.when(low >= 0)(lambda: others(p, low)))
                inside(p, lambda p=p: pl.when((k > 1) & (high < Z))(lambda: others(p, high)))
            return carry

        lax.fori_loop(1, Z + 1, around, 0)

        def rest(t, carry):
            @pl.when(t != me)
            def _():
                for p in mine:
                    def forward(p=p):
                        arrived(p, t)
                        c_copy(p, t).start()
                    outside(p, forward)
            return carry

        lax.fori_loop(0, T, rest, 0)

        def finish(t, carry):
            @pl.when(t != me)
            def _():
                for p in theirs:
                    arrived(p, t)
                for p in mine:
                    c_copy(p, t).wait_send()
                    if pieces[p].part != 1:
                        inside(p, lambda p=p: y_copy(p, t).wait_send())
            return carry

        lax.fori_loop(0, T, finish, 0)
        for p in mine:
            def end(p=p):
                def each(zz, carry):
                    pl.when((zz <= z) & above)(lambda: z_copy(p, zz, 1, False).wait_send())
                    pl.when((zz >= z) & below)(lambda: z_copy(p, zz, -1, False).wait_send())
                    for copy in x_copies(p, zz, False):
                        copy.wait_send()
                    return carry
                lax.fori_loop(0, Z, each, 0)
            inside(p, end)

    pl.when(c == 0)(lambda: run(0))
    pl.when(c == 1)(lambda: run(1))
    for copy in own:
        copy.wait()


def gather_weights(topo, shards):
    pieces = cut_pieces([s.shape for s in shards])
    T = topo.T
    DMA = pltpu.SemaphoreType.DMA
    hbm = pl.BlockSpec(memory_space=pl.ANY)
    outs = pl.pallas_call(
        functools.partial(gather_kernel, topo, pieces),
        in_specs=[hbm] * 5,
        out_specs=[hbm] * 5,
        out_shape=[jax.ShapeDtypeStruct((T,) + s.shape, s.dtype) for s in shards],
        scratch_shapes=[
            DMA((5,)), DMA((len(pieces), T)), DMA((4, topo.Z, 2)), DMA((4, topo.Z, topo.X - 1)),
            DMA((4, T)), DMA((4, T)),
        ],
        compiler_params=pltpu.CompilerParams(collective_id=0, has_side_effects=True),
        name="gather_weights",
    )(*shards)
    return [o.reshape(-1, o.shape[-1]) for o in outs]


class Share:
    def __init__(self, array, start, shape, part):
        self.array, self.start, self.shape, self.part = array, start, shape, part

    def of(self, ref, core, *lead):
        rows, columns = self.shape
        if self.array == 2:
            return ref.at[lead + (slice(None), pl.ds(self.start, columns))]
        if self.array == 3:
            at = pl.multiple_of(core * rows, rows)
            return ref.at[lead + (pl.ds(at, rows), slice(None))]
        at = pl.multiple_of(core * columns, 128)
        return ref.at[lead + (slice(None), pl.ds(at, columns))]


def cut_shares(shapes):
    rows, ff = shapes[2][1], shapes[2][2]
    one = ff * 3 // 20 // 128 * 128
    two = ff * 33 // 40 // 128 * 128
    return [
        Share(2, one, (rows, two - one), 0),
        Share(3, 0, (shapes[3][1] // 2, shapes[3][2]), 2),
        Share(2, two, (rows, ff - two), 2),
        Share(0, 0, (rows, shapes[0][2] // 2), 1),
        Share(1, 0, (rows, shapes[1][2] // 2), 1),
        Share(2, 0, (rows, one), 1),
    ]


def reduce_kernel(topo, shares, *refs):
    grads, outs = refs[:5], refs[5:9]
    count = len(shares)
    groups = []
    at = 9
    for _ in range(7):
        groups.append(refs[at:at + count])
        at += count
    held, from_c, from_y, from_x, from_low, from_high, from_f = groups
    (load_sem, c_send, c_recv, y_send, y_recv, x_send, x_recv, z_send, z_recv, f_send, f_recv,
     o_send, o_recv, o_local) = refs[at:]
    x, y, z, c = coordinates(topo)
    X, Z, T = topo.X, topo.Z, topo.T
    g, me = lax.axis_index("grp"), lax.axis_index("tok")
    odd = lax.rem(y, 2)
    below, above = z > 0, z < Z - 1
    kind = pl.DeviceIdType.MESH

    def over_y(k):
        high = lax.rem(lax.div(y, 1 << k), 2)
        return {"grp": g + (2 - 4 * high) * (1 << k), "tok": me}

    over_c = {"grp": g + 1 - 2 * c, "tok": me}

    def over_z(k):
        return {"grp": g, "tok": (z + k) * X + x}

    def over_x(k):
        return {"grp": g, "tok": z * X + lax.rem(x + k, X)}

    barrier = pltpu.get_barrier_semaphore()
    partners = [over_c] + [over_y(k) for k in range(topo.bits["y"])]
    partners += [over_x(k) for k in range(1, X)]

    def greet(partner):
        pl.semaphore_signal(barrier, inc=1, device_id=partner, device_id_type=kind)

    for partner in partners:
        greet(partner)
    pl.when(below)(lambda: greet(over_z(-1)))
    pl.when(above)(lambda: greet(over_z(1)))
    every = range(count)

    def source(s, core, t, up):
        place = {2: 4 if up else 2, 3: 3}.get(s.array, s.array)
        return s.of(grads[place], core, t)

    def load(p, t, up=False):
        return pltpu.make_async_copy(
            source(shares[p], c, t, up), held[p].at[t], load_sem.at[p, t]
        )

    def start(p, make, up_core):
        if shares[p].array == 2:
            pl.when(c != up_core)(lambda: make(False).start())
            pl.when(c == up_core)(lambda: make(True).start())
        else:
            make(False).start()

    def remote(source, landing, send, recv, target):
        return pltpu.make_async_remote_copy(
            src_ref=source, dst_ref=landing, send_sem=send, recv_sem=recv, device_id=target,
            device_id_type=kind,
        )

    def c_copy(p, t, up=False):
        return remote(
            source(shares[p], 1 - c, t, up), from_c[p].at[t], c_send.at[p, t], c_recv.at[p, t],
            over_c,
        )

    def y_copy(p, t):
        return remote(
            held[p].at[t], from_y[p].at[t], y_send.at[p, t], y_recv.at[p, t], over_y(0)
        )

    def x_copy(p, zz, k):
        t = zz * X + lax.rem(x + k, X)
        return remote(
            held[p].at[t], from_x[p].at[zz, k - 1], x_send.at[p, zz, k - 1],
            x_recv.at[p, zz, k - 1], over_x(k),
        )

    def z_copy(p, zz, k):
        landing = from_low if k > 0 else from_high
        way = (k + 1) // 2
        return remote(
            held[p].at[zz * X + x], landing[p].at[zz], z_send.at[p, zz, way],
            z_recv.at[p, zz, way], over_z(k),
        )

    def f_copy(p, k):
        return remote(
            held[p].at[me], from_f[p].at[k], f_send.at[p, k], f_recv.at[p, k], over_y(k)
        )

    def result(s, core):
        if s.array == 2:
            return outs[2].at[core, :, pl.ds(s.start, s.shape[1])]
        return s.of(outs[s.array], core)

    def o_copy(p):
        s = shares[p]
        return remote(
            held[p].at[me], result(s, c), o_send.at[p], o_recv.at[p], over_c
        )

    def o_arrived(p):
        s = shares[p]
        return remote(
            held[p].at[me], result(s, 1 - c), o_send.at[p], o_recv.at[p], over_c
        )

    def o_keep(p):
        s = shares[p]
        return pltpu.make_async_copy(held[p].at[me], result(s, c), o_local.at[p])

    def add(p, t, other):
        held[p][t] = held[p][t] + other

    def layers(body):
        def step(i, carry):
            k = Z - 1 - i
            pl.when(z + k < Z)(lambda: body(z + k))
            pl.when((k > 0) & (z - k >= 0))(lambda: body(z - k))
            return carry
        return step

    def inside(p, body):
        if shares[p].part == 1:
            body()
        else:
            pl.when(odd == shares[p].part // 2)(body)

    def outside(p, body):
        if shares[p].part != 1:
            pl.when(odd != shares[p].part // 2)(body)

    def start_loads(zz):
        def each(j, carry):
            t = zz * X + lax.rem(x + j, X)
            for p in every:
                start(p, lambda up, p=p: load(p, t, up), 1)
            return carry
        lax.fori_loop(0, X, each, 0)

    lax.fori_loop(0, Z, layers(start_loads), 0)
    pl.semaphore_wait(barrier, len(partners) + below.astype(jnp.int32) + above.astype(jnp.int32))

    def start_cores(zz):
        def each(j, carry):
            t = zz * X + lax.rem(x + j, X)
            for p in every:
                start(p, lambda up, p=p: c_copy(p, t, up), 0)
            return carry
        lax.fori_loop(0, X, each, 0)

    lax.fori_loop(0, Z, layers(start_cores), 0)

    def cores(zz):
        def each(j, carry):
            t = zz * X + lax.rem(x + j + 1, X)
            for p in every:
                load(p, t).wait()
                c_copy(p, t).wait_recv()
                add(p, t, from_c[p][t])
                outside(p, lambda p=p: y_copy(p, t).start())
                if shares[p].part == 1:
                    for k in range(1, X):
                        pl.when(j + 1 == k)(lambda p=p, k=k: x_copy(p, zz, k).start())
            return carry
        lax.fori_loop(0, X, each, 0)

    lax.fori_loop(0, Z, layers(cores), 0)

    def over(zz):
        def each(j, carry):
            t = zz * X + lax.rem(x + j + 1, X)
            for p in every:
                if shares[p].part != 1:
                    def body(p=p):
                        y_copy(p, t).wait_recv()
                        add(p, t, from_y[p][t])
                        for k in range(1, X):
                            pl.when(j + 1 == k)(lambda: x_copy(p, zz, k).start())
                    inside(p, body)
            return carry
        lax.fori_loop(0, X, each, 0)

    def join(p, zz):
        t = zz * X + x
        for k in range(1, X):
            x_copy(p, zz, k).wait_recv()
            add(p, t, from_x[p][zz, k - 1])

        def low():
            z_copy(p, zz, 1).wait_recv()
            add(p, t, from_low[p][zz])

        def high():
            z_copy(p, zz, -1).wait_recv()
            add(p, t, from_high[p][zz])

        pl.when((zz >= z) & below)(low)
        pl.when((zz <= z) & above)(high)
        pl.when(zz > z)(lambda: z_copy(p, zz, 1).start())
        pl.when(zz < z)(lambda: z_copy(p, zz, -1).start())

    single = topo.bits["y"] == 1

    def first_joins(zz):
        for p in every:
            if shares[p].part == 1:
                join(p, zz)
                if single:
                    pl.when(zz == z)(lambda p=p: f_copy(p, 0).start())

    def last_joins(zz):
        for p in every:
            if shares[p].part != 1:
                def body(p=p):
                    join(p, zz)
                    if single:
                        pl.when(zz == z)(lambda: f_copy(p, 0).start())
                inside(p, body)

    def main(i, carry):
        @pl.when(i < Z)
        def _():
            layers(first_joins)(i, 0)
            layers(over)(i, 0)

        @pl.when(i > 0)
        def _():
            layers(last_joins)(i - 1, 0)

        return carry

    lax.fori_loop(0, Z + 1, main, 0)

    for k in range(1, topo.bits["y"]):
        for p in every:
            inside(p, lambda p=p: f_copy(p, k).start())
        for p in every:
            def fold(p=p):
                f_copy(p, k).wait()
                add(p, me, from_f[p][k])
            inside(p, fold)
    if not single:
        for p in every:
            inside(p, lambda p=p: f_copy(p, 0).start())
    for p in every:
        if shares[p].part == 1:
            f_copy(p, 0).wait()
            add(p, me, from_f[p][0])
        else:
            def take(p=p):
                f_copy(p, 0).wait_recv()
                held[p][me] = from_f[p][0]
            outside(p, lambda p=p: y_copy(p, me).wait_send())
            outside(p, take)
        o_copy(p).start()
        o_keep(p).start()

    def ends(t, carry):
        for p in every:
            c_copy(p, t).wait_send()
            outside(p, lambda p=p: pl.when(t != me)(lambda: y_copy(p, t).wait_send()))
        return carry

    lax.fori_loop(0, T, ends, 0)

    def z_ends(zz, carry):
        for p in every:
            def body(p=p):
                for k in range(1, X):
                    x_copy(p, zz, k).wait_send()
                pl.when(zz > z)(lambda: z_copy(p, zz, 1).wait_send())
                pl.when(zz < z)(lambda: z_copy(p, zz, -1).wait_send())
            inside(p, body)
        return carry

    lax.fori_loop(0, Z, z_ends, 0)
    for p in every:
        if shares[p].part != 1:
            inside(p, lambda p=p: f_copy(p, 0).wait_send())
        o_copy(p).wait_send()
        o_arrived(p).wait_recv()
        o_keep(p).wait()


def reduce_gradients(topo, grads):
    shares = cut_shares([v.shape for v in grads])
    X, Z, T = topo.X, topo.Z, topo.T
    n = len(shares)
    folds = max(1, topo.bits["y"])
    DMA = pltpu.SemaphoreType.DMA
    hbm = pl.BlockSpec(memory_space=pl.ANY)
    lead = [(T,), (T,), (T,), (Z, X - 1), (Z,), (Z,), (folds,)]
    rooms = [
        pltpu.VMEM(front + s.shape, BF)
        for front in lead for s in shares
    ]
    outs = [grads[0].shape[1:], grads[1].shape[1:], (2,) + grads[2].shape[1:], grads[3].shape[1:]]
    return pl.pallas_call(
        functools.partial(reduce_kernel, topo, shares),
        in_specs=[hbm] * 5,
        out_specs=[hbm] * 4,
        out_shape=[jax.ShapeDtypeStruct(s, BF) for s in outs],
        scratch_shapes=rooms + [
            DMA((n, T)), DMA((n, T)), DMA((n, T)), DMA((n, T)), DMA((n, T)),
            DMA((n, Z, X - 1)), DMA((n, Z, X - 1)), DMA((n, Z, 2)), DMA((n, Z, 2)),
            DMA((n, folds)), DMA((n, folds)), DMA((n,)), DMA((n,)), DMA((n,)),
        ],
        compiler_params=pltpu.CompilerParams(
            collective_id=1, has_side_effects=True, vmem_limit_bytes=60 << 20
        ),
        name="reduce_gradients",
    )(*grads)


def group_order(topo):
    return list(reversed(topo.keys("y"))) + topo.keys("c") + list(reversed(topo.keys("x")))


def group_gather(topo, arr, order):
    names = group_order(topo)
    held = []
    shape = arr.shape
    for key in order:
        place = sum(1 for h in held if names.index(h) < names.index(key))
        arr = double(topo, arr, key, place, True)
        held.append(key)
    return arr.reshape((topo.T,) + shape)


def group_scatter(topo, arr, order):
    names = group_order(topo)
    held = list(names)
    arr = arr.reshape((2,) * len(names) + arr.shape[1:])
    for key in order:
        arr = halve(topo, arr, key, held.index(key), True)
        held.remove(key)
    return arr


def small_layer(topo):
    return topo.X == 2 and topo.Y == 2


class Layer:
    def __init__(self, topo):
        self.topo = topo
        x, y, z, c = coordinates(topo)
        self.c = c
        far_x, far_y = 1 - x, 1 - y
        a = (x + c * (far_x - x), far_y + c * (y - far_y))
        b = (far_x + c * (x - far_x), y + c * (far_y - y))
        self.chips = [(x, y), a, b, (far_x, far_y)]
        self.z = z

    def pack(self, slot, core):
        x, y = self.chips[slot]
        return (y * 2 + core) * self.topo.X + x

    def device(self, slot, core):
        x, y = self.chips[slot]
        return {"grp": y * 2 + core, "tok": self.z * self.topo.X + x}

    def meet(self):
        barrier = pltpu.get_barrier_semaphore()
        for target in (self.device(1, self.c), self.device(2, self.c), self.device(0, 1 - self.c)):
            pl.semaphore_signal(
                barrier, inc=1, device_id=target, device_id_type=pl.DeviceIdType.MESH
            )
        pl.semaphore_wait(barrier, 3)


def remote_copy(source, landing, send, recv, target):
    return pltpu.make_async_remote_copy(
        src_ref=source, dst_ref=landing, send_sem=send, recv_sem=recv, device_id=target,
        device_id_type=pl.DeviceIdType.MESH,
    )


def group_gather_kernel(topo, count, *refs):
    mine, outs = refs[:count], refs[count:2 * count]
    local_sem, send_sem, recv_sem = refs[2 * count:]
    layer = Layer(topo)
    c = layer.c
    arrays = range(count)
    a, b, sibling = layer.device(1, c), layer.device(2, c), layer.device(0, 1 - c)
    own = layer.pack(0, c)

    def send(i, way, pack, target):
        landing = outs[i].at[pack]
        source = mine[i] if way in (0, 1, 3) else landing
        return remote_copy(source, landing, send_sem.at[i, way], recv_sem.at[i, pack], target)

    ways = [
        (0, own, a), (1, own, b), (2, layer.pack(1, c), b), (3, own, sibling),
        (4, layer.pack(1, c), sibling), (5, layer.pack(2, c), sibling),
        (6, layer.pack(3, c), sibling),
    ]

    def start(k):
        for i in arrays:
            send(i, *ways[k]).start()

    def arrived(pack):
        for i in arrays:
            send(i, 2, pack, sibling).wait_recv()

    keep = [pltpu.make_async_copy(mine[i], outs[i].at[own], local_sem.at[i]) for i in arrays]
    for copy in keep:
        copy.start()
    layer.meet()
    start(0)
    start(1)
    start(3)
    arrived(layer.pack(1, c))
    start(2)
    start(4)
    arrived(layer.pack(2, c))
    start(5)
    arrived(layer.pack(3, c))
    start(6)
    for slot in range(4):
        arrived(layer.pack(slot, 1 - c))
    for way in ways:
        for i in arrays:
            send(i, *way).wait_send()
    for copy in keep:
        copy.wait()


def gather_layer(topo, arrays, ident):
    DMA = pltpu.SemaphoreType.DMA
    hbm = pl.BlockSpec(memory_space=pl.ANY)
    n = len(arrays)
    return pl.pallas_call(
        functools.partial(group_gather_kernel, topo, n),
        in_specs=[hbm] * n,
        out_specs=[hbm] * n,
        out_shape=[jax.ShapeDtypeStruct((topo.T,) + v.shape, v.dtype) for v in arrays],
        scratch_shapes=[DMA((n,)), DMA((n, 7)), DMA((n, topo.T))],
        compiler_params=pltpu.CompilerParams(collective_id=ident, has_side_effects=True),
        name="gather_layer",
    )(*arrays)


def group_reduce_kernel(topo, grads, out, held, from_c, from_b, from_a, load_sem, c_send, c_recv,
                        send_sem, recv_sem):
    layer = Layer(topo)
    c = layer.c
    a, b, sibling = layer.device(1, c), layer.device(2, c), layer.device(0, 1 - c)
    order = (3, 2, 1, 0)

    def load(slot):
        return pltpu.make_async_copy(
            grads.at[layer.pack(slot, c)], held.at[slot], load_sem.at[slot]
        )

    def c_copy(slot):
        theirs = (0, 2, 1, 3)[slot]
        return remote_copy(
            grads.at[layer.pack(slot, 1 - c)], from_c.at[theirs], c_send.at[theirs],
            c_recv.at[theirs], sibling,
        )

    def c_arrived(slot):
        remote_copy(
            grads.at[layer.pack(slot, c)], from_c.at[slot], c_send.at[slot], c_recv.at[slot],
            sibling,
        ).wait_recv()

    across = remote_copy(held.at[3], from_b.at[1], send_sem.at[0], recv_sem.at[0], b)
    direct = remote_copy(held.at[2], from_b.at[0], send_sem.at[1], recv_sem.at[1], b)
    passed = remote_copy(held.at[1], from_a, send_sem.at[2], recv_sem.at[2], a)

    for slot in order:
        load(slot).start()
    layer.meet()
    for slot in (3, 1, 2, 0):
        c_copy(slot).start()
    for slot in order:
        load(slot).wait()
        c_arrived(slot)
        held[slot] = held[slot] + from_c[slot]
        if slot == 3:
            across.start()
        if slot == 2:
            direct.start()
    across.wait_recv()
    held[1] = held[1] + from_b[1]
    passed.start()
    direct.wait_recv()
    held[0] = held[0] + from_b[0]
    passed.wait_recv()
    out[...] = held[0] + from_a[...]
    across.wait_send()
    direct.wait_send()
    passed.wait_send()
    for slot in range(4):
        c_copy(slot).wait_send()


def reduce_layer(topo, grads, ident):
    DMA = pltpu.SemaphoreType.DMA
    block = grads.shape[1:]
    return pl.pallas_call(
        functools.partial(group_reduce_kernel, topo),
        in_specs=[pl.BlockSpec(memory_space=pl.ANY)],
        out_specs=pl.BlockSpec(memory_space=pltpu.VMEM),
        out_shape=jax.ShapeDtypeStruct(block, BF),
        scratch_shapes=[
            pltpu.VMEM((4,) + block, BF), pltpu.VMEM((4,) + block, BF),
            pltpu.VMEM((2,) + block, BF), pltpu.VMEM(block, BF),
            DMA((4,)), DMA((4,)), DMA((4,)), DMA((3,)), DMA((3,)),
        ],
        compiler_params=pltpu.CompilerParams(
            collective_id=ident, has_side_effects=True, vmem_limit_bytes=32 << 20
        ),
        name="reduce_layer",
    )(grads)


NT = (((1,), (1,)), ((), ()))
TN = (((0,), (0,)), ((), ()))
LANES = 2 * HD
CHUNKS = (HEADS + 1) // 2
ROOM = 60 << 20


def lanes_of(rows):
    return lax.broadcasted_iota(jnp.int32, (rows, LANES), 1)


def spin(v):
    first = lax.rem(lanes_of(v.shape[0]), HD) < HD // 2
    return jnp.where(first, -pltpu.roll(v, LANES - HD // 2, 1), pltpu.roll(v, HD // 2, 1))


def whole(*shape):
    return pl.BlockSpec(shape, lambda *i: (0,) * len(shape))


def normed(v, gain):
    return v * lax.rsqrt(jnp.mean(v * v, axis=-1, keepdims=True) + EPS) * gain


def project_kernel(state_ref, w_ref, turn_ref, n1_ref, q_ref, kv_ref, small_ref):
    start = (CHUNKS - 1) * LANES
    small = jnp.transpose(w_ref[:, start:start + LANES].astype(F32))[HD:HD + 8]
    small_ref[...] = small
    project_into(
        state_ref[...].astype(F32), small[RECS:RECS + 1], w_ref, turn_ref, n1_ref, q_ref, kv_ref
    )


def project(state, w, turns):
    n, model = state.shape
    return pl.pallas_call(
        project_kernel,
        grid=(1,),
        in_specs=[whole(n, model), whole(*w.shape), whole(*turns.shape)],
        out_specs=[
            whole(n, model), whole(CHUNKS, n, LANES), whole(n, KV_HEADS * LANES),
            whole(8, model),
        ],
        out_shape=[
            jax.ShapeDtypeStruct((n, model), BF),
            jax.ShapeDtypeStruct((CHUNKS, n, LANES), BF),
            jax.ShapeDtypeStruct((n, KV_HEADS * LANES), BF),
            jax.ShapeDtypeStruct((8, model), F32),
        ],
        compiler_params=pltpu.CompilerParams(vmem_limit_bytes=ROOM),
        name="project",
    )(state, w, turns)


def attend_kernel(rows, recursion, span, key_ref, query_ref, kv_ref, q_ref, mixed_ref, out_ref, stat_ref,
                  stacked, mixing, tops, sums):
    low = lanes_of(rows) < HD
    wide = SHARES * rows
    for h in range(KV_HEADS):
        for j in range(SHARES):
            head = h * SHARES + j
            chunk = q_ref[head // 2].astype(F32)
            if head % 2:
                chunk = pltpu.roll(chunk, HD, 1)
            stacked[h, j * rows:(j + 1) * rows, :] = jnp.where(low, chunk, 0.0).astype(BF)
    mixing[...] = jnp.zeros(mixing.shape, F32)
    sums[...] = jnp.zeros(sums.shape, F32)
    tops[...] = jnp.full(tops.shape, BIG, F32)

    def body(t, carry):
        at = pl.ds(pl.multiple_of(t * rows, rows), rows)
        bias = block_bias(key_ref[t], query_ref, recursion, rows)
        def score(h):
            kv = kv_ref[at, h * LANES:(h + 1) * LANES]
            return lax.dot_general(kv, stacked[h], NT, preferred_element_type=F32) + bias

        def end(h, p, fade):
            kv = kv_ref[at, h * LANES:(h + 1) * LANES]
            mixing[h] = mixing[h] * fade + lax.dot_general(
                kv[:, HD:], p, TN, preferred_element_type=F32
            )

        ahead = score(0)
        before = None
        for h in range(KV_HEADS):
            s = ahead
            if h + 1 < KV_HEADS:
                ahead = score(h + 1)
            if before is not None:
                end(*before)
            old = tops[h, 0:1, :]
            top = jnp.max(s.reshape(rows // 8, 8, wide), axis=0)
            top = jnp.maximum(old, jnp.max(top, axis=0, keepdims=True))
            p = jnp.exp(s - top)
            fade = jnp.exp(old - top)
            sums[h] = sums[h] * fade + jnp.sum(p.reshape(rows // 8, 8, wide), axis=0)
            tops[h] = jnp.broadcast_to(top, (8, wide))
            before = (h, p.astype(BF), fade)
        end(*before)
        return carry

    lax.fori_loop(span[0], span[1], body, 0)
    for h in range(KV_HEADS):
        total = jnp.sum(sums[h], axis=0, keepdims=True)
        stat_ref[h] = tops[h] + jnp.log(total)
        mixing[h] = mixing[h] / total
    for j in range(CHUNKS):
        both = head_pair(mixing, j, rows)
        out_ref[j] = both
        size = min(LANES, HEADS * HD - j * LANES)
        mixed_ref[:, j * LANES:j * LANES + size] = both.astype(BF)[:, :size]


def block_bias(labels, query_ref, recursion, rows):
    keys = jnp.transpose(labels.astype(F32))[:rows]
    order, level = keys[:, 0:1], keys[:, 2:3]
    live = jnp.where(level > recursion, order, -1.0)
    place, begin = query_ref[0:1, :].astype(F32), query_ref[1:2, :].astype(F32)
    allowed = ((live >= begin) & (live <= place)) | (order == place)
    return jnp.where(allowed, 0.0, BIG)


def head_pair(mixing, j, rows):
    def one(head):
        if head >= HEADS:
            return jnp.zeros((HD, rows), F32)
        at = head % SHARES * rows
        return mixing[head // SHARES, :, at:at + rows]

    return jnp.transpose(jnp.concatenate([one(2 * j), one(2 * j + 1)], axis=0))


def attend(rows, recursion, span, key_labels, query_labels, kv_all, q):
    count, columns = kv_all.shape
    wide = SHARES * rows
    return pl.pallas_call(
        functools.partial(attend_kernel, rows, recursion),
        grid_spec=pltpu.PrefetchScalarGridSpec(
            num_scalar_prefetch=1,
            grid=(1,),
            in_specs=[
                whole(*key_labels.shape), whole(8, wide), whole(count, columns),
                whole(CHUNKS, rows, LANES),
            ],
            out_specs=[
                whole(rows, HEADS * HD), whole(CHUNKS, rows, LANES), whole(KV_HEADS, 8, wide),
            ],
            scratch_shapes=[
                pltpu.VMEM((KV_HEADS, wide, LANES), BF), pltpu.VMEM((KV_HEADS, HD, wide), F32),
                pltpu.VMEM((KV_HEADS, 8, wide), F32), pltpu.VMEM((KV_HEADS, 8, wide), F32),
            ],
        ),
        out_shape=[
            jax.ShapeDtypeStruct((rows, HEADS * HD), BF),
            jax.ShapeDtypeStruct((CHUNKS, rows, LANES), F32),
            jax.ShapeDtypeStruct((KV_HEADS, 8, wide), F32),
        ],
        compiler_params=pltpu.CompilerParams(vmem_limit_bytes=62 << 20),
        cost_estimate=pl.CostEstimate(
            flops=16 * KV_HEADS * wide * count * HD, bytes_accessed=4 * count * columns,
            transcendentals=KV_HEADS * wide * count,
        ),
        name="attend",
    )(span, key_labels, query_labels, kv_all, q)


def attend_back_kernel(rows, recursion, span, key_ref, query_ref, kv_ref, q_ref, d_ref, out_ref, stat_ref,
                       turn_ref, dq_ref, dkv_ref, stacked, part, mixing, deltas):
    low = lanes_of(rows) < HD
    wide = SHARES * rows
    ones = jnp.ones((8, LANES), BF)
    for h in range(KV_HEADS):
        for j in range(SHARES):
            head = h * SHARES + j
            q = q_ref[head // 2].astype(F32)
            d = d_ref[head // 2].astype(F32)
            if head % 2:
                q = pltpu.roll(q, HD, 1)
            product = d * out_ref[head // 2]
            mine = ~low if head % 2 else low
            if head % 2 == 0:
                d = pltpu.roll(d, HD, 1)
            at = pl.ds(j * rows, rows)
            stacked[h, at, :] = jnp.where(low, q, d).astype(BF)
            part[at, :] = jnp.where(mine, product, 0.0)
        coarse = part[...].astype(BF)
        fine = (part[...] - coarse.astype(F32)).astype(BF)
        deltas[h] = lax.dot_general(
            ones, coarse, NT, preferred_element_type=F32
        ) + lax.dot_general(ones, fine, NT, preferred_element_type=F32)
    dkv_ref[...] = jnp.zeros(dkv_ref.shape, BF)
    mixing[...] = jnp.zeros(mixing.shape, F32)

    def body(t, carry):
        at = pl.ds(pl.multiple_of(t * rows, rows), rows)
        bias = block_bias(key_ref[t], query_ref, recursion, rows)
        for h in range(KV_HEADS):
            kv = kv_ref[at, h * LANES:(h + 1) * LANES]
            zero = jnp.zeros_like(kv)
            queries = stacked[h]
            s = lax.dot_general(jnp.where(low, kv, zero), queries, NT, preferred_element_type=F32)
            p = jnp.exp(s + bias - stat_ref[h, 0:1, :])
            dp = lax.dot_general(jnp.where(low, zero, kv), queries, NT, preferred_element_type=F32)
            ds = (p * (dp - deltas[h, 0:1, :])).astype(BF)
            dk = jnp.dot(ds, queries, preferred_element_type=F32)
            dv = jnp.dot(p.astype(BF), queries, preferred_element_type=F32)
            dkv_ref[at, h * LANES:(h + 1) * LANES] = jnp.where(low, dk, dv).astype(BF)
            mixing[h] += lax.dot_general(kv[:, :HD], ds, TN, preferred_element_type=F32)
        return carry

    lax.fori_loop(span[0], span[1], body, 0)
    cosine, sine = turn_ref[0], turn_ref[1]
    for j in range(CHUNKS):
        both = head_pair(mixing, j, rows) * HD ** -0.5
        both = both * cosine - spin(both) * sine
        dq_ref[:, j * LANES:(j + 1) * LANES] = both.astype(BF)


def attend_back(rows, recursion, span, key_labels, query_labels, kv_all, q, d_mixed, out, stat, turns):
    count, columns = kv_all.shape
    wide = SHARES * rows
    return pl.pallas_call(
        functools.partial(attend_back_kernel, rows, recursion),
        grid_spec=pltpu.PrefetchScalarGridSpec(
            num_scalar_prefetch=1,
            grid=(1,),
            in_specs=[
                whole(*key_labels.shape), whole(8, wide), whole(count, columns),
                whole(CHUNKS, rows, LANES), whole(CHUNKS, rows, LANES),
                whole(CHUNKS, rows, LANES), whole(KV_HEADS, 8, wide), whole(2, rows, LANES),
            ],
            out_specs=[whole(rows, CHUNKS * LANES), whole(count, columns)],
            scratch_shapes=[
                pltpu.VMEM((KV_HEADS, wide, LANES), BF), pltpu.VMEM((wide, LANES), F32),
                pltpu.VMEM((KV_HEADS, HD, wide), F32), pltpu.VMEM((KV_HEADS, 8, wide), F32),
            ],
        ),
        out_shape=[
            jax.ShapeDtypeStruct((rows, CHUNKS * LANES), BF),
            jax.ShapeDtypeStruct((count, columns), BF),
        ],
        compiler_params=pltpu.CompilerParams(vmem_limit_bytes=62 << 20),
        name="attend_back",
    )(span, key_labels, query_labels, kv_all, q, d_mixed, out, stat, turns)


def out_back_kernel(d_ref, w_ref, out_ref):
    d = d_ref[...]
    for j in range(CHUNKS):
        size = min(LANES, w_ref.shape[0] - j * LANES)
        v = lax.dot_general(
            d, w_ref[j * LANES:j * LANES + size, :], NT, preferred_element_type=F32
        ).astype(BF)
        if size < LANES:
            v = jnp.concatenate([v, jnp.zeros((d.shape[0], LANES - size), BF)], axis=1)
        out_ref[j] = v


def project_back_kernel(gradient_ref, state_ref, small_ref, w_ref, turn_ref, dq_ref, raw_ref,
                        grad_ref, joint_ref, dgain_ref):
    cosine, sine = turn_ref[0], turn_ref[1]
    key = lanes_of(dq_ref.shape[0]) < HD
    for j in range(KV_HEADS):
        v = raw_ref[:, j * LANES:(j + 1) * LANES].astype(F32)
        turned = v * cosine - spin(v) * sine
        at = (CHUNKS + j) * LANES
        joint_ref[:, at:at + LANES] = jnp.where(key, turned, v).astype(BF)
    split, full = CHUNKS * LANES, w_ref.shape[1]
    joint_ref[:, :split] = dq_ref[...]
    if joint_ref.shape[1] > full:
        joint_ref[:, full:] = jnp.zeros((key.shape[0], joint_ref.shape[1] - full), BF)
    d = lax.dot_general(joint_ref[:, :full], w_ref[...], NT, preferred_element_type=F32)
    v = state_ref[...].astype(F32)
    inv = lax.rsqrt(jnp.mean(v * v, axis=-1, keepdims=True) + EPS)
    scaled = d * small_ref[RECS:RECS + 1, :]
    dot = jnp.mean(scaled * v, axis=-1, keepdims=True)
    grad_ref[...] = gradient_ref[...] + inv * scaled - v * (inv * inv * inv * dot)
    dgain_ref[...] = jnp.sum(d * v * inv, axis=0, keepdims=True)


def project_back(gradient, state, small, w, turns, dq, dkv):
    n, model = dq.shape[0], state.shape[1]
    joint = -(-w.shape[1] // 256) * 256
    return pl.pallas_call(
        project_back_kernel,
        grid=(1,),
        in_specs=[
            whole(n, model), whole(n, model), whole(8, model), whole(*w.shape),
            whole(2, n, LANES), whole(*dq.shape), whole(*dkv.shape),
        ],
        out_specs=[whole(n, model), whole(n, joint), whole(1, model)],
        out_shape=[
            jax.ShapeDtypeStruct((n, model), F32),
            jax.ShapeDtypeStruct((n, joint), BF),
            jax.ShapeDtypeStruct((1, model), F32),
        ],
        compiler_params=pltpu.CompilerParams(vmem_limit_bytes=ROOM),
        name="project_back",
    )(gradient, state, small, w, turns, dq, dkv)


def project_into(state, gain, w_ref, turn_ref, n1_ref, q_ref, kv_ref):
    n1 = normed(state, gain).astype(BF)
    n1_ref[...] = n1
    rows = n1.shape[0]
    cosine, sine = turn_ref[0, :rows], turn_ref[1, :rows]
    key = lanes_of(rows) < HD
    columns = w_ref.shape[1]
    for start in range(0, columns, 2 * LANES):
        wide = min(2 * LANES, columns - start)
        both = jnp.dot(n1, w_ref[:, start:start + wide], preferred_element_type=F32)
        for half in range(wide // LANES):
            j = start // LANES + half
            v = both[:, half * LANES:(half + 1) * LANES]
            turned = v * cosine + spin(v) * sine
            if j < CHUNKS:
                q_ref[j] = (turned * HD ** -0.5).astype(BF)
            else:
                j -= CHUNKS
                kv_ref[:, j * LANES:(j + 1) * LANES] = jnp.where(key, turned, v).astype(BF)


def active_column(label_ref, recursion, rows):
    level = jnp.transpose(label_ref[...].astype(F32))[:rows, 2:3]
    return jnp.where(level > recursion, 1.0, 0.0)


def feed_kernel(recursion, following, mixed_ref, state_ref, w_out_ref, small_ref, label_ref,
                w_gate_ref, w_up_ref, w_down_ref, *refs):
    if following:
        w_ref, turn_ref = refs[:2]
        refs = refs[2:]
    (new_ref, middle_ref, n2_ref, gated_ref, up_ref, hidden_ref, both_ref, gate_ref) = refs[:8]
    step = pl.program_id(0)

    @pl.when(step == 0)
    def _():
        att = jnp.dot(mixed_ref[...], w_out_ref[...], preferred_element_type=F32)
        middle = state_ref[...].astype(F32) + att
        middle_ref[...] = middle
        n2_ref[...] = normed(middle, small_ref[RECS + 1:RECS + 2, :]).astype(BF)
        both_ref[...] = att

    n2 = n2_ref[...]
    gated = jnp.dot(n2, w_gate_ref[...], preferred_element_type=F32)
    upward = jnp.dot(n2, w_up_ref[...], preferred_element_type=F32)
    hidden = (gated * jax.nn.sigmoid(gated) * upward).astype(BF)
    gated_ref[...] = gated.astype(BF)
    up_ref[...] = upward.astype(BF)
    hidden_ref[...] = hidden
    both_ref[...] += jnp.dot(hidden, w_down_ref[...], preferred_element_type=F32)

    @pl.when(step == pl.num_programs(0) - 1)
    def _():
        state = state_ref[...].astype(F32)
        router = small_ref[recursion:recursion + 1, :]
        gate = jax.nn.sigmoid(jnp.sum(state * router, axis=-1, keepdims=True))
        active = active_column(label_ref, recursion, state.shape[0])
        gate_ref[...] = gate
        new_ref[...] = state + active * gate * both_ref[...]
        if following:
            project_into(
                new_ref[:following, :], small_ref[RECS:RECS + 1, :], w_ref, turn_ref, *refs[8:11]
            )


def feed(recursion, mixed, state, w_out, small, labels, w_gate, w_up, w_down, following, then=()):
    n, model = mixed.shape
    ff = w_gate.shape[1]
    tile = 512 if ff % 512 == 0 else ff
    across = pl.BlockSpec((model, tile), lambda i: (0, i))
    made = pl.BlockSpec((n, tile), lambda i: (0, i))
    out_specs = [
        whole(n, model), whole(n, model), whole(n, model), made, made, made, whole(n, model),
        whole(n, 1),
    ]
    wide = lambda dtype: jax.ShapeDtypeStruct((n, model), dtype)
    tall = jax.ShapeDtypeStruct((n, ff), BF)
    out_shape = [
        wide(F32), wide(F32), wide(BF), tall, tall, tall, wide(F32),
        jax.ShapeDtypeStruct((n, 1), F32),
    ]
    if following:
        shapes = [(following, model), (CHUNKS, following, LANES), (following, KV_HEADS * LANES)]
        out_specs += [whole(*s) for s in shapes]
        out_shape += [jax.ShapeDtypeStruct(s, BF) for s in shapes]
    return pl.pallas_call(
        functools.partial(feed_kernel, recursion, following),
        grid=(ff // tile,),
        in_specs=[
            whole(n, model), whole(n, model), whole(*w_out.shape), whole(8, model),
            whole(*labels.shape), across, across,
            pl.BlockSpec((tile, model), lambda i: (i, 0)),
        ] + ([whole(*then[0].shape), whole(2, following, LANES)] if following else []),
        out_specs=out_specs,
        out_shape=out_shape,
        compiler_params=pltpu.CompilerParams(vmem_limit_bytes=ROOM),
        name="feed",
    )(mixed, state, w_out, small, labels, w_gate, w_up, w_down, *then)


def feed_back_kernel(recursion, gradient_ref, both_ref, gate_ref, label_ref, state_ref,
                     small_ref, middle_ref, w_out_ref, gated_ref, up_ref, w_gate_ref, w_up_ref,
                     w_down_ref, d_fed_ref, d_gated_ref, d_up_ref, d_att_ref, grad_ref,
                     d_mixed_ref, d_router_ref, d_gain_ref, total):
    step = pl.program_id(0)

    @pl.when(step == 0)
    def _():
        active = active_column(label_ref, recursion, gate_ref.shape[0])
        d_fed_ref[...] = (active * gate_ref[...] * gradient_ref[...].astype(F32)).astype(BF)
        total[...] = jnp.zeros(total.shape, F32)

    d_hidden = lax.dot_general(d_fed_ref[...], w_down_ref[...], NT, preferred_element_type=F32)
    gated, upward = gated_ref[...].astype(F32), up_ref[...].astype(F32)
    sig = jax.nn.sigmoid(gated)
    part = d_hidden * sig
    d_up = (part * gated).astype(BF)
    d_gated = (part * upward * (1.0 + gated * (1.0 - sig))).astype(BF)
    d_up_ref[...] = d_up
    d_gated_ref[...] = d_gated
    total[...] += lax.dot_general(
        d_gated, w_gate_ref[...], NT, preferred_element_type=F32
    ) + lax.dot_general(d_up, w_up_ref[...], NT, preferred_element_type=F32)

    @pl.when(step == pl.num_programs(0) - 1)
    def _():
        gradient, gate = gradient_ref[...].astype(F32), gate_ref[...]
        active = active_column(label_ref, recursion, gate.shape[0])
        router = small_ref[recursion:recursion + 1, :]
        d = total[...]
        v = middle_ref[...]
        inv = lax.rsqrt(jnp.mean(v * v, axis=-1, keepdims=True) + EPS)
        d_gain_ref[...] = jnp.sum(d * v * inv, axis=0, keepdims=True)
        scaled = d * small_ref[RECS + 1:RECS + 2, :]
        dot = jnp.mean(scaled * v, axis=-1, keepdims=True)
        d_middle = inv * scaled - v * (inv * inv * inv * dot)
        d_gate = active * gate * (1.0 - gate) * jnp.sum(
            gradient * both_ref[...], axis=-1, keepdims=True
        )
        d_router_ref[...] = jnp.sum(state_ref[...].astype(F32) * d_gate, axis=0, keepdims=True)
        grad_ref[...] = gradient + d_gate * router + d_middle
        d_att_ref[...] = (active * gate * gradient + d_middle).astype(BF)
        out_back_kernel(d_att_ref, w_out_ref, d_mixed_ref)


def feed_back(recursion, gradient, both, gate, labels, state, small, middle, w_out, gated, upward,
              w_gate, w_up, w_down):
    n, model = both.shape
    ff = w_gate.shape[1]
    tile = 512 if ff % 512 == 0 else ff
    across = pl.BlockSpec((model, tile), lambda i: (0, i))
    made = pl.BlockSpec((n, tile), lambda i: (0, i))
    wide = whole(n, model)
    flat = lambda dtype: jax.ShapeDtypeStruct((n, model), dtype)
    tall = jax.ShapeDtypeStruct((n, ff), BF)
    row = jax.ShapeDtypeStruct((1, model), F32)
    return pl.pallas_call(
        functools.partial(feed_back_kernel, recursion),
        grid=(ff // tile,),
        in_specs=[
            wide, wide, whole(n, 1), whole(*labels.shape), wide, whole(8, model), wide,
            whole(*w_out.shape), made, made, across, across,
            pl.BlockSpec((tile, model), lambda i: (i, 0)),
        ],
        out_specs=[
            wide, made, made, wide, wide, whole(CHUNKS, n, LANES), whole(1, model),
            whole(1, model),
        ],
        out_shape=[
            flat(BF), tall, tall, flat(BF), flat(F32),
            jax.ShapeDtypeStruct((CHUNKS, n, LANES), BF), row, row,
        ],
        scratch_shapes=[pltpu.VMEM((n, model), F32)],
        compiler_params=pltpu.CompilerParams(vmem_limit_bytes=ROOM),
        name="feed_back",
    )(gradient, both, gate, labels, state, small, middle, w_out, gated, upward, w_gate, w_up,
      w_down)


def outer_rows_kernel(count, *refs):
    xs, ds, out_ref = refs[:count], refs[count:2 * count], refs[2 * count]
    total = None
    for x_ref, d_ref in zip(xs, ds):
        part = jnp.dot(jnp.transpose(x_ref[...]), d_ref[...], preferred_element_type=F32)
        total = part if total is None else total + part
    out_ref[...] = total.astype(BF)


def outer_rows(xs, ds, tile):
    rows, columns = xs[0].shape[1], ds[0].shape[1]
    tokens = sum(x.shape[0] for x in xs)
    return pl.pallas_call(
        functools.partial(outer_rows_kernel, len(xs)),
        grid=(rows // tile,),
        in_specs=[pl.BlockSpec((x.shape[0], tile), lambda i: (0, i)) for x in xs]
        + [whole(*d.shape) for d in ds],
        out_specs=pl.BlockSpec((tile, columns), lambda i: (i, 0)),
        out_shape=jax.ShapeDtypeStruct((rows, columns), BF),
        compiler_params=pltpu.CompilerParams(vmem_limit_bytes=ROOM),
        cost_estimate=pl.CostEstimate(
            flops=2 * tokens * rows * columns, transcendentals=0,
            bytes_accessed=2 * (tokens * (columns + rows) + rows * columns),
        ),
        name="outer_rows",
    )(*xs, *ds)


def mm(a, b):
    return jnp.dot(a, b, preferred_element_type=F32)


def mm_tn(a, b):
    return lax.dot_general(a, b, TN, preferred_element_type=F32)


def per_device(topo, *args):
    (tokens, w_query, w_key, w_value, w_out, w_gate, w_up, w_down, router, norm_attn, norm_ffn,
     lengths, depths, padding, cotangent) = args
    rows, model = tokens.shape
    kv_cols = w_key.shape[1]
    ff = w_gate.shape[1]
    shard = w_query.shape[0]
    deep_rows = rows * 3 // 4
    xk, yk, ck = (topo.keys(d) for d in "xyc")

    small = jnp.concatenate([router, norm_attn[:, None], norm_ffn[:, None]], axis=1)
    small = jnp.pad(small, ((0, 0), (0, HD - small.shape[1])))
    w_kv = jnp.stack(
        [w_key.reshape(shard, KV_HEADS, HD), w_value.reshape(shard, KV_HEADS, HD)], axis=2
    ).reshape(shard, 2 * kv_cols)
    first = jnp.concatenate([w_query, small, w_kv], axis=1)
    weight_qkv, weight_g, weight_u, weight_d, weight_o = gather_weights(
        topo, [first, w_gate, w_up, w_down, w_out]
    )

    own = lax.axis_index("tok") * rows + jnp.arange(rows, dtype=jnp.int32)
    eligible = (depths >= 2) & (padding > 0)
    flags = jnp.stack([eligible, ~eligible]).astype(BF)
    upto = (jnp.arange(rows)[:, None] <= jnp.arange(rows)[None, :]).astype(BF)
    counts = mm(flags, upto).astype(jnp.int32)
    slot = jnp.where(eligible, counts[0] - 1, counts[0, -1] + counts[1] - 1)
    chosen = jnp.arange(rows, dtype=jnp.int32)[:, None] == slot[None, :]
    onehot = chosen.astype(BF)
    doc_ends = jnp.cumsum(lengths[0])
    begins = jnp.sum(
        jnp.where(own[:, None] >= doc_ends[None, :], lengths[0][None, :], 0), axis=1
    )
    levels = jnp.where(padding > 0, depths, 0)
    labels = jnp.stack([own, begins, levels])
    labels = jnp.sum(jnp.where(chosen[None], labels[:, None, :], 0), axis=2)
    labels = jnp.pad(labels, ((0, 5), (0, 0)))
    swap = topo.swap_pairs()
    state = lax.ppermute(mm(onehot, tokens).astype(BF), AXES, swap)
    labels = lax.ppermute(labels, AXES, swap)
    cotangent = mm(onehot, cotangent).astype(BF)

    def collect(arrays, ident):
        if small_layer(topo):
            return gather_layer(topo, arrays, ident)
        return [group_gather(topo, v, xk + yk + ck) for v in arrays]

    def distribute(grads, ident):
        if small_layer(topo):
            return reduce_layer(topo, grads, ident)
        return group_scatter(topo, grads, ck + yk + xk)


    pack = (lax.axis_index("grp") * topo.X) + lax.axis_index("tok") % topo.X
    lowest = jnp.min(labels[1])
    span = jnp.stack([lowest // rows, pack + 1]).astype(jnp.int32)
    places = (labels[0] - labels[1]).astype(F32)
    turn = (jnp.arange(LANES) % (HD // 2)).astype(F32)
    freqs = 10000.0 ** (-(turn * 2.0 / HD))
    angles = places[:, None] * freqs[None, :]
    turns = jnp.stack([jnp.cos(angles), jnp.sin(angles)])
    query_labels = {
        n: jnp.concatenate([labels[:, :n]] * SHARES, axis=1) for n in (rows, deep_rows)
    }

    def forward(state, projected, recursion, labels_all=None):
        extra = None
        n1, q, kv = projected
        n = n1.shape[0]
        if recursion == 0:
            kv_all, labels_all = collect([kv, labels], 2)
            kv_all, later = lax.optimization_barrier((kv_all, cotangent))
            later = lax.ppermute(later, AXES, swap)
        else:
            kv_all, = collect([kv], 3)
        kv_all = kv_all.reshape(topo.T * n, 2 * kv_cols)
        mixed, out, stat = attend(n, recursion, span, labels_all, query_labels[n], kv_all, q)
        if recursion == 0:
            mixed, later = lax.optimization_barrier((mixed, later))
            extra = (labels_all, later)
        following = deep_rows if recursion + 1 < RECS else 0
        new, middle, n2, gated, upward, hidden, both, gate, *projected = feed(
            recursion, mixed, state, weight_o, small, labels, weight_g, weight_u, weight_d,
            following, (weight_qkv, turns) if following else (),
        )
        kept = (state, n1, q, kv_all, labels_all, out, stat, mixed, middle, n2, gated, upward,
                hidden, both, gate)
        return (new, projected, kept, extra)

    def backward(gradient, recursion, kept):
        (state, n1, q, kv_all, labels_all, out, stat, mixed, middle, n2, gated, upward, hidden,
         both, gate) = kept
        n = n1.shape[0]
        d_fed, d_gated, d_up, d_att, gradient, d_mixed, d_router, d_gain_two = feed_back(
            recursion, gradient, both, gate, labels, state, small, middle, weight_o, gated,
            upward, weight_g, weight_u, weight_d,
        )
        dq, dkv = attend_back(
            n, recursion, span, labels_all, query_labels[n], kv_all, q, d_mixed, out, stat, turns
        )
        dkv = distribute(dkv.reshape(topo.T, n, 2 * kv_cols), 5 if recursion else 4)
        gradient, dqkv, d_gain_one = project_back(
            gradient, state, small, weight_qkv, turns, dq, dkv
        )
        left = (n1, dqkv, mixed, d_att, n2, d_gated, d_up, hidden, d_fed)
        return (gradient, left, (d_router[0], d_gain_one[0], d_gain_two[0]))

    *projected, small = project(state, weight_qkv, turns)
    whole_state, projected, kept, (labels_all, gradient) = forward(state, projected, 0)
    deep = whole_state
    all_kept = [kept]
    for recursion in range(1, RECS):
        deep, projected, kept, _ = forward(deep, projected, recursion, labels_all)
        all_kept.append(kept)
    final = jnp.concatenate([deep, whole_state[deep_rows:]], axis=0).astype(BF)

    deep_grad = gradient
    lefts, smalls = [], []
    for recursion in reversed(range(1, RECS)):
        deep_grad, left, tiny = backward(deep_grad, recursion, all_kept[recursion])
        lefts.append(left)
        smalls.append(tiny)
    gradient = jnp.concatenate([deep_grad, gradient[deep_rows:].astype(F32)], axis=0)
    gradient, left, tiny = backward(gradient, 0, all_kept[0])
    lefts.append(left)
    smalls.append(tiny)
    final, gradient = lax.optimization_barrier((final, gradient.astype(BF)))
    final = lax.ppermute(final, AXES, swap)
    gradient = lax.ppermute(gradient, AXES, swap)

    n1, dqkv, mixed, d_att, n2, d_gated, d_up, hidden, d_fed = zip(*lefts)

    def outer(xs, ds):
        return mm_tn(jnp.concatenate(xs, axis=0), jnp.concatenate(ds, axis=0))

    cut = lambda v: v.astype(BF).reshape(topo.T, -1, v.shape[-1])
    tiny = jnp.stack(
        [smalls[2][0], smalls[1][0], smalls[0][0],
         smalls[0][1] + smalls[1][1] + smalls[2][1],
         smalls[0][2] + smalls[1][2] + smalls[2][2]], axis=1
    )
    wide_out = -(-(model + tiny.shape[1]) // 256) * 256
    tiny = jnp.pad(tiny, ((0, 0), (0, wide_out - model - tiny.shape[1])))
    grad_qkv, grad_o, grad_gu, grad_down = reduce_gradients(topo, [
        cut(outer(n1, dqkv)),
        cut(jnp.concatenate([outer(mixed, d_att), tiny], axis=1)),
        cut(outer(n2, d_gated)),
        outer_rows(hidden, d_fed, 640).reshape(topo.T, -1, model),
        cut(outer(n2, d_up)),
    ])
    grad_query = grad_qkv[:, :model].astype(F32)
    pair = grad_qkv[:, model + HD:model + HD + 2 * kv_cols].astype(F32)
    pair = pair.reshape(shard, KV_HEADS, 2, HD)
    grad_key = pair[:, :, 0].reshape(shard, kv_cols)
    grad_value = pair[:, :, 1].reshape(shard, kv_cols)
    grad_out = grad_o[:, :model].astype(F32)
    tiny = grad_o[:, model:].astype(F32)
    grad_gate, grad_up = grad_gu[0].astype(F32), grad_gu[1].astype(F32)
    grad_down = grad_down.astype(F32)

    def unsort(v):
        return mm_tn(onehot, v).astype(BF)

    return (
        unsort(final), unsort(gradient), grad_query, grad_key, grad_value, grad_out,
        grad_gate, grad_up, grad_down, tiny[:, :RECS], tiny[:, RECS],
        tiny[:, RECS + 1],
    )


def solution(mesh):
    topo = Topo(mesh.shape["grp"], mesh.shape["tok"])
    both = P(("grp", "tok"))
    wide = P(("grp", "tok"), None)
    rows = P("tok", None)
    row = P("tok")
    return jax.shard_map(
        functools.partial(per_device, topo),
        mesh=mesh,
        in_specs=(wide,) + (rows,) * 8 + (row, row, P("grp", None), both, both, wide),
        out_specs=(wide, wide) + (rows,) * 8 + (row, row),
        check_vma=False,
    )
```

```python
import functools

import jax
import jax.numpy as jnp
from jax import lax
from jax.experimental import pallas as pl
from jax.experimental.pallas import tpu as pltpu
from jax.sharding import PartitionSpec as P

HEADS = 15
KV_HEADS = 5
SHARES = HEADS // KV_HEADS
HD = 64
RECS = 3
EPS = 1e-05
BF = jnp.bfloat16
F32 = jnp.float32
BIG = -1e30
AXES = ("grp", "tok")


class Topo:
    def __init__(self, groups, spread):
        self.G = groups
        self.T = spread
        self.X = spread // groups
        self.Z = groups
        self.Y = groups // 2
        self.bits = {
            "z": self.Z.bit_length() - 1,
            "x": self.X.bit_length() - 1,
            "y": self.Y.bit_length() - 1,
            "c": 1,
        }

    def keys(self, dim):
        return [(dim, k) for k in range(self.bits[dim])]

    def masks(self, key):
        dim, k = key
        if dim == "c":
            return (1, 0)
        if dim == "y":
            return (2 << k, 0)
        if dim == "x":
            return (0, 1 << k)
        return (0, self.X << k)

    def pairs(self, key):
        mg, mt = self.masks(key)
        return [
            (g * self.T + t, (g ^ mg) * self.T + (t ^ mt))
            for g in range(self.G)
            for t in range(self.T)
        ]

    def swap_pairs(self):
        out = []
        for g in range(self.G):
            for t in range(self.T):
                z, x = t // self.X, t % self.X
                out.append((g * self.T + t, z * self.T + g * self.X + x))
        return out

    def bit(self, key):
        mg, mt = self.masks(key)
        if mg:
            return (lax.axis_index("grp") // mg) % 2
        return (lax.axis_index("tok") // mt) % 2


def exchange(topo, arr, key):
    return lax.ppermute(arr, AXES, topo.pairs(key))


def double(topo, arr, key, axis, stack):
    other = exchange(topo, arr, key)
    mine_is_high = topo.bit(key) == 1
    low = jnp.where(mine_is_high, other, arr)
    high = jnp.where(mine_is_high, arr, other)
    if stack:
        return jnp.stack([low, high], axis=axis)
    return jnp.concatenate([low, high], axis=axis)


def halve(topo, arr, key, axis, stack):
    mine_is_high = topo.bit(key) == 1
    if stack:
        low = lax.index_in_dim(arr, 0, axis, keepdims=False)
        high = lax.index_in_dim(arr, 1, axis, keepdims=False)
    else:
        half = arr.shape[axis] // 2
        low = lax.slice_in_dim(arr, 0, half, axis=axis)
        high = lax.slice_in_dim(arr, half, 2 * half, axis=axis)
    send = jnp.where(mine_is_high, low, high).astype(BF)
    keep = jnp.where(mine_is_high, high, low).astype(F32)
    return (keep + exchange(topo, send, key).astype(F32)).astype(BF)


class Piece:
    def __init__(self, array, dim, start, size, core, part):
        self.array, self.dim, self.start, self.size = array, dim, start, size
        self.core, self.part = core, part

    def of(self, ref):
        if self.dim == 0:
            return ref.at[pl.ds(self.start, self.size), :]
        return ref.at[:, pl.ds(self.start, self.size)]


def cut_pieces(shapes):
    near = lambda v, unit: max(unit, int(round(v / unit)) * unit)
    wide_a, wide_g, wide_u, tall = shapes[0][1], shapes[1][1], shapes[2][1], shapes[3][0]
    g = near(wide_g * 0.7, 128)
    u = near(wide_u * 0.65, 128)
    d = near(tall * 0.3, 8)
    return [
        Piece(1, 1, 0, g, 0, 0),
        Piece(4, 1, 0, shapes[4][1], 0, 2),
        Piece(1, 1, g, wide_g - g, 0, 2),
        Piece(0, 1, 0, wide_a, 0, 1),
        Piece(2, 1, u, wide_u - u, 1, 0),
        Piece(3, 0, 0, d, 1, 0),
        Piece(3, 0, d, tall - d, 1, 2),
        Piece(2, 1, 0, u, 1, 1),
    ]


def coordinates(topo):
    g, t = lax.axis_index("grp"), lax.axis_index("tok")
    return lax.rem(t, topo.X), lax.div(g, 2), lax.div(t, topo.X), lax.rem(g, 2)


def gather_kernel(topo, pieces, *refs):
    shards, outs = refs[:5], refs[5:10]
    local_sem, recv_sem, z_sem, x_sem, y_sem, c_sem = refs[10:]
    x, y, z, c = coordinates(topo)
    X, Z, T = topo.X, topo.Z, topo.T
    g, me = lax.axis_index("grp"), lax.axis_index("tok")
    odd = lax.rem(y, 2)
    over_y = {"grp": g + 2 - 4 * odd, "tok": me}
    over_c = {"grp": g + 1 - 2 * c, "tok": me}

    def over_z(k):
        return {"grp": g, "tok": (z + k) * X + x}

    def over_x(k):
        return {"grp": g, "tok": z * X + lax.rem(x + k, X)}

    barrier = pltpu.get_barrier_semaphore()
    partners = [over_y, over_c] + [over_x(k) for k in range(1, X)]
    for partner in partners:
        pl.semaphore_signal(barrier, inc=1, device_id=partner, device_id_type=pl.DeviceIdType.MESH)
    below, above = z > 0, z < Z - 1

    def greet(k):
        pl.semaphore_signal(
            barrier, inc=1, device_id=over_z(k), device_id_type=pl.DeviceIdType.MESH
        )

    pl.when(below)(lambda: greet(-1))
    pl.when(above)(lambda: greet(1))
    own = [
        pltpu.make_async_copy(shards[i], outs[i].at[me], local_sem.at[i]) for i in range(5)
    ]
    for copy in own:
        copy.start()
    pl.semaphore_wait(barrier, len(partners) + below.astype(jnp.int32) + above.astype(jnp.int32))

    def send(p, t, sem, target, mine=False):
        piece = pieces[p]
        landing = piece.of(outs[piece.array].at[t])
        source = piece.of(shards[piece.array]) if mine else landing
        return pltpu.make_async_remote_copy(
            src_ref=source, dst_ref=landing, send_sem=sem, recv_sem=recv_sem.at[p, t],
            device_id=target, device_id_type=pl.DeviceIdType.MESH,
        )

    def arrived(p, t):
        send(p, t, c_sem.at[0, 0], over_c).wait_recv()

    def run(core):
        mine = [p for p in range(len(pieces)) if pieces[p].core == core]
        theirs = [p for p in range(len(pieces)) if pieces[p].core != core]
        slot = {p: i for i, p in enumerate(mine)}

        def inside(p, body):
            part = pieces[p].part
            if part == 1:
                body()
            else:
                pl.when(odd == part // 2)(body)

        def outside(p, body):
            if pieces[p].part != 1:
                pl.when(odd != pieces[p].part // 2)(body)

        def x_copies(p, zz, first):
            t = zz * X + x
            return [
                send(p, t, x_sem.at[slot[p], zz, k - 1], over_x(k), first) for k in range(1, X)
            ]

        def y_copy(p, t):
            return send(p, t, y_sem.at[slot[p], t], over_y)

        def c_copy(p, t):
            return send(p, t, c_sem.at[slot[p], t], over_c)

        def z_copy(p, zz, k, first):
            return send(p, zz * X + x, z_sem.at[slot[p], zz, (k + 1) // 2], over_z(k), first)

        for p in mine:
            def begin(p=p):
                pl.when(below)(lambda: z_copy(p, z, -1, True).start())
                pl.when(above)(lambda: z_copy(p, z, 1, True).start())
                for copy in x_copies(p, z, True):
                    copy.start()
            inside(p, begin)

        def share(p, t):
            if pieces[p].part != 1:
                y_copy(p, t).start()
            c_copy(p, t).start()

        def relay(p, zz, k):
            arrived(p, zz * X + x)
            pl.when(above if k > 0 else below)(lambda: z_copy(p, zz, k, False).start())
            for copy in x_copies(p, zz, False):
                copy.start()
            share(p, zz * X + x)

        def others(p, zz):
            for j in range(1, X):
                t = zz * X + lax.rem(x + j, X)
                arrived(p, t)
                share(p, t)

        def around(k, carry):
            low, high = z - k, z + k
            for p in mine:
                inside(p, lambda p=p: pl.when(low >= 0)(lambda: relay(p, low, 1)))
                inside(p, lambda p=p: pl.when(high < Z)(lambda: relay(p, high, -1)))
            low, high = z - k + 1, z + k - 1
            for p in mine:
                inside(p, lambda p=p: pl.when(low >= 0)(lambda: others(p, low)))
                inside(p, lambda p=p: pl.when((k > 1) & (high < Z))(lambda: others(p, high)))
            return carry

        lax.fori_loop(1, Z + 1, around, 0)

        def rest(t, carry):
            @pl.when(t != me)
            def _():
                for p in mine:
                    def forward(p=p):
                        arrived(p, t)
                        c_copy(p, t).start()
                    outside(p, forward)
            return carry

        lax.fori_loop(0, T, rest, 0)

        def finish(t, carry):
            @pl.when(t != me)
            def _():
                for p in theirs:
                    arrived(p, t)
                for p in mine:
                    c_copy(p, t).wait_send()
                    if pieces[p].part != 1:
                        inside(p, lambda p=p: y_copy(p, t).wait_send())
            return carry

        lax.fori_loop(0, T, finish, 0)
        for p in mine:
            def end(p=p):
                def each(zz, carry):
                    pl.when((zz <= z) & above)(lambda: z_copy(p, zz, 1, False).wait_send())
                    pl.when((zz >= z) & below)(lambda: z_copy(p, zz, -1, False).wait_send())
                    for copy in x_copies(p, zz, False):
                        copy.wait_send()
                    return carry
                lax.fori_loop(0, Z, each, 0)
            inside(p, end)

    pl.when(c == 0)(lambda: run(0))
    pl.when(c == 1)(lambda: run(1))
    for copy in own:
        copy.wait()


def gather_weights(topo, shards):
    pieces = cut_pieces([s.shape for s in shards])
    T = topo.T
    DMA = pltpu.SemaphoreType.DMA
    hbm = pl.BlockSpec(memory_space=pl.ANY)
    outs = pl.pallas_call(
        functools.partial(gather_kernel, topo, pieces),
        in_specs=[hbm] * 5,
        out_specs=[hbm] * 5,
        out_shape=[jax.ShapeDtypeStruct((T,) + s.shape, s.dtype) for s in shards],
        scratch_shapes=[
            DMA((5,)), DMA((len(pieces), T)), DMA((4, topo.Z, 2)), DMA((4, topo.Z, topo.X - 1)),
            DMA((4, T)), DMA((4, T)),
        ],
        compiler_params=pltpu.CompilerParams(collective_id=0, has_side_effects=True),
        name="gather_weights",
    )(*shards)
    return [o.reshape(-1, o.shape[-1]) for o in outs]


class Share:
    def __init__(self, array, start, shape, part):
        self.array, self.start, self.shape, self.part = array, start, shape, part

    def of(self, ref, core, *lead):
        rows, columns = self.shape
        if self.array == 2:
            return ref.at[lead + (slice(None), pl.ds(self.start, columns))]
        if self.array == 3:
            at = pl.multiple_of(core * rows, rows)
            return ref.at[lead + (pl.ds(at, rows), slice(None))]
        at = pl.multiple_of(core * columns, 128)
        return ref.at[lead + (slice(None), pl.ds(at, columns))]


def cut_shares(shapes):
    rows, ff = shapes[2][1], shapes[2][2]
    one = ff * 3 // 20 // 128 * 128
    two = ff * 33 // 40 // 128 * 128
    return [
        Share(2, one, (rows, two - one), 0),
        Share(3, 0, (shapes[3][1] // 2, shapes[3][2]), 2),
        Share(2, two, (rows, ff - two), 2),
        Share(0, 0, (rows, shapes[0][2] // 2), 1),
        Share(1, 0, (rows, shapes[1][2] // 2), 1),
        Share(2, 0, (rows, one), 1),
    ]


def reduce_kernel(topo, shares, *refs):
    grads, outs = refs[:5], refs[5:9]
    count = len(shares)
    groups = []
    at = 9
    for _ in range(7):
        groups.append(refs[at:at + count])
        at += count
    held, from_c, from_y, from_x, from_low, from_high, from_f = groups
    (load_sem, c_send, c_recv, y_send, y_recv, x_send, x_recv, z_send, z_recv, f_send, f_recv,
     o_send, o_recv, o_local) = refs[at:]
    x, y, z, c = coordinates(topo)
    X, Z, T = topo.X, topo.Z, topo.T
    g, me = lax.axis_index("grp"), lax.axis_index("tok")
    odd = lax.rem(y, 2)
    below, above = z > 0, z < Z - 1
    kind = pl.DeviceIdType.MESH

    def over_y(k):
        high = lax.rem(lax.div(y, 1 << k), 2)
        return {"grp": g + (2 - 4 * high) * (1 << k), "tok": me}

    over_c = {"grp": g + 1 - 2 * c, "tok": me}

    def over_z(k):
        return {"grp": g, "tok": (z + k) * X + x}

    def over_x(k):
        return {"grp": g, "tok": z * X + lax.rem(x + k, X)}

    barrier = pltpu.get_barrier_semaphore()
    partners = [over_c] + [over_y(k) for k in range(topo.bits["y"])]
    partners += [over_x(k) for k in range(1, X)]

    def greet(partner):
        pl.semaphore_signal(barrier, inc=1, device_id=partner, device_id_type=kind)

    for partner in partners:
        greet(partner)
    pl.when(below)(lambda: greet(over_z(-1)))
    pl.when(above)(lambda: greet(over_z(1)))
    every = range(count)

    def source(s, core, t, up):
        place = {2: 4 if up else 2, 3: 3}.get(s.array, s.array)
        return s.of(grads[place], core, t)

    def load(p, t, up=False):
        return pltpu.make_async_copy(
            source(shares[p], c, t, up), held[p].at[t], load_sem.at[p, t]
        )

    def start(p, make, up_core):
        if shares[p].array == 2:
            pl.when(c != up_core)(lambda: make(False).start())
            pl.when(c == up_core)(lambda: make(True).start())
        else:
            make(False).start()

    def remote(source, landing, send, recv, target):
        return pltpu.make_async_remote_copy(
            src_ref=source, dst_ref=landing, send_sem=send, recv_sem=recv, device_id=target,
            device_id_type=kind,
        )

    def c_copy(p, t, up=False):
        return remote(
            source(shares[p], 1 - c, t, up), from_c[p].at[t], c_send.at[p, t], c_recv.at[p, t],
            over_c,
        )

    def y_copy(p, t):
        return remote(
            held[p].at[t], from_y[p].at[t], y_send.at[p, t], y_recv.at[p, t], over_y(0)
        )

    def x_copy(p, zz, k):
        t = zz * X + lax.rem(x + k, X)
        return remote(
            held[p].at[t], from_x[p].at[zz, k - 1], x_send.at[p, zz, k - 1],
            x_recv.at[p, zz, k - 1], over_x(k),
        )

    def z_copy(p, zz, k):
        landing = from_low if k > 0 else from_high
        way = (k + 1) // 2
        return remote(
            held[p].at[zz * X + x], landing[p].at[zz], z_send.at[p, zz, way],
            z_recv.at[p, zz, way], over_z(k),
        )

    def f_copy(p, k):
        return remote(
            held[p].at[me], from_f[p].at[k], f_send.at[p, k], f_recv.at[p, k], over_y(k)
        )

    def result(s, core):
        if s.array == 2:
            return outs[2].at[core, :, pl.ds(s.start, s.shape[1])]
        return s.of(outs[s.array], core)

    def o_copy(p):
        s = shares[p]
        return remote(
            held[p].at[me], result(s, c), o_send.at[p], o_recv.at[p], over_c
        )

    def o_arrived(p):
        s = shares[p]
        return remote(
            held[p].at[me], result(s, 1 - c), o_send.at[p], o_recv.at[p], over_c
        )

    def o_keep(p):
        s = shares[p]
        return pltpu.make_async_copy(held[p].at[me], result(s, c), o_local.at[p])

    def add(p, t, other):
        held[p][t] = held[p][t] + other

    def layers(body):
        def step(i, carry):
            k = Z - 1 - i
            pl.when(z + k < Z)(lambda: body(z + k))
            pl.when((k > 0) & (z - k >= 0))(lambda: body(z - k))
            return carry
        return step

    def inside(p, body):
        if shares[p].part == 1:
            body()
        else:
            pl.when(odd == shares[p].part // 2)(body)

    def outside(p, body):
        if shares[p].part != 1:
            pl.when(odd != shares[p].part // 2)(body)

    def start_loads(zz):
        def each(j, carry):
            t = zz * X + lax.rem(x + j, X)
            for p in every:
                start(p, lambda up, p=p: load(p, t, up), 1)
            return carry
        lax.fori_loop(0, X, each, 0)

    lax.fori_loop(0, Z, layers(start_loads), 0)
    pl.semaphore_wait(barrier, len(partners) + below.astype(jnp.int32) + above.astype(jnp.int32))

    def start_cores(zz):
        def each(j, carry):
            t = zz * X + lax.rem(x + j, X)
            for p in every:
                start(p, lambda up, p=p: c_copy(p, t, up), 0)
            return carry
        lax.fori_loop(0, X, each, 0)

    lax.fori_loop(0, Z, layers(start_cores), 0)

    def cores(zz):
        def each(j, carry):
            t = zz * X + lax.rem(x + j + 1, X)
            for p in every:
                load(p, t).wait()
                c_copy(p, t).wait_recv()
                add(p, t, from_c[p][t])
                outside(p, lambda p=p: y_copy(p, t).start())
                if shares[p].part == 1:
                    for k in range(1, X):
                        pl.when(j + 1 == k)(lambda p=p, k=k: x_copy(p, zz, k).start())
            return carry
        lax.fori_loop(0, X, each, 0)

    lax.fori_loop(0, Z, layers(cores), 0)

    def over(zz):
        def each(j, carry):
            t = zz * X + lax.rem(x + j + 1, X)
            for p in every:
                if shares[p].part != 1:
                    def body(p=p):
                        y_copy(p, t).wait_recv()
                        add(p, t, from_y[p][t])
                        for k in range(1, X):
                            pl.when(j + 1 == k)(lambda: x_copy(p, zz, k).start())
                    inside(p, body)
            return carry
        lax.fori_loop(0, X, each, 0)

    def join(p, zz):
        t = zz * X + x
        for k in range(1, X):
            x_copy(p, zz, k).wait_recv()
            add(p, t, from_x[p][zz, k - 1])

        def low():
            z_copy(p, zz, 1).wait_recv()
            add(p, t, from_low[p][zz])

        def high():
            z_copy(p, zz, -1).wait_recv()
            add(p, t, from_high[p][zz])

        pl.when((zz >= z) & below)(low)
        pl.when((zz <= z) & above)(high)
        pl.when(zz > z)(lambda: z_copy(p, zz, 1).start())
        pl.when(zz < z)(lambda: z_copy(p, zz, -1).start())

    single = topo.bits["y"] == 1

    def first_joins(zz):
        for p in every:
            if shares[p].part == 1:
                join(p, zz)
                if single:
                    pl.when(zz == z)(lambda p=p: f_copy(p, 0).start())

    def last_joins(zz):
        for p in every:
            if shares[p].part != 1:
                def body(p=p):
                    join(p, zz)
                    if single:
                        pl.when(zz == z)(lambda: f_copy(p, 0).start())
                inside(p, body)

    def main(i, carry):
        @pl.when(i < Z)
        def _():
            layers(first_joins)(i, 0)
            layers(over)(i, 0)

        @pl.when(i > 0)
        def _():
            layers(last_joins)(i - 1, 0)

        return carry

    lax.fori_loop(0, Z + 1, main, 0)

    for k in range(1, topo.bits["y"]):
        for p in every:
            inside(p, lambda p=p: f_copy(p, k).start())
        for p in every:
            def fold(p=p):
                f_copy(p, k).wait()
                add(p, me, from_f[p][k])
            inside(p, fold)
    if not single:
        for p in every:
            inside(p, lambda p=p: f_copy(p, 0).start())
    for p in every:
        if shares[p].part == 1:
            f_copy(p, 0).wait()
            add(p, me, from_f[p][0])
        else:
            def take(p=p):
                f_copy(p, 0).wait_recv()
                held[p][me] = from_f[p][0]
            outside(p, lambda p=p: y_copy(p, me).wait_send())
            outside(p, take)
        o_copy(p).start()
        o_keep(p).start()

    def ends(t, carry):
        for p in every:
            c_copy(p, t).wait_send()
            outside(p, lambda p=p: pl.when(t != me)(lambda: y_copy(p, t).wait_send()))
        return carry

    lax.fori_loop(0, T, ends, 0)

    def z_ends(zz, carry):
        for p in every:
            def body(p=p):
                for k in range(1, X):
                    x_copy(p, zz, k).wait_send()
                pl.when(zz > z)(lambda: z_copy(p, zz, 1).wait_send())
                pl.when(zz < z)(lambda: z_copy(p, zz, -1).wait_send())
            inside(p, body)
        return carry

    lax.fori_loop(0, Z, z_ends, 0)
    for p in every:
        if shares[p].part != 1:
            inside(p, lambda p=p: f_copy(p, 0).wait_send())
        o_copy(p).wait_send()
        o_arrived(p).wait_recv()
        o_keep(p).wait()


def reduce_gradients(topo, grads):
    shares = cut_shares([v.shape for v in grads])
    X, Z, T = topo.X, topo.Z, topo.T
    n = len(shares)
    folds = max(1, topo.bits["y"])
    DMA = pltpu.SemaphoreType.DMA
    hbm = pl.BlockSpec(memory_space=pl.ANY)
    lead = [(T,), (T,), (T,), (Z, X - 1), (Z,), (Z,), (folds,)]
    rooms = [
        pltpu.VMEM(front + s.shape, BF)
        for front in lead for s in shares
    ]
    outs = [grads[0].shape[1:], grads[1].shape[1:], (2,) + grads[2].shape[1:], grads[3].shape[1:]]
    return pl.pallas_call(
        functools.partial(reduce_kernel, topo, shares),
        in_specs=[hbm] * 5,
        out_specs=[hbm] * 4,
        out_shape=[jax.ShapeDtypeStruct(s, BF) for s in outs],
        scratch_shapes=rooms + [
            DMA((n, T)), DMA((n, T)), DMA((n, T)), DMA((n, T)), DMA((n, T)),
            DMA((n, Z, X - 1)), DMA((n, Z, X - 1)), DMA((n, Z, 2)), DMA((n, Z, 2)),
            DMA((n, folds)), DMA((n, folds)), DMA((n,)), DMA((n,)), DMA((n,)),
        ],
        compiler_params=pltpu.CompilerParams(
            collective_id=1, has_side_effects=True, vmem_limit_bytes=60 << 20
        ),
        name="reduce_gradients",
    )(*grads)


def group_order(topo):
    return list(reversed(topo.keys("y"))) + topo.keys("c") + list(reversed(topo.keys("x")))


def group_gather(topo, arr, order):
    names = group_order(topo)
    held = []
    shape = arr.shape
    for key in order:
        place = sum(1 for h in held if names.index(h) < names.index(key))
        arr = double(topo, arr, key, place, True)
        held.append(key)
    return arr.reshape((topo.T,) + shape)


def group_scatter(topo, arr, order):
    names = group_order(topo)
    held = list(names)
    arr = arr.reshape((2,) * len(names) + arr.shape[1:])
    for key in order:
        arr = halve(topo, arr, key, held.index(key), True)
        held.remove(key)
    return arr


def small_layer(topo):
    return topo.X == 2 and topo.Y == 2


class Layer:
    def __init__(self, topo):
        self.topo = topo
        x, y, z, c = coordinates(topo)
        self.c = c
        far_x, far_y = 1 - x, 1 - y
        a = (x + c * (far_x - x), far_y + c * (y - far_y))
        b = (far_x + c * (x - far_x), y + c * (far_y - y))
        self.chips = [(x, y), a, b, (far_x, far_y)]
        self.z = z

    def pack(self, slot, core):
        x, y = self.chips[slot]
        return (y * 2 + core) * self.topo.X + x

    def device(self, slot, core):
        x, y = self.chips[slot]
        return {"grp": y * 2 + core, "tok": self.z * self.topo.X + x}

    def meet(self):
        barrier = pltpu.get_barrier_semaphore()
        for target in (self.device(1, self.c), self.device(2, self.c), self.device(0, 1 - self.c)):
            pl.semaphore_signal(
                barrier, inc=1, device_id=target, device_id_type=pl.DeviceIdType.MESH
            )
        pl.semaphore_wait(barrier, 3)


def remote_copy(source, landing, send, recv, target):
    return pltpu.make_async_remote_copy(
        src_ref=source, dst_ref=landing, send_sem=send, recv_sem=recv, device_id=target,
        device_id_type=pl.DeviceIdType.MESH,
    )


def group_gather_kernel(topo, count, *refs):
    mine, outs = refs[:count], refs[count:2 * count]
    local_sem, send_sem, recv_sem = refs[2 * count:]
    layer = Layer(topo)
    c = layer.c
    arrays = range(count)
    a, b, sibling = layer.device(1, c), layer.device(2, c), layer.device(0, 1 - c)
    own = layer.pack(0, c)

    def send(i, way, pack, target):
        landing = outs[i].at[pack]
        source = mine[i] if way in (0, 1, 3) else landing
        return remote_copy(source, landing, send_sem.at[i, way], recv_sem.at[i, pack], target)

    ways = [
        (0, own, a), (1, own, b), (2, layer.pack(1, c), b), (3, own, sibling),
        (4, layer.pack(1, c), sibling), (5, layer.pack(2, c), sibling),
        (6, layer.pack(3, c), sibling),
    ]

    def start(k):
        for i in arrays:
            send(i, *ways[k]).start()

    def arrived(pack):
        for i in arrays:
            send(i, 2, pack, sibling).wait_recv()

    keep = [pltpu.make_async_copy(mine[i], outs[i].at[own], local_sem.at[i]) for i in arrays]
    for copy in keep:
        copy.start()
    layer.meet()
    start(0)
    start(1)
    start(3)
    arrived(layer.pack(1, c))
    start(2)
    start(4)
    arrived(layer.pack(2, c))
    start(5)
    arrived(layer.pack(3, c))
    start(6)
    for slot in range(4):
        arrived(layer.pack(slot, 1 - c))
    for way in ways:
        for i in arrays:
            send(i, *way).wait_send()
    for copy in keep:
        copy.wait()


def gather_layer(topo, arrays, ident):
    DMA = pltpu.SemaphoreType.DMA
    hbm = pl.BlockSpec(memory_space=pl.ANY)
    n = len(arrays)
    return pl.pallas_call(
        functools.partial(group_gather_kernel, topo, n),
        in_specs=[hbm] * n,
        out_specs=[hbm] * n,
        out_shape=[jax.ShapeDtypeStruct((topo.T,) + v.shape, v.dtype) for v in arrays],
        scratch_shapes=[DMA((n,)), DMA((n, 7)), DMA((n, topo.T))],
        compiler_params=pltpu.CompilerParams(collective_id=ident, has_side_effects=True),
        name="gather_layer",
    )(*arrays)


def group_reduce_kernel(topo, grads, out, held, from_c, from_b, from_a, c_send, c_recv, send_sem,
                        recv_sem):
    layer = Layer(topo)
    c = layer.c
    a, b, sibling = layer.device(1, c), layer.device(2, c), layer.device(0, 1 - c)
    order = (3, 2, 1, 0)

    def c_copy(slot):
        theirs = (0, 2, 1, 3)[slot]
        return remote_copy(
            grads.at[layer.pack(slot, 1 - c)], from_c.at[theirs], c_send.at[theirs],
            c_recv.at[theirs], sibling,
        )

    def c_arrived(slot):
        remote_copy(
            grads.at[layer.pack(slot, c)], from_c.at[slot], c_send.at[slot], c_recv.at[slot],
            sibling,
        ).wait_recv()

    across = remote_copy(held.at[3], from_b.at[1], send_sem.at[0], recv_sem.at[0], b)
    direct = remote_copy(held.at[2], from_b.at[0], send_sem.at[1], recv_sem.at[1], b)
    passed = remote_copy(held.at[1], from_a, send_sem.at[2], recv_sem.at[2], a)

    layer.meet()
    for slot in (3, 1, 2, 0):
        c_copy(slot).start()
    for slot in order:
        c_arrived(slot)
        held[slot] = grads[layer.pack(slot, c)] + from_c[slot]
        if slot == 3:
            across.start()
        if slot == 2:
            direct.start()
    across.wait_recv()
    held[1] = held[1] + from_b[1]
    passed.start()
    direct.wait_recv()
    held[0] = held[0] + from_b[0]
    passed.wait_recv()
    out[...] = held[0] + from_a[...]
    across.wait_send()
    direct.wait_send()
    passed.wait_send()
    for slot in range(4):
        c_copy(slot).wait_send()


def reduce_layer(topo, grads, ident):
    DMA = pltpu.SemaphoreType.DMA
    block = grads.shape[1:]
    return pl.pallas_call(
        functools.partial(group_reduce_kernel, topo),
        in_specs=[pl.BlockSpec(memory_space=pltpu.VMEM)],
        out_specs=pl.BlockSpec(memory_space=pltpu.VMEM),
        out_shape=jax.ShapeDtypeStruct(block, BF),
        scratch_shapes=[
            pltpu.VMEM((4,) + block, BF), pltpu.VMEM((4,) + block, BF),
            pltpu.VMEM((2,) + block, BF), pltpu.VMEM(block, BF),
            DMA((4,)), DMA((4,)), DMA((3,)), DMA((3,)),
        ],
        compiler_params=pltpu.CompilerParams(
            collective_id=ident, has_side_effects=True, vmem_limit_bytes=32 << 20
        ),
        name="reduce_layer",
    )(grads)


NT = (((1,), (1,)), ((), ()))
TN = (((0,), (0,)), ((), ()))
LANES = 2 * HD
CHUNKS = (HEADS + 1) // 2
ROOM = 60 << 20


def lanes_of(rows):
    return lax.broadcasted_iota(jnp.int32, (rows, LANES), 1)


def spin(v):
    first = lax.rem(lanes_of(v.shape[0]), HD) < HD // 2
    return jnp.where(first, -pltpu.roll(v, LANES - HD // 2, 1), pltpu.roll(v, HD // 2, 1))


def whole(*shape):
    return pl.BlockSpec(shape, lambda *i: (0,) * len(shape))


def normed(v, gain):
    return v * lax.rsqrt(jnp.mean(v * v, axis=-1, keepdims=True) + EPS) * gain


def project_kernel(state_ref, w_ref, turn_ref, n1_ref, q_ref, kv_ref, small_ref):
    start = (CHUNKS - 1) * LANES
    small = jnp.transpose(w_ref[:, start:start + LANES].astype(F32))[HD:HD + 8]
    small_ref[...] = small
    project_into(
        state_ref[...].astype(F32), small[RECS:RECS + 1], w_ref, turn_ref, n1_ref, q_ref, kv_ref
    )


def project(state, w, turns):
    n, model = state.shape
    return pl.pallas_call(
        project_kernel,
        grid=(1,),
        in_specs=[whole(n, model), whole(*w.shape), whole(*turns.shape)],
        out_specs=[
            whole(n, model), whole(CHUNKS, n, LANES), whole(n, KV_HEADS * LANES),
            whole(8, model),
        ],
        out_shape=[
            jax.ShapeDtypeStruct((n, model), BF),
            jax.ShapeDtypeStruct((CHUNKS, n, LANES), BF),
            jax.ShapeDtypeStruct((n, KV_HEADS * LANES), BF),
            jax.ShapeDtypeStruct((8, model), F32),
        ],
        compiler_params=pltpu.CompilerParams(vmem_limit_bytes=ROOM),
        name="project",
    )(state, w, turns)


def attend_kernel(rows, recursion, span, key_ref, query_ref, kv_ref, q_ref, mixed_ref, out_ref, stat_ref,
                  stacked, mixing, tops, sums):
    low = lanes_of(rows) < HD
    wide = SHARES * rows
    for h in range(KV_HEADS):
        for j in range(SHARES):
            head = h * SHARES + j
            chunk = q_ref[head // 2].astype(F32)
            if head % 2:
                chunk = pltpu.roll(chunk, HD, 1)
            stacked[h, j * rows:(j + 1) * rows, :] = jnp.where(low, chunk, 0.0).astype(BF)
    mixing[...] = jnp.zeros(mixing.shape, F32)
    sums[...] = jnp.zeros(sums.shape, F32)
    tops[...] = jnp.full(tops.shape, BIG, F32)

    def body(t, carry):
        at = pl.ds(pl.multiple_of(t * rows, rows), rows)
        bias = block_bias(key_ref[t], query_ref, recursion, rows)
        def score(h):
            kv = kv_ref[at, h * LANES:(h + 1) * LANES]
            return lax.dot_general(kv, stacked[h], NT, preferred_element_type=F32) + bias

        def end(h, p, fade):
            kv = kv_ref[at, h * LANES:(h + 1) * LANES]
            mixing[h] = mixing[h] * fade + lax.dot_general(
                kv[:, HD:], p, TN, preferred_element_type=F32
            )

        ahead = score(0)
        before = None
        for h in range(KV_HEADS):
            s = ahead
            if h + 1 < KV_HEADS:
                ahead = score(h + 1)
            if before is not None:
                end(*before)
            old = tops[h, 0:1, :]
            top = jnp.max(s.reshape(rows // 8, 8, wide), axis=0)
            top = jnp.maximum(old, jnp.max(top, axis=0, keepdims=True))
            p = jnp.exp(s - top)
            fade = jnp.exp(old - top)
            sums[h] = sums[h] * fade + jnp.sum(p.reshape(rows // 8, 8, wide), axis=0)
            tops[h] = jnp.broadcast_to(top, (8, wide))
            before = (h, p.astype(BF), fade)
        end(*before)
        return carry

    lax.fori_loop(span[0], span[1], body, 0)
    for h in range(KV_HEADS):
        total = jnp.sum(sums[h], axis=0, keepdims=True)
        stat_ref[h] = tops[h] + jnp.log(total)
        mixing[h] = mixing[h] / total
    for j in range(CHUNKS):
        both = head_pair(mixing, j, rows)
        out_ref[j] = both
        size = min(LANES, HEADS * HD - j * LANES)
        mixed_ref[:, j * LANES:j * LANES + size] = both.astype(BF)[:, :size]


def block_bias(labels, query_ref, recursion, rows):
    keys = jnp.transpose(labels.astype(F32))[:rows]
    order, level = keys[:, 0:1], keys[:, 2:3]
    live = jnp.where(level > recursion, order, -1.0)
    place, begin = query_ref[0:1, :].astype(F32), query_ref[1:2, :].astype(F32)
    allowed = ((live >= begin) & (live <= place)) | (order == place)
    return jnp.where(allowed, 0.0, BIG)


def head_pair(mixing, j, rows):
    def one(head):
        if head >= HEADS:
            return jnp.zeros((HD, rows), F32)
        at = head % SHARES * rows
        return mixing[head // SHARES, :, at:at + rows]

    return jnp.transpose(jnp.concatenate([one(2 * j), one(2 * j + 1)], axis=0))


def attend(rows, recursion, span, key_labels, query_labels, kv_all, q):
    count, columns = kv_all.shape
    wide = SHARES * rows
    return pl.pallas_call(
        functools.partial(attend_kernel, rows, recursion),
        grid_spec=pltpu.PrefetchScalarGridSpec(
            num_scalar_prefetch=1,
            grid=(1,),
            in_specs=[
                whole(*key_labels.shape), whole(8, wide), whole(count, columns),
                whole(CHUNKS, rows, LANES),
            ],
            out_specs=[
                whole(rows, HEADS * HD), whole(CHUNKS, rows, LANES), whole(KV_HEADS, 8, wide),
            ],
            scratch_shapes=[
                pltpu.VMEM((KV_HEADS, wide, LANES), BF), pltpu.VMEM((KV_HEADS, HD, wide), F32),
                pltpu.VMEM((KV_HEADS, 8, wide), F32), pltpu.VMEM((KV_HEADS, 8, wide), F32),
            ],
        ),
        out_shape=[
            jax.ShapeDtypeStruct((rows, HEADS * HD), BF),
            jax.ShapeDtypeStruct((CHUNKS, rows, LANES), F32),
            jax.ShapeDtypeStruct((KV_HEADS, 8, wide), F32),
        ],
        compiler_params=pltpu.CompilerParams(vmem_limit_bytes=62 << 20),
        cost_estimate=pl.CostEstimate(
            flops=16 * KV_HEADS * wide * count * HD, bytes_accessed=4 * count * columns,
            transcendentals=KV_HEADS * wide * count,
        ),
        name="attend",
    )(span, key_labels, query_labels, kv_all, q)


def attend_back_kernel(rows, recursion, span, key_ref, query_ref, kv_ref, q_ref, d_ref, out_ref, stat_ref,
                       turn_ref, dq_ref, dkv_ref, stacked, part, mixing, deltas):
    low = lanes_of(rows) < HD
    wide = SHARES * rows
    ones = jnp.ones((8, LANES), BF)
    for h in range(KV_HEADS):
        for j in range(SHARES):
            head = h * SHARES + j
            q = q_ref[head // 2].astype(F32)
            d = d_ref[head // 2].astype(F32)
            if head % 2:
                q = pltpu.roll(q, HD, 1)
            product = d * out_ref[head // 2]
            mine = ~low if head % 2 else low
            if head % 2 == 0:
                d = pltpu.roll(d, HD, 1)
            at = pl.ds(j * rows, rows)
            stacked[h, at, :] = jnp.where(low, q, d).astype(BF)
            part[at, :] = jnp.where(mine, product, 0.0)
        coarse = part[...].astype(BF)
        fine = (part[...] - coarse.astype(F32)).astype(BF)
        deltas[h] = lax.dot_general(
            ones, coarse, NT, preferred_element_type=F32
        ) + lax.dot_general(ones, fine, NT, preferred_element_type=F32)
    dkv_ref[...] = jnp.zeros(dkv_ref.shape, BF)
    mixing[...] = jnp.zeros(mixing.shape, F32)

    def body(t, carry):
        at = pl.ds(pl.multiple_of(t * rows, rows), rows)
        bias = block_bias(key_ref[t], query_ref, recursion, rows)
        for h in range(KV_HEADS):
            kv = kv_ref[at, h * LANES:(h + 1) * LANES]
            zero = jnp.zeros_like(kv)
            queries = stacked[h]
            s = lax.dot_general(jnp.where(low, kv, zero), queries, NT, preferred_element_type=F32)
            p = jnp.exp(s + bias - stat_ref[h, 0:1, :])
            dp = lax.dot_general(jnp.where(low, zero, kv), queries, NT, preferred_element_type=F32)
            ds = (p * (dp - deltas[h, 0:1, :])).astype(BF)
            dk = jnp.dot(ds, queries, preferred_element_type=F32)
            dv = jnp.dot(p.astype(BF), queries, preferred_element_type=F32)
            dkv_ref[at, h * LANES:(h + 1) * LANES] = jnp.where(low, dk, dv).astype(BF)
            mixing[h] += lax.dot_general(kv[:, :HD], ds, TN, preferred_element_type=F32)
        return carry

    lax.fori_loop(span[0], span[1], body, 0)
    cosine, sine = turn_ref[0], turn_ref[1]
    for j in range(CHUNKS):
        both = head_pair(mixing, j, rows) * HD ** -0.5
        both = both * cosine - spin(both) * sine
        dq_ref[:, j * LANES:(j + 1) * LANES] = both.astype(BF)


def attend_back(rows, recursion, span, key_labels, query_labels, kv_all, q, d_mixed, out, stat, turns):
    count, columns = kv_all.shape
    wide = SHARES * rows
    return pl.pallas_call(
        functools.partial(attend_back_kernel, rows, recursion),
        grid_spec=pltpu.PrefetchScalarGridSpec(
            num_scalar_prefetch=1,
            grid=(1,),
            in_specs=[
                whole(*key_labels.shape), whole(8, wide), whole(count, columns),
                whole(CHUNKS, rows, LANES), whole(CHUNKS, rows, LANES),
                whole(CHUNKS, rows, LANES), whole(KV_HEADS, 8, wide), whole(2, rows, LANES),
            ],
            out_specs=[whole(rows, CHUNKS * LANES), whole(count, columns)],
            scratch_shapes=[
                pltpu.VMEM((KV_HEADS, wide, LANES), BF), pltpu.VMEM((wide, LANES), F32),
                pltpu.VMEM((KV_HEADS, HD, wide), F32), pltpu.VMEM((KV_HEADS, 8, wide), F32),
            ],
        ),
        out_shape=[
            jax.ShapeDtypeStruct((rows, CHUNKS * LANES), BF),
            jax.ShapeDtypeStruct((count, columns), BF),
        ],
        compiler_params=pltpu.CompilerParams(vmem_limit_bytes=62 << 20),
        name="attend_back",
    )(span, key_labels, query_labels, kv_all, q, d_mixed, out, stat, turns)


def out_back_kernel(d_ref, w_ref, out_ref):
    d = d_ref[...]
    for j in range(CHUNKS):
        size = min(LANES, w_ref.shape[0] - j * LANES)
        v = lax.dot_general(
            d, w_ref[j * LANES:j * LANES + size, :], NT, preferred_element_type=F32
        ).astype(BF)
        if size < LANES:
            v = jnp.concatenate([v, jnp.zeros((d.shape[0], LANES - size), BF)], axis=1)
        out_ref[j] = v


def project_back_kernel(gradient_ref, state_ref, small_ref, w_ref, turn_ref, dq_ref, raw_ref,
                        grad_ref, joint_ref, dgain_ref):
    cosine, sine = turn_ref[0], turn_ref[1]
    key = lanes_of(dq_ref.shape[0]) < HD
    for j in range(KV_HEADS):
        v = raw_ref[:, j * LANES:(j + 1) * LANES].astype(F32)
        turned = v * cosine - spin(v) * sine
        at = (CHUNKS + j) * LANES
        joint_ref[:, at:at + LANES] = jnp.where(key, turned, v).astype(BF)
    split, full = CHUNKS * LANES, w_ref.shape[1]
    joint_ref[:, :split] = dq_ref[...]
    if joint_ref.shape[1] > full:
        joint_ref[:, full:] = jnp.zeros((key.shape[0], joint_ref.shape[1] - full), BF)
    d = lax.dot_general(joint_ref[:, :full], w_ref[...], NT, preferred_element_type=F32)
    v = state_ref[...].astype(F32)
    inv = lax.rsqrt(jnp.mean(v * v, axis=-1, keepdims=True) + EPS)
    scaled = d * small_ref[RECS:RECS + 1, :]
    dot = jnp.mean(scaled * v, axis=-1, keepdims=True)
    grad_ref[...] = gradient_ref[...] + inv * scaled - v * (inv * inv * inv * dot)
    dgain_ref[...] = jnp.sum(d * v * inv, axis=0, keepdims=True)


def project_back(gradient, state, small, w, turns, dq, dkv):
    n, model = dq.shape[0], state.shape[1]
    joint = -(-w.shape[1] // 256) * 256
    return pl.pallas_call(
        project_back_kernel,
        grid=(1,),
        in_specs=[
            whole(n, model), whole(n, model), whole(8, model), whole(*w.shape),
            whole(2, n, LANES), whole(*dq.shape), whole(*dkv.shape),
        ],
        out_specs=[whole(n, model), whole(n, joint), whole(1, model)],
        out_shape=[
            jax.ShapeDtypeStruct((n, model), F32),
            jax.ShapeDtypeStruct((n, joint), BF),
            jax.ShapeDtypeStruct((1, model), F32),
        ],
        compiler_params=pltpu.CompilerParams(vmem_limit_bytes=ROOM),
        name="project_back",
    )(gradient, state, small, w, turns, dq, dkv)


def project_into(state, gain, w_ref, turn_ref, n1_ref, q_ref, kv_ref):
    n1 = normed(state, gain).astype(BF)
    n1_ref[...] = n1
    rows = n1.shape[0]
    cosine, sine = turn_ref[0, :rows], turn_ref[1, :rows]
    key = lanes_of(rows) < HD
    columns = w_ref.shape[1]
    for start in range(0, columns, 2 * LANES):
        wide = min(2 * LANES, columns - start)
        both = jnp.dot(n1, w_ref[:, start:start + wide], preferred_element_type=F32)
        for half in range(wide // LANES):
            j = start // LANES + half
            v = both[:, half * LANES:(half + 1) * LANES]
            turned = v * cosine + spin(v) * sine
            if j < CHUNKS:
                q_ref[j] = (turned * HD ** -0.5).astype(BF)
            else:
                j -= CHUNKS
                kv_ref[:, j * LANES:(j + 1) * LANES] = jnp.where(key, turned, v).astype(BF)


def active_column(label_ref, recursion, rows):
    level = jnp.transpose(label_ref[...].astype(F32))[:rows, 2:3]
    return jnp.where(level > recursion, 1.0, 0.0)


def feed_kernel(recursion, following, mixed_ref, state_ref, w_out_ref, small_ref, label_ref,
                w_gate_ref, w_up_ref, w_down_ref, *refs):
    if following:
        w_ref, turn_ref = refs[:2]
        refs = refs[2:]
    (new_ref, middle_ref, n2_ref, gated_ref, up_ref, hidden_ref, both_ref, gate_ref) = refs[:8]
    step = pl.program_id(0)

    @pl.when(step == 0)
    def _():
        att = jnp.dot(mixed_ref[...], w_out_ref[...], preferred_element_type=F32)
        middle = state_ref[...].astype(F32) + att
        middle_ref[...] = middle
        n2_ref[...] = normed(middle, small_ref[RECS + 1:RECS + 2, :]).astype(BF)
        both_ref[...] = att

    n2 = n2_ref[...]
    gated = jnp.dot(n2, w_gate_ref[...], preferred_element_type=F32)
    upward = jnp.dot(n2, w_up_ref[...], preferred_element_type=F32)
    hidden = (gated * jax.nn.sigmoid(gated) * upward).astype(BF)
    gated_ref[...] = gated.astype(BF)
    up_ref[...] = upward.astype(BF)
    hidden_ref[...] = hidden
    both_ref[...] += jnp.dot(hidden, w_down_ref[...], preferred_element_type=F32)

    @pl.when(step == pl.num_programs(0) - 1)
    def _():
        state = state_ref[...].astype(F32)
        router = small_ref[recursion:recursion + 1, :]
        gate = jax.nn.sigmoid(jnp.sum(state * router, axis=-1, keepdims=True))
        active = active_column(label_ref, recursion, state.shape[0])
        gate_ref[...] = gate
        new_ref[...] = state + active * gate * both_ref[...]
        if following:
            project_into(
                new_ref[:following, :], small_ref[RECS:RECS + 1, :], w_ref, turn_ref, *refs[8:11]
            )


def feed(recursion, mixed, state, w_out, small, labels, w_gate, w_up, w_down, following, then=()):
    n, model = mixed.shape
    ff = w_gate.shape[1]
    tile = 512 if ff % 512 == 0 else ff
    across = pl.BlockSpec((model, tile), lambda i: (0, i))
    made = pl.BlockSpec((n, tile), lambda i: (0, i))
    out_specs = [
        whole(n, model), whole(n, model), whole(n, model), made, made, made, whole(n, model),
        whole(n, 1),
    ]
    wide = lambda dtype: jax.ShapeDtypeStruct((n, model), dtype)
    tall = jax.ShapeDtypeStruct((n, ff), BF)
    out_shape = [
        wide(F32), wide(F32), wide(BF), tall, tall, tall, wide(F32),
        jax.ShapeDtypeStruct((n, 1), F32),
    ]
    if following:
        shapes = [(following, model), (CHUNKS, following, LANES), (following, KV_HEADS * LANES)]
        out_specs += [whole(*s) for s in shapes]
        out_shape += [jax.ShapeDtypeStruct(s, BF) for s in shapes]
    return pl.pallas_call(
        functools.partial(feed_kernel, recursion, following),
        grid=(ff // tile,),
        in_specs=[
            whole(n, model), whole(n, model), whole(*w_out.shape), whole(8, model),
            whole(*labels.shape), across, across,
            pl.BlockSpec((tile, model), lambda i: (i, 0)),
        ] + ([whole(*then[0].shape), whole(2, following, LANES)] if following else []),
        out_specs=out_specs,
        out_shape=out_shape,
        compiler_params=pltpu.CompilerParams(vmem_limit_bytes=ROOM),
        cost_estimate=pl.CostEstimate(
            flops=2 * n * model * (model + 3 * ff), transcendentals=n * ff,
            bytes_accessed=2 * model * (model + 3 * ff) + 24 * n * model + 6 * n * ff,
        ),
        name="feed",
    )(mixed, state, w_out, small, labels, w_gate, w_up, w_down, *then)


def feed_back_kernel(recursion, gradient_ref, both_ref, gate_ref, label_ref, state_ref,
                     small_ref, middle_ref, w_out_ref, gated_ref, up_ref, w_gate_ref, w_up_ref,
                     w_down_ref, d_fed_ref, d_gated_ref, d_up_ref, d_att_ref, grad_ref,
                     d_mixed_ref, d_router_ref, d_gain_ref, total):
    step = pl.program_id(0)

    @pl.when(step == 0)
    def _():
        active = active_column(label_ref, recursion, gate_ref.shape[0])
        d_fed_ref[...] = (active * gate_ref[...] * gradient_ref[...].astype(F32)).astype(BF)
        total[...] = jnp.zeros(total.shape, F32)

    d_hidden = lax.dot_general(d_fed_ref[...], w_down_ref[...], NT, preferred_element_type=F32)
    gated, upward = gated_ref[...].astype(F32), up_ref[...].astype(F32)
    sig = jax.nn.sigmoid(gated)
    part = d_hidden * sig
    d_up = (part * gated).astype(BF)
    d_gated = (part * upward * (1.0 + gated * (1.0 - sig))).astype(BF)
    d_up_ref[...] = d_up
    d_gated_ref[...] = d_gated
    total[...] += lax.dot_general(
        d_gated, w_gate_ref[...], NT, preferred_element_type=F32
    ) + lax.dot_general(d_up, w_up_ref[...], NT, preferred_element_type=F32)

    @pl.when(step == pl.num_programs(0) - 1)
    def _():
        gradient, gate = gradient_ref[...].astype(F32), gate_ref[...]
        active = active_column(label_ref, recursion, gate.shape[0])
        router = small_ref[recursion:recursion + 1, :]
        d = total[...]
        v = middle_ref[...]
        inv = lax.rsqrt(jnp.mean(v * v, axis=-1, keepdims=True) + EPS)
        d_gain_ref[...] = jnp.sum(d * v * inv, axis=0, keepdims=True)
        scaled = d * small_ref[RECS + 1:RECS + 2, :]
        dot = jnp.mean(scaled * v, axis=-1, keepdims=True)
        d_middle = inv * scaled - v * (inv * inv * inv * dot)
        d_gate = active * gate * (1.0 - gate) * jnp.sum(
            gradient * both_ref[...], axis=-1, keepdims=True
        )
        d_router_ref[...] = jnp.sum(state_ref[...].astype(F32) * d_gate, axis=0, keepdims=True)
        grad_ref[...] = gradient + d_gate * router + d_middle
        d_att_ref[...] = (active * gate * gradient + d_middle).astype(BF)
        out_back_kernel(d_att_ref, w_out_ref, d_mixed_ref)


def feed_back(recursion, gradient, both, gate, labels, state, small, middle, w_out, gated, upward,
              w_gate, w_up, w_down):
    n, model = both.shape
    ff = w_gate.shape[1]
    tile = 512 if ff % 512 == 0 else ff
    across = pl.BlockSpec((model, tile), lambda i: (0, i))
    made = pl.BlockSpec((n, tile), lambda i: (0, i))
    wide = whole(n, model)
    flat = lambda dtype: jax.ShapeDtypeStruct((n, model), dtype)
    tall = jax.ShapeDtypeStruct((n, ff), BF)
    row = jax.ShapeDtypeStruct((1, model), F32)
    return pl.pallas_call(
        functools.partial(feed_back_kernel, recursion),
        grid=(ff // tile,),
        in_specs=[
            wide, wide, whole(n, 1), whole(*labels.shape), wide, whole(8, model), wide,
            whole(*w_out.shape), made, made, across, across,
            pl.BlockSpec((tile, model), lambda i: (i, 0)),
        ],
        out_specs=[
            wide, made, made, wide, wide, whole(CHUNKS, n, LANES), whole(1, model),
            whole(1, model),
        ],
        out_shape=[
            flat(BF), tall, tall, flat(BF), flat(F32),
            jax.ShapeDtypeStruct((CHUNKS, n, LANES), BF), row, row,
        ],
        scratch_shapes=[pltpu.VMEM((n, model), F32)],
        compiler_params=pltpu.CompilerParams(vmem_limit_bytes=ROOM),
        cost_estimate=pl.CostEstimate(
            flops=2 * n * model * (model + 3 * ff), transcendentals=n * ff,
            bytes_accessed=2 * model * (model + 3 * ff) + 24 * n * model + 8 * n * ff,
        ),
        name="feed_back",
    )(gradient, both, gate, labels, state, small, middle, w_out, gated, upward, w_gate, w_up,
      w_down)


def outer_rows_kernel(count, *refs):
    xs, ds, out_ref = refs[:count], refs[count:2 * count], refs[2 * count]
    total = None
    for x_ref, d_ref in zip(xs, ds):
        part = jnp.dot(jnp.transpose(x_ref[...]), d_ref[...], preferred_element_type=F32)
        total = part if total is None else total + part
    out_ref[...] = total.astype(BF)


def outer_rows(xs, ds, tile):
    rows, columns = xs[0].shape[1], ds[0].shape[1]
    tokens = sum(x.shape[0] for x in xs)
    return pl.pallas_call(
        functools.partial(outer_rows_kernel, len(xs)),
        grid=(rows // tile,),
        in_specs=[pl.BlockSpec((x.shape[0], tile), lambda i: (0, i)) for x in xs]
        + [whole(*d.shape) for d in ds],
        out_specs=pl.BlockSpec((tile, columns), lambda i: (i, 0)),
        out_shape=jax.ShapeDtypeStruct((rows, columns), BF),
        compiler_params=pltpu.CompilerParams(vmem_limit_bytes=ROOM),
        cost_estimate=pl.CostEstimate(
            flops=2 * tokens * rows * columns, transcendentals=0,
            bytes_accessed=2 * (tokens * (columns + rows) + rows * columns),
        ),
        name="outer_rows",
    )(*xs, *ds)


def finish_kernel(onehot_ref, final_ref, gradient_ref, qkv_ref, o_ref, gu_ref, down_ref,
                  block_ref, token_ref, query_ref, key_ref, value_ref, out_ref, gate_ref, up_ref,
                  gdown_ref, tiny_ref):
    onehot = onehot_ref[...]
    block_ref[...] = lax.dot_general(
        final_ref[...], onehot, TN, preferred_element_type=F32
    ).astype(BF)
    token_ref[...] = lax.dot_general(
        gradient_ref[...], onehot, TN, preferred_element_type=F32
    ).astype(BF)
    model = query_ref.shape[1]
    query_ref[...] = qkv_ref[:, :model].astype(F32)
    out_ref[...] = o_ref[:, :model].astype(F32)
    rows = query_ref.shape[0]
    room = jnp.zeros((-rows % LANES, LANES), F32)

    def across(v):
        return jnp.transpose(jnp.concatenate([v, room], axis=0))[:, :rows]

    tiny = jnp.concatenate(
        [o_ref[:, model:].astype(F32), jnp.zeros((rows, LANES - HD), F32)], axis=1
    )
    tiny_ref[...] = across(tiny)[:8]
    gate_ref[...] = gu_ref[0].astype(F32)
    up_ref[...] = gu_ref[1].astype(F32)
    gdown_ref[...] = down_ref[...].astype(F32)
    low = lanes_of(rows) < HD
    heads = [
        qkv_ref[:, (CHUNKS + h) * LANES:(CHUNKS + h + 1) * LANES].astype(F32)
        for h in range(KV_HEADS)
    ]
    for h in range(0, KV_HEADS, 2):
        even, odd = heads[h], heads[min(h + 1, KV_HEADS - 1)]
        at = slice(h * HD, min(h + 2, KV_HEADS) * HD)
        size = at.stop - at.start
        key_ref[at, :] = across(jnp.where(low, even, pltpu.roll(odd, HD, 1)))[:size]
        value_ref[at, :] = across(jnp.where(low, pltpu.roll(even, HD, 1), odd))[:size]


def finish(onehot, final, gradient, qkv, o, gu, down):
    rows, model = final.shape
    shard, ff = gu.shape[1:]
    kv = KV_HEADS * HD
    shapes = [
        (model, rows), (model, rows), (shard, model), (kv, shard), (kv, shard), (shard, model),
        (shard, ff), (shard, ff), down.shape, (8, shard),
    ]
    args = (onehot, final, gradient, qkv, o, gu, down)
    return pl.pallas_call(
        finish_kernel,
        grid=(1,),
        in_specs=[whole(*v.shape) for v in args],
        out_specs=[whole(*v) for v in shapes],
        out_shape=[jax.ShapeDtypeStruct(v, BF if i < 2 else F32) for i, v in enumerate(shapes)],
        compiler_params=pltpu.CompilerParams(vmem_limit_bytes=ROOM),
        name="finish",
    )(*args)


def mm(a, b):
    return jnp.dot(a, b, preferred_element_type=F32)


def mm_tn(a, b):
    return lax.dot_general(a, b, TN, preferred_element_type=F32)


def per_device(topo, *args):
    (tokens, w_query, w_key, w_value, w_out, w_gate, w_up, w_down, router, norm_attn, norm_ffn,
     lengths, depths, padding, cotangent) = args
    rows, model = tokens.shape
    kv_cols = w_key.shape[1]
    ff = w_gate.shape[1]
    shard = w_query.shape[0]
    deep_rows = rows * 3 // 4
    xk, yk, ck = (topo.keys(d) for d in "xyc")

    small = jnp.concatenate([router, norm_attn[:, None], norm_ffn[:, None]], axis=1)
    small = jnp.pad(small, ((0, 0), (0, HD - small.shape[1])))
    w_kv = jnp.stack(
        [w_key.reshape(shard, KV_HEADS, HD), w_value.reshape(shard, KV_HEADS, HD)], axis=2
    ).reshape(shard, 2 * kv_cols)
    first = jnp.concatenate([w_query, small, w_kv], axis=1)
    weight_qkv, weight_g, weight_u, weight_d, weight_o = gather_weights(
        topo, [first, w_gate, w_up, w_down, w_out]
    )

    own = lax.axis_index("tok") * rows + jnp.arange(rows, dtype=jnp.int32)
    eligible = (depths >= 2) & (padding > 0)
    flags = jnp.stack([eligible, ~eligible]).astype(BF)
    upto = (jnp.arange(rows)[:, None] <= jnp.arange(rows)[None, :]).astype(BF)
    counts = mm(flags, upto).astype(jnp.int32)
    slot = jnp.where(eligible, counts[0] - 1, counts[0, -1] + counts[1] - 1)
    chosen = jnp.arange(rows, dtype=jnp.int32)[:, None] == slot[None, :]
    onehot = chosen.astype(BF)
    doc_ends = jnp.cumsum(lengths[0])
    begins = jnp.sum(
        jnp.where(own[:, None] >= doc_ends[None, :], lengths[0][None, :], 0), axis=1
    )
    levels = jnp.where(padding > 0, depths, 0)
    labels = jnp.stack([own, begins, levels])
    labels = jnp.sum(jnp.where(chosen[None], labels[:, None, :], 0), axis=2)
    labels = jnp.pad(labels, ((0, 5), (0, 0)))
    swap = topo.swap_pairs()
    state = lax.ppermute(mm(onehot, tokens).astype(BF), AXES, swap)
    labels = lax.ppermute(labels, AXES, swap)
    cotangent = mm(onehot, cotangent).astype(BF)

    def collect(arrays, ident):
        if small_layer(topo):
            return gather_layer(topo, arrays, ident)
        return [group_gather(topo, v, xk + yk + ck) for v in arrays]

    def distribute(grads, ident):
        if small_layer(topo):
            return reduce_layer(topo, grads, ident)
        return group_scatter(topo, grads, ck + yk + xk)


    pack = (lax.axis_index("grp") * topo.X) + lax.axis_index("tok") % topo.X
    lowest = jnp.min(labels[1])
    span = jnp.stack([lowest // rows, pack + 1]).astype(jnp.int32)
    places = (labels[0] - labels[1]).astype(F32)
    turn = (jnp.arange(LANES) % (HD // 2)).astype(F32)
    freqs = 10000.0 ** (-(turn * 2.0 / HD))
    angles = places[:, None] * freqs[None, :]
    turns = jnp.stack([jnp.cos(angles), jnp.sin(angles)])
    query_labels = {
        n: jnp.concatenate([labels[:, :n]] * SHARES, axis=1) for n in (rows, deep_rows)
    }

    def forward(state, projected, recursion, labels_all=None):
        extra = None
        n1, q, kv = projected
        n = n1.shape[0]
        if recursion == 0:
            kv_all, labels_all = collect([kv, labels], 2)
            kv_all, later = lax.optimization_barrier((kv_all, cotangent))
            later = lax.ppermute(later, AXES, swap)
        else:
            kv_all, = collect([kv], 3)
        kv_all = kv_all.reshape(topo.T * n, 2 * kv_cols)
        mixed, out, stat = attend(n, recursion, span, labels_all, query_labels[n], kv_all, q)
        if recursion == 0:
            extra = (labels_all, later)
        following = deep_rows if recursion + 1 < RECS else 0
        new, middle, n2, gated, upward, hidden, both, gate, *projected = feed(
            recursion, mixed, state, weight_o, small, labels, weight_g, weight_u, weight_d,
            following, (weight_qkv, turns) if following else (),
        )
        kept = (state, n1, q, kv_all, labels_all, out, stat, mixed, middle, n2, gated, upward,
                hidden, both, gate)
        return (new, projected, kept, extra)

    def backward(gradient, recursion, kept):
        (state, n1, q, kv_all, labels_all, out, stat, mixed, middle, n2, gated, upward, hidden,
         both, gate) = kept
        n = n1.shape[0]
        d_fed, d_gated, d_up, d_att, gradient, d_mixed, d_router, d_gain_two = feed_back(
            recursion, gradient, both, gate, labels, state, small, middle, weight_o, gated,
            upward, weight_g, weight_u, weight_d,
        )
        dq, dkv = attend_back(
            n, recursion, span, labels_all, query_labels[n], kv_all, q, d_mixed, out, stat, turns
        )
        dkv = distribute(dkv.reshape(topo.T, n, 2 * kv_cols), 5 if recursion else 4)
        gradient, dqkv, d_gain_one = project_back(
            gradient, state, small, weight_qkv, turns, dq, dkv
        )
        left = (n1, dqkv, mixed, d_att, n2, d_gated, d_up, hidden, d_fed)
        return (gradient, left, (d_router[0], d_gain_one[0], d_gain_two[0]))

    *projected, small = project(state, weight_qkv, turns)
    whole_state, projected, kept, (labels_all, gradient) = forward(state, projected, 0)
    deep = whole_state
    all_kept = [kept]
    for recursion in range(1, RECS):
        deep, projected, kept, _ = forward(deep, projected, recursion, labels_all)
        all_kept.append(kept)
    final = jnp.concatenate([deep, whole_state[deep_rows:]], axis=0).astype(BF)

    deep_grad = gradient
    lefts, smalls = [], []
    for recursion in reversed(range(1, RECS)):
        deep_grad, left, tiny = backward(deep_grad, recursion, all_kept[recursion])
        lefts.append(left)
        smalls.append(tiny)
    gradient = jnp.concatenate([deep_grad, gradient[deep_rows:].astype(F32)], axis=0)
    gradient, left, tiny = backward(gradient, 0, all_kept[0])
    lefts.append(left)
    smalls.append(tiny)
    final, gradient = lax.optimization_barrier((final, gradient.astype(BF)))
    final = lax.ppermute(final, AXES, swap)
    gradient = lax.ppermute(gradient, AXES, swap)

    n1, dqkv, mixed, d_att, n2, d_gated, d_up, hidden, d_fed = zip(*lefts)

    def outer(xs, ds):
        return mm_tn(jnp.concatenate(xs, axis=0), jnp.concatenate(ds, axis=0))

    cut = lambda v: v.astype(BF).reshape(topo.T, -1, v.shape[-1])
    tiny = jnp.stack(
        [smalls[2][0], smalls[1][0], smalls[0][0],
         smalls[0][1] + smalls[1][1] + smalls[2][1],
         smalls[0][2] + smalls[1][2] + smalls[2][2]], axis=1
    )
    wide_out = -(-(model + tiny.shape[1]) // 256) * 256
    tiny = jnp.pad(tiny, ((0, 0), (0, wide_out - model - tiny.shape[1])))
    grad_qkv, grad_o, grad_gu, grad_down = reduce_gradients(topo, [
        cut(outer(n1, dqkv)),
        cut(jnp.concatenate([outer(mixed, d_att), tiny], axis=1)),
        cut(outer(n2, d_gated)),
        outer_rows(hidden, d_fed, 640).reshape(topo.T, -1, model),
        cut(outer(n2, d_up)),
    ])
    block, token, grad_query, grad_key, grad_value, *others, tiny = finish(
        onehot, final, gradient, grad_qkv, grad_o, grad_gu, grad_down
    )
    return (block.T, token.T, grad_query, grad_key.T, grad_value.T) + tuple(others) + (
        tiny[:RECS].T, tiny[RECS], tiny[RECS + 1]
    )


def solution(mesh):
    topo = Topo(mesh.shape["grp"], mesh.shape["tok"])
    both = P(("grp", "tok"))
    wide = P(("grp", "tok"), None)
    rows = P("tok", None)
    row = P("tok")
    return jax.shard_map(
        functools.partial(per_device, topo),
        mesh=mesh,
        in_specs=(wide,) + (rows,) * 8 + (row, row, P("grp", None), both, both, wide),
        out_specs=(wide, wide) + (rows,) * 8 + (row, row),
        check_vma=False,
    )
```

```python
import functools

import jax
import jax.numpy as jnp
from jax import lax
from jax.experimental import pallas as pl
from jax.experimental.pallas import tpu as pltpu
from jax.sharding import PartitionSpec as P

HEADS = 15
KV_HEADS = 5
SHARES = HEADS // KV_HEADS
HD = 64
RECS = 3
EPS = 1e-05
BF = jnp.bfloat16
F32 = jnp.float32
BIG = -1e30
AXES = ("grp", "tok")


class Topo:
    def __init__(self, groups, spread):
        self.G = groups
        self.T = spread
        self.X = spread // groups
        self.Z = groups
        self.Y = groups // 2
        self.bits = {
            "z": self.Z.bit_length() - 1,
            "x": self.X.bit_length() - 1,
            "y": self.Y.bit_length() - 1,
            "c": 1,
        }

    def keys(self, dim):
        return [(dim, k) for k in range(self.bits[dim])]

    def masks(self, key):
        dim, k = key
        if dim == "c":
            return (1, 0)
        if dim == "y":
            return (2 << k, 0)
        if dim == "x":
            return (0, 1 << k)
        return (0, self.X << k)

    def pairs(self, key):
        mg, mt = self.masks(key)
        return [
            (g * self.T + t, (g ^ mg) * self.T + (t ^ mt))
            for g in range(self.G)
            for t in range(self.T)
        ]

    def swap_pairs(self):
        out = []
        for g in range(self.G):
            for t in range(self.T):
                z, x = t // self.X, t % self.X
                out.append((g * self.T + t, z * self.T + g * self.X + x))
        return out

    def bit(self, key):
        mg, mt = self.masks(key)
        if mg:
            return (lax.axis_index("grp") // mg) % 2
        return (lax.axis_index("tok") // mt) % 2


def exchange(topo, arr, key):
    return lax.ppermute(arr, AXES, topo.pairs(key))


def double(topo, arr, key, axis, stack):
    other = exchange(topo, arr, key)
    mine_is_high = topo.bit(key) == 1
    low = jnp.where(mine_is_high, other, arr)
    high = jnp.where(mine_is_high, arr, other)
    if stack:
        return jnp.stack([low, high], axis=axis)
    return jnp.concatenate([low, high], axis=axis)


def halve(topo, arr, key, axis, stack):
    mine_is_high = topo.bit(key) == 1
    if stack:
        low = lax.index_in_dim(arr, 0, axis, keepdims=False)
        high = lax.index_in_dim(arr, 1, axis, keepdims=False)
    else:
        half = arr.shape[axis] // 2
        low = lax.slice_in_dim(arr, 0, half, axis=axis)
        high = lax.slice_in_dim(arr, half, 2 * half, axis=axis)
    send = jnp.where(mine_is_high, low, high).astype(BF)
    keep = jnp.where(mine_is_high, high, low).astype(F32)
    return (keep + exchange(topo, send, key).astype(F32)).astype(BF)


class Piece:
    def __init__(self, array, dim, start, size, core, part):
        self.array, self.dim, self.start, self.size = array, dim, start, size
        self.core, self.part = core, part

    def of(self, ref):
        if self.dim == 0:
            return ref.at[pl.ds(self.start, self.size), :]
        return ref.at[:, pl.ds(self.start, self.size)]


def cut_pieces(shapes):
    near = lambda v, unit: max(unit, int(round(v / unit)) * unit)
    wide_a, wide_g, wide_u, tall = shapes[0][1], shapes[1][1], shapes[2][1], shapes[3][0]
    g = near(wide_g * 0.7, 128)
    u = near(wide_u * 0.65, 128)
    d = near(tall * 0.3, 8)
    return [
        Piece(1, 1, 0, g, 0, 0),
        Piece(4, 1, 0, shapes[4][1], 0, 2),
        Piece(1, 1, g, wide_g - g, 0, 2),
        Piece(0, 1, 0, wide_a, 0, 1),
        Piece(2, 1, u, wide_u - u, 1, 0),
        Piece(3, 0, 0, d, 1, 0),
        Piece(3, 0, d, tall - d, 1, 2),
        Piece(2, 1, 0, u, 1, 1),
    ]


def coordinates(topo):
    g, t = lax.axis_index("grp"), lax.axis_index("tok")
    return lax.rem(t, topo.X), lax.div(g, 2), lax.div(t, topo.X), lax.rem(g, 2)


def gather_kernel(topo, pieces, *refs):
    shards, outs = refs[:5], refs[5:10]
    local_sem, recv_sem, z_sem, x_sem, y_sem, c_sem = refs[10:]
    x, y, z, c = coordinates(topo)
    X, Z, T = topo.X, topo.Z, topo.T
    g, me = lax.axis_index("grp"), lax.axis_index("tok")
    odd = lax.rem(y, 2)
    over_y = {"grp": g + 2 - 4 * odd, "tok": me}
    over_c = {"grp": g + 1 - 2 * c, "tok": me}

    def over_z(k):
        return {"grp": g, "tok": (z + k) * X + x}

    def over_x(k):
        return {"grp": g, "tok": z * X + lax.rem(x + k, X)}

    barrier = pltpu.get_barrier_semaphore()
    partners = [over_y, over_c] + [over_x(k) for k in range(1, X)]
    for partner in partners:
        pl.semaphore_signal(barrier, inc=1, device_id=partner, device_id_type=pl.DeviceIdType.MESH)
    below, above = z > 0, z < Z - 1

    def greet(k):
        pl.semaphore_signal(
            barrier, inc=1, device_id=over_z(k), device_id_type=pl.DeviceIdType.MESH
        )

    pl.when(below)(lambda: greet(-1))
    pl.when(above)(lambda: greet(1))
    own = [
        pltpu.make_async_copy(shards[i], outs[i].at[me], local_sem.at[i]) for i in range(5)
    ]
    for copy in own:
        copy.start()
    pl.semaphore_wait(barrier, len(partners) + below.astype(jnp.int32) + above.astype(jnp.int32))

    def send(p, t, sem, target, mine=False):
        piece = pieces[p]
        landing = piece.of(outs[piece.array].at[t])
        source = piece.of(shards[piece.array]) if mine else landing
        return pltpu.make_async_remote_copy(
            src_ref=source, dst_ref=landing, send_sem=sem, recv_sem=recv_sem.at[p, t],
            device_id=target, device_id_type=pl.DeviceIdType.MESH,
        )

    def arrived(p, t):
        send(p, t, c_sem.at[0, 0], over_c).wait_recv()

    def run(core):
        mine = [p for p in range(len(pieces)) if pieces[p].core == core]
        theirs = [p for p in range(len(pieces)) if pieces[p].core != core]
        slot = {p: i for i, p in enumerate(mine)}

        def inside(p, body):
            part = pieces[p].part
            if part == 1:
                body()
            else:
                pl.when(odd == part // 2)(body)

        def outside(p, body):
            if pieces[p].part != 1:
                pl.when(odd != pieces[p].part // 2)(body)

        def x_copies(p, zz, first):
            t = zz * X + x
            return [
                send(p, t, x_sem.at[slot[p], zz, k - 1], over_x(k), first) for k in range(1, X)
            ]

        def y_copy(p, t):
            return send(p, t, y_sem.at[slot[p], t], over_y)

        def c_copy(p, t):
            return send(p, t, c_sem.at[slot[p], t], over_c)

        def z_copy(p, zz, k, first):
            return send(p, zz * X + x, z_sem.at[slot[p], zz, (k + 1) // 2], over_z(k), first)

        for p in mine:
            def begin(p=p):
                pl.when(below)(lambda: z_copy(p, z, -1, True).start())
                pl.when(above)(lambda: z_copy(p, z, 1, True).start())
                for copy in x_copies(p, z, True):
                    copy.start()
            inside(p, begin)

        def share(p, t):
            if pieces[p].part != 1:
                y_copy(p, t).start()
            c_copy(p, t).start()

        def relay(p, zz, k):
            arrived(p, zz * X + x)
            pl.when(above if k > 0 else below)(lambda: z_copy(p, zz, k, False).start())
            for copy in x_copies(p, zz, False):
                copy.start()
            share(p, zz * X + x)

        def others(p, zz):
            for j in range(1, X):
                t = zz * X + lax.rem(x + j, X)
                arrived(p, t)
                share(p, t)

        def around(k, carry):
            low, high = z - k, z + k
            for p in mine:
                inside(p, lambda p=p: pl.when(low >= 0)(lambda: relay(p, low, 1)))
                inside(p, lambda p=p: pl.when(high < Z)(lambda: relay(p, high, -1)))
            low, high = z - k + 1, z + k - 1
            for p in mine:
                inside(p, lambda p=p: pl.when(low >= 0)(lambda: others(p, low)))
                inside(p, lambda p=p: pl.when((k > 1) & (high < Z))(lambda: others(p, high)))
            return carry

        lax.fori_loop(1, Z + 1, around, 0)

        def rest(t, carry):
            @pl.when(t != me)
            def _():
                for p in mine:
                    def forward(p=p):
                        arrived(p, t)
                        c_copy(p, t).start()
                    outside(p, forward)
            return carry

        lax.fori_loop(0, T, rest, 0)

        def finish(t, carry):
            @pl.when(t != me)
            def _():
                for p in theirs:
                    arrived(p, t)
                for p in mine:
                    c_copy(p, t).wait_send()
                    if pieces[p].part != 1:
                        inside(p, lambda p=p: y_copy(p, t).wait_send())
            return carry

        lax.fori_loop(0, T, finish, 0)
        for p in mine:
            def end(p=p):
                def each(zz, carry):
                    pl.when((zz <= z) & above)(lambda: z_copy(p, zz, 1, False).wait_send())
                    pl.when((zz >= z) & below)(lambda: z_copy(p, zz, -1, False).wait_send())
                    for copy in x_copies(p, zz, False):
                        copy.wait_send()
                    return carry
                lax.fori_loop(0, Z, each, 0)
            inside(p, end)

    pl.when(c == 0)(lambda: run(0))
    pl.when(c == 1)(lambda: run(1))
    for copy in own:
        copy.wait()


def gather_weights(topo, shards):
    pieces = cut_pieces([s.shape for s in shards])
    T = topo.T
    DMA = pltpu.SemaphoreType.DMA
    hbm = pl.BlockSpec(memory_space=pl.ANY)
    outs = pl.pallas_call(
        functools.partial(gather_kernel, topo, pieces),
        in_specs=[hbm] * 5,
        out_specs=[hbm] * 5,
        out_shape=[jax.ShapeDtypeStruct((T,) + s.shape, s.dtype) for s in shards],
        scratch_shapes=[
            DMA((5,)), DMA((len(pieces), T)), DMA((4, topo.Z, 2)), DMA((4, topo.Z, topo.X - 1)),
            DMA((4, T)), DMA((4, T)),
        ],
        compiler_params=pltpu.CompilerParams(collective_id=0, has_side_effects=True),
        name="gather_weights",
    )(*shards)
    return [o.reshape(-1, o.shape[-1]) for o in outs]


class Share:
    def __init__(self, array, start, shape, part):
        self.array, self.start, self.shape, self.part = array, start, shape, part

    def of(self, ref, core, *lead):
        rows, columns = self.shape
        if self.array == 2:
            return ref.at[lead + (slice(None), pl.ds(self.start, columns))]
        if self.array == 3:
            at = pl.multiple_of(core * rows, rows)
            return ref.at[lead + (pl.ds(at, rows), slice(None))]
        at = pl.multiple_of(core * columns, 128)
        return ref.at[lead + (slice(None), pl.ds(at, columns))]


def cut_shares(shapes):
    rows, ff = shapes[2][1], shapes[2][2]
    one = ff * 3 // 20 // 128 * 128
    two = ff * 33 // 40 // 128 * 128
    return [
        Share(2, one, (rows, two - one), 0),
        Share(3, 0, (shapes[3][1] // 2, shapes[3][2]), 2),
        Share(2, two, (rows, ff - two), 2),
        Share(0, 0, (rows, shapes[0][2] // 2), 1),
        Share(1, 0, (rows, shapes[1][2] // 2), 1),
        Share(2, 0, (rows, one), 1),
    ]


def reduce_kernel(topo, shares, *refs):
    grads, outs = refs[:5], refs[5:9]
    count = len(shares)
    groups = []
    at = 9
    for _ in range(7):
        groups.append(refs[at:at + count])
        at += count
    held, from_c, from_y, from_x, from_low, from_high, from_f = groups
    (load_sem, c_send, c_recv, y_send, y_recv, x_send, x_recv, z_send, z_recv, f_send, f_recv,
     o_send, o_recv, o_local) = refs[at:]
    x, y, z, c = coordinates(topo)
    X, Z, T = topo.X, topo.Z, topo.T
    g, me = lax.axis_index("grp"), lax.axis_index("tok")
    odd = lax.rem(y, 2)
    below, above = z > 0, z < Z - 1
    kind = pl.DeviceIdType.MESH

    def over_y(k):
        high = lax.rem(lax.div(y, 1 << k), 2)
        return {"grp": g + (2 - 4 * high) * (1 << k), "tok": me}

    over_c = {"grp": g + 1 - 2 * c, "tok": me}

    def over_z(k):
        return {"grp": g, "tok": (z + k) * X + x}

    def over_x(k):
        return {"grp": g, "tok": z * X + lax.rem(x + k, X)}

    barrier = pltpu.get_barrier_semaphore()
    partners = [over_c] + [over_y(k) for k in range(topo.bits["y"])]
    partners += [over_x(k) for k in range(1, X)]

    def greet(partner):
        pl.semaphore_signal(barrier, inc=1, device_id=partner, device_id_type=kind)

    for partner in partners:
        greet(partner)
    pl.when(below)(lambda: greet(over_z(-1)))
    pl.when(above)(lambda: greet(over_z(1)))
    every = range(count)

    def source(s, core, t, up):
        place = {2: 4 if up else 2, 3: 3}.get(s.array, s.array)
        return s.of(grads[place], core, t)

    def load(p, t, up=False):
        return pltpu.make_async_copy(
            source(shares[p], c, t, up), held[p].at[t], load_sem.at[p, t]
        )

    def start(p, make, up_core):
        if shares[p].array == 2:
            pl.when(c != up_core)(lambda: make(False).start())
            pl.when(c == up_core)(lambda: make(True).start())
        else:
            make(False).start()

    def remote(source, landing, send, recv, target):
        return pltpu.make_async_remote_copy(
            src_ref=source, dst_ref=landing, send_sem=send, recv_sem=recv, device_id=target,
            device_id_type=kind,
        )

    def c_copy(p, t, up=False):
        return remote(
            source(shares[p], 1 - c, t, up), from_c[p].at[t], c_send.at[p, t], c_recv.at[p, t],
            over_c,
        )

    def y_copy(p, t):
        return remote(
            held[p].at[t], from_y[p].at[t], y_send.at[p, t], y_recv.at[p, t], over_y(0)
        )

    def x_copy(p, zz, k):
        t = zz * X + lax.rem(x + k, X)
        return remote(
            held[p].at[t], from_x[p].at[zz, k - 1], x_send.at[p, zz, k - 1],
            x_recv.at[p, zz, k - 1], over_x(k),
        )

    def z_copy(p, zz, k):
        landing = from_low if k > 0 else from_high
        way = (k + 1) // 2
        return remote(
            held[p].at[zz * X + x], landing[p].at[zz], z_send.at[p, zz, way],
            z_recv.at[p, zz, way], over_z(k),
        )

    def f_copy(p, k):
        return remote(
            held[p].at[me], from_f[p].at[k], f_send.at[p, k], f_recv.at[p, k], over_y(k)
        )

    def result(s, core):
        if s.array == 2:
            return outs[2].at[core, :, pl.ds(s.start, s.shape[1])]
        return s.of(outs[s.array], core)

    def o_copy(p):
        s = shares[p]
        return remote(
            held[p].at[me], result(s, c), o_send.at[p], o_recv.at[p], over_c
        )

    def o_arrived(p):
        s = shares[p]
        return remote(
            held[p].at[me], result(s, 1 - c), o_send.at[p], o_recv.at[p], over_c
        )

    def o_keep(p):
        s = shares[p]
        return pltpu.make_async_copy(held[p].at[me], result(s, c), o_local.at[p])

    def add(p, t, other):
        held[p][t] = held[p][t] + other

    def layers(body):
        def step(i, carry):
            k = Z - 1 - i
            pl.when(z + k < Z)(lambda: body(z + k))
            pl.when((k > 0) & (z - k >= 0))(lambda: body(z - k))
            return carry
        return step

    def inside(p, body):
        if shares[p].part == 1:
            body()
        else:
            pl.when(odd == shares[p].part // 2)(body)

    def outside(p, body):
        if shares[p].part != 1:
            pl.when(odd != shares[p].part // 2)(body)

    def start_loads(zz):
        def each(j, carry):
            t = zz * X + lax.rem(x + j, X)
            for p in every:
                start(p, lambda up, p=p: load(p, t, up), 1)
            return carry
        lax.fori_loop(0, X, each, 0)

    lax.fori_loop(0, Z, layers(start_loads), 0)
    pl.semaphore_wait(barrier, len(partners) + below.astype(jnp.int32) + above.astype(jnp.int32))

    def start_cores(zz):
        def each(j, carry):
            t = zz * X + lax.rem(x + j, X)
            for p in every:
                start(p, lambda up, p=p: c_copy(p, t, up), 0)
            return carry
        lax.fori_loop(0, X, each, 0)

    lax.fori_loop(0, Z, layers(start_cores), 0)

    def cores(zz):
        def each(j, carry):
            t = zz * X + lax.rem(x + j + 1, X)
            for p in every:
                load(p, t).wait()
                c_copy(p, t).wait_recv()
                add(p, t, from_c[p][t])
                outside(p, lambda p=p: y_copy(p, t).start())
                if shares[p].part == 1:
                    for k in range(1, X):
                        pl.when(j + 1 == k)(lambda p=p, k=k: x_copy(p, zz, k).start())
            return carry
        lax.fori_loop(0, X, each, 0)

    lax.fori_loop(0, Z, layers(cores), 0)

    def over(zz):
        def each(j, carry):
            t = zz * X + lax.rem(x + j + 1, X)
            for p in every:
                if shares[p].part != 1:
                    def body(p=p):
                        y_copy(p, t).wait_recv()
                        add(p, t, from_y[p][t])
                        for k in range(1, X):
                            pl.when(j + 1 == k)(lambda: x_copy(p, zz, k).start())
                    inside(p, body)
            return carry
        lax.fori_loop(0, X, each, 0)

    def join(p, zz):
        t = zz * X + x
        for k in range(1, X):
            x_copy(p, zz, k).wait_recv()
            add(p, t, from_x[p][zz, k - 1])

        def low():
            z_copy(p, zz, 1).wait_recv()
            add(p, t, from_low[p][zz])

        def high():
            z_copy(p, zz, -1).wait_recv()
            add(p, t, from_high[p][zz])

        pl.when((zz >= z) & below)(low)
        pl.when((zz <= z) & above)(high)
        pl.when(zz > z)(lambda: z_copy(p, zz, 1).start())
        pl.when(zz < z)(lambda: z_copy(p, zz, -1).start())

    single = topo.bits["y"] == 1

    def first_joins(zz):
        for p in every:
            if shares[p].part == 1:
                join(p, zz)
                if single:
                    pl.when(zz == z)(lambda p=p: f_copy(p, 0).start())

    def last_joins(zz):
        for p in every:
            if shares[p].part != 1:
                def body(p=p):
                    join(p, zz)
                    if single:
                        pl.when(zz == z)(lambda: f_copy(p, 0).start())
                inside(p, body)

    def main(i, carry):
        @pl.when(i < Z)
        def _():
            layers(first_joins)(i, 0)
            layers(over)(i, 0)

        @pl.when(i > 0)
        def _():
            layers(last_joins)(i - 1, 0)

        return carry

    lax.fori_loop(0, Z + 1, main, 0)

    for k in range(1, topo.bits["y"]):
        for p in every:
            inside(p, lambda p=p: f_copy(p, k).start())
        for p in every:
            def fold(p=p):
                f_copy(p, k).wait()
                add(p, me, from_f[p][k])
            inside(p, fold)
    if not single:
        for p in every:
            inside(p, lambda p=p: f_copy(p, 0).start())
    for p in every:
        if shares[p].part == 1:
            f_copy(p, 0).wait()
            add(p, me, from_f[p][0])
        else:
            def take(p=p):
                f_copy(p, 0).wait_recv()
                held[p][me] = from_f[p][0]
            outside(p, lambda p=p: y_copy(p, me).wait_send())
            outside(p, take)
        o_copy(p).start()
        o_keep(p).start()

    def ends(t, carry):
        for p in every:
            c_copy(p, t).wait_send()
            outside(p, lambda p=p: pl.when(t != me)(lambda: y_copy(p, t).wait_send()))
        return carry

    lax.fori_loop(0, T, ends, 0)

    def z_ends(zz, carry):
        for p in every:
            def body(p=p):
                for k in range(1, X):
                    x_copy(p, zz, k).wait_send()
                pl.when(zz > z)(lambda: z_copy(p, zz, 1).wait_send())
                pl.when(zz < z)(lambda: z_copy(p, zz, -1).wait_send())
            inside(p, body)
        return carry

    lax.fori_loop(0, Z, z_ends, 0)
    for p in every:
        if shares[p].part != 1:
            inside(p, lambda p=p: f_copy(p, 0).wait_send())
        o_copy(p).wait_send()
        o_arrived(p).wait_recv()
        o_keep(p).wait()


def reduce_gradients(topo, grads):
    shares = cut_shares([v.shape for v in grads])
    X, Z, T = topo.X, topo.Z, topo.T
    n = len(shares)
    folds = max(1, topo.bits["y"])
    DMA = pltpu.SemaphoreType.DMA
    hbm = pl.BlockSpec(memory_space=pl.ANY)
    lead = [(T,), (T,), (T,), (Z, X - 1), (Z,), (Z,), (folds,)]
    rooms = [
        pltpu.VMEM(front + s.shape, BF)
        for front in lead for s in shares
    ]
    outs = [grads[0].shape[1:], grads[1].shape[1:], (2,) + grads[2].shape[1:], grads[3].shape[1:]]
    return pl.pallas_call(
        functools.partial(reduce_kernel, topo, shares),
        in_specs=[hbm] * 5,
        out_specs=[hbm] * 4,
        out_shape=[jax.ShapeDtypeStruct(s, BF) for s in outs],
        scratch_shapes=rooms + [
            DMA((n, T)), DMA((n, T)), DMA((n, T)), DMA((n, T)), DMA((n, T)),
            DMA((n, Z, X - 1)), DMA((n, Z, X - 1)), DMA((n, Z, 2)), DMA((n, Z, 2)),
            DMA((n, folds)), DMA((n, folds)), DMA((n,)), DMA((n,)), DMA((n,)),
        ],
        compiler_params=pltpu.CompilerParams(
            collective_id=1, has_side_effects=True, vmem_limit_bytes=60 << 20
        ),
        name="reduce_gradients",
    )(*grads)


def group_order(topo):
    return list(reversed(topo.keys("y"))) + topo.keys("c") + list(reversed(topo.keys("x")))


def group_gather(topo, arr, order):
    names = group_order(topo)
    held = []
    shape = arr.shape
    for key in order:
        place = sum(1 for h in held if names.index(h) < names.index(key))
        arr = double(topo, arr, key, place, True)
        held.append(key)
    return arr.reshape((topo.T,) + shape)


def group_scatter(topo, arr, order):
    names = group_order(topo)
    held = list(names)
    arr = arr.reshape((2,) * len(names) + arr.shape[1:])
    for key in order:
        arr = halve(topo, arr, key, held.index(key), True)
        held.remove(key)
    return arr


def small_layer(topo):
    return topo.X == 2 and topo.Y == 2


class Layer:
    def __init__(self, topo):
        self.topo = topo
        x, y, z, c = coordinates(topo)
        self.c = c
        far_x, far_y = 1 - x, 1 - y
        a = (x + c * (far_x - x), far_y + c * (y - far_y))
        b = (far_x + c * (x - far_x), y + c * (far_y - y))
        self.chips = [(x, y), a, b, (far_x, far_y)]
        self.z = z

    def pack(self, slot, core):
        x, y = self.chips[slot]
        return (y * 2 + core) * self.topo.X + x

    def device(self, slot, core):
        x, y = self.chips[slot]
        return {"grp": y * 2 + core, "tok": self.z * self.topo.X + x}

    def meet(self):
        barrier = pltpu.get_barrier_semaphore()
        for target in (self.device(1, self.c), self.device(2, self.c), self.device(0, 1 - self.c)):
            pl.semaphore_signal(
                barrier, inc=1, device_id=target, device_id_type=pl.DeviceIdType.MESH
            )
        pl.semaphore_wait(barrier, 3)


def remote_copy(source, landing, send, recv, target):
    return pltpu.make_async_remote_copy(
        src_ref=source, dst_ref=landing, send_sem=send, recv_sem=recv, device_id=target,
        device_id_type=pl.DeviceIdType.MESH,
    )


def group_gather_kernel(topo, count, *refs):
    mine, outs = refs[:count], refs[count:2 * count]
    local_sem, send_sem, recv_sem = refs[2 * count:]
    layer = Layer(topo)
    c = layer.c
    arrays = range(count)
    a, b, sibling = layer.device(1, c), layer.device(2, c), layer.device(0, 1 - c)
    own = layer.pack(0, c)

    def send(i, way, pack, target):
        landing = outs[i].at[pack]
        source = mine[i] if way in (0, 1, 3) else landing
        return remote_copy(source, landing, send_sem.at[i, way], recv_sem.at[i, pack], target)

    ways = [
        (0, own, a), (1, own, b), (2, layer.pack(1, c), b), (3, own, sibling),
        (4, layer.pack(1, c), sibling), (5, layer.pack(2, c), sibling),
        (6, layer.pack(3, c), sibling),
    ]

    def start(k):
        for i in arrays:
            send(i, *ways[k]).start()

    def arrived(pack):
        for i in arrays:
            send(i, 2, pack, sibling).wait_recv()

    keep = [pltpu.make_async_copy(mine[i], outs[i].at[own], local_sem.at[i]) for i in arrays]
    for copy in keep:
        copy.start()
    layer.meet()
    start(0)
    start(1)
    start(3)
    arrived(layer.pack(1, c))
    start(2)
    start(4)
    arrived(layer.pack(2, c))
    start(5)
    arrived(layer.pack(3, c))
    start(6)
    for slot in range(4):
        arrived(layer.pack(slot, 1 - c))
    for way in ways:
        for i in arrays:
            send(i, *way).wait_send()
    for copy in keep:
        copy.wait()


def gather_layer(topo, arrays, ident):
    DMA = pltpu.SemaphoreType.DMA
    hbm = pl.BlockSpec(memory_space=pl.ANY)
    n = len(arrays)
    return pl.pallas_call(
        functools.partial(group_gather_kernel, topo, n),
        in_specs=[hbm] * n,
        out_specs=[hbm] * n,
        out_shape=[jax.ShapeDtypeStruct((topo.T,) + v.shape, v.dtype) for v in arrays],
        scratch_shapes=[DMA((n,)), DMA((n, 7)), DMA((n, topo.T))],
        compiler_params=pltpu.CompilerParams(collective_id=ident, has_side_effects=True),
        name="gather_layer",
    )(*arrays)


def group_reduce_kernel(topo, grads, out, held, from_c, from_b, from_a, c_send, c_recv, send_sem,
                        recv_sem):
    layer = Layer(topo)
    c = layer.c
    a, b, sibling = layer.device(1, c), layer.device(2, c), layer.device(0, 1 - c)
    order = (3, 2, 1, 0)

    def c_copy(slot):
        theirs = (0, 2, 1, 3)[slot]
        return remote_copy(
            grads.at[layer.pack(slot, 1 - c)], from_c.at[theirs], c_send.at[theirs],
            c_recv.at[theirs], sibling,
        )

    def c_arrived(slot):
        remote_copy(
            grads.at[layer.pack(slot, c)], from_c.at[slot], c_send.at[slot], c_recv.at[slot],
            sibling,
        ).wait_recv()

    across = remote_copy(held.at[3], from_b.at[1], send_sem.at[0], recv_sem.at[0], b)
    direct = remote_copy(held.at[2], from_b.at[0], send_sem.at[1], recv_sem.at[1], b)
    passed = remote_copy(held.at[1], from_a, send_sem.at[2], recv_sem.at[2], a)

    layer.meet()
    for slot in (3, 1, 2, 0):
        c_copy(slot).start()
    for slot in order:
        c_arrived(slot)
        held[slot] = grads[layer.pack(slot, c)] + from_c[slot]
        if slot == 3:
            across.start()
        if slot == 2:
            direct.start()
    across.wait_recv()
    held[1] = held[1] + from_b[1]
    passed.start()
    direct.wait_recv()
    held[0] = held[0] + from_b[0]
    passed.wait_recv()
    out[...] = held[0] + from_a[...]
    across.wait_send()
    direct.wait_send()
    passed.wait_send()
    for slot in range(4):
        c_copy(slot).wait_send()


def reduce_layer(topo, grads, ident):
    DMA = pltpu.SemaphoreType.DMA
    block = grads.shape[1:]
    return pl.pallas_call(
        functools.partial(group_reduce_kernel, topo),
        in_specs=[pl.BlockSpec(memory_space=pltpu.VMEM)],
        out_specs=pl.BlockSpec(memory_space=pltpu.VMEM),
        out_shape=jax.ShapeDtypeStruct(block, BF),
        scratch_shapes=[
            pltpu.VMEM((4,) + block, BF), pltpu.VMEM((4,) + block, BF),
            pltpu.VMEM((2,) + block, BF), pltpu.VMEM(block, BF),
            DMA((4,)), DMA((4,)), DMA((3,)), DMA((3,)),
        ],
        compiler_params=pltpu.CompilerParams(
            collective_id=ident, has_side_effects=True, vmem_limit_bytes=32 << 20
        ),
        name="reduce_layer",
    )(grads)


NT = (((1,), (1,)), ((), ()))
TN = (((0,), (0,)), ((), ()))
LANES = 2 * HD
CHUNKS = (HEADS + 1) // 2
ROOM = 60 << 20


def lanes_of(rows):
    return lax.broadcasted_iota(jnp.int32, (rows, LANES), 1)


def spin(v):
    first = lax.rem(lanes_of(v.shape[0]), HD) < HD // 2
    return jnp.where(first, -pltpu.roll(v, LANES - HD // 2, 1), pltpu.roll(v, HD // 2, 1))


def whole(*shape):
    return pl.BlockSpec(shape, lambda *i: (0,) * len(shape))


def normed(v, gain):
    return v * lax.rsqrt(jnp.mean(v * v, axis=-1, keepdims=True) + EPS) * gain


def project_kernel(state_ref, w_ref, turn_ref, n1_ref, q_ref, kv_ref, small_ref):
    start = (CHUNKS - 1) * LANES
    small = jnp.transpose(w_ref[:, start:start + LANES].astype(F32))[HD:HD + 8]
    small_ref[...] = small
    project_into(
        state_ref[...].astype(F32), small[RECS:RECS + 1], w_ref, turn_ref, n1_ref, q_ref, kv_ref
    )


def project(state, w, turns):
    n, model = state.shape
    return pl.pallas_call(
        project_kernel,
        grid=(1,),
        in_specs=[whole(n, model), whole(*w.shape), whole(*turns.shape)],
        out_specs=[
            whole(n, model), whole(CHUNKS, n, LANES), whole(n, KV_HEADS * LANES),
            whole(8, model),
        ],
        out_shape=[
            jax.ShapeDtypeStruct((n, model), BF),
            jax.ShapeDtypeStruct((CHUNKS, n, LANES), BF),
            jax.ShapeDtypeStruct((n, KV_HEADS * LANES), BF),
            jax.ShapeDtypeStruct((8, model), F32),
        ],
        compiler_params=pltpu.CompilerParams(vmem_limit_bytes=ROOM),
        name="project",
    )(state, w, turns)


def attend_kernel(rows, recursion, span, key_ref, query_ref, kv_ref, q_ref, mixed_ref, out_ref, stat_ref,
                  stacked, mixing, tops, sums):
    low = lanes_of(rows) < HD
    wide = SHARES * rows
    for h in range(KV_HEADS):
        for j in range(SHARES):
            head = h * SHARES + j
            chunk = q_ref[head // 2].astype(F32)
            if head % 2:
                chunk = pltpu.roll(chunk, HD, 1)
            stacked[h, j * rows:(j + 1) * rows, :] = jnp.where(low, chunk, 0.0).astype(BF)
    mixing[...] = jnp.zeros(mixing.shape, F32)
    sums[...] = jnp.zeros(sums.shape, F32)
    tops[...] = jnp.full(tops.shape, BIG, F32)

    def body(t, carry):
        at = pl.ds(pl.multiple_of(t * rows, rows), rows)
        bias = block_bias(key_ref[t], query_ref, recursion, rows)
        def score(h):
            kv = kv_ref[at, h * LANES:(h + 1) * LANES]
            return lax.dot_general(kv, stacked[h], NT, preferred_element_type=F32) + bias

        def end(h, p, fade):
            kv = kv_ref[at, h * LANES:(h + 1) * LANES]
            mixing[h] = mixing[h] * fade + lax.dot_general(
                kv[:, HD:], p, TN, preferred_element_type=F32
            )

        ahead = score(0)
        before = None
        for h in range(KV_HEADS):
            s = ahead
            if h + 1 < KV_HEADS:
                ahead = score(h + 1)
            if before is not None:
                end(*before)
            old = tops[h, 0:1, :]
            top = jnp.max(s.reshape(rows // 8, 8, wide), axis=0)
            top = jnp.maximum(old, jnp.max(top, axis=0, keepdims=True))
            p = jnp.exp(s - top)
            fade = jnp.exp(old - top)
            sums[h] = sums[h] * fade + jnp.sum(p.reshape(rows // 8, 8, wide), axis=0)
            tops[h] = jnp.broadcast_to(top, (8, wide))
            before = (h, p.astype(BF), fade)
        end(*before)
        return carry

    lax.fori_loop(span[0], span[1], body, 0)
    for h in range(KV_HEADS):
        total = jnp.sum(sums[h], axis=0, keepdims=True)
        stat_ref[h] = tops[h] + jnp.log(total)
        mixing[h] = mixing[h] / total
    for j in range(CHUNKS):
        both = head_pair(mixing, j, rows)
        out_ref[j] = both
        size = min(LANES, HEADS * HD - j * LANES)
        mixed_ref[:, j * LANES:j * LANES + size] = both.astype(BF)[:, :size]


def block_bias(labels, query_ref, recursion, rows):
    keys = jnp.transpose(labels.astype(F32))[:rows]
    order, level = keys[:, 0:1], keys[:, 2:3]
    live = jnp.where(level > recursion, order, -1.0)
    place, begin = query_ref[0:1, :].astype(F32), query_ref[1:2, :].astype(F32)
    allowed = ((live >= begin) & (live <= place)) | (order == place)
    return jnp.where(allowed, 0.0, BIG)


def head_pair(mixing, j, rows):
    def one(head):
        if head >= HEADS:
            return jnp.zeros((HD, rows), F32)
        at = head % SHARES * rows
        return mixing[head // SHARES, :, at:at + rows]

    return jnp.transpose(jnp.concatenate([one(2 * j), one(2 * j + 1)], axis=0))


def attend(rows, recursion, span, key_labels, query_labels, kv_all, q):
    count, columns = kv_all.shape
    wide = SHARES * rows
    return pl.pallas_call(
        functools.partial(attend_kernel, rows, recursion),
        grid_spec=pltpu.PrefetchScalarGridSpec(
            num_scalar_prefetch=1,
            grid=(1,),
            in_specs=[
                whole(*key_labels.shape), whole(8, wide), whole(count, columns),
                whole(CHUNKS, rows, LANES),
            ],
            out_specs=[
                whole(rows, HEADS * HD), whole(CHUNKS, rows, LANES), whole(KV_HEADS, 8, wide),
            ],
            scratch_shapes=[
                pltpu.VMEM((KV_HEADS, wide, LANES), BF), pltpu.VMEM((KV_HEADS, HD, wide), F32),
                pltpu.VMEM((KV_HEADS, 8, wide), F32), pltpu.VMEM((KV_HEADS, 8, wide), F32),
            ],
        ),
        out_shape=[
            jax.ShapeDtypeStruct((rows, HEADS * HD), BF),
            jax.ShapeDtypeStruct((CHUNKS, rows, LANES), F32),
            jax.ShapeDtypeStruct((KV_HEADS, 8, wide), F32),
        ],
        compiler_params=pltpu.CompilerParams(vmem_limit_bytes=62 << 20),
        cost_estimate=pl.CostEstimate(
            flops=16 * KV_HEADS * wide * count * HD, bytes_accessed=4 * count * columns,
            transcendentals=KV_HEADS * wide * count,
        ),
        name="attend",
    )(span, key_labels, query_labels, kv_all, q)


def attend_back_kernel(rows, recursion, span, key_ref, query_ref, kv_ref, q_ref, d_ref, out_ref, stat_ref,
                       turn_ref, dq_ref, dkv_ref, stacked, part, mixing, deltas):
    low = lanes_of(rows) < HD
    wide = SHARES * rows
    ones = jnp.ones((8, LANES), BF)
    for h in range(KV_HEADS):
        for j in range(SHARES):
            head = h * SHARES + j
            q = q_ref[head // 2].astype(F32)
            d = d_ref[head // 2].astype(F32)
            if head % 2:
                q = pltpu.roll(q, HD, 1)
            product = d * out_ref[head // 2]
            mine = ~low if head % 2 else low
            if head % 2 == 0:
                d = pltpu.roll(d, HD, 1)
            at = pl.ds(j * rows, rows)
            stacked[h, at, :] = jnp.where(low, q, d).astype(BF)
            part[at, :] = jnp.where(mine, product, 0.0)
        coarse = part[...].astype(BF)
        fine = (part[...] - coarse.astype(F32)).astype(BF)
        deltas[h] = lax.dot_general(
            ones, coarse, NT, preferred_element_type=F32
        ) + lax.dot_general(ones, fine, NT, preferred_element_type=F32)
    dkv_ref[...] = jnp.zeros(dkv_ref.shape, BF)
    mixing[...] = jnp.zeros(mixing.shape, F32)

    def body(t, carry):
        at = pl.ds(pl.multiple_of(t * rows, rows), rows)
        bias = block_bias(key_ref[t], query_ref, recursion, rows)
        for h in range(KV_HEADS):
            kv = kv_ref[at, h * LANES:(h + 1) * LANES]
            zero = jnp.zeros_like(kv)
            queries = stacked[h]
            s = lax.dot_general(jnp.where(low, kv, zero), queries, NT, preferred_element_type=F32)
            p = jnp.exp(s + bias - stat_ref[h, 0:1, :])
            dp = lax.dot_general(jnp.where(low, zero, kv), queries, NT, preferred_element_type=F32)
            ds = (p * (dp - deltas[h, 0:1, :])).astype(BF)
            dk = jnp.dot(ds, queries, preferred_element_type=F32)
            dv = jnp.dot(p.astype(BF), queries, preferred_element_type=F32)
            dkv_ref[at, h * LANES:(h + 1) * LANES] = jnp.where(low, dk, dv).astype(BF)
            mixing[h] += lax.dot_general(kv[:, :HD], ds, TN, preferred_element_type=F32)
        return carry

    lax.fori_loop(span[0], span[1], body, 0)
    cosine, sine = turn_ref[0], turn_ref[1]
    for j in range(CHUNKS):
        both = head_pair(mixing, j, rows) * HD ** -0.5
        both = both * cosine - spin(both) * sine
        dq_ref[:, j * LANES:(j + 1) * LANES] = both.astype(BF)


def attend_back(rows, recursion, span, key_labels, query_labels, kv_all, q, d_mixed, out, stat, turns):
    count, columns = kv_all.shape
    wide = SHARES * rows
    return pl.pallas_call(
        functools.partial(attend_back_kernel, rows, recursion),
        grid_spec=pltpu.PrefetchScalarGridSpec(
            num_scalar_prefetch=1,
            grid=(1,),
            in_specs=[
                whole(*key_labels.shape), whole(8, wide), whole(count, columns),
                whole(CHUNKS, rows, LANES), whole(CHUNKS, rows, LANES),
                whole(CHUNKS, rows, LANES), whole(KV_HEADS, 8, wide), whole(2, rows, LANES),
            ],
            out_specs=[whole(rows, CHUNKS * LANES), whole(count, columns)],
            scratch_shapes=[
                pltpu.VMEM((KV_HEADS, wide, LANES), BF), pltpu.VMEM((wide, LANES), F32),
                pltpu.VMEM((KV_HEADS, HD, wide), F32), pltpu.VMEM((KV_HEADS, 8, wide), F32),
            ],
        ),
        out_shape=[
            jax.ShapeDtypeStruct((rows, CHUNKS * LANES), BF),
            jax.ShapeDtypeStruct((count, columns), BF),
        ],
        compiler_params=pltpu.CompilerParams(vmem_limit_bytes=62 << 20),
        name="attend_back",
    )(span, key_labels, query_labels, kv_all, q, d_mixed, out, stat, turns)


def out_back_kernel(d_ref, w_ref, out_ref):
    d = d_ref[...]
    for j in range(CHUNKS):
        size = min(LANES, w_ref.shape[0] - j * LANES)
        v = lax.dot_general(
            d, w_ref[j * LANES:j * LANES + size, :], NT, preferred_element_type=F32
        ).astype(BF)
        if size < LANES:
            v = jnp.concatenate([v, jnp.zeros((d.shape[0], LANES - size), BF)], axis=1)
        out_ref[j] = v


def project_back_kernel(gradient_ref, state_ref, small_ref, w_ref, turn_ref, dq_ref, raw_ref,
                        grad_ref, joint_ref, dgain_ref):
    cosine, sine = turn_ref[0], turn_ref[1]
    key = lanes_of(dq_ref.shape[0]) < HD
    for j in range(KV_HEADS):
        v = raw_ref[:, j * LANES:(j + 1) * LANES].astype(F32)
        turned = v * cosine - spin(v) * sine
        at = (CHUNKS + j) * LANES
        joint_ref[:, at:at + LANES] = jnp.where(key, turned, v).astype(BF)
    split, full = CHUNKS * LANES, w_ref.shape[1]
    joint_ref[:, :split] = dq_ref[...]
    if joint_ref.shape[1] > full:
        joint_ref[:, full:] = jnp.zeros((key.shape[0], joint_ref.shape[1] - full), BF)
    d = lax.dot_general(joint_ref[:, :full], w_ref[...], NT, preferred_element_type=F32)
    v = state_ref[...].astype(F32)
    inv = lax.rsqrt(jnp.mean(v * v, axis=-1, keepdims=True) + EPS)
    scaled = d * small_ref[RECS:RECS + 1, :]
    dot = jnp.mean(scaled * v, axis=-1, keepdims=True)
    grad_ref[...] = gradient_ref[...] + inv * scaled - v * (inv * inv * inv * dot)
    dgain_ref[...] = jnp.sum(d * v * inv, axis=0, keepdims=True)


def project_back(gradient, state, small, w, turns, dq, dkv):
    n, model = dq.shape[0], state.shape[1]
    joint = -(-w.shape[1] // 256) * 256
    return pl.pallas_call(
        project_back_kernel,
        grid=(1,),
        in_specs=[
            whole(n, model), whole(n, model), whole(8, model), whole(*w.shape),
            whole(2, n, LANES), whole(*dq.shape), whole(*dkv.shape),
        ],
        out_specs=[whole(n, model), whole(n, joint), whole(1, model)],
        out_shape=[
            jax.ShapeDtypeStruct((n, model), F32),
            jax.ShapeDtypeStruct((n, joint), BF),
            jax.ShapeDtypeStruct((1, model), F32),
        ],
        compiler_params=pltpu.CompilerParams(vmem_limit_bytes=ROOM),
        name="project_back",
    )(gradient, state, small, w, turns, dq, dkv)


def project_into(state, gain, w_ref, turn_ref, n1_ref, q_ref, kv_ref):
    n1 = normed(state, gain).astype(BF)
    n1_ref[...] = n1
    rows = n1.shape[0]
    cosine, sine = turn_ref[0, :rows], turn_ref[1, :rows]
    key = lanes_of(rows) < HD
    columns = w_ref.shape[1]
    for start in range(0, columns, 2 * LANES):
        wide = min(2 * LANES, columns - start)
        both = jnp.dot(n1, w_ref[:, start:start + wide], preferred_element_type=F32)
        for half in range(wide // LANES):
            j = start // LANES + half
            v = both[:, half * LANES:(half + 1) * LANES]
            turned = v * cosine + spin(v) * sine
            if j < CHUNKS:
                q_ref[j] = (turned * HD ** -0.5).astype(BF)
            else:
                j -= CHUNKS
                kv_ref[:, j * LANES:(j + 1) * LANES] = jnp.where(key, turned, v).astype(BF)


def active_column(label_ref, recursion, rows):
    level = jnp.transpose(label_ref[...].astype(F32))[:rows, 2:3]
    return jnp.where(level > recursion, 1.0, 0.0)


def feed_kernel(recursion, following, mixed_ref, state_ref, w_out_ref, small_ref, label_ref,
                w_gate_ref, w_up_ref, w_down_ref, *refs):
    if following:
        w_ref, turn_ref = refs[:2]
        refs = refs[2:]
    (new_ref, middle_ref, n2_ref, gated_ref, up_ref, hidden_ref, both_ref, gate_ref) = refs[:8]
    step = pl.program_id(0)

    @pl.when(step == 0)
    def _():
        att = jnp.dot(mixed_ref[...], w_out_ref[...], preferred_element_type=F32)
        middle = state_ref[...].astype(F32) + att
        middle_ref[...] = middle
        n2_ref[...] = normed(middle, small_ref[RECS + 1:RECS + 2, :]).astype(BF)
        both_ref[...] = att

    n2 = n2_ref[...]
    gated = jnp.dot(n2, w_gate_ref[...], preferred_element_type=F32)
    upward = jnp.dot(n2, w_up_ref[...], preferred_element_type=F32)
    hidden = (gated * jax.nn.sigmoid(gated) * upward).astype(BF)
    gated_ref[...] = gated.astype(BF)
    up_ref[...] = upward.astype(BF)
    hidden_ref[...] = hidden
    both_ref[...] += jnp.dot(hidden, w_down_ref[...], preferred_element_type=F32)

    @pl.when(step == pl.num_programs(0) - 1)
    def _():
        state = state_ref[...].astype(F32)
        router = small_ref[recursion:recursion + 1, :]
        gate = jax.nn.sigmoid(jnp.sum(state * router, axis=-1, keepdims=True))
        active = active_column(label_ref, recursion, state.shape[0])
        gate_ref[...] = gate
        new_ref[...] = state + active * gate * both_ref[...]
        if following:
            project_into(
                new_ref[:following, :], small_ref[RECS:RECS + 1, :], w_ref, turn_ref, *refs[8:11]
            )


def feed(recursion, mixed, state, w_out, small, labels, w_gate, w_up, w_down, following, then=()):
    n, model = mixed.shape
    ff = w_gate.shape[1]
    tile = ff // 2 if ff % 256 == 0 else ff
    across = pl.BlockSpec((model, tile), lambda i: (0, i))
    made = pl.BlockSpec((n, tile), lambda i: (0, i))
    out_specs = [
        whole(n, model), whole(n, model), whole(n, model), made, made, made, whole(n, model),
        whole(n, 1),
    ]
    wide = lambda dtype: jax.ShapeDtypeStruct((n, model), dtype)
    tall = jax.ShapeDtypeStruct((n, ff), BF)
    out_shape = [
        wide(F32), wide(F32), wide(BF), tall, tall, tall, wide(F32),
        jax.ShapeDtypeStruct((n, 1), F32),
    ]
    if following:
        shapes = [(following, model), (CHUNKS, following, LANES), (following, KV_HEADS * LANES)]
        out_specs += [whole(*s) for s in shapes]
        out_shape += [jax.ShapeDtypeStruct(s, BF) for s in shapes]
    return pl.pallas_call(
        functools.partial(feed_kernel, recursion, following),
        grid=(ff // tile,),
        in_specs=[
            whole(n, model), whole(n, model), whole(*w_out.shape), whole(8, model),
            whole(*labels.shape), across, across,
            pl.BlockSpec((tile, model), lambda i: (i, 0)),
        ] + ([whole(*then[0].shape), whole(2, following, LANES)] if following else []),
        out_specs=out_specs,
        out_shape=out_shape,
        compiler_params=pltpu.CompilerParams(vmem_limit_bytes=ROOM),
        cost_estimate=pl.CostEstimate(
            flops=2 * n * model * (model + 3 * ff), transcendentals=n * ff,
            bytes_accessed=2 * model * (model + 3 * ff) + 24 * n * model + 6 * n * ff,
        ),
        name="feed",
    )(mixed, state, w_out, small, labels, w_gate, w_up, w_down, *then)


def feed_back_kernel(recursion, gradient_ref, both_ref, gate_ref, label_ref, state_ref,
                     small_ref, middle_ref, w_out_ref, gated_ref, up_ref, w_gate_ref, w_up_ref,
                     w_down_ref, d_fed_ref, d_gated_ref, d_up_ref, d_att_ref, grad_ref,
                     d_mixed_ref, d_router_ref, d_gain_ref, total):
    step = pl.program_id(0)

    @pl.when(step == 0)
    def _():
        active = active_column(label_ref, recursion, gate_ref.shape[0])
        d_fed_ref[...] = (active * gate_ref[...] * gradient_ref[...].astype(F32)).astype(BF)
        total[...] = jnp.zeros(total.shape, F32)

    d_hidden = lax.dot_general(d_fed_ref[...], w_down_ref[...], NT, preferred_element_type=F32)
    gated, upward = gated_ref[...].astype(F32), up_ref[...].astype(F32)
    sig = jax.nn.sigmoid(gated)
    part = d_hidden * sig
    d_up = (part * gated).astype(BF)
    d_gated = (part * upward * (1.0 + gated * (1.0 - sig))).astype(BF)
    d_up_ref[...] = d_up
    d_gated_ref[...] = d_gated
    total[...] += lax.dot_general(
        d_gated, w_gate_ref[...], NT, preferred_element_type=F32
    ) + lax.dot_general(d_up, w_up_ref[...], NT, preferred_element_type=F32)

    @pl.when(step == pl.num_programs(0) - 1)
    def _():
        gradient, gate = gradient_ref[...].astype(F32), gate_ref[...]
        active = active_column(label_ref, recursion, gate.shape[0])
        router = small_ref[recursion:recursion + 1, :]
        d = total[...]
        v = middle_ref[...]
        inv = lax.rsqrt(jnp.mean(v * v, axis=-1, keepdims=True) + EPS)
        d_gain_ref[...] = jnp.sum(d * v * inv, axis=0, keepdims=True)
        scaled = d * small_ref[RECS + 1:RECS + 2, :]
        dot = jnp.mean(scaled * v, axis=-1, keepdims=True)
        d_middle = inv * scaled - v * (inv * inv * inv * dot)
        d_gate = active * gate * (1.0 - gate) * jnp.sum(
            gradient * both_ref[...], axis=-1, keepdims=True
        )
        d_router_ref[...] = jnp.sum(state_ref[...].astype(F32) * d_gate, axis=0, keepdims=True)
        grad_ref[...] = gradient + d_gate * router + d_middle
        d_att_ref[...] = (active * gate * gradient + d_middle).astype(BF)
        out_back_kernel(d_att_ref, w_out_ref, d_mixed_ref)


def feed_back(recursion, gradient, both, gate, labels, state, small, middle, w_out, gated, upward,
              w_gate, w_up, w_down):
    n, model = both.shape
    ff = w_gate.shape[1]
    tile = ff // 2 if ff % 256 == 0 else ff
    across = pl.BlockSpec((model, tile), lambda i: (0, i))
    made = pl.BlockSpec((n, tile), lambda i: (0, i))
    wide = whole(n, model)
    flat = lambda dtype: jax.ShapeDtypeStruct((n, model), dtype)
    tall = jax.ShapeDtypeStruct((n, ff), BF)
    row = jax.ShapeDtypeStruct((1, model), F32)
    return pl.pallas_call(
        functools.partial(feed_back_kernel, recursion),
        grid=(ff // tile,),
        in_specs=[
            wide, wide, whole(n, 1), whole(*labels.shape), wide, whole(8, model), wide,
            whole(*w_out.shape), made, made, across, across,
            pl.BlockSpec((tile, model), lambda i: (i, 0)),
        ],
        out_specs=[
            wide, made, made, wide, wide, whole(CHUNKS, n, LANES), whole(1, model),
            whole(1, model),
        ],
        out_shape=[
            flat(BF), tall, tall, flat(BF), flat(F32),
            jax.ShapeDtypeStruct((CHUNKS, n, LANES), BF), row, row,
        ],
        scratch_shapes=[pltpu.VMEM((n, model), F32)],
        compiler_params=pltpu.CompilerParams(vmem_limit_bytes=ROOM),
        cost_estimate=pl.CostEstimate(
            flops=2 * n * model * (model + 3 * ff), transcendentals=n * ff,
            bytes_accessed=2 * model * (model + 3 * ff) + 24 * n * model + 8 * n * ff,
        ),
        name="feed_back",
    )(gradient, both, gate, labels, state, small, middle, w_out, gated, upward, w_gate, w_up,
      w_down)


def outer_rows_kernel(count, *refs):
    xs, ds, out_ref = refs[:count], refs[count:2 * count], refs[2 * count]
    total = None
    for x_ref, d_ref in zip(xs, ds):
        part = jnp.dot(jnp.transpose(x_ref[...]), d_ref[...], preferred_element_type=F32)
        total = part if total is None else total + part
    out_ref[...] = total.astype(BF)


def outer_rows(xs, ds, tile):
    rows, columns = xs[0].shape[1], ds[0].shape[1]
    tokens = sum(x.shape[0] for x in xs)
    return pl.pallas_call(
        functools.partial(outer_rows_kernel, len(xs)),
        grid=(rows // tile,),
        in_specs=[pl.BlockSpec((x.shape[0], tile), lambda i: (0, i)) for x in xs]
        + [whole(*d.shape) for d in ds],
        out_specs=pl.BlockSpec((tile, columns), lambda i: (i, 0)),
        out_shape=jax.ShapeDtypeStruct((rows, columns), BF),
        compiler_params=pltpu.CompilerParams(vmem_limit_bytes=ROOM),
        cost_estimate=pl.CostEstimate(
            flops=2 * tokens * rows * columns, transcendentals=0,
            bytes_accessed=2 * (tokens * (columns + rows) + rows * columns),
        ),
        name="outer_rows",
    )(*xs, *ds)


def finish_kernel(onehot_ref, final_ref, gradient_ref, qkv_ref, o_ref, gu_ref, down_ref,
                  block_ref, token_ref, query_ref, key_ref, value_ref, out_ref, gate_ref, up_ref,
                  gdown_ref, tiny_ref):
    onehot = onehot_ref[...]
    block_ref[...] = lax.dot_general(
        final_ref[...], onehot, TN, preferred_element_type=F32
    ).astype(BF)
    token_ref[...] = lax.dot_general(
        gradient_ref[...], onehot, TN, preferred_element_type=F32
    ).astype(BF)
    model = query_ref.shape[1]
    query_ref[...] = qkv_ref[:, :model].astype(F32)
    out_ref[...] = o_ref[:, :model].astype(F32)
    rows = query_ref.shape[0]
    room = jnp.zeros((-rows % LANES, LANES), F32)

    def across(v):
        return jnp.transpose(jnp.concatenate([v, room], axis=0))[:, :rows]

    tiny = jnp.concatenate(
        [o_ref[:, model:].astype(F32), jnp.zeros((rows, LANES - HD), F32)], axis=1
    )
    tiny_ref[...] = across(tiny)[:8]
    gate_ref[...] = gu_ref[0].astype(F32)
    up_ref[...] = gu_ref[1].astype(F32)
    gdown_ref[...] = down_ref[...].astype(F32)
    low = lanes_of(rows) < HD
    heads = [
        qkv_ref[:, (CHUNKS + h) * LANES:(CHUNKS + h + 1) * LANES].astype(F32)
        for h in range(KV_HEADS)
    ]
    for h in range(0, KV_HEADS, 2):
        even, odd = heads[h], heads[min(h + 1, KV_HEADS - 1)]
        at = slice(h * HD, min(h + 2, KV_HEADS) * HD)
        size = at.stop - at.start
        key_ref[at, :] = across(jnp.where(low, even, pltpu.roll(odd, HD, 1)))[:size]
        value_ref[at, :] = across(jnp.where(low, pltpu.roll(even, HD, 1), odd))[:size]


def finish(onehot, final, gradient, qkv, o, gu, down):
    rows, model = final.shape
    shard, ff = gu.shape[1:]
    kv = KV_HEADS * HD
    shapes = [
        (model, rows), (model, rows), (shard, model), (kv, shard), (kv, shard), (shard, model),
        (shard, ff), (shard, ff), down.shape, (8, shard),
    ]
    args = (onehot, final, gradient, qkv, o, gu, down)
    return pl.pallas_call(
        finish_kernel,
        grid=(1,),
        in_specs=[whole(*v.shape) for v in args],
        out_specs=[whole(*v) for v in shapes],
        out_shape=[jax.ShapeDtypeStruct(v, BF if i < 2 else F32) for i, v in enumerate(shapes)],
        compiler_params=pltpu.CompilerParams(vmem_limit_bytes=ROOM),
        name="finish",
    )(*args)


def mm(a, b):
    return jnp.dot(a, b, preferred_element_type=F32)


def mm_tn(a, b):
    return lax.dot_general(a, b, TN, preferred_element_type=F32)


def per_device(topo, *args):
    (tokens, w_query, w_key, w_value, w_out, w_gate, w_up, w_down, router, norm_attn, norm_ffn,
     lengths, depths, padding, cotangent) = args
    rows, model = tokens.shape
    kv_cols = w_key.shape[1]
    ff = w_gate.shape[1]
    shard = w_query.shape[0]
    deep_rows = rows * 3 // 4
    xk, yk, ck = (topo.keys(d) for d in "xyc")

    small = jnp.concatenate([router, norm_attn[:, None], norm_ffn[:, None]], axis=1)
    small = jnp.pad(small, ((0, 0), (0, HD - small.shape[1])))
    w_kv = jnp.stack(
        [w_key.reshape(shard, KV_HEADS, HD), w_value.reshape(shard, KV_HEADS, HD)], axis=2
    ).reshape(shard, 2 * kv_cols)
    first = jnp.concatenate([w_query, small, w_kv], axis=1)
    weight_qkv, weight_g, weight_u, weight_d, weight_o = gather_weights(
        topo, [first, w_gate, w_up, w_down, w_out]
    )

    own = lax.axis_index("tok") * rows + jnp.arange(rows, dtype=jnp.int32)
    eligible = (depths >= 2) & (padding > 0)
    flags = jnp.stack([eligible, ~eligible]).astype(BF)
    upto = (jnp.arange(rows)[:, None] <= jnp.arange(rows)[None, :]).astype(BF)
    counts = mm(flags, upto).astype(jnp.int32)
    slot = jnp.where(eligible, counts[0] - 1, counts[0, -1] + counts[1] - 1)
    chosen = jnp.arange(rows, dtype=jnp.int32)[:, None] == slot[None, :]
    onehot = chosen.astype(BF)
    doc_ends = jnp.cumsum(lengths[0])
    begins = jnp.sum(
        jnp.where(own[:, None] >= doc_ends[None, :], lengths[0][None, :], 0), axis=1
    )
    levels = jnp.where(padding > 0, depths, 0)
    labels = jnp.stack([own, begins, levels])
    labels = jnp.sum(jnp.where(chosen[None], labels[:, None, :], 0), axis=2)
    labels = jnp.pad(labels, ((0, 5), (0, 0)))
    swap = topo.swap_pairs()
    state = lax.ppermute(mm(onehot, tokens).astype(BF), AXES, swap)
    labels = lax.ppermute(labels, AXES, swap)
    cotangent = mm(onehot, cotangent).astype(BF)

    def collect(arrays, ident):
        if small_layer(topo):
            return gather_layer(topo, arrays, ident)
        return [group_gather(topo, v, xk + yk + ck) for v in arrays]

    def distribute(grads, ident):
        if small_layer(topo):
            return reduce_layer(topo, grads, ident)
        return group_scatter(topo, grads, ck + yk + xk)


    pack = (lax.axis_index("grp") * topo.X) + lax.axis_index("tok") % topo.X
    lowest = jnp.min(labels[1])
    span = jnp.stack([lowest // rows, pack + 1]).astype(jnp.int32)
    places = (labels[0] - labels[1]).astype(F32)
    turn = (jnp.arange(LANES) % (HD // 2)).astype(F32)
    freqs = 10000.0 ** (-(turn * 2.0 / HD))
    angles = places[:, None] * freqs[None, :]
    turns = jnp.stack([jnp.cos(angles), jnp.sin(angles)])
    query_labels = {
        n: jnp.concatenate([labels[:, :n]] * SHARES, axis=1) for n in (rows, deep_rows)
    }

    def forward(state, projected, recursion, labels_all=None, pending=None):
        extra = None
        n1, q, kv = projected
        n = n1.shape[0]
        if recursion == 0:
            kv_all, labels_all = collect([kv, labels], 2)
            kv_all, later = lax.optimization_barrier((kv_all, cotangent))
            later = lax.ppermute(later, AXES, swap)
        else:
            kv_all, = collect([kv], 3)
        kv_all = kv_all.reshape(topo.T * n, 2 * kv_cols)
        mixed, out, stat = attend(n, recursion, span, labels_all, query_labels[n], kv_all, q)
        if recursion == 0:
            extra = (labels_all, later)
        if pending is not None:
            mixed, extra = lax.optimization_barrier((mixed, pending))
        following = deep_rows if recursion + 1 < RECS else 0
        new, middle, n2, gated, upward, hidden, both, gate, *projected = feed(
            recursion, mixed, state, weight_o, small, labels, weight_g, weight_u, weight_d,
            following, (weight_qkv, turns) if following else (),
        )
        kept = (state, n1, q, kv_all, labels_all, out, stat, mixed, middle, n2, gated, upward,
                hidden, both, gate)
        return (new, projected, kept, extra)

    def backward(gradient, recursion, kept):
        (state, n1, q, kv_all, labels_all, out, stat, mixed, middle, n2, gated, upward, hidden,
         both, gate) = kept
        n = n1.shape[0]
        d_fed, d_gated, d_up, d_att, gradient, d_mixed, d_router, d_gain_two = feed_back(
            recursion, gradient, both, gate, labels, state, small, middle, weight_o, gated,
            upward, weight_g, weight_u, weight_d,
        )
        dq, dkv = attend_back(
            n, recursion, span, labels_all, query_labels[n], kv_all, q, d_mixed, out, stat, turns
        )
        dkv = distribute(dkv.reshape(topo.T, n, 2 * kv_cols), 5 if recursion else 4)
        gradient, dqkv, d_gain_one = project_back(
            gradient, state, small, weight_qkv, turns, dq, dkv
        )
        left = (n1, dqkv, mixed, d_att, n2, d_gated, d_up, hidden, d_fed)
        return (gradient, left, (d_router[0], d_gain_one[0], d_gain_two[0]))

    *projected, small = project(state, weight_qkv, turns)
    whole_state, projected, kept, (labels_all, gradient) = forward(state, projected, 0)
    deep = whole_state
    all_kept = [kept]
    for recursion in range(1, RECS):
        pending = gradient if recursion == 1 else None
        deep, projected, kept, extra = forward(deep, projected, recursion, labels_all, pending)
        gradient = extra if recursion == 1 else gradient
        all_kept.append(kept)
    final = jnp.concatenate([deep, whole_state[deep_rows:]], axis=0).astype(BF)

    deep_grad = gradient
    lefts, smalls = [], []
    for recursion in reversed(range(1, RECS)):
        deep_grad, left, tiny = backward(deep_grad, recursion, all_kept[recursion])
        lefts.append(left)
        smalls.append(tiny)
    deep_grad, final = lax.optimization_barrier((deep_grad, lax.ppermute(final, AXES, swap)))
    gradient = jnp.concatenate([deep_grad, gradient[deep_rows:].astype(F32)], axis=0)
    gradient, left, tiny = backward(gradient, 0, all_kept[0])
    lefts.append(left)
    smalls.append(tiny)
    gradient = lax.ppermute(gradient.astype(BF), AXES, swap)

    n1, dqkv, mixed, d_att, n2, d_gated, d_up, hidden, d_fed = zip(*lefts)

    def outer(xs, ds):
        return mm_tn(jnp.concatenate(xs, axis=0), jnp.concatenate(ds, axis=0))

    cut = lambda v: v.astype(BF).reshape(topo.T, -1, v.shape[-1])
    tiny = jnp.stack(
        [smalls[2][0], smalls[1][0], smalls[0][0],
         smalls[0][1] + smalls[1][1] + smalls[2][1],
         smalls[0][2] + smalls[1][2] + smalls[2][2]], axis=1
    )
    wide_out = -(-(model + tiny.shape[1]) // 256) * 256
    tiny = jnp.pad(tiny, ((0, 0), (0, wide_out - model - tiny.shape[1])))
    grad_qkv, grad_o, grad_gu, grad_down = reduce_gradients(topo, [
        cut(outer(n1, dqkv)),
        cut(jnp.concatenate([outer(mixed, d_att), tiny], axis=1)),
        cut(outer(n2, d_gated)),
        outer_rows(hidden, d_fed, 640).reshape(topo.T, -1, model),
        cut(outer(n2, d_up)),
    ])
    block, token, grad_query, grad_key, grad_value, *others, tiny = finish(
        onehot, final, gradient, grad_qkv, grad_o, grad_gu, grad_down
    )
    return (block.T, token.T, grad_query, grad_key.T, grad_value.T) + tuple(others) + (
        tiny[:RECS].T, tiny[RECS], tiny[RECS + 1]
    )


def solution(mesh):
    topo = Topo(mesh.shape["grp"], mesh.shape["tok"])
    both = P(("grp", "tok"))
    wide = P(("grp", "tok"), None)
    rows = P("tok", None)
    row = P("tok")
    return jax.shard_map(
        functools.partial(per_device, topo),
        mesh=mesh,
        in_specs=(wide,) + (rows,) * 8 + (row, row, P("grp", None), both, both, wide),
        out_specs=(wide, wide) + (rows,) * 8 + (row, row),
        check_vma=False,
    )
```

```python
import functools

import jax
import jax.numpy as jnp
from jax import lax
from jax.experimental import pallas as pl
from jax.experimental.pallas import tpu as pltpu
from jax.sharding import PartitionSpec as P

HEADS = 15
KV_HEADS = 5
SHARES = HEADS // KV_HEADS
HD = 64
RECS = 3
EPS = 1e-05
BF = jnp.bfloat16
F32 = jnp.float32
BIG = -1e30
AXES = ("grp", "tok")


class Topo:
    def __init__(self, groups, spread):
        self.G = groups
        self.T = spread
        self.X = spread // groups
        self.Z = groups
        self.Y = groups // 2
        self.bits = {
            "z": self.Z.bit_length() - 1,
            "x": self.X.bit_length() - 1,
            "y": self.Y.bit_length() - 1,
            "c": 1,
        }

    def keys(self, dim):
        return [(dim, k) for k in range(self.bits[dim])]

    def masks(self, key):
        dim, k = key
        if dim == "c":
            return (1, 0)
        if dim == "y":
            return (2 << k, 0)
        if dim == "x":
            return (0, 1 << k)
        return (0, self.X << k)

    def pairs(self, key):
        mg, mt = self.masks(key)
        return [
            (g * self.T + t, (g ^ mg) * self.T + (t ^ mt))
            for g in range(self.G)
            for t in range(self.T)
        ]

    def swap_pairs(self):
        out = []
        for g in range(self.G):
            for t in range(self.T):
                z, x = t // self.X, t % self.X
                out.append((g * self.T + t, z * self.T + g * self.X + x))
        return out

    def bit(self, key):
        mg, mt = self.masks(key)
        if mg:
            return (lax.axis_index("grp") // mg) % 2
        return (lax.axis_index("tok") // mt) % 2


def exchange(topo, arr, key):
    return lax.ppermute(arr, AXES, topo.pairs(key))


def double(topo, arr, key, axis, stack):
    other = exchange(topo, arr, key)
    mine_is_high = topo.bit(key) == 1
    low = jnp.where(mine_is_high, other, arr)
    high = jnp.where(mine_is_high, arr, other)
    if stack:
        return jnp.stack([low, high], axis=axis)
    return jnp.concatenate([low, high], axis=axis)


def halve(topo, arr, key, axis, stack):
    mine_is_high = topo.bit(key) == 1
    if stack:
        low = lax.index_in_dim(arr, 0, axis, keepdims=False)
        high = lax.index_in_dim(arr, 1, axis, keepdims=False)
    else:
        half = arr.shape[axis] // 2
        low = lax.slice_in_dim(arr, 0, half, axis=axis)
        high = lax.slice_in_dim(arr, half, 2 * half, axis=axis)
    send = jnp.where(mine_is_high, low, high).astype(BF)
    keep = jnp.where(mine_is_high, high, low).astype(F32)
    return (keep + exchange(topo, send, key).astype(F32)).astype(BF)


class Piece:
    def __init__(self, array, dim, start, size, core, part):
        self.array, self.dim, self.start, self.size = array, dim, start, size
        self.core, self.part = core, part

    def of(self, ref):
        if self.dim == 0:
            return ref.at[pl.ds(self.start, self.size), :]
        return ref.at[:, pl.ds(self.start, self.size)]


def cut_pieces(shapes):
    near = lambda v, unit: max(unit, int(round(v / unit)) * unit)
    wide_a, wide_g, wide_u, tall = shapes[0][1], shapes[1][1], shapes[2][1], shapes[3][0]
    g = near(wide_g * 0.7, 128)
    u = near(wide_u * 0.65, 128)
    d = near(tall * 0.3, 8)
    return [
        Piece(1, 1, 0, g, 0, 0),
        Piece(4, 1, 0, shapes[4][1], 0, 2),
        Piece(1, 1, g, wide_g - g, 0, 2),
        Piece(0, 1, 0, wide_a, 0, 1),
        Piece(2, 1, u, wide_u - u, 1, 0),
        Piece(3, 0, 0, d, 1, 0),
        Piece(3, 0, d, tall - d, 1, 2),
        Piece(2, 1, 0, u, 1, 1),
    ]


def coordinates(topo):
    g, t = lax.axis_index("grp"), lax.axis_index("tok")
    return lax.rem(t, topo.X), lax.div(g, 2), lax.div(t, topo.X), lax.rem(g, 2)


def gather_kernel(topo, pieces, *refs):
    shards, outs = refs[:5], refs[5:10]
    local_sem, recv_sem, z_sem, x_sem, y_sem, c_sem = refs[10:]
    x, y, z, c = coordinates(topo)
    X, Z, T = topo.X, topo.Z, topo.T
    g, me = lax.axis_index("grp"), lax.axis_index("tok")
    odd = lax.rem(y, 2)
    over_y = {"grp": g + 2 - 4 * odd, "tok": me}
    over_c = {"grp": g + 1 - 2 * c, "tok": me}

    def over_z(k):
        return {"grp": g, "tok": (z + k) * X + x}

    def over_x(k):
        return {"grp": g, "tok": z * X + lax.rem(x + k, X)}

    barrier = pltpu.get_barrier_semaphore()
    partners = [over_y, over_c] + [over_x(k) for k in range(1, X)]
    for partner in partners:
        pl.semaphore_signal(barrier, inc=1, device_id=partner, device_id_type=pl.DeviceIdType.MESH)
    below, above = z > 0, z < Z - 1

    def greet(k):
        pl.semaphore_signal(
            barrier, inc=1, device_id=over_z(k), device_id_type=pl.DeviceIdType.MESH
        )

    pl.when(below)(lambda: greet(-1))
    pl.when(above)(lambda: greet(1))
    own = [
        pltpu.make_async_copy(shards[i], outs[i].at[me], local_sem.at[i]) for i in range(5)
    ]
    for copy in own:
        copy.start()
    pl.semaphore_wait(barrier, len(partners) + below.astype(jnp.int32) + above.astype(jnp.int32))

    def send(p, t, sem, target, mine=False):
        piece = pieces[p]
        landing = piece.of(outs[piece.array].at[t])
        source = piece.of(shards[piece.array]) if mine else landing
        return pltpu.make_async_remote_copy(
            src_ref=source, dst_ref=landing, send_sem=sem, recv_sem=recv_sem.at[p, t],
            device_id=target, device_id_type=pl.DeviceIdType.MESH,
        )

    def arrived(p, t):
        send(p, t, c_sem.at[0, 0], over_c).wait_recv()

    def run(core):
        mine = [p for p in range(len(pieces)) if pieces[p].core == core]
        theirs = [p for p in range(len(pieces)) if pieces[p].core != core]
        slot = {p: i for i, p in enumerate(mine)}

        def inside(p, body):
            part = pieces[p].part
            if part == 1:
                body()
            else:
                pl.when(odd == part // 2)(body)

        def outside(p, body):
            if pieces[p].part != 1:
                pl.when(odd != pieces[p].part // 2)(body)

        def x_copies(p, zz, first):
            t = zz * X + x
            return [
                send(p, t, x_sem.at[slot[p], zz, k - 1], over_x(k), first) for k in range(1, X)
            ]

        def y_copy(p, t):
            return send(p, t, y_sem.at[slot[p], t], over_y)

        def c_copy(p, t):
            return send(p, t, c_sem.at[slot[p], t], over_c)

        def z_copy(p, zz, k, first):
            return send(p, zz * X + x, z_sem.at[slot[p], zz, (k + 1) // 2], over_z(k), first)

        for p in mine:
            def begin(p=p):
                pl.when(below)(lambda: z_copy(p, z, -1, True).start())
                pl.when(above)(lambda: z_copy(p, z, 1, True).start())
                for copy in x_copies(p, z, True):
                    copy.start()
            inside(p, begin)

        def share(p, t):
            if pieces[p].part != 1:
                y_copy(p, t).start()
            c_copy(p, t).start()

        def relay(p, zz, k):
            arrived(p, zz * X + x)
            pl.when(above if k > 0 else below)(lambda: z_copy(p, zz, k, False).start())
            for copy in x_copies(p, zz, False):
                copy.start()
            share(p, zz * X + x)

        def others(p, zz):
            for j in range(1, X):
                t = zz * X + lax.rem(x + j, X)
                arrived(p, t)
                share(p, t)

        def around(k, carry):
            low, high = z - k, z + k
            for p in mine:
                inside(p, lambda p=p: pl.when(low >= 0)(lambda: relay(p, low, 1)))
                inside(p, lambda p=p: pl.when(high < Z)(lambda: relay(p, high, -1)))
            low, high = z - k + 1, z + k - 1
            for p in mine:
                inside(p, lambda p=p: pl.when(low >= 0)(lambda: others(p, low)))
                inside(p, lambda p=p: pl.when((k > 1) & (high < Z))(lambda: others(p, high)))
            return carry

        lax.fori_loop(1, Z + 1, around, 0)

        def rest(t, carry):
            @pl.when(t != me)
            def _():
                for p in mine:
                    def forward(p=p):
                        arrived(p, t)
                        c_copy(p, t).start()
                    outside(p, forward)
            return carry

        lax.fori_loop(0, T, rest, 0)

        def finish(t, carry):
            @pl.when(t != me)
            def _():
                for p in theirs:
                    arrived(p, t)
                for p in mine:
                    c_copy(p, t).wait_send()
                    if pieces[p].part != 1:
                        inside(p, lambda p=p: y_copy(p, t).wait_send())
            return carry

        lax.fori_loop(0, T, finish, 0)
        for p in mine:
            def end(p=p):
                def each(zz, carry):
                    pl.when((zz <= z) & above)(lambda: z_copy(p, zz, 1, False).wait_send())
                    pl.when((zz >= z) & below)(lambda: z_copy(p, zz, -1, False).wait_send())
                    for copy in x_copies(p, zz, False):
                        copy.wait_send()
                    return carry
                lax.fori_loop(0, Z, each, 0)
            inside(p, end)

    pl.when(c == 0)(lambda: run(0))
    pl.when(c == 1)(lambda: run(1))
    for copy in own:
        copy.wait()


def gather_weights(topo, shards):
    pieces = cut_pieces([s.shape for s in shards])
    T = topo.T
    DMA = pltpu.SemaphoreType.DMA
    hbm = pl.BlockSpec(memory_space=pl.ANY)
    outs = pl.pallas_call(
        functools.partial(gather_kernel, topo, pieces),
        in_specs=[hbm] * 5,
        out_specs=[hbm] * 5,
        out_shape=[jax.ShapeDtypeStruct((T,) + s.shape, s.dtype) for s in shards],
        scratch_shapes=[
            DMA((5,)), DMA((len(pieces), T)), DMA((4, topo.Z, 2)), DMA((4, topo.Z, topo.X - 1)),
            DMA((4, T)), DMA((4, T)),
        ],
        compiler_params=pltpu.CompilerParams(collective_id=0, has_side_effects=True),
        name="gather_weights",
    )(*shards)
    return [o.reshape(-1, o.shape[-1]) for o in outs]


class Share:
    def __init__(self, array, start, shape, part):
        self.array, self.start, self.shape, self.part = array, start, shape, part

    def of(self, ref, core, *lead):
        rows, columns = self.shape
        if self.array == 2:
            return ref.at[lead + (slice(None), pl.ds(self.start, columns))]
        if self.array == 3:
            at = pl.multiple_of(core * rows, rows)
            return ref.at[lead + (pl.ds(at, rows), slice(None))]
        at = pl.multiple_of(core * columns, 128)
        return ref.at[lead + (slice(None), pl.ds(at, columns))]


def cut_shares(shapes):
    rows, ff = shapes[2][1], shapes[2][2]
    one = ff * 3 // 20 // 128 * 128
    two = ff * 33 // 40 // 128 * 128
    return [
        Share(2, one, (rows, two - one), 0),
        Share(3, 0, (shapes[3][1] // 2, shapes[3][2]), 2),
        Share(2, two, (rows, ff - two), 2),
        Share(0, 0, (rows, shapes[0][2] // 2), 1),
        Share(1, 0, (rows, shapes[1][2] // 2), 1),
        Share(2, 0, (rows, one), 1),
    ]


def reduce_kernel(topo, shares, *refs):
    grads, outs = refs[:5], refs[5:9]
    count = len(shares)
    groups = []
    at = 9
    for _ in range(7):
        groups.append(refs[at:at + count])
        at += count
    held, from_c, from_y, from_x, from_low, from_high, from_f = groups
    (load_sem, c_send, c_recv, y_send, y_recv, x_send, x_recv, z_send, z_recv, f_send, f_recv,
     o_send, o_recv, o_local) = refs[at:]
    x, y, z, c = coordinates(topo)
    X, Z, T = topo.X, topo.Z, topo.T
    g, me = lax.axis_index("grp"), lax.axis_index("tok")
    odd = lax.rem(y, 2)
    below, above = z > 0, z < Z - 1
    kind = pl.DeviceIdType.MESH

    def over_y(k):
        high = lax.rem(lax.div(y, 1 << k), 2)
        return {"grp": g + (2 - 4 * high) * (1 << k), "tok": me}

    over_c = {"grp": g + 1 - 2 * c, "tok": me}

    def over_z(k):
        return {"grp": g, "tok": (z + k) * X + x}

    def over_x(k):
        return {"grp": g, "tok": z * X + lax.rem(x + k, X)}

    barrier = pltpu.get_barrier_semaphore()
    partners = [over_c] + [over_y(k) for k in range(topo.bits["y"])]
    partners += [over_x(k) for k in range(1, X)]

    def greet(partner):
        pl.semaphore_signal(barrier, inc=1, device_id=partner, device_id_type=kind)

    for partner in partners:
        greet(partner)
    pl.when(below)(lambda: greet(over_z(-1)))
    pl.when(above)(lambda: greet(over_z(1)))
    every = range(count)

    def source(s, core, t, up):
        place = {2: 4 if up else 2, 3: 3}.get(s.array, s.array)
        return s.of(grads[place], core, t)

    def load(p, t, up=False):
        return pltpu.make_async_copy(
            source(shares[p], c, t, up), held[p].at[t], load_sem.at[p, t]
        )

    def start(p, make, up_core):
        if shares[p].array == 2:
            pl.when(c != up_core)(lambda: make(False).start())
            pl.when(c == up_core)(lambda: make(True).start())
        else:
            make(False).start()

    def remote(source, landing, send, recv, target):
        return pltpu.make_async_remote_copy(
            src_ref=source, dst_ref=landing, send_sem=send, recv_sem=recv, device_id=target,
            device_id_type=kind,
        )

    def c_copy(p, t, up=False):
        return remote(
            source(shares[p], 1 - c, t, up), from_c[p].at[t], c_send.at[p, t], c_recv.at[p, t],
            over_c,
        )

    def y_copy(p, t):
        return remote(
            held[p].at[t], from_y[p].at[t], y_send.at[p, t], y_recv.at[p, t], over_y(0)
        )

    def x_copy(p, zz, k):
        t = zz * X + lax.rem(x + k, X)
        return remote(
            held[p].at[t], from_x[p].at[zz, k - 1], x_send.at[p, zz, k - 1],
            x_recv.at[p, zz, k - 1], over_x(k),
        )

    def z_copy(p, zz, k):
        landing = from_low if k > 0 else from_high
        way = (k + 1) // 2
        return remote(
            held[p].at[zz * X + x], landing[p].at[zz], z_send.at[p, zz, way],
            z_recv.at[p, zz, way], over_z(k),
        )

    def f_copy(p, k):
        return remote(
            held[p].at[me], from_f[p].at[k], f_send.at[p, k], f_recv.at[p, k], over_y(k)
        )

    def result(s, core):
        if s.array == 2:
            return outs[2].at[core, :, pl.ds(s.start, s.shape[1])]
        return s.of(outs[s.array], core)

    def o_copy(p):
        s = shares[p]
        return remote(
            held[p].at[me], result(s, c), o_send.at[p], o_recv.at[p], over_c
        )

    def o_arrived(p):
        s = shares[p]
        return remote(
            held[p].at[me], result(s, 1 - c), o_send.at[p], o_recv.at[p], over_c
        )

    def o_keep(p):
        s = shares[p]
        return pltpu.make_async_copy(held[p].at[me], result(s, c), o_local.at[p])

    def add(p, t, other):
        held[p][t] = held[p][t] + other

    def layers(body):
        def step(i, carry):
            k = Z - 1 - i
            pl.when(z + k < Z)(lambda: body(z + k))
            pl.when((k > 0) & (z - k >= 0))(lambda: body(z - k))
            return carry
        return step

    def inside(p, body):
        if shares[p].part == 1:
            body()
        else:
            pl.when(odd == shares[p].part // 2)(body)

    def outside(p, body):
        if shares[p].part != 1:
            pl.when(odd != shares[p].part // 2)(body)

    def start_loads(zz):
        def each(j, carry):
            t = zz * X + lax.rem(x + j, X)
            for p in every:
                start(p, lambda up, p=p: load(p, t, up), 1)
            return carry
        lax.fori_loop(0, X, each, 0)

    lax.fori_loop(0, Z, layers(start_loads), 0)
    pl.semaphore_wait(barrier, len(partners) + below.astype(jnp.int32) + above.astype(jnp.int32))

    def start_cores(zz):
        def each(j, carry):
            t = zz * X + lax.rem(x + j, X)
            for p in every:
                start(p, lambda up, p=p: c_copy(p, t, up), 0)
            return carry
        lax.fori_loop(0, X, each, 0)

    lax.fori_loop(0, Z, layers(start_cores), 0)

    def cores(zz):
        def each(j, carry):
            t = zz * X + lax.rem(x + j + 1, X)
            for p in every:
                load(p, t).wait()
                c_copy(p, t).wait_recv()
                add(p, t, from_c[p][t])
                outside(p, lambda p=p: y_copy(p, t).start())
                if shares[p].part == 1:
                    for k in range(1, X):
                        pl.when(j + 1 == k)(lambda p=p, k=k: x_copy(p, zz, k).start())
            return carry
        lax.fori_loop(0, X, each, 0)

    lax.fori_loop(0, Z, layers(cores), 0)

    def over(zz):
        def each(j, carry):
            t = zz * X + lax.rem(x + j + 1, X)
            for p in every:
                if shares[p].part != 1:
                    def body(p=p):
                        y_copy(p, t).wait_recv()
                        add(p, t, from_y[p][t])
                        for k in range(1, X):
                            pl.when(j + 1 == k)(lambda: x_copy(p, zz, k).start())
                    inside(p, body)
            return carry
        lax.fori_loop(0, X, each, 0)

    def join(p, zz):
        t = zz * X + x
        for k in range(1, X):
            x_copy(p, zz, k).wait_recv()
            add(p, t, from_x[p][zz, k - 1])

        def low():
            z_copy(p, zz, 1).wait_recv()
            add(p, t, from_low[p][zz])

        def high():
            z_copy(p, zz, -1).wait_recv()
            add(p, t, from_high[p][zz])

        pl.when((zz >= z) & below)(low)
        pl.when((zz <= z) & above)(high)
        pl.when(zz > z)(lambda: z_copy(p, zz, 1).start())
        pl.when(zz < z)(lambda: z_copy(p, zz, -1).start())

    single = topo.bits["y"] == 1

    def first_joins(zz):
        for p in every:
            if shares[p].part == 1:
                join(p, zz)
                if single:
                    pl.when(zz == z)(lambda p=p: f_copy(p, 0).start())

    def last_joins(zz):
        for p in every:
            if shares[p].part != 1:
                def body(p=p):
                    join(p, zz)
                    if single:
                        pl.when(zz == z)(lambda: f_copy(p, 0).start())
                inside(p, body)

    def main(i, carry):
        @pl.when(i < Z)
        def _():
            layers(first_joins)(i, 0)
            layers(over)(i, 0)

        @pl.when(i > 0)
        def _():
            layers(last_joins)(i - 1, 0)

        return carry

    lax.fori_loop(0, Z + 1, main, 0)

    for k in range(1, topo.bits["y"]):
        for p in every:
            inside(p, lambda p=p: f_copy(p, k).start())
        for p in every:
            def fold(p=p):
                f_copy(p, k).wait()
                add(p, me, from_f[p][k])
            inside(p, fold)
    if not single:
        for p in every:
            inside(p, lambda p=p: f_copy(p, 0).start())
    for p in every:
        if shares[p].part == 1:
            f_copy(p, 0).wait()
            add(p, me, from_f[p][0])
        else:
            def take(p=p):
                f_copy(p, 0).wait_recv()
                held[p][me] = from_f[p][0]
            outside(p, lambda p=p: y_copy(p, me).wait_send())
            outside(p, take)
        o_copy(p).start()
        o_keep(p).start()

    def ends(t, carry):
        for p in every:
            c_copy(p, t).wait_send()
            outside(p, lambda p=p: pl.when(t != me)(lambda: y_copy(p, t).wait_send()))
        return carry

    lax.fori_loop(0, T, ends, 0)

    def z_ends(zz, carry):
        for p in every:
            def body(p=p):
                for k in range(1, X):
                    x_copy(p, zz, k).wait_send()
                pl.when(zz > z)(lambda: z_copy(p, zz, 1).wait_send())
                pl.when(zz < z)(lambda: z_copy(p, zz, -1).wait_send())
            inside(p, body)
        return carry

    lax.fori_loop(0, Z, z_ends, 0)
    for p in every:
        if shares[p].part != 1:
            inside(p, lambda p=p: f_copy(p, 0).wait_send())
        o_copy(p).wait_send()
        o_arrived(p).wait_recv()
        o_keep(p).wait()


def reduce_gradients(topo, grads):
    shares = cut_shares([v.shape for v in grads])
    X, Z, T = topo.X, topo.Z, topo.T
    n = len(shares)
    folds = max(1, topo.bits["y"])
    DMA = pltpu.SemaphoreType.DMA
    hbm = pl.BlockSpec(memory_space=pl.ANY)
    lead = [(T,), (T,), (T,), (Z, X - 1), (Z,), (Z,), (folds,)]
    rooms = [
        pltpu.VMEM(front + s.shape, BF)
        for front in lead for s in shares
    ]
    outs = [grads[0].shape[1:], grads[1].shape[1:], (2,) + grads[2].shape[1:], grads[3].shape[1:]]
    return pl.pallas_call(
        functools.partial(reduce_kernel, topo, shares),
        in_specs=[hbm] * 5,
        out_specs=[hbm] * 4,
        out_shape=[jax.ShapeDtypeStruct(s, BF) for s in outs],
        scratch_shapes=rooms + [
            DMA((n, T)), DMA((n, T)), DMA((n, T)), DMA((n, T)), DMA((n, T)),
            DMA((n, Z, X - 1)), DMA((n, Z, X - 1)), DMA((n, Z, 2)), DMA((n, Z, 2)),
            DMA((n, folds)), DMA((n, folds)), DMA((n,)), DMA((n,)), DMA((n,)),
        ],
        compiler_params=pltpu.CompilerParams(
            collective_id=1, has_side_effects=True, vmem_limit_bytes=60 << 20
        ),
        name="reduce_gradients",
    )(*grads)


def group_order(topo):
    return list(reversed(topo.keys("y"))) + topo.keys("c") + list(reversed(topo.keys("x")))


def group_gather(topo, arr, order):
    names = group_order(topo)
    held = []
    shape = arr.shape
    for key in order:
        place = sum(1 for h in held if names.index(h) < names.index(key))
        arr = double(topo, arr, key, place, True)
        held.append(key)
    return arr.reshape((topo.T,) + shape)


def group_scatter(topo, arr, order):
    names = group_order(topo)
    held = list(names)
    arr = arr.reshape((2,) * len(names) + arr.shape[1:])
    for key in order:
        arr = halve(topo, arr, key, held.index(key), True)
        held.remove(key)
    return arr


def small_layer(topo):
    return topo.X == 2 and topo.Y == 2


class Layer:
    def __init__(self, topo):
        self.topo = topo
        x, y, z, c = coordinates(topo)
        self.c = c
        far_x, far_y = 1 - x, 1 - y
        a = (x + c * (far_x - x), far_y + c * (y - far_y))
        b = (far_x + c * (x - far_x), y + c * (far_y - y))
        self.chips = [(x, y), a, b, (far_x, far_y)]
        self.z = z

    def pack(self, slot, core):
        x, y = self.chips[slot]
        return (y * 2 + core) * self.topo.X + x

    def device(self, slot, core):
        x, y = self.chips[slot]
        return {"grp": y * 2 + core, "tok": self.z * self.topo.X + x}

    def meet(self):
        barrier = pltpu.get_barrier_semaphore()
        for target in (self.device(1, self.c), self.device(2, self.c), self.device(0, 1 - self.c)):
            pl.semaphore_signal(
                barrier, inc=1, device_id=target, device_id_type=pl.DeviceIdType.MESH
            )
        pl.semaphore_wait(barrier, 3)


def remote_copy(source, landing, send, recv, target):
    return pltpu.make_async_remote_copy(
        src_ref=source, dst_ref=landing, send_sem=send, recv_sem=recv, device_id=target,
        device_id_type=pl.DeviceIdType.MESH,
    )


def group_gather_kernel(topo, count, *refs):
    mine, outs = refs[:count], refs[count:2 * count]
    local_sem, send_sem, recv_sem = refs[2 * count:]
    layer = Layer(topo)
    c = layer.c
    arrays = range(count)
    a, b, sibling = layer.device(1, c), layer.device(2, c), layer.device(0, 1 - c)
    own = layer.pack(0, c)

    def send(i, way, pack, target):
        landing = outs[i].at[pack]
        source = mine[i] if way in (0, 1, 3) else landing
        return remote_copy(source, landing, send_sem.at[i, way], recv_sem.at[i, pack], target)

    ways = [
        (0, own, a), (1, own, b), (2, layer.pack(1, c), b), (3, own, sibling),
        (4, layer.pack(1, c), sibling), (5, layer.pack(2, c), sibling),
        (6, layer.pack(3, c), sibling),
    ]

    def start(k):
        for i in arrays:
            send(i, *ways[k]).start()

    def arrived(pack):
        for i in arrays:
            send(i, 2, pack, sibling).wait_recv()

    keep = [pltpu.make_async_copy(mine[i], outs[i].at[own], local_sem.at[i]) for i in arrays]
    for copy in keep:
        copy.start()
    layer.meet()
    start(0)
    start(1)
    start(3)
    arrived(layer.pack(1, c))
    start(2)
    start(4)
    arrived(layer.pack(2, c))
    start(5)
    arrived(layer.pack(3, c))
    start(6)
    for slot in range(4):
        arrived(layer.pack(slot, 1 - c))
    for way in ways:
        for i in arrays:
            send(i, *way).wait_send()
    for copy in keep:
        copy.wait()


def gather_layer(topo, arrays, ident):
    DMA = pltpu.SemaphoreType.DMA
    hbm = pl.BlockSpec(memory_space=pl.ANY)
    n = len(arrays)
    return pl.pallas_call(
        functools.partial(group_gather_kernel, topo, n),
        in_specs=[hbm] * n,
        out_specs=[hbm] * n,
        out_shape=[jax.ShapeDtypeStruct((topo.T,) + v.shape, v.dtype) for v in arrays],
        scratch_shapes=[DMA((n,)), DMA((n, 7)), DMA((n, topo.T))],
        compiler_params=pltpu.CompilerParams(collective_id=ident, has_side_effects=True),
        name="gather_layer",
    )(*arrays)


def group_reduce_kernel(topo, grads, out, held, from_c, from_b, from_a, c_send, c_recv, send_sem,
                        recv_sem):
    layer = Layer(topo)
    c = layer.c
    a, b, sibling = layer.device(1, c), layer.device(2, c), layer.device(0, 1 - c)
    order = (3, 2, 1, 0)

    def c_copy(slot):
        theirs = (0, 2, 1, 3)[slot]
        return remote_copy(
            grads.at[layer.pack(slot, 1 - c)], from_c.at[theirs], c_send.at[theirs],
            c_recv.at[theirs], sibling,
        )

    def c_arrived(slot):
        remote_copy(
            grads.at[layer.pack(slot, c)], from_c.at[slot], c_send.at[slot], c_recv.at[slot],
            sibling,
        ).wait_recv()

    across = remote_copy(held.at[3], from_b.at[1], send_sem.at[0], recv_sem.at[0], b)
    direct = remote_copy(held.at[2], from_b.at[0], send_sem.at[1], recv_sem.at[1], b)
    passed = remote_copy(held.at[1], from_a, send_sem.at[2], recv_sem.at[2], a)

    layer.meet()
    for slot in (3, 1, 2, 0):
        c_copy(slot).start()
    for slot in order:
        c_arrived(slot)
        held[slot] = grads[layer.pack(slot, c)] + from_c[slot]
        if slot == 3:
            across.start()
        if slot == 2:
            direct.start()
    across.wait_recv()
    held[1] = held[1] + from_b[1]
    passed.start()
    direct.wait_recv()
    held[0] = held[0] + from_b[0]
    passed.wait_recv()
    out[...] = held[0] + from_a[...]
    across.wait_send()
    direct.wait_send()
    passed.wait_send()
    for slot in range(4):
        c_copy(slot).wait_send()


def reduce_layer(topo, grads, ident):
    DMA = pltpu.SemaphoreType.DMA
    block = grads.shape[1:]
    return pl.pallas_call(
        functools.partial(group_reduce_kernel, topo),
        in_specs=[pl.BlockSpec(memory_space=pltpu.VMEM)],
        out_specs=pl.BlockSpec(memory_space=pltpu.VMEM),
        out_shape=jax.ShapeDtypeStruct(block, BF),
        scratch_shapes=[
            pltpu.VMEM((4,) + block, BF), pltpu.VMEM((4,) + block, BF),
            pltpu.VMEM((2,) + block, BF), pltpu.VMEM(block, BF),
            DMA((4,)), DMA((4,)), DMA((3,)), DMA((3,)),
        ],
        compiler_params=pltpu.CompilerParams(
            collective_id=ident, has_side_effects=True, vmem_limit_bytes=32 << 20
        ),
        name="reduce_layer",
    )(grads)


NT = (((1,), (1,)), ((), ()))
TN = (((0,), (0,)), ((), ()))
LANES = 2 * HD
CHUNKS = (HEADS + 1) // 2
ROOM = 60 << 20


def lanes_of(rows):
    return lax.broadcasted_iota(jnp.int32, (rows, LANES), 1)


def spin(v):
    first = lax.rem(lanes_of(v.shape[0]), HD) < HD // 2
    return jnp.where(first, -pltpu.roll(v, LANES - HD // 2, 1), pltpu.roll(v, HD // 2, 1))


def whole(*shape):
    return pl.BlockSpec(shape, lambda *i: (0,) * len(shape))


def normed(v, gain):
    return v * lax.rsqrt(jnp.mean(v * v, axis=-1, keepdims=True) + EPS) * gain


def project_kernel(state_ref, w_ref, turn_ref, n1_ref, q_ref, kv_ref, small_ref):
    start = (CHUNKS - 1) * LANES
    small = jnp.transpose(w_ref[:, start:start + LANES].astype(F32))[HD:HD + 8]
    small_ref[...] = small
    project_into(
        state_ref[...].astype(F32), small[RECS:RECS + 1], w_ref, turn_ref, n1_ref, q_ref, kv_ref
    )


def project(state, w, turns):
    n, model = state.shape
    return pl.pallas_call(
        project_kernel,
        grid=(1,),
        in_specs=[whole(n, model), whole(*w.shape), whole(*turns.shape)],
        out_specs=[
            whole(n, model), whole(CHUNKS, n, LANES), whole(n, KV_HEADS * LANES),
            whole(8, model),
        ],
        out_shape=[
            jax.ShapeDtypeStruct((n, model), BF),
            jax.ShapeDtypeStruct((CHUNKS, n, LANES), BF),
            jax.ShapeDtypeStruct((n, KV_HEADS * LANES), BF),
            jax.ShapeDtypeStruct((8, model), F32),
        ],
        compiler_params=pltpu.CompilerParams(vmem_limit_bytes=ROOM),
        name="project",
    )(state, w, turns)


def attend_kernel(rows, recursion, span, key_ref, query_ref, kv_ref, q_ref, mixed_ref, out_ref, stat_ref,
                  stacked, mixing, tops, sums):
    low = lanes_of(rows) < HD
    wide = SHARES * rows
    for h in range(KV_HEADS):
        for j in range(SHARES):
            head = h * SHARES + j
            chunk = q_ref[head // 2].astype(F32)
            if head % 2:
                chunk = pltpu.roll(chunk, HD, 1)
            stacked[h, j * rows:(j + 1) * rows, :] = jnp.where(low, chunk, 0.0).astype(BF)
    mixing[...] = jnp.zeros(mixing.shape, F32)
    sums[...] = jnp.zeros(sums.shape, F32)
    tops[...] = jnp.full(tops.shape, BIG, F32)

    def body(t, carry):
        at = pl.ds(pl.multiple_of(t * rows, rows), rows)
        bias = block_bias(key_ref[t], query_ref, recursion, rows)
        def score(h):
            kv = kv_ref[at, h * LANES:(h + 1) * LANES]
            return lax.dot_general(kv, stacked[h], NT, preferred_element_type=F32) + bias

        def end(h, p, fade):
            kv = kv_ref[at, h * LANES:(h + 1) * LANES]
            mixing[h] = mixing[h] * fade + lax.dot_general(
                kv[:, HD:], p, TN, preferred_element_type=F32
            )

        ahead = score(0)
        before = None
        for h in range(KV_HEADS):
            s = ahead
            if h + 1 < KV_HEADS:
                ahead = score(h + 1)
            if before is not None:
                end(*before)
            old = tops[h, 0:1, :]
            top = jnp.max(s.reshape(rows // 8, 8, wide), axis=0)
            top = jnp.maximum(old, jnp.max(top, axis=0, keepdims=True))
            p = jnp.exp(s - top)
            fade = jnp.exp(old - top)
            sums[h] = sums[h] * fade + jnp.sum(p.reshape(rows // 8, 8, wide), axis=0)
            tops[h] = jnp.broadcast_to(top, (8, wide))
            before = (h, p.astype(BF), fade)
        end(*before)
        return carry

    lax.fori_loop(span[0], span[1], body, 0)
    for h in range(KV_HEADS):
        total = jnp.sum(sums[h], axis=0, keepdims=True)
        stat_ref[h] = tops[h] + jnp.log(total)
        mixing[h] = mixing[h] / total
    for j in range(CHUNKS):
        both = head_pair(mixing, j, rows)
        out_ref[j] = both
        size = min(LANES, HEADS * HD - j * LANES)
        mixed_ref[:, j * LANES:j * LANES + size] = both.astype(BF)[:, :size]


def block_bias(labels, query_ref, recursion, rows):
    keys = jnp.transpose(labels.astype(F32))[:rows]
    order, level = keys[:, 0:1], keys[:, 2:3]
    live = jnp.where(level > recursion, order, -1.0)
    place, begin = query_ref[0:1, :].astype(F32), query_ref[1:2, :].astype(F32)
    allowed = ((live >= begin) & (live <= place)) | (order == place)
    return jnp.where(allowed, 0.0, BIG)


def head_pair(mixing, j, rows):
    def one(head):
        if head >= HEADS:
            return jnp.zeros((HD, rows), F32)
        at = head % SHARES * rows
        return mixing[head // SHARES, :, at:at + rows]

    return jnp.transpose(jnp.concatenate([one(2 * j), one(2 * j + 1)], axis=0))


def attend(rows, recursion, span, key_labels, query_labels, kv_all, q):
    count, columns = kv_all.shape
    wide = SHARES * rows
    return pl.pallas_call(
        functools.partial(attend_kernel, rows, recursion),
        grid_spec=pltpu.PrefetchScalarGridSpec(
            num_scalar_prefetch=1,
            grid=(1,),
            in_specs=[
                whole(*key_labels.shape), whole(8, wide), whole(count, columns),
                whole(CHUNKS, rows, LANES),
            ],
            out_specs=[
                whole(rows, HEADS * HD), whole(CHUNKS, rows, LANES), whole(KV_HEADS, 8, wide),
            ],
            scratch_shapes=[
                pltpu.VMEM((KV_HEADS, wide, LANES), BF), pltpu.VMEM((KV_HEADS, HD, wide), F32),
                pltpu.VMEM((KV_HEADS, 8, wide), F32), pltpu.VMEM((KV_HEADS, 8, wide), F32),
            ],
        ),
        out_shape=[
            jax.ShapeDtypeStruct((rows, HEADS * HD), BF),
            jax.ShapeDtypeStruct((CHUNKS, rows, LANES), F32),
            jax.ShapeDtypeStruct((KV_HEADS, 8, wide), F32),
        ],
        compiler_params=pltpu.CompilerParams(vmem_limit_bytes=62 << 20),
        cost_estimate=pl.CostEstimate(
            flops=16 * KV_HEADS * wide * count * HD, bytes_accessed=4 * count * columns,
            transcendentals=KV_HEADS * wide * count,
        ),
        name="attend",
    )(span, key_labels, query_labels, kv_all, q)


def attend_back_kernel(rows, recursion, span, key_ref, query_ref, kv_ref, q_ref, d_ref, out_ref, stat_ref,
                       turn_ref, dq_ref, dkv_ref, stacked, part, mixing, deltas):
    low = lanes_of(rows) < HD
    wide = SHARES * rows
    ones = jnp.ones((8, LANES), BF)
    for h in range(KV_HEADS):
        for j in range(SHARES):
            head = h * SHARES + j
            q = q_ref[head // 2].astype(F32)
            d = d_ref[head // 2].astype(F32)
            if head % 2:
                q = pltpu.roll(q, HD, 1)
            product = d * out_ref[head // 2]
            mine = ~low if head % 2 else low
            if head % 2 == 0:
                d = pltpu.roll(d, HD, 1)
            at = pl.ds(j * rows, rows)
            stacked[h, at, :] = jnp.where(low, q, d).astype(BF)
            part[at, :] = jnp.where(mine, product, 0.0)
        coarse = part[...].astype(BF)
        fine = (part[...] - coarse.astype(F32)).astype(BF)
        deltas[h] = lax.dot_general(
            ones, coarse, NT, preferred_element_type=F32
        ) + lax.dot_general(ones, fine, NT, preferred_element_type=F32)
    dkv_ref[...] = jnp.zeros(dkv_ref.shape, BF)
    mixing[...] = jnp.zeros(mixing.shape, F32)

    def body(t, carry):
        at = pl.ds(pl.multiple_of(t * rows, rows), rows)
        bias = block_bias(key_ref[t], query_ref, recursion, rows)
        for h in range(KV_HEADS):
            kv = kv_ref[at, h * LANES:(h + 1) * LANES]
            zero = jnp.zeros_like(kv)
            queries = stacked[h]
            s = lax.dot_general(jnp.where(low, kv, zero), queries, NT, preferred_element_type=F32)
            p = jnp.exp(s + bias - stat_ref[h, 0:1, :])
            dp = lax.dot_general(jnp.where(low, zero, kv), queries, NT, preferred_element_type=F32)
            ds = (p * (dp - deltas[h, 0:1, :])).astype(BF)
            dk = jnp.dot(ds, queries, preferred_element_type=F32)
            dv = jnp.dot(p.astype(BF), queries, preferred_element_type=F32)
            dkv_ref[at, h * LANES:(h + 1) * LANES] = jnp.where(low, dk, dv).astype(BF)
            mixing[h] += lax.dot_general(kv[:, :HD], ds, TN, preferred_element_type=F32)
        return carry

    lax.fori_loop(span[0], span[1], body, 0)
    cosine, sine = turn_ref[0], turn_ref[1]
    for j in range(CHUNKS):
        both = head_pair(mixing, j, rows) * HD ** -0.5
        both = both * cosine - spin(both) * sine
        dq_ref[:, j * LANES:(j + 1) * LANES] = both.astype(BF)


def attend_back(rows, recursion, span, key_labels, query_labels, kv_all, q, d_mixed, out, stat, turns):
    count, columns = kv_all.shape
    wide = SHARES * rows
    return pl.pallas_call(
        functools.partial(attend_back_kernel, rows, recursion),
        grid_spec=pltpu.PrefetchScalarGridSpec(
            num_scalar_prefetch=1,
            grid=(1,),
            in_specs=[
                whole(*key_labels.shape), whole(8, wide), whole(count, columns),
                whole(CHUNKS, rows, LANES), whole(CHUNKS, rows, LANES),
                whole(CHUNKS, rows, LANES), whole(KV_HEADS, 8, wide), whole(2, rows, LANES),
            ],
            out_specs=[whole(rows, CHUNKS * LANES), whole(count, columns)],
            scratch_shapes=[
                pltpu.VMEM((KV_HEADS, wide, LANES), BF), pltpu.VMEM((wide, LANES), F32),
                pltpu.VMEM((KV_HEADS, HD, wide), F32), pltpu.VMEM((KV_HEADS, 8, wide), F32),
            ],
        ),
        out_shape=[
            jax.ShapeDtypeStruct((rows, CHUNKS * LANES), BF),
            jax.ShapeDtypeStruct((count, columns), BF),
        ],
        compiler_params=pltpu.CompilerParams(vmem_limit_bytes=62 << 20),
        name="attend_back",
    )(span, key_labels, query_labels, kv_all, q, d_mixed, out, stat, turns)


def out_back_kernel(d_ref, w_ref, out_ref):
    d = d_ref[...]
    for j in range(CHUNKS):
        size = min(LANES, w_ref.shape[0] - j * LANES)
        v = lax.dot_general(
            d, w_ref[j * LANES:j * LANES + size, :], NT, preferred_element_type=F32
        ).astype(BF)
        if size < LANES:
            v = jnp.concatenate([v, jnp.zeros((d.shape[0], LANES - size), BF)], axis=1)
        out_ref[j] = v


def project_back_kernel(gradient_ref, state_ref, small_ref, w_ref, turn_ref, dq_ref, raw_ref,
                        grad_ref, joint_ref, dgain_ref):
    cosine, sine = turn_ref[0], turn_ref[1]
    key = lanes_of(dq_ref.shape[0]) < HD
    for j in range(KV_HEADS):
        v = raw_ref[:, j * LANES:(j + 1) * LANES].astype(F32)
        turned = v * cosine - spin(v) * sine
        at = (CHUNKS + j) * LANES
        joint_ref[:, at:at + LANES] = jnp.where(key, turned, v).astype(BF)
    split, full = CHUNKS * LANES, w_ref.shape[1]
    joint_ref[:, :split] = dq_ref[...]
    if joint_ref.shape[1] > full:
        joint_ref[:, full:] = jnp.zeros((key.shape[0], joint_ref.shape[1] - full), BF)
    d = lax.dot_general(joint_ref[:, :full], w_ref[...], NT, preferred_element_type=F32)
    v = state_ref[...].astype(F32)
    inv = lax.rsqrt(jnp.mean(v * v, axis=-1, keepdims=True) + EPS)
    scaled = d * small_ref[RECS:RECS + 1, :]
    dot = jnp.mean(scaled * v, axis=-1, keepdims=True)
    grad_ref[...] = gradient_ref[...] + inv * scaled - v * (inv * inv * inv * dot)
    dgain_ref[...] = jnp.sum(d * v * inv, axis=0, keepdims=True)


def project_back(gradient, state, small, w, turns, dq, dkv):
    n, model = dq.shape[0], state.shape[1]
    joint = -(-w.shape[1] // 256) * 256
    return pl.pallas_call(
        project_back_kernel,
        grid=(1,),
        in_specs=[
            whole(n, model), whole(n, model), whole(8, model), whole(*w.shape),
            whole(2, n, LANES), whole(*dq.shape), whole(*dkv.shape),
        ],
        out_specs=[whole(n, model), whole(n, joint), whole(1, model)],
        out_shape=[
            jax.ShapeDtypeStruct((n, model), F32),
            jax.ShapeDtypeStruct((n, joint), BF),
            jax.ShapeDtypeStruct((1, model), F32),
        ],
        compiler_params=pltpu.CompilerParams(vmem_limit_bytes=ROOM),
        name="project_back",
    )(gradient, state, small, w, turns, dq, dkv)


def project_into(state, gain, w_ref, turn_ref, n1_ref, q_ref, kv_ref):
    n1 = normed(state, gain).astype(BF)
    n1_ref[...] = n1
    rows = n1.shape[0]
    cosine, sine = turn_ref[0, :rows], turn_ref[1, :rows]
    key = lanes_of(rows) < HD
    columns = w_ref.shape[1]
    for start in range(0, columns, 2 * LANES):
        wide = min(2 * LANES, columns - start)
        both = jnp.dot(n1, w_ref[:, start:start + wide], preferred_element_type=F32)
        for half in range(wide // LANES):
            j = start // LANES + half
            v = both[:, half * LANES:(half + 1) * LANES]
            turned = v * cosine + spin(v) * sine
            if j < CHUNKS:
                q_ref[j] = (turned * HD ** -0.5).astype(BF)
            else:
                j -= CHUNKS
                kv_ref[:, j * LANES:(j + 1) * LANES] = jnp.where(key, turned, v).astype(BF)


def active_column(label_ref, recursion, rows):
    level = jnp.transpose(label_ref[...].astype(F32))[:rows, 2:3]
    return jnp.where(level > recursion, 1.0, 0.0)


def feed_kernel(recursion, following, mixed_ref, state_ref, w_out_ref, small_ref, label_ref,
                w_gate_ref, w_up_ref, w_down_ref, *refs):
    if following:
        w_ref, turn_ref = refs[:2]
        refs = refs[2:]
    (new_ref, middle_ref, n2_ref, gated_ref, up_ref, hidden_ref, both_ref, gate_ref) = refs[:8]
    step = pl.program_id(0)

    @pl.when(step == 0)
    def _():
        att = jnp.dot(mixed_ref[...], w_out_ref[...], preferred_element_type=F32)
        middle = state_ref[...].astype(F32) + att
        middle_ref[...] = middle
        n2_ref[...] = normed(middle, small_ref[RECS + 1:RECS + 2, :]).astype(BF)
        both_ref[...] = att

    n2 = n2_ref[...]
    gated = jnp.dot(n2, w_gate_ref[...], preferred_element_type=F32)
    upward = jnp.dot(n2, w_up_ref[...], preferred_element_type=F32)
    hidden = (gated * jax.nn.sigmoid(gated) * upward).astype(BF)
    gated_ref[...] = gated.astype(BF)
    up_ref[...] = upward.astype(BF)
    hidden_ref[...] = hidden
    both_ref[...] += jnp.dot(hidden, w_down_ref[...], preferred_element_type=F32)

    @pl.when(step == pl.num_programs(0) - 1)
    def _():
        state = state_ref[...].astype(F32)
        router = small_ref[recursion:recursion + 1, :]
        gate = jax.nn.sigmoid(jnp.sum(state * router, axis=-1, keepdims=True))
        active = active_column(label_ref, recursion, state.shape[0])
        gate_ref[...] = gate
        new_ref[...] = state + active * gate * both_ref[...]
        if following:
            project_into(
                new_ref[:following, :], small_ref[RECS:RECS + 1, :], w_ref, turn_ref, *refs[8:11]
            )


def feed(recursion, mixed, state, w_out, small, labels, w_gate, w_up, w_down, following, then=()):
    n, model = mixed.shape
    ff = w_gate.shape[1]
    tile = ff // 2 if ff % 256 == 0 else ff
    across = pl.BlockSpec((model, tile), lambda i: (0, i))
    made = pl.BlockSpec((n, tile), lambda i: (0, i))
    out_specs = [
        whole(n, model), whole(n, model), whole(n, model), made, made, made, whole(n, model),
        whole(n, 1),
    ]
    wide = lambda dtype: jax.ShapeDtypeStruct((n, model), dtype)
    tall = jax.ShapeDtypeStruct((n, ff), BF)
    out_shape = [
        wide(F32), wide(F32), wide(BF), tall, tall, tall, wide(F32),
        jax.ShapeDtypeStruct((n, 1), F32),
    ]
    if following:
        shapes = [(following, model), (CHUNKS, following, LANES), (following, KV_HEADS * LANES)]
        out_specs += [whole(*s) for s in shapes]
        out_shape += [jax.ShapeDtypeStruct(s, BF) for s in shapes]
    return pl.pallas_call(
        functools.partial(feed_kernel, recursion, following),
        grid=(ff // tile,),
        in_specs=[
            whole(n, model), whole(n, model), whole(*w_out.shape), whole(8, model),
            whole(*labels.shape), across, across,
            pl.BlockSpec((tile, model), lambda i: (i, 0)),
        ] + ([whole(*then[0].shape), whole(2, following, LANES)] if following else []),
        out_specs=out_specs,
        out_shape=out_shape,
        compiler_params=pltpu.CompilerParams(vmem_limit_bytes=ROOM),
        cost_estimate=pl.CostEstimate(
            flops=2 * n * model * (model + 3 * ff), transcendentals=n * ff,
            bytes_accessed=2 * model * (model + 3 * ff) + 24 * n * model + 6 * n * ff,
        ),
        name="feed",
    )(mixed, state, w_out, small, labels, w_gate, w_up, w_down, *then)


def feed_back_kernel(recursion, gradient_ref, both_ref, gate_ref, label_ref, state_ref,
                     small_ref, middle_ref, w_out_ref, gated_ref, up_ref, w_gate_ref, w_up_ref,
                     w_down_ref, d_fed_ref, d_gated_ref, d_up_ref, d_att_ref, grad_ref,
                     d_mixed_ref, d_router_ref, d_gain_ref, total):
    step = pl.program_id(0)

    @pl.when(step == 0)
    def _():
        active = active_column(label_ref, recursion, gate_ref.shape[0])
        d_fed_ref[...] = (active * gate_ref[...] * gradient_ref[...].astype(F32)).astype(BF)
        total[...] = jnp.zeros(total.shape, F32)

    d_hidden = lax.dot_general(d_fed_ref[...], w_down_ref[...], NT, preferred_element_type=F32)
    gated, upward = gated_ref[...].astype(F32), up_ref[...].astype(F32)
    sig = jax.nn.sigmoid(gated)
    part = d_hidden * sig
    d_up = (part * gated).astype(BF)
    d_gated = (part * upward * (1.0 + gated * (1.0 - sig))).astype(BF)
    d_up_ref[...] = d_up
    d_gated_ref[...] = d_gated
    total[...] += lax.dot_general(
        d_gated, w_gate_ref[...], NT, preferred_element_type=F32
    ) + lax.dot_general(d_up, w_up_ref[...], NT, preferred_element_type=F32)

    @pl.when(step == pl.num_programs(0) - 1)
    def _():
        gradient, gate = gradient_ref[...].astype(F32), gate_ref[...]
        active = active_column(label_ref, recursion, gate.shape[0])
        router = small_ref[recursion:recursion + 1, :]
        d = total[...]
        v = middle_ref[...]
        inv = lax.rsqrt(jnp.mean(v * v, axis=-1, keepdims=True) + EPS)
        d_gain_ref[...] = jnp.sum(d * v * inv, axis=0, keepdims=True)
        scaled = d * small_ref[RECS + 1:RECS + 2, :]
        dot = jnp.mean(scaled * v, axis=-1, keepdims=True)
        d_middle = inv * scaled - v * (inv * inv * inv * dot)
        d_gate = active * gate * (1.0 - gate) * jnp.sum(
            gradient * both_ref[...], axis=-1, keepdims=True
        )
        d_router_ref[...] = jnp.sum(state_ref[...].astype(F32) * d_gate, axis=0, keepdims=True)
        grad_ref[...] = gradient + d_gate * router + d_middle
        d_att_ref[...] = (active * gate * gradient + d_middle).astype(BF)
        out_back_kernel(d_att_ref, w_out_ref, d_mixed_ref)


def feed_back(recursion, gradient, both, gate, labels, state, small, middle, w_out, gated, upward,
              w_gate, w_up, w_down):
    n, model = both.shape
    ff = w_gate.shape[1]
    tile = ff // 2 if ff % 256 == 0 else ff
    across = pl.BlockSpec((model, tile), lambda i: (0, i))
    made = pl.BlockSpec((n, tile), lambda i: (0, i))
    wide = whole(n, model)
    flat = lambda dtype: jax.ShapeDtypeStruct((n, model), dtype)
    tall = jax.ShapeDtypeStruct((n, ff), BF)
    row = jax.ShapeDtypeStruct((1, model), F32)
    return pl.pallas_call(
        functools.partial(feed_back_kernel, recursion),
        grid=(ff // tile,),
        in_specs=[
            wide, wide, whole(n, 1), whole(*labels.shape), wide, whole(8, model), wide,
            whole(*w_out.shape), made, made, across, across,
            pl.BlockSpec((tile, model), lambda i: (i, 0)),
        ],
        out_specs=[
            wide, made, made, wide, wide, whole(CHUNKS, n, LANES), whole(1, model),
            whole(1, model),
        ],
        out_shape=[
            flat(BF), tall, tall, flat(BF), flat(F32),
            jax.ShapeDtypeStruct((CHUNKS, n, LANES), BF), row, row,
        ],
        scratch_shapes=[pltpu.VMEM((n, model), F32)],
        compiler_params=pltpu.CompilerParams(vmem_limit_bytes=ROOM),
        cost_estimate=pl.CostEstimate(
            flops=2 * n * model * (model + 3 * ff), transcendentals=n * ff,
            bytes_accessed=2 * model * (model + 3 * ff) + 24 * n * model + 8 * n * ff,
        ),
        name="feed_back",
    )(gradient, both, gate, labels, state, small, middle, w_out, gated, upward, w_gate, w_up,
      w_down)


def outer_rows_kernel(count, *refs):
    xs, ds, out_ref = refs[:count], refs[count:2 * count], refs[2 * count]
    total = None
    for x_ref, d_ref in zip(xs, ds):
        part = jnp.dot(jnp.transpose(x_ref[...]), d_ref[...], preferred_element_type=F32)
        total = part if total is None else total + part
    out_ref[...] = total.astype(BF)


def outer_rows(xs, ds, tile):
    rows, columns = xs[0].shape[1], ds[0].shape[1]
    tokens = sum(x.shape[0] for x in xs)
    return pl.pallas_call(
        functools.partial(outer_rows_kernel, len(xs)),
        grid=(rows // tile,),
        in_specs=[pl.BlockSpec((x.shape[0], tile), lambda i: (0, i)) for x in xs]
        + [whole(*d.shape) for d in ds],
        out_specs=pl.BlockSpec((tile, columns), lambda i: (i, 0)),
        out_shape=jax.ShapeDtypeStruct((rows, columns), BF),
        compiler_params=pltpu.CompilerParams(vmem_limit_bytes=ROOM),
        cost_estimate=pl.CostEstimate(
            flops=2 * tokens * rows * columns, transcendentals=0,
            bytes_accessed=2 * (tokens * (columns + rows) + rows * columns),
        ),
        name="outer_rows",
    )(*xs, *ds)


def finish_kernel(onehot_ref, final_ref, gradient_ref, qkv_ref, o_ref, gu_ref, down_ref,
                  block_ref, token_ref, query_ref, key_ref, value_ref, out_ref, gate_ref, up_ref,
                  gdown_ref, tiny_ref):
    onehot = onehot_ref[...]
    block_ref[...] = lax.dot_general(
        final_ref[...], onehot, TN, preferred_element_type=F32
    ).astype(BF)
    token_ref[...] = lax.dot_general(
        gradient_ref[...], onehot, TN, preferred_element_type=F32
    ).astype(BF)
    model = query_ref.shape[1]
    query_ref[...] = qkv_ref[:, :model].astype(F32)
    out_ref[...] = o_ref[:, :model].astype(F32)
    rows = query_ref.shape[0]
    room = jnp.zeros((-rows % LANES, LANES), F32)

    def across(v):
        return jnp.transpose(jnp.concatenate([v, room], axis=0))[:, :rows]

    tiny = jnp.concatenate(
        [o_ref[:, model:].astype(F32), jnp.zeros((rows, LANES - HD), F32)], axis=1
    )
    tiny_ref[...] = across(tiny)[:8]
    gate_ref[...] = gu_ref[0].astype(F32)
    up_ref[...] = gu_ref[1].astype(F32)
    gdown_ref[...] = down_ref[...].astype(F32)
    low = lanes_of(rows) < HD
    heads = [
        qkv_ref[:, (CHUNKS + h) * LANES:(CHUNKS + h + 1) * LANES].astype(F32)
        for h in range(KV_HEADS)
    ]
    for h in range(0, KV_HEADS, 2):
        even, odd = heads[h], heads[min(h + 1, KV_HEADS - 1)]
        at = slice(h * HD, min(h + 2, KV_HEADS) * HD)
        size = at.stop - at.start
        key_ref[at, :] = across(jnp.where(low, even, pltpu.roll(odd, HD, 1)))[:size]
        value_ref[at, :] = across(jnp.where(low, pltpu.roll(even, HD, 1), odd))[:size]


def finish(onehot, final, gradient, qkv, o, gu, down):
    rows, model = final.shape
    shard, ff = gu.shape[1:]
    kv = KV_HEADS * HD
    shapes = [
        (model, rows), (model, rows), (shard, model), (kv, shard), (kv, shard), (shard, model),
        (shard, ff), (shard, ff), down.shape, (8, shard),
    ]
    args = (onehot, final, gradient, qkv, o, gu, down)
    return pl.pallas_call(
        finish_kernel,
        grid=(1,),
        in_specs=[whole(*v.shape) for v in args],
        out_specs=[whole(*v) for v in shapes],
        out_shape=[jax.ShapeDtypeStruct(v, BF if i < 2 else F32) for i, v in enumerate(shapes)],
        compiler_params=pltpu.CompilerParams(vmem_limit_bytes=ROOM),
        name="finish",
    )(*args)


def mm(a, b):
    return jnp.dot(a, b, preferred_element_type=F32)


def mm_tn(a, b):
    return lax.dot_general(a, b, TN, preferred_element_type=F32)


def per_device(topo, *args):
    (tokens, w_query, w_key, w_value, w_out, w_gate, w_up, w_down, router, norm_attn, norm_ffn,
     lengths, depths, padding, cotangent) = args
    rows, model = tokens.shape
    kv_cols = w_key.shape[1]
    ff = w_gate.shape[1]
    shard = w_query.shape[0]
    deep_rows = rows * 3 // 4
    xk, yk, ck = (topo.keys(d) for d in "xyc")

    small = jnp.concatenate([router, norm_attn[:, None], norm_ffn[:, None]], axis=1)
    small = jnp.pad(small, ((0, 0), (0, HD - small.shape[1])))
    w_kv = jnp.stack(
        [w_key.reshape(shard, KV_HEADS, HD), w_value.reshape(shard, KV_HEADS, HD)], axis=2
    ).reshape(shard, 2 * kv_cols)
    first = jnp.concatenate([w_query, small, w_kv], axis=1)
    weight_qkv, weight_g, weight_u, weight_d, weight_o = gather_weights(
        topo, [first, w_gate, w_up, w_down, w_out]
    )

    own = lax.axis_index("tok") * rows + jnp.arange(rows, dtype=jnp.int32)
    eligible = (depths >= 2) & (padding > 0)
    flags = jnp.stack([eligible, ~eligible]).astype(BF)
    upto = (jnp.arange(rows)[:, None] <= jnp.arange(rows)[None, :]).astype(BF)
    counts = mm(flags, upto).astype(jnp.int32)
    slot = jnp.where(eligible, counts[0] - 1, counts[0, -1] + counts[1] - 1)
    chosen = jnp.arange(rows, dtype=jnp.int32)[:, None] == slot[None, :]
    onehot = chosen.astype(BF)
    doc_ends = jnp.cumsum(lengths[0])
    begins = jnp.sum(
        jnp.where(own[:, None] >= doc_ends[None, :], lengths[0][None, :], 0), axis=1
    )
    levels = jnp.where(padding > 0, depths, 0)
    labels = jnp.stack([own, begins, levels])
    labels = jnp.sum(jnp.where(chosen[None], labels[:, None, :], 0), axis=2)
    labels = jnp.pad(labels, ((0, 5), (0, 0)))
    swap = topo.swap_pairs()
    state = lax.ppermute(mm(onehot, tokens).astype(BF), AXES, swap)
    labels = lax.ppermute(labels, AXES, swap)
    cotangent = mm(onehot, cotangent).astype(BF)

    def collect(arrays, ident):
        if small_layer(topo):
            return gather_layer(topo, arrays, ident)
        return [group_gather(topo, v, xk + yk + ck) for v in arrays]

    def distribute(grads, ident):
        if small_layer(topo):
            return reduce_layer(topo, grads, ident)
        return group_scatter(topo, grads, ck + yk + xk)


    pack = (lax.axis_index("grp") * topo.X) + lax.axis_index("tok") % topo.X
    lowest = jnp.min(labels[1])
    span = jnp.stack([lowest // rows, pack + 1]).astype(jnp.int32)
    places = (labels[0] - labels[1]).astype(F32)
    turn = (jnp.arange(LANES) % (HD // 2)).astype(F32)
    freqs = 10000.0 ** (-(turn * 2.0 / HD))
    angles = places[:, None] * freqs[None, :]
    turns = jnp.stack([jnp.cos(angles), jnp.sin(angles)])
    query_labels = {
        n: jnp.concatenate([labels[:, :n]] * SHARES, axis=1) for n in (rows, deep_rows)
    }

    def forward(state, projected, recursion, labels_all=None, pending=None):
        extra = None
        n1, q, kv = projected
        n = n1.shape[0]
        if recursion == 0:
            kv_all, labels_all = collect([kv, labels], 2)
            kv_all, later = lax.optimization_barrier((kv_all, cotangent))
            later = lax.ppermute(later, AXES, swap)
        else:
            kv_all, = collect([kv], 3)
        kv_all = kv_all.reshape(topo.T * n, 2 * kv_cols)
        mixed, out, stat = attend(n, recursion, span, labels_all, query_labels[n], kv_all, q)
        if recursion == 0:
            extra = (labels_all, later)
        if pending is not None:
            mixed, extra = lax.optimization_barrier((mixed, pending))
        following = deep_rows if recursion + 1 < RECS else 0
        new, middle, n2, gated, upward, hidden, both, gate, *projected = feed(
            recursion, mixed, state, weight_o, small, labels, weight_g, weight_u, weight_d,
            following, (weight_qkv, turns) if following else (),
        )
        kept = (state, n1, q, kv_all, labels_all, out, stat, mixed, middle, n2, gated, upward,
                hidden, both, gate)
        return (new, projected, kept, extra)

    def backward(gradient, recursion, kept):
        (state, n1, q, kv_all, labels_all, out, stat, mixed, middle, n2, gated, upward, hidden,
         both, gate) = kept
        n = n1.shape[0]
        d_fed, d_gated, d_up, d_att, gradient, d_mixed, d_router, d_gain_two = feed_back(
            recursion, gradient, both, gate, labels, state, small, middle, weight_o, gated,
            upward, weight_g, weight_u, weight_d,
        )
        dq, dkv = attend_back(
            n, recursion, span, labels_all, query_labels[n], kv_all, q, d_mixed, out, stat, turns
        )
        dkv = distribute(dkv.reshape(topo.T, n, 2 * kv_cols), 5 if recursion else 4)
        gradient, dqkv, d_gain_one = project_back(
            gradient, state, small, weight_qkv, turns, dq, dkv
        )
        left = (n1, dqkv, mixed, d_att, n2, d_gated, d_up, hidden, d_fed)
        return (gradient, left, (d_router[0], d_gain_one[0], d_gain_two[0]))

    *projected, small = project(state, weight_qkv, turns)
    whole_state, projected, kept, (labels_all, gradient) = forward(state, projected, 0)
    deep = whole_state
    all_kept = [kept]
    for recursion in range(1, RECS):
        pending = gradient if recursion == 1 else None
        deep, projected, kept, extra = forward(deep, projected, recursion, labels_all, pending)
        gradient = extra if recursion == 1 else gradient
        all_kept.append(kept)
    final = jnp.concatenate([deep, whole_state[deep_rows:]], axis=0).astype(BF)

    deep_grad = gradient
    lefts, smalls = [], []
    for recursion in reversed(range(1, RECS)):
        deep_grad, left, tiny = backward(deep_grad, recursion, all_kept[recursion])
        lefts.append(left)
        smalls.append(tiny)
    deep_grad, final = lax.optimization_barrier((deep_grad, lax.ppermute(final, AXES, swap)))
    gradient = jnp.concatenate([deep_grad, gradient[deep_rows:].astype(F32)], axis=0)
    gradient, left, tiny = backward(gradient, 0, all_kept[0])
    lefts.append(left)
    smalls.append(tiny)
    gradient = lax.ppermute(gradient.astype(BF), AXES, swap)

    n1, dqkv, mixed, d_att, n2, d_gated, d_up, hidden, d_fed = zip(*lefts)

    def outer(xs, ds):
        return mm_tn(jnp.concatenate(xs, axis=0), jnp.concatenate(ds, axis=0))

    cut = lambda v: v.astype(BF).reshape(topo.T, -1, v.shape[-1])
    tiny = jnp.stack(
        [smalls[2][0], smalls[1][0], smalls[0][0],
         smalls[0][1] + smalls[1][1] + smalls[2][1],
         smalls[0][2] + smalls[1][2] + smalls[2][2]], axis=1
    )
    wide_out = -(-(model + tiny.shape[1]) // 256) * 256
    tiny = jnp.pad(tiny, ((0, 0), (0, wide_out - model - tiny.shape[1])))
    grad_qkv, grad_o, grad_gu, grad_down = reduce_gradients(topo, [
        cut(outer(n1, dqkv)),
        cut(jnp.concatenate([outer(mixed, d_att), tiny], axis=1)),
        cut(outer(n2, d_gated)),
        outer_rows(hidden, d_fed, 1280).reshape(topo.T, -1, model),
        cut(outer(n2, d_up)),
    ])
    block, token, grad_query, grad_key, grad_value, *others, tiny = finish(
        onehot, final, gradient, grad_qkv, grad_o, grad_gu, grad_down
    )
    return (block.T, token.T, grad_query, grad_key.T, grad_value.T) + tuple(others) + (
        tiny[:RECS].T, tiny[RECS], tiny[RECS + 1]
    )


def solution(mesh):
    topo = Topo(mesh.shape["grp"], mesh.shape["tok"])
    both = P(("grp", "tok"))
    wide = P(("grp", "tok"), None)
    rows = P("tok", None)
    row = P("tok")
    return jax.shard_map(
        functools.partial(per_device, topo),
        mesh=mesh,
        in_specs=(wide,) + (rows,) * 8 + (row, row, P("grp", None), both, both, wide),
        out_specs=(wide, wide) + (rows,) * 8 + (row, row),
        check_vma=False,
    )
```
